32 devices in a mesh: dp: 8 (over y, x, core), ctx: 4 (over z).
Axes of the slice: x: 2, y: 2, z: 4, core: 2. Of those that a mesh axis runs over, the one named last changes fastest.
Arguments:
- activations: bfloat16 [8, 1024, 1024], P('dp', 'ctx'), may hold values from -6 to 6
- block_ids: int32 [8, 1024], P('dp'), may hold values from 0 to 7, never falling along the last dimension, each value on 1 to 256 neighbouring positions
- cotangent: bfloat16 [8, 1024, 1024], P('dp', 'ctx'), may hold values from -6 to 6
- w_query: bfloat16 [1024, 1024], P(('dp', 'ctx'))
- w_key: bfloat16 [1024, 1024], P(('dp', 'ctx')), may hold values from -0.1875 to 0.1875
- w_value: bfloat16 [1024, 1024], P(('dp', 'ctx')), may hold values from -0.1875 to 0.1875
- w_out: bfloat16 [1024, 1024], P(('dp', 'ctx')), may hold values from -0.75 to 0.75
- w_gate: bfloat16 [1024, 2816], P(('dp', 'ctx')), may hold values from -0.1875 to 0.1875
- w_up: bfloat16 [1024, 2816], P(('dp', 'ctx')), may hold values from -0.1875 to 0.1875
- w_down: bfloat16 [2816, 1024], P(('dp', 'ctx')), may hold values from -0.109375 to 0.109375
- m_query: float32 [1024, 1024], P(('dp', 'ctx')), may hold values from -512 to 512
- m_key: float32 [1024, 1024], P(('dp', 'ctx')), may hold values from -512 to 512
- m_value: float32 [1024, 1024], P(('dp', 'ctx')), may hold values from -512 to 512
- m_out: float32 [1024, 1024], P(('dp', 'ctx')), may hold values from -512 to 512
- m_gate: float32 [1024, 2816], P(('dp', 'ctx')), may hold values from -512 to 512
- m_up: float32 [1024, 2816], P(('dp', 'ctx')), may hold values from -512 to 512
- m_down: float32 [2816, 1024], P(('dp', 'ctx')), may hold values from -512 to 512
- clip_threshold: float32 [], replicated, may hold values from 2.5 to 4.5
- momentum_coeff: float32 [], replicated, may hold values from 0.5 to 0.95
Outputs:
- layer_out: bfloat16 [8, 1024, 1024], P('dp', 'ctx')
- input_grad: float32 [8, 1024, 1024], P('dp', 'ctx')
- grad_query: float32 [1024, 1024], P(('dp', 'ctx'))
- grad_key: float32 [1024, 1024], P(('dp', 'ctx'))
- grad_value: float32 [1024, 1024], P(('dp', 'ctx'))
- grad_out: float32 [1024, 1024], P(('dp', 'ctx'))
- grad_gate: float32 [1024, 2816], P(('dp', 'ctx'))
- grad_up: float32 [1024, 2816], P(('dp', 'ctx'))
- grad_down: float32 [2816, 1024], P(('dp', 'ctx'))
- new_m_query: float32 [1024, 1024], P(('dp', 'ctx'))
- new_m_key: float32 [1024, 1024], P(('dp', 'ctx'))
- new_m_value: float32 [1024, 1024], P(('dp', 'ctx'))
- new_m_out: float32 [1024, 1024], P(('dp', 'ctx'))
- new_m_gate: float32 [1024, 2816], P(('dp', 'ctx'))
- new_m_up: float32 [1024, 2816], P(('dp', 'ctx'))
- new_m_down: float32 [2816, 1024], P(('dp', 'ctx'))
- new_w_query: bfloat16 [1024, 1024], P(('dp', 'ctx'))
- new_w_key: bfloat16 [1024, 1024], P(('dp', 'ctx'))
- new_w_value: bfloat16 [1024, 1024], P(('dp', 'ctx'))
- new_w_out: bfloat16 [1024, 1024], P(('dp', 'ctx'))
- new_w_gate: bfloat16 [1024, 2816], P(('dp', 'ctx'))
- new_w_up: bfloat16 [1024, 2816], P(('dp', 'ctx'))
- new_w_down: bfloat16 [2816, 1024], P(('dp', 'ctx'))
- head_peaks: float32 [16], replicated
- head_scale: float32 [16], replicated
The draws below stay inside these ranges and needn't reach their ends.
Inputs may be any that keep to these rules, and one draw needn't show every extreme that they name: `block_ids`: along each sequence the block ids never fall, and each id covers 1 to 256 consecutive tokens.
All inputs are finite; a program needn't handle non-finite values.
Results may differ from the reference program's by a relative error of at most 0.017.
Values may be sent and summed in bfloat16 or wider, within the bound.
No kernel may reach another device: no remote copies, remote signals or barrier semaphores. Data moves between devices by JAX's collectives and lax.ppermute only.
A program may use at most 192 MiB of HBM per device.

```python
import math
import jax
import jax.numpy as jnp
import numpy as np
from jax import lax

D = 1024
HEADS = 16
HEAD_DIM = 64
FF = 2816
LENGTH = 1024
BLOCK = 256
SEQS = 8
TOKENS = 8192
SEG_COUNT = 8


def draw_w_query(key, part):
    base = jnp.clip(jax.random.normal(jax.random.fold_in(key, 11), (D, D), jnp.float32), -4.0, 4.0)
    gains = jnp.exp(jax.random.uniform(jax.random.fold_in(key, 12), (HEADS,), jnp.float32, 0.0, math.log(4.0)))
    return (base * D ** (-0.5) * jnp.repeat(gains, HEAD_DIM)[None, :]).astype(jnp.bfloat16)


def level_of(key, extent, split, low, top_value):
    loudness = 1.0
    for position, shards_of in split:
        steps = jax.random.uniform(jax.random.fold_in(jax.random.fold_in(key, 6), position), (shards_of,), jnp.float32, low / len(split), top_value / len(split))
        loudness = loudness * jnp.repeat(jnp.exp(steps), extent[position] // shards_of).reshape((-1,) + (1,) * (len(extent) - 1 - position))
    return loudness


def profile(number_of, total, most, skew):
    portions = [(1 << 20) // math.isqrt(rank ** skew) + 1 for rank in range(2, number_of + 1)]
    spare, counts = total - most - (number_of - 1), [1] * (number_of - 1)
    while spare > 0:
        candidates = [i for i in range(number_of - 1) if counts[i] < most]
        pool, budget = sum([portions[i] for i in candidates]), spare
        for i in candidates:
            addition = min(most - counts[i], max(1, budget * portions[i] // pool), spare)
            counts[i] = counts[i] + addition
            spare = spare - addition
    return np.array([most] + counts)


def ragged(own_key, number_of, total, most, lean):
    if number_of == 2:
        one = jax.random.randint(own_key, (), max(1, total - most), min(most, total - 1) + 1)
        return jnp.stack([one, total - one])
    tallies = jnp.asarray(profile(number_of, total, most, lean), jnp.int32)
    couples = (number_of - 1) // 2
    donor, sink = tallies[1:1 + 2 * couples:2], tallies[2:2 + 2 * couples:2]
    room = jnp.minimum(donor - 1, most - sink)
    moved = jax.random.randint(jax.random.fold_in(own_key, 1), (couples,), 0, 1 << 20) % (room + 1)
    tallies = tallies.at[1:1 + 2 * couples:2].set(donor - moved).at[2:2 + 2 * couples:2].set(sink + moved)
    return tallies[jax.random.permutation(jax.random.fold_in(own_key, 2), number_of)]


def normal_values(key, shape, deviation, limit, pieces=(), kind=jnp.bfloat16):
    loudness = level_of(key, shape, pieces, -0.22, 0.18) if pieces else 1.0
    array = jax.random.normal(key, shape, jnp.float32) * deviation * loudness
    return jnp.minimum(jnp.maximum(array, -limit), limit).astype(kind)


def setup_inputs(seed: int = 0) -> dict:
    key_list = jax.random.split(jax.random.key(seed), 20)
    return {
        "activations": normal_values(key_list[0], (SEQS, LENGTH, D), 1.0, 6.0, ((0, 8), (1, 4))),
        "block_ids": jax.vmap(lambda own: jnp.searchsorted(jnp.cumsum(ragged(own, SEG_COUNT, LENGTH, BLOCK, 1)), jnp.arange(LENGTH), side="right"))(jax.random.split(key_list[1], SEQS)).reshape((SEQS, LENGTH)).astype(jnp.int32),
        "cotangent": normal_values(key_list[2], (SEQS, LENGTH, D), 1.0, 6.0, ((0, 8), (1, 4))),
        "w_query": draw_w_query(jax.random.fold_in(key_list[19], 71), 0),
        "w_key": normal_values(key_list[4], (D, D), D ** -0.5, 0.1875, ((0, 32),)),
        "w_value": normal_values(key_list[5], (D, D), D ** -0.5, 0.1875, ((0, 32),)),
        "w_out": normal_values(key_list[6], (D, D), (D // 16) ** -0.5, 0.75, ((0, 32),)),
        "w_gate": normal_values(key_list[7], (D, FF), D ** -0.5, 0.1875, ((0, 32),)),
        "w_up": normal_values(key_list[8], (D, FF), D ** -0.5, 0.1875, ((0, 32),)),
        "w_down": normal_values(key_list[9], (FF, D), FF ** -0.5, 0.109375, ((0, 32),)),
        "m_query": normal_values(key_list[10], (D, D), (TOKENS ** 0.5), 512.0, ((0, 32),), jnp.float32),
        "m_key": normal_values(key_list[11], (D, D), (TOKENS ** 0.5), 512.0, ((0, 32),), jnp.float32),
        "m_value": normal_values(key_list[12], (D, D), (TOKENS ** 0.5), 512.0, ((0, 32),), jnp.float32),
        "m_out": normal_values(key_list[13], (D, D), (TOKENS ** 0.5), 512.0, ((0, 32),), jnp.float32),
        "m_gate": normal_values(key_list[14], (D, FF), (TOKENS ** 0.5), 512.0, ((0, 32),), jnp.float32),
        "m_up": normal_values(key_list[15], (D, FF), (TOKENS ** 0.5), 512.0, ((0, 32),), jnp.float32),
        "m_down": normal_values(key_list[16], (FF, D), (TOKENS ** 0.5), 512.0, ((0, 32),), jnp.float32),
        "clip_threshold": jnp.clip(jax.random.uniform(key_list[17], (), jnp.float32, 2.5, 4.5), 2.5, 4.5),
        "momentum_coeff": jnp.clip(jax.random.uniform(key_list[18], (), jnp.float32, 0.5, 0.95), 0.5, 0.95),
    }


NORM_EPS = 1e-05
ROPE_BASE = 10000.0
LEARN_RATE = 0.0001
OUT_RATE = 0.0016
MASK_FILL = -1e+30

@jax.custom_vjp
def low(v):
    return lax.optimization_barrier(v.astype(jnp.bfloat16)).astype(jnp.float32)

@jax.custom_vjp
def low_back(v):
    return v

def low_keep(v):
    return (low(v), None)

def low_pass(kept, grad):
    return (grad,)

def back_keep(v):
    return (v, None)

def back_low(kept, grad):
    return (low(grad),)
low.defvjp(low_keep, low_pass)
low_back.defvjp(back_keep, back_low)

def matmul(left_side, operand):
    return jnp.dot(left_side, operand, precision=lax.Precision.HIGHEST, preferred_element_type=jnp.float32)

def normalize(values):
    centred = values - lax.optimization_barrier(jnp.mean(values, axis=-1, keepdims=True))
    spread = lax.optimization_barrier(jnp.mean(centred * centred, axis=-1, keepdims=True))
    return centred * lax.rsqrt(spread + NORM_EPS)

def rotary_tables(positions, head_width):
    half_width = head_width // 2
    frequency = ROPE_BASE ** (-(jnp.arange(half_width, dtype=jnp.float32) * 2.0 / head_width))
    angles = positions.astype(jnp.float32)[:, None] * frequency[None, :]
    return (jnp.cos(angles), jnp.sin(angles))

def rotate(vectors, cosine, sine_table):
    half_width = vectors.shape[-1] // 2
    first_half = vectors[..., :half_width]
    second = vectors[..., half_width:]
    cos_wide = cosine[:, None, :]
    sin_wide = sine_table[:, None, :]
    return jnp.concatenate([first_half * cos_wide - second * sin_wide, second * cos_wide + first_half * sin_wide], axis=-1)

def attend(queries, key_rot, value_rot, block_row):
    score_scale = 1.0 / math.sqrt(HEAD_DIM)
    scores = jnp.einsum('qhd,khd->hqk', queries, key_rot, precision=lax.Precision.HIGHEST) * score_scale
    scores = low_back(scores)
    allowed = block_row[None, :] <= block_row[:, None]
    masked = jnp.where(allowed[None], scores, MASK_FILL)
    peak_list = lax.optimization_barrier(jnp.max(masked, axis=(1, 2)))
    weights = low(jax.nn.softmax(masked, axis=-1))
    attended = jnp.einsum('hqk,khd->qhd', weights, value_rot, precision=lax.Precision.HIGHEST)
    return (attended, peak_list)

def group_forward(inputs, block_rows, weight_list):
    w_query, w_key, w_value, w_out, w_gate, w_up, w_down = weight_list
    seq_count, length_now, model_width = inputs.shape
    tokens_flat = inputs.reshape(-1, model_width)
    normed = low(normalize(tokens_flat))
    cosine, sine_table = rotary_tables(jnp.arange(length_now, dtype=jnp.int32), HEAD_DIM)

    def split_heads(matrix):
        return matrix.reshape(seq_count, length_now, HEADS, HEAD_DIM)
    queries = low(rotate(split_heads(low_back(matmul(normed, w_query))), cosine, sine_table))
    key_rot = low(rotate(split_heads(low_back(matmul(normed, w_key))), cosine, sine_table))
    value_rot = low(low_back(split_heads(matmul(normed, w_value))))
    attend_saved = jax.checkpoint(attend)
    attended, peak_rows = lax.map(lambda packed: attend_saved(packed[0], packed[1], packed[2], packed[3]), (queries, key_rot, value_rot, block_rows))
    attended = low(low_back(attended.reshape(-1, model_width)))
    branch_out = low_back(matmul(attended, w_out))
    residual = tokens_flat + branch_out
    normed2 = low(normalize(residual))
    gate_proj = low_back(matmul(normed2, w_gate))
    up_proj = low_back(matmul(normed2, w_up))
    hidden = low(jax.nn.silu(gate_proj) * up_proj)
    mixed = low_back(matmul(hidden, w_down))
    return ((residual + mixed).reshape(seq_count, length_now, model_width), lax.optimization_barrier(jnp.max(peak_rows, axis=0)))

def reference(activations, block_ids, cotangent, w_query, w_key, w_value, w_out, w_gate, w_up, w_down, m_query, m_key, m_value, m_out, m_gate, m_up, m_down, clip_threshold, momentum_coeff):
    group_size = math.gcd(SEQS, 4)
    group_count = SEQS // group_size
    weights_wide = tuple((matrix.astype(jnp.float32) for matrix in (w_query, w_key, w_value, w_out, w_gate, w_up, w_down)))

    def forward(inputs, *weight_list):
        grouped = inputs.reshape(group_count, group_size, LENGTH, D)
        id_groups = block_ids.reshape(group_count, group_size, LENGTH)
        group_step = jax.checkpoint(lambda packed: group_forward(packed[0], packed[1], weight_list))
        results, peak_rows = lax.map(group_step, (grouped, id_groups))
        return (results.reshape(SEQS, LENGTH, D), lax.optimization_barrier(jnp.max(peak_rows, axis=0)))
    layer_wide, pullback, head_peaks = jax.vjp(forward, activations.astype(jnp.float32), *weights_wide, has_aux=True)
    gradients = pullback(cotangent.astype(jnp.float32))
    moments = (m_query, m_key, m_value, m_out, m_gate, m_up, m_down)
    new_moments = tuple((momentum_coeff * moment + gradient for moment, gradient in zip(moments, gradients[1:])))
    head_scale = jnp.sqrt(clip_threshold / jnp.maximum(head_peaks, clip_threshold))
    column_scale = jnp.repeat(head_scale, HEAD_DIM)
    rates = (LEARN_RATE, LEARN_RATE, LEARN_RATE, OUT_RATE, LEARN_RATE, LEARN_RATE, LEARN_RATE)
    updated = [matrix - rate * moment for matrix, moment, rate in zip(weights_wide, new_moments, rates)]
    updated[0] = updated[0] * column_scale[None, :]
    updated[1] = updated[1] * column_scale[None, :]
    updated = [matrix.astype(jnp.bfloat16) for matrix in updated]
    return (layer_wide.astype(jnp.bfloat16), gradients[0], gradients[1], gradients[2], gradients[3], gradients[4], gradients[5], gradients[6], gradients[7], new_moments[0], new_moments[1], new_moments[2], new_moments[3], new_moments[4], new_moments[5], new_moments[6], updated[0], updated[1], updated[2], updated[3], updated[4], updated[5], updated[6], head_peaks, head_scale)
```

```python
import math

import jax
import jax.numpy as jnp
from jax import lax
from jax.sharding import PartitionSpec as P

HEADS = 16
HEAD_DIM = 64


NORM_EPS = 1e-05
ROPE_BASE = 10000.0
LEARN_RATE = 0.0001
OUT_RATE = 0.0016
MASK_FILL = -1e30


def normalize(values):
    centred = values - jnp.mean(values, axis=-1, keepdims=True)
    spread = jnp.mean(centred * centred, axis=-1, keepdims=True)
    return centred * lax.rsqrt(spread + NORM_EPS)


def rotary_tables(positions, head_width):
    half_width = head_width // 2
    frequency = ROPE_BASE ** (-(jnp.arange(half_width, dtype=jnp.float32) * 2.0 / head_width))
    angles = positions.astype(jnp.float32)[:, None] * frequency[None, :]
    return (jnp.cos(angles), jnp.sin(angles))


def rotate(vectors, cosine, sine_table):
    half_width = vectors.shape[-1] // 2
    first_half = vectors[..., :half_width]
    second = vectors[..., half_width:]
    cos_wide = cosine[:, None, :]
    sin_wide = sine_table[:, None, :]
    return jnp.concatenate(
        [first_half * cos_wide - second * sin_wide, second * cos_wide + first_half * sin_wide],
        axis=-1,
    )


def swiglu(gate_proj, up_proj):
    return jax.nn.silu(gate_proj) * up_proj


def project(left_rows, matrix):
    return jnp.dot(left_rows, matrix, preferred_element_type=jnp.float32)


def project_back(grad_rows, matrix):
    return lax.dot_general(
        grad_rows, matrix, (((1,), (1,)), ((), ())), preferred_element_type=jnp.float32
    )


def shard_gradient(left_rows, right_rows):
    return lax.psum_scatter(
        lax.dot_general(
            left_rows, right_rows, (((0,), (0,)), ((), ())), preferred_element_type=jnp.float32
        ),
        ("dp", "ctx"),
        scatter_dimension=0,
        tiled=True,
    )


def per_device(
    activations,
    block_ids,
    cotangent,
    w_query,
    w_key,
    w_value,
    w_out,
    w_gate,
    w_up,
    w_down,
    m_query,
    m_key,
    m_value,
    m_out,
    m_gate,
    m_up,
    m_down,
    clip_threshold,
    momentum_coeff,
):
    shard_list = (w_query, w_key, w_value, w_out, w_gate, w_up, w_down)
    gathered = (
        lax.all_gather(shard_list[0], ("dp", "ctx"), axis=0, tiled=True),
        lax.all_gather(shard_list[1], ("dp", "ctx"), axis=0, tiled=True),
        lax.all_gather(shard_list[2], ("dp", "ctx"), axis=0, tiled=True),
        lax.all_gather(shard_list[3], ("dp", "ctx"), axis=0, tiled=True),
        lax.all_gather(shard_list[4], ("dp", "ctx"), axis=0, tiled=True),
        lax.all_gather(shard_list[5], ("dp", "ctx"), axis=0, tiled=True),
        lax.all_gather(shard_list[6], ("dp", "ctx"), axis=0, tiled=True),
    )
    full_query, full_key, full_value, full_out, full_gate, full_up, full_down = gathered
    seq_count, span_len, model_width = activations.shape
    ctx_place = lax.axis_index("ctx")
    positions = ctx_place * span_len + jnp.arange(span_len, dtype=jnp.int32)
    cosine, sine_table = rotary_tables(positions, HEAD_DIM)
    score_scale = 1.0 / math.sqrt(HEAD_DIM)

    def split_heads(matrix):
        return matrix.reshape(seq_count, span_len, HEADS, HEAD_DIM)

    tokens_flat = activations.astype(jnp.float32).reshape(-1, model_width)
    normed = normalize(tokens_flat).astype(jnp.bfloat16)
    queries = rotate(split_heads(project(normed, full_query)), cosine, sine_table).astype(
        jnp.bfloat16
    )
    key_rot = rotate(split_heads(project(normed, full_key)), cosine, sine_table).astype(
        jnp.bfloat16
    )
    value_rot = split_heads(project(normed, full_value)).astype(jnp.bfloat16)
    key_all, value_all = (
        lax.all_gather(key_rot, "ctx", axis=1, tiled=True),
        lax.all_gather(value_rot, "ctx", axis=1, tiled=True),
    )
    query_ids = lax.dynamic_slice_in_dim(block_ids, ctx_place * span_len, span_len, 1)
    allowed = (block_ids[:, None, :] <= query_ids[:, :, None])[:, None]

    def masked_scores():
        scores = (
            jnp.einsum("sqhd,skhd->shqk", queries, key_all, preferred_element_type=jnp.float32)
            * score_scale
        )
        return jnp.where(allowed, scores, MASK_FILL)

    masked = masked_scores()
    local_peaks = jnp.max(masked, axis=(0, 2, 3))
    row_top = jnp.max(masked, axis=-1, keepdims=True)
    log_total = row_top + jnp.log(jnp.sum(jnp.exp(masked - row_top), axis=-1, keepdims=True))
    probs_low = jnp.exp(masked - log_total).astype(jnp.bfloat16)
    attended = jnp.einsum(
        "shqk,skhd->sqhd", probs_low, value_all, preferred_element_type=jnp.float32
    )
    attended_low = attended.reshape(-1, model_width).astype(jnp.bfloat16)
    head_peaks = lax.pmax(local_peaks, ("dp", "ctx"))
    residual = tokens_flat + project(attended_low, full_out)
    normed2 = normalize(residual).astype(jnp.bfloat16)
    gate_proj = project(normed2, full_gate)
    up_proj = project(normed2, full_up)
    hidden_low = swiglu(gate_proj, up_proj).astype(jnp.bfloat16)
    layer_out = (
        (residual + project(hidden_low, full_down))
        .astype(jnp.bfloat16)
        .reshape(seq_count, span_len, model_width)
    )
    back_weights = (
        lax.all_gather(shard_list[0], ("dp", "ctx"), axis=0, tiled=True),
        lax.all_gather(shard_list[1], ("dp", "ctx"), axis=0, tiled=True),
        lax.all_gather(shard_list[2], ("dp", "ctx"), axis=0, tiled=True),
        lax.all_gather(shard_list[3], ("dp", "ctx"), axis=0, tiled=True),
        lax.all_gather(shard_list[4], ("dp", "ctx"), axis=0, tiled=True),
        lax.all_gather(shard_list[5], ("dp", "ctx"), axis=0, tiled=True),
        lax.all_gather(shard_list[6], ("dp", "ctx"), axis=0, tiled=True),
    )
    back_query, back_key, back_value, back_out, back_gate, back_up, back_down = back_weights
    grad_rows = cotangent.reshape(-1, model_width)
    grad_hidden = project_back(grad_rows, back_down)
    unused, gate_pull = jax.vjp(swiglu, gate_proj, up_proj)
    grad_gate_wide, grad_up_wide = gate_pull(grad_hidden)
    grad_gate_low = grad_gate_wide.astype(jnp.bfloat16)
    grad_up_low = grad_up_wide.astype(jnp.bfloat16)
    grad_normed2 = project_back(grad_gate_low, back_gate) + project_back(grad_up_low, back_up)
    unused, second_pull = jax.vjp(normalize, residual)
    grad_residual = grad_rows.astype(jnp.float32) + second_pull(grad_normed2)[0]
    grad_branch = grad_residual.astype(jnp.bfloat16)
    grad_attended = split_heads(project_back(grad_branch, back_out).astype(jnp.bfloat16))
    masked = masked_scores()
    probs = jnp.exp(masked - log_total)
    probs_again = probs.astype(jnp.bfloat16)
    grad_values_all = jnp.einsum(
        "shqk,sqhd->skhd", probs_again, grad_attended, preferred_element_type=jnp.float32
    )
    grad_probs = jnp.einsum(
        "sqhd,skhd->shqk", grad_attended, value_all, preferred_element_type=jnp.float32
    )
    score_grad = (
        probs * (grad_probs - jnp.sum(probs * grad_probs, axis=-1, keepdims=True))
    ).astype(jnp.bfloat16)
    grad_queries = (
        jnp.einsum("shqk,skhd->sqhd", score_grad, key_all, preferred_element_type=jnp.float32)
        * score_scale
    )
    grad_keys_all = (
        jnp.einsum("shqk,sqhd->skhd", score_grad, queries, preferred_element_type=jnp.float32)
        * score_scale
    )
    grad_keys, grad_values = (
        lax.psum_scatter(
            grad_keys_all.astype(jnp.bfloat16), "ctx", scatter_dimension=1, tiled=True
        ).astype(jnp.float32),
        lax.psum_scatter(
            grad_values_all.astype(jnp.bfloat16), "ctx", scatter_dimension=1, tiled=True
        ).astype(jnp.float32),
    )
    grad_query_low = (
        rotate(grad_queries, cosine, -sine_table).reshape(-1, model_width).astype(jnp.bfloat16)
    )
    grad_key_low = (
        rotate(grad_keys, cosine, -sine_table).reshape(-1, model_width).astype(jnp.bfloat16)
    )
    grad_value_low = grad_values.reshape(-1, model_width).astype(jnp.bfloat16)
    grad_normed = (
        project_back(grad_query_low, back_query)
        + project_back(grad_key_low, back_key)
        + project_back(grad_value_low, back_value)
    )
    unused, first_pull = jax.vjp(normalize, tokens_flat)
    input_grad = (grad_residual + first_pull(grad_normed)[0]).reshape(
        seq_count, span_len, model_width
    )
    weight_grads = (
        shard_gradient(normed, grad_query_low),
        shard_gradient(normed, grad_key_low),
        shard_gradient(normed, grad_value_low),
        shard_gradient(attended_low, grad_branch),
        shard_gradient(normed2, grad_gate_low),
        shard_gradient(normed2, grad_up_low),
        shard_gradient(hidden_low, grad_rows),
    )
    moments = (m_query, m_key, m_value, m_out, m_gate, m_up, m_down)
    new_moments = tuple(
        (momentum_coeff * moment + gradient for moment, gradient in zip(moments, weight_grads))
    )
    head_scale = jnp.sqrt(clip_threshold / jnp.maximum(head_peaks, clip_threshold))
    column_scale = jnp.repeat(head_scale, HEAD_DIM)
    rates = (LEARN_RATE, LEARN_RATE, LEARN_RATE, OUT_RATE, LEARN_RATE, LEARN_RATE, LEARN_RATE)
    updated = [
        matrix.astype(jnp.float32) - rate * moment
        for matrix, moment, rate in zip(shard_list, new_moments, rates)
    ]
    updated[0] = updated[0] * column_scale[None, :]
    updated[1] = updated[1] * column_scale[None, :]
    updated = [matrix.astype(jnp.bfloat16) for matrix in updated]
    return (
        layer_out,
        input_grad,
        weight_grads[0],
        weight_grads[1],
        weight_grads[2],
        weight_grads[3],
        weight_grads[4],
        weight_grads[5],
        weight_grads[6],
        new_moments[0],
        new_moments[1],
        new_moments[2],
        new_moments[3],
        new_moments[4],
        new_moments[5],
        new_moments[6],
        updated[0],
        updated[1],
        updated[2],
        updated[3],
        updated[4],
        updated[5],
        updated[6],
        head_peaks,
        head_scale,
    )


HALF = 512


def swap(array, bit):
    return lax.ppermute(array, "dp", [(i, i ^ bit) for i in range(8)])


def order_of(first, second):
    return [c * 1 + f * first + s * second for c in (0, 1) for f in (0, 1) for s in (0, 1)]


ORDER_A = order_of(2, 4)
ORDER_B = order_of(4, 2)


def pick_columns(matrix, order, me, width):
    return jnp.concatenate(
        [lax.dynamic_slice_in_dim(matrix, (r ^ me) * width, width, 1) for r in order], axis=1
    )


def pick_rows(matrix, order, me, width):
    return jnp.concatenate(
        [lax.dynamic_slice_in_dim(matrix, (r ^ me) * width, width, 0) for r in order], axis=0
    )


def place_of(order, block, me):
    table = [0] * 8
    for place, r in enumerate(order):
        table[r] = place
    return jnp.asarray(table, jnp.int32)[block ^ me]


def restore_columns(matrix, order, me, width):
    return jnp.concatenate(
        [
            lax.dynamic_slice_in_dim(matrix, place_of(order, b, me) * width, width, 1)
            for b in range(8)
        ],
        axis=1,
    )


def restore_rows(matrix, order, me, width):
    return jnp.concatenate(
        [
            lax.dynamic_slice_in_dim(matrix, place_of(order, b, me) * width, width, 0)
            for b in range(8)
        ],
        axis=0,
    )


def spread(own, first, second):
    near = swap(own, first)
    pair = jnp.concatenate([own, near], axis=0)
    far = swap(pair, second)
    rows = own.shape[0]
    four = jnp.concatenate([own, far[:rows], near, far[rows:]], axis=0)
    return jnp.concatenate([four, swap(four, 1)], axis=0)


def halve(matrix, bit):
    rows = matrix.shape[0] // 2
    other = swap(matrix[rows:], bit)
    return (matrix[:rows].astype(jnp.float32) + other.astype(jnp.float32)).astype(jnp.bfloat16)


def collect(matrix):
    return lax.psum_scatter(matrix, "ctx", scatter_dimension=0, tiled=True)


def transposed_product(left, right):
    return lax.dot_general(
        left, right, (((0,), (0,)), ((), ())), preferred_element_type=jnp.float32
    )


def fast_device(
    activations,
    block_ids,
    cotangent,
    w_query,
    w_key,
    w_value,
    w_out,
    w_gate,
    w_up,
    w_down,
    m_query,
    m_key,
    m_value,
    m_out,
    m_gate,
    m_up,
    m_down,
    clip_threshold,
    momentum_coeff,
):
    low = jnp.bfloat16
    me = lax.axis_index("dp")
    _, span, width = activations.shape
    length = block_ids.shape[1]
    group = length // span
    own_heads = HEADS // group
    own_width = own_heads * HEAD_DIM
    rows = w_query.shape[0]
    ff = w_gate.shape[1]
    tokens_low = activations.reshape(span, width)
    grad_rows = cotangent.reshape(span, width)
    wide = jnp.concatenate([w_gate, w_out[:, :HALF], w_up, w_out[:, HALF:]], axis=1)
    wide = lax.all_gather(wide, "ctx", axis=0, tiled=True)
    tall = lax.all_gather(w_down, "ctx", axis=0, tiled=True)
    all_low = lax.all_gather(tokens_low, "ctx", axis=0, tiled=True)
    heads_own = jnp.stack([w_query, w_key, w_value], axis=1).reshape(rows, 3, group, own_width)
    heads_own = heads_own.transpose(2, 0, 1, 3).reshape(group, rows, 3 * own_width)
    heads_own = lax.all_to_all(heads_own, "ctx", 0, 0, tiled=True)
    block = group * rows
    heads_rel = spread(heads_own.reshape(block, 3 * own_width), 2, 4)
    weight_a = spread(wide[:, : ff + HALF], 2, 4)
    weight_b = spread(wide[:, ff + HALF :], 4, 2)
    tall_block = group * w_down.shape[0]
    down_a = restore_rows(spread(tall[:, :HALF], 2, 4), ORDER_A, me, tall_block)
    down_b = restore_rows(spread(tall[:, HALF:], 4, 2), ORDER_B, me, tall_block)
    full_down = jnp.concatenate([down_a, down_b], axis=1)
    cosine, sine_table = rotary_tables(jnp.arange(length, dtype=jnp.int32), HEAD_DIM)
    score_scale = 1.0 / math.sqrt(HEAD_DIM)
    all_wide = all_low.astype(jnp.float32)
    normed = normalize(all_wide).astype(low)
    normed_rel = pick_columns(normed, ORDER_A, me, block)
    mixed = project(normed_rel, heads_rel)

    def split_heads(matrix):
        return matrix.reshape(length, own_heads, HEAD_DIM)

    queries = rotate(split_heads(mixed[:, :own_width]), cosine, sine_table).astype(low)
    key_rot = rotate(split_heads(mixed[:, own_width : 2 * own_width]), cosine, sine_table).astype(
        low
    )
    value_rot = split_heads(mixed[:, 2 * own_width :]).astype(low)
    ids = block_ids[0]
    allowed = (ids[None, :] <= ids[:, None])[None]

    def masked_scores():
        scores = (
            jnp.einsum("qhd,khd->hqk", queries, key_rot, preferred_element_type=jnp.float32)
            * score_scale
        )
        return jnp.where(allowed, scores, MASK_FILL)

    masked = masked_scores()
    local_peaks = jnp.max(masked, axis=(1, 2))
    row_top = jnp.max(masked, axis=-1, keepdims=True)
    log_total = row_top + jnp.log(jnp.sum(jnp.exp(masked - row_top), axis=-1, keepdims=True))
    probs = jnp.exp(masked - log_total)
    attended = jnp.einsum(
        "hqk,khd->qhd", probs.astype(low), value_rot, preferred_element_type=jnp.float32
    )
    attended = attended.astype(low).reshape(group, span, own_width)
    attended = lax.all_to_all(attended, "ctx", 0, 0, tiled=True)
    attended = attended.transpose(1, 0, 2).reshape(span, width)
    peaks = lax.all_gather(local_peaks, ("dp", "ctx"), axis=0, tiled=False)
    head_peaks = jnp.max(peaks.reshape(-1, group, own_heads), axis=0).reshape(HEADS)
    attended_a = pick_columns(attended, ORDER_A, me, block)
    attended_b = pick_columns(attended, ORDER_B, me, block)
    branch = jnp.concatenate(
        [project(attended_a, weight_a[:, ff:]), project(attended_b, weight_b[:, ff:])], axis=1
    )
    residual = tokens_low.astype(jnp.float32) + branch
    normed2 = normalize(residual).astype(low)
    normed2_a = pick_columns(normed2, ORDER_A, me, block)
    normed2_b = pick_columns(normed2, ORDER_B, me, block)
    gate_proj = project(normed2_a, weight_a[:, :ff])
    up_proj = project(normed2_b, weight_b[:, :ff])
    hidden_low = swiglu(gate_proj, up_proj).astype(low)
    layer_out = (residual + project(hidden_low, full_down)).astype(low)
    grad_hidden = project_back(grad_rows, full_down)
    unused, gate_pull = jax.vjp(swiglu, gate_proj, up_proj)
    grad_gate_wide, grad_up_wide = gate_pull(grad_hidden)
    grad_gate_low = grad_gate_wide.astype(low)
    grad_up_low = grad_up_wide.astype(low)
    grad_normed2 = restore_columns(
        project_back(grad_gate_low, weight_a[:, :ff]), ORDER_A, me, block
    ) + restore_columns(project_back(grad_up_low, weight_b[:, :ff]), ORDER_B, me, block)
    unused, second_pull = jax.vjp(normalize, residual)
    grad_residual = grad_rows.astype(jnp.float32) + second_pull(grad_normed2)[0]
    grad_branch = grad_residual.astype(low)
    grad_a = jnp.concatenate(
        [
            transposed_product(normed2_a, grad_gate_low).astype(low),
            transposed_product(attended_a, grad_branch[:, :HALF]).astype(low),
        ],
        axis=1,
    )
    grad_b = jnp.concatenate(
        [
            transposed_product(normed2_b, grad_up_low).astype(low),
            transposed_product(attended_b, grad_branch[:, HALF:]).astype(low),
        ],
        axis=1,
    )
    grad_a = halve(grad_a, 1)
    grad_b = halve(grad_b, 1)
    grad_a = halve(grad_a, 2)
    grad_b = halve(grad_b, 4)
    grad_a = halve(grad_a, 4)
    grad_b = halve(grad_b, 2)
    grad_tall = transposed_product(hidden_low, grad_rows).astype(low)
    grad_tall = halve(
        jnp.concatenate(
            [
                pick_rows(grad_tall[:, :HALF], ORDER_A, me, tall_block),
                pick_rows(grad_tall[:, HALF:], ORDER_B, me, tall_block),
            ],
            axis=1,
        ),
        1,
    )
    grad_da = halve(grad_tall[:, :HALF], 2)
    grad_db = halve(grad_tall[:, HALF:], 4)
    grad_da = halve(grad_da, 4)
    grad_db = halve(grad_db, 2)
    grad_ab = collect(jnp.concatenate([grad_a, grad_b], axis=1)).astype(jnp.float32)
    grad_d = collect(jnp.concatenate([grad_da, grad_db], axis=1)).astype(jnp.float32)
    grad_attended = restore_columns(
        project_back(grad_branch[:, :HALF], weight_a[:, ff:]), ORDER_A, me, block
    ) + restore_columns(
        project_back(grad_branch[:, HALF:], weight_b[:, ff:]), ORDER_B, me, block
    )
    grad_attended = grad_attended.astype(low).reshape(span, group, own_width).transpose(1, 0, 2)
    grad_attended = lax.all_to_all(grad_attended, "ctx", 0, 0, tiled=True)
    grad_attended = split_heads(grad_attended.reshape(length, own_width))
    probs = jnp.exp(masked_scores() - log_total)
    grad_values = jnp.einsum(
        "hqk,qhd->khd", probs.astype(low), grad_attended, preferred_element_type=jnp.float32
    )
    grad_probs = jnp.einsum(
        "qhd,khd->hqk", grad_attended, value_rot, preferred_element_type=jnp.float32
    )
    score_grad = (
        probs * (grad_probs - jnp.sum(probs * grad_probs, axis=-1, keepdims=True))
    ).astype(low)
    grad_queries = (
        jnp.einsum("hqk,khd->qhd", score_grad, key_rot, preferred_element_type=jnp.float32)
        * score_scale
    )
    grad_keys = (
        jnp.einsum("hqk,qhd->khd", score_grad, queries, preferred_element_type=jnp.float32)
        * score_scale
    )
    grad_mixed = jnp.concatenate(
        [
            rotate(grad_queries, cosine, -sine_table).astype(low).reshape(length, own_width),
            rotate(grad_keys, cosine, -sine_table).astype(low).reshape(length, own_width),
            grad_values.astype(low).reshape(length, own_width),
        ],
        axis=1,
    )
    grad_normed = restore_columns(
        project_back(grad_mixed, heads_rel).astype(low), ORDER_A, me, block
    )
    grad_normed = collect(grad_normed).astype(jnp.float32)
    tokens_wide = tokens_low.astype(jnp.float32)
    unused, first_pull = jax.vjp(normalize, tokens_wide)
    input_grad = grad_residual + first_pull(grad_normed)[0]
    grad_heads = transposed_product(normed_rel, grad_mixed).astype(low)
    grad_heads = halve(halve(halve(grad_heads, 1), 2), 4)
    grad_heads = lax.all_to_all(
        grad_heads.reshape(group, rows, 3 * own_width), "ctx", 0, 0, tiled=True
    ).astype(jnp.float32)
    grad_heads = grad_heads.reshape(group, rows, 3, own_width).transpose(2, 1, 0, 3)
    grad_heads = grad_heads.reshape(3, rows, width)
    weight_grads = (
        grad_heads[0],
        grad_heads[1],
        grad_heads[2],
        jnp.concatenate([grad_ab[:, ff : ff + HALF], grad_ab[:, 2 * ff + HALF :]], axis=1),
        grad_ab[:, :ff],
        grad_ab[:, ff + HALF : 2 * ff + HALF],
        grad_d,
    )
    moments = (m_query, m_key, m_value, m_out, m_gate, m_up, m_down)
    new_moments = tuple(
        (momentum_coeff * moment + gradient for moment, gradient in zip(moments, weight_grads))
    )
    head_scale = jnp.sqrt(clip_threshold / jnp.maximum(head_peaks, clip_threshold))
    column_scale = jnp.repeat(head_scale, HEAD_DIM)
    rates = (LEARN_RATE, LEARN_RATE, LEARN_RATE, OUT_RATE, LEARN_RATE, LEARN_RATE, LEARN_RATE)
    shard_list = (w_query, w_key, w_value, w_out, w_gate, w_up, w_down)
    updated = [
        matrix.astype(jnp.float32) - rate * moment
        for matrix, moment, rate in zip(shard_list, new_moments, rates)
    ]
    updated[0] = updated[0] * column_scale[None, :]
    updated[1] = updated[1] * column_scale[None, :]
    updated = [matrix.astype(low) for matrix in updated]
    return (
        layer_out[None],
        input_grad[None],
        *weight_grads,
        *new_moments,
        *updated,
        head_peaks,
        head_scale,
    )


def solution(mesh):
    placed = (
        P("dp", "ctx", None),
        P("dp", None),
        P("dp", "ctx", None),
        P(("dp", "ctx"), None),
        P(("dp", "ctx"), None),
        P(("dp", "ctx"), None),
        P(("dp", "ctx"), None),
        P(("dp", "ctx"), None),
        P(("dp", "ctx"), None),
        P(("dp", "ctx"), None),
        P(("dp", "ctx"), None),
        P(("dp", "ctx"), None),
        P(("dp", "ctx"), None),
        P(("dp", "ctx"), None),
        P(("dp", "ctx"), None),
        P(("dp", "ctx"), None),
        P(("dp", "ctx"), None),
        P(),
        P(),
    )
    fits = mesh.shape["dp"] == 8 and mesh.shape["ctx"] == 4
    return jax.shard_map(
        fast_device if fits else per_device,
        mesh=mesh,
        in_specs=placed,
        out_specs=(
            P("dp", "ctx", None),
            P("dp", "ctx", None),
            P(("dp", "ctx"), None),
            P(("dp", "ctx"), None),
            P(("dp", "ctx"), None),
            P(("dp", "ctx"), None),
            P(("dp", "ctx"), None),
            P(("dp", "ctx"), None),
            P(("dp", "ctx"), None),
            P(("dp", "ctx"), None),
            P(("dp", "ctx"), None),
            P(("dp", "ctx"), None),
            P(("dp", "ctx"), None),
            P(("dp", "ctx"), None),
            P(("dp", "ctx"), None),
            P(("dp", "ctx"), None),
            P(("dp", "ctx"), None),
            P(("dp", "ctx"), None),
            P(("dp", "ctx"), None),
            P(("dp", "ctx"), None),
            P(("dp", "ctx"), None),
            P(("dp", "ctx"), None),
            P(("dp", "ctx"), None),
            P(),
            P(),
        ),
        check_vma=False,
    )
```

```python
import math

import jax
import jax.numpy as jnp
from jax import lax
from jax.experimental import pallas as pl
from jax.experimental.pallas import tpu as pltpu
from jax.sharding import PartitionSpec as P

HEADS = 16
HEAD_DIM = 64


NORM_EPS = 1e-05
ROPE_BASE = 10000.0
LEARN_RATE = 0.0001
OUT_RATE = 0.0016
MASK_FILL = -1e30


def normalize(values):
    centred = values - jnp.mean(values, axis=-1, keepdims=True)
    spread = jnp.mean(centred * centred, axis=-1, keepdims=True)
    return centred * lax.rsqrt(spread + NORM_EPS)


def rotary_tables(positions, head_width):
    half_width = head_width // 2
    frequency = ROPE_BASE ** (-(jnp.arange(half_width, dtype=jnp.float32) * 2.0 / head_width))
    angles = positions.astype(jnp.float32)[:, None] * frequency[None, :]
    return (jnp.cos(angles), jnp.sin(angles))


def rotate(vectors, cosine, sine_table):
    half_width = vectors.shape[-1] // 2
    first_half = vectors[..., :half_width]
    second = vectors[..., half_width:]
    cos_wide = cosine[:, None, :]
    sin_wide = sine_table[:, None, :]
    return jnp.concatenate(
        [first_half * cos_wide - second * sin_wide, second * cos_wide + first_half * sin_wide],
        axis=-1,
    )


def swiglu(gate_proj, up_proj):
    return jax.nn.silu(gate_proj) * up_proj


def project(left_rows, matrix):
    return jnp.dot(left_rows, matrix, preferred_element_type=jnp.float32)


def project_back(grad_rows, matrix):
    return lax.dot_general(
        grad_rows, matrix, (((1,), (1,)), ((), ())), preferred_element_type=jnp.float32
    )


def shard_gradient(left_rows, right_rows):
    return lax.psum_scatter(
        lax.dot_general(
            left_rows, right_rows, (((0,), (0,)), ((), ())), preferred_element_type=jnp.float32
        ),
        ("dp", "ctx"),
        scatter_dimension=0,
        tiled=True,
    )


def per_device(
    activations,
    block_ids,
    cotangent,
    w_query,
    w_key,
    w_value,
    w_out,
    w_gate,
    w_up,
    w_down,
    m_query,
    m_key,
    m_value,
    m_out,
    m_gate,
    m_up,
    m_down,
    clip_threshold,
    momentum_coeff,
):
    shard_list = (w_query, w_key, w_value, w_out, w_gate, w_up, w_down)
    gathered = (
        lax.all_gather(shard_list[0], ("dp", "ctx"), axis=0, tiled=True),
        lax.all_gather(shard_list[1], ("dp", "ctx"), axis=0, tiled=True),
        lax.all_gather(shard_list[2], ("dp", "ctx"), axis=0, tiled=True),
        lax.all_gather(shard_list[3], ("dp", "ctx"), axis=0, tiled=True),
        lax.all_gather(shard_list[4], ("dp", "ctx"), axis=0, tiled=True),
        lax.all_gather(shard_list[5], ("dp", "ctx"), axis=0, tiled=True),
        lax.all_gather(shard_list[6], ("dp", "ctx"), axis=0, tiled=True),
    )
    full_query, full_key, full_value, full_out, full_gate, full_up, full_down = gathered
    seq_count, span_len, model_width = activations.shape
    ctx_place = lax.axis_index("ctx")
    positions = ctx_place * span_len + jnp.arange(span_len, dtype=jnp.int32)
    cosine, sine_table = rotary_tables(positions, HEAD_DIM)
    score_scale = 1.0 / math.sqrt(HEAD_DIM)

    def split_heads(matrix):
        return matrix.reshape(seq_count, span_len, HEADS, HEAD_DIM)

    tokens_flat = activations.astype(jnp.float32).reshape(-1, model_width)
    normed = normalize(tokens_flat).astype(jnp.bfloat16)
    queries = rotate(split_heads(project(normed, full_query)), cosine, sine_table).astype(
        jnp.bfloat16
    )
    key_rot = rotate(split_heads(project(normed, full_key)), cosine, sine_table).astype(
        jnp.bfloat16
    )
    value_rot = split_heads(project(normed, full_value)).astype(jnp.bfloat16)
    key_all, value_all = (
        lax.all_gather(key_rot, "ctx", axis=1, tiled=True),
        lax.all_gather(value_rot, "ctx", axis=1, tiled=True),
    )
    query_ids = lax.dynamic_slice_in_dim(block_ids, ctx_place * span_len, span_len, 1)
    allowed = (block_ids[:, None, :] <= query_ids[:, :, None])[:, None]

    def masked_scores():
        scores = (
            jnp.einsum("sqhd,skhd->shqk", queries, key_all, preferred_element_type=jnp.float32)
            * score_scale
        )
        return jnp.where(allowed, scores, MASK_FILL)

    masked = masked_scores()
    local_peaks = jnp.max(masked, axis=(0, 2, 3))
    row_top = jnp.max(masked, axis=-1, keepdims=True)
    log_total = row_top + jnp.log(jnp.sum(jnp.exp(masked - row_top), axis=-1, keepdims=True))
    probs_low = jnp.exp(masked - log_total).astype(jnp.bfloat16)
    attended = jnp.einsum(
        "shqk,skhd->sqhd", probs_low, value_all, preferred_element_type=jnp.float32
    )
    attended_low = attended.reshape(-1, model_width).astype(jnp.bfloat16)
    head_peaks = lax.pmax(local_peaks, ("dp", "ctx"))
    residual = tokens_flat + project(attended_low, full_out)
    normed2 = normalize(residual).astype(jnp.bfloat16)
    gate_proj = project(normed2, full_gate)
    up_proj = project(normed2, full_up)
    hidden_low = swiglu(gate_proj, up_proj).astype(jnp.bfloat16)
    layer_out = (
        (residual + project(hidden_low, full_down))
        .astype(jnp.bfloat16)
        .reshape(seq_count, span_len, model_width)
    )
    back_weights = (
        lax.all_gather(shard_list[0], ("dp", "ctx"), axis=0, tiled=True),
        lax.all_gather(shard_list[1], ("dp", "ctx"), axis=0, tiled=True),
        lax.all_gather(shard_list[2], ("dp", "ctx"), axis=0, tiled=True),
        lax.all_gather(shard_list[3], ("dp", "ctx"), axis=0, tiled=True),
        lax.all_gather(shard_list[4], ("dp", "ctx"), axis=0, tiled=True),
        lax.all_gather(shard_list[5], ("dp", "ctx"), axis=0, tiled=True),
        lax.all_gather(shard_list[6], ("dp", "ctx"), axis=0, tiled=True),
    )
    back_query, back_key, back_value, back_out, back_gate, back_up, back_down = back_weights
    grad_rows = cotangent.reshape(-1, model_width)
    grad_hidden = project_back(grad_rows, back_down)
    unused, gate_pull = jax.vjp(swiglu, gate_proj, up_proj)
    grad_gate_wide, grad_up_wide = gate_pull(grad_hidden)
    grad_gate_low = grad_gate_wide.astype(jnp.bfloat16)
    grad_up_low = grad_up_wide.astype(jnp.bfloat16)
    grad_normed2 = project_back(grad_gate_low, back_gate) + project_back(grad_up_low, back_up)
    unused, second_pull = jax.vjp(normalize, residual)
    grad_residual = grad_rows.astype(jnp.float32) + second_pull(grad_normed2)[0]
    grad_branch = grad_residual.astype(jnp.bfloat16)
    grad_attended = split_heads(project_back(grad_branch, back_out).astype(jnp.bfloat16))
    masked = masked_scores()
    probs = jnp.exp(masked - log_total)
    probs_again = probs.astype(jnp.bfloat16)
    grad_values_all = jnp.einsum(
        "shqk,sqhd->skhd", probs_again, grad_attended, preferred_element_type=jnp.float32
    )
    grad_probs = jnp.einsum(
        "sqhd,skhd->shqk", grad_attended, value_all, preferred_element_type=jnp.float32
    )
    score_grad = (
        probs * (grad_probs - jnp.sum(probs * grad_probs, axis=-1, keepdims=True))
    ).astype(jnp.bfloat16)
    grad_queries = (
        jnp.einsum("shqk,skhd->sqhd", score_grad, key_all, preferred_element_type=jnp.float32)
        * score_scale
    )
    grad_keys_all = (
        jnp.einsum("shqk,sqhd->skhd", score_grad, queries, preferred_element_type=jnp.float32)
        * score_scale
    )
    grad_keys, grad_values = (
        lax.psum_scatter(
            grad_keys_all.astype(jnp.bfloat16), "ctx", scatter_dimension=1, tiled=True
        ).astype(jnp.float32),
        lax.psum_scatter(
            grad_values_all.astype(jnp.bfloat16), "ctx", scatter_dimension=1, tiled=True
        ).astype(jnp.float32),
    )
    grad_query_low = (
        rotate(grad_queries, cosine, -sine_table).reshape(-1, model_width).astype(jnp.bfloat16)
    )
    grad_key_low = (
        rotate(grad_keys, cosine, -sine_table).reshape(-1, model_width).astype(jnp.bfloat16)
    )
    grad_value_low = grad_values.reshape(-1, model_width).astype(jnp.bfloat16)
    grad_normed = (
        project_back(grad_query_low, back_query)
        + project_back(grad_key_low, back_key)
        + project_back(grad_value_low, back_value)
    )
    unused, first_pull = jax.vjp(normalize, tokens_flat)
    input_grad = (grad_residual + first_pull(grad_normed)[0]).reshape(
        seq_count, span_len, model_width
    )
    weight_grads = (
        shard_gradient(normed, grad_query_low),
        shard_gradient(normed, grad_key_low),
        shard_gradient(normed, grad_value_low),
        shard_gradient(attended_low, grad_branch),
        shard_gradient(normed2, grad_gate_low),
        shard_gradient(normed2, grad_up_low),
        shard_gradient(hidden_low, grad_rows),
    )
    moments = (m_query, m_key, m_value, m_out, m_gate, m_up, m_down)
    new_moments = tuple(
        (momentum_coeff * moment + gradient for moment, gradient in zip(moments, weight_grads))
    )
    head_scale = jnp.sqrt(clip_threshold / jnp.maximum(head_peaks, clip_threshold))
    column_scale = jnp.repeat(head_scale, HEAD_DIM)
    rates = (LEARN_RATE, LEARN_RATE, LEARN_RATE, OUT_RATE, LEARN_RATE, LEARN_RATE, LEARN_RATE)
    updated = [
        matrix.astype(jnp.float32) - rate * moment
        for matrix, moment, rate in zip(shard_list, new_moments, rates)
    ]
    updated[0] = updated[0] * column_scale[None, :]
    updated[1] = updated[1] * column_scale[None, :]
    updated = [matrix.astype(jnp.bfloat16) for matrix in updated]
    return (
        layer_out,
        input_grad,
        weight_grads[0],
        weight_grads[1],
        weight_grads[2],
        weight_grads[3],
        weight_grads[4],
        weight_grads[5],
        weight_grads[6],
        new_moments[0],
        new_moments[1],
        new_moments[2],
        new_moments[3],
        new_moments[4],
        new_moments[5],
        new_moments[6],
        updated[0],
        updated[1],
        updated[2],
        updated[3],
        updated[4],
        updated[5],
        updated[6],
        head_peaks,
        head_scale,
    )


f32=jnp.float32; bf=jnp.bfloat16
NT=(((1,),(1,)),((),())); TN=(((0,),(0,)),((),())); NN=(((1,),(0,)),((),()))
def dot(a,b,dims): return lax.dot_general(a,b,dims,preferred_element_type=f32)

def turn(values, cosine, signed_sine):
    lane = lax.broadcasted_iota(jnp.int32, cosine.shape, 1)
    first = lane % 64 < 32
    parts = []
    for j in range(values.shape[1] // 128):
        part = values[:, 128 * j : 128 * j + 128]
        partner = jnp.where(first, pltpu.roll(part, 96, 1), pltpu.roll(part, 32, 1))
        parts.append(part * cosine + partner * signed_sine)
    return jnp.concatenate(parts, axis=1)

def attend_kernel(place_ref, act_ref, weight_hbm, cos_ref, sin_ref, id_col, id_row,
                  normed_ref, mixed_ref, attended_ref, total_ref, peak_ref,
                  weight, value_t, sems):
    copies = []
    for p in range(8):
        copies.append(pltpu.make_async_copy(
            weight_hbm.at[pl.ds(128 * p, 128)],
            weight.at[pl.ds(pl.multiple_of(place_ref[p] * 128, 128), 128)], sems.at[p]))
        copies[-1].start()
    n = act_ref.shape[0]
    @pl.loop(0, n // 128)
    def _(i):
        rows = pl.ds(pl.multiple_of(i * 128, 128), 128)
        x = act_ref[rows, :].astype(f32)
        c = x - jnp.mean(x, axis=-1, keepdims=True)
        v = jnp.mean(c * c, axis=-1, keepdims=True)
        normed_ref[rows, :] = (c * lax.rsqrt(v + NORM_EPS)).astype(bf)
    for c in copies: c.wait()
    @pl.loop(0, n // 256)
    def _(i):
        rows = pl.ds(pl.multiple_of(i * 256, 256), 256)
        mixed = dot(normed_ref[rows, :], weight[...], NN)
        cosine = cos_ref[rows, :]; sine = sin_ref[rows, :]
        mixed_ref[rows, 0:256] = (turn(mixed[:, 0:256], cosine, sine).astype(bf).astype(f32) * 0.125).astype(bf)
        mixed_ref[rows, 256:512] = turn(mixed[:, 256:512], cosine, sine).astype(bf)
        val = mixed[:, 512:768].astype(bf)
        mixed_ref[rows, 512:768] = val
        value_t[:, rows] = val.astype(f32).T.astype(bf)
    peak_ref[...] = jnp.zeros_like(peak_ref)
    @pl.loop(0, 4)
    def _(h):
        pair = h // 2
        lanes = pl.multiple_of(pair * 128, 128)
        lane = lax.broadcasted_iota(jnp.int32, (256, 128), 1)
        mine = lane // 64 == h % 2
        best = None
        for i in range(4):
            width = min(256 * (i + 2), 1024)
            low = 256 * i
            q = mixed_ref[low:low + 256, pl.ds(lanes, 128)]
            q = jnp.where(mine, q, jnp.zeros_like(q))
            s = dot(mixed_ref[0:width, pl.ds(pl.multiple_of(256 + lanes, 128), 128)], q, NT)
            ok = id_col[low:width, :][:, 0:1] <= id_row[0:1, low:low + 256]
            tail = jnp.where(ok, s[low:width], MASK_FILL)
            top = jnp.max(tail, axis=0, keepdims=True)
            if i:
                head = s[0:low]
                top = jnp.maximum(top, jnp.max(head, axis=0, keepdims=True))
                s = jnp.concatenate([head, tail], axis=0)
            else:
                s = tail
            e = jnp.exp(s - top)
            total = jnp.sum(e, axis=0, keepdims=True)
            o = dot(value_t[pl.ds(lanes, 128), 0:width], e.astype(bf), NN)
            o = o * (1.0 / total)
            o = o.T.astype(bf)
            old = attended_ref[low:low + 256, pl.ds(lanes, 128)]
            attended_ref[low:low + 256, pl.ds(lanes, 128)] = jnp.where(mine, o, old)
            total_ref[pl.ds(h, 1), low:low + 256] = top + jnp.log(total)
            m = jnp.max(top, axis=1, keepdims=True)
            best = m if best is None else jnp.maximum(best, m)
        peak_ref[pl.ds(h, 1), :] = jnp.broadcast_to(best, (1, 128))

def attend(place, act, weight, cosine, sine, id_col, id_row):
    n = act.shape[0]
    vm = pl.BlockSpec(memory_space=pltpu.VMEM)
    return pl.pallas_call(
        attend_kernel,
        out_shape=(jax.ShapeDtypeStruct((n, 1024), bf), jax.ShapeDtypeStruct((n, 768), bf),
                   jax.ShapeDtypeStruct((n, 256), bf), jax.ShapeDtypeStruct((8, n), f32),
                   jax.ShapeDtypeStruct((8, 128), f32)),
        in_specs=[pl.BlockSpec(memory_space=pltpu.SMEM), vm, pl.BlockSpec(memory_space=pl.ANY), vm, vm, vm, vm],
        out_specs=(vm,) * 5,
        scratch_shapes=[pltpu.VMEM((1024, 768), bf), pltpu.VMEM((256, n), bf), pltpu.SemaphoreType.DMA((8,))],
        compiler_params=pltpu.CompilerParams(vmem_limit_bytes=48 << 20),
        cost_estimate=pl.CostEstimate(flops=4 << 30, bytes_accessed=10 << 20, transcendentals=4 << 20),
        name="attend",
    )(place, act, weight, cosine, sine, id_col, id_row)

def attend_back_kernel(mixed_ref, ga_ref, total_ref, cos_ref, sin_ref, id_col, id_row,
                       gm_ref, gk_acc, gv_acc, key_t):
    n = ga_ref.shape[0]
    gk_acc[...] = jnp.zeros_like(gk_acc)
    gv_acc[...] = jnp.zeros_like(gv_acc)
    @pl.loop(0, n // 256)
    def _(i):
        rows = pl.ds(pl.multiple_of(i * 256, 256), 256)
        key_t[:, rows] = mixed_ref[rows, 256:512].astype(f32).T.astype(bf)
    @pl.loop(0, 2)
    def _(pair):
        lanes = pl.multiple_of(pair * 128, 128)
        lane = lax.broadcasted_iota(jnp.int32, (256, 128), 1)
        sub = lax.broadcasted_iota(jnp.int32, (128, 256), 0)
        for i in range(4):
            width = min(256 * (i + 2), 1024)
            low = 256 * i
            k = mixed_ref[0:width, pl.ds(pl.multiple_of(256 + lanes, 128), 128)]
            v = mixed_ref[0:width, pl.ds(pl.multiple_of(512 + lanes, 128), 128)]
            q_all = mixed_ref[low:low + 256, pl.ds(lanes, 128)]
            g_all = ga_ref[low:low + 256, pl.ds(lanes, 128)]
            kt = key_t[pl.ds(lanes, 128), 0:width]
            ok = id_col[low:width, :][:, 0:1] <= id_row[0:1, low:low + 256]
            def one(half, gq):
                mine = lane // 64 == half
                q = jnp.where(mine, q_all, jnp.zeros_like(q_all))
                g = jnp.where(mine, g_all, jnp.zeros_like(g_all))
                s = dot(k, q, NT) - total_ref[pl.ds(pair * 2 + half, 1), low:low + 256]
                tail = jnp.where(ok, s[low:width], MASK_FILL)
                s = jnp.concatenate([s[0:low], tail], axis=0) if i else tail
                p = jnp.exp(s)
                gp = dot(v, g, NT)
                t = p * gp
                delta = jnp.sum(t, axis=0, keepdims=True)
                ds = (t - p * delta).astype(bf)
                gv_acc[0:width, pl.ds(lanes, 128)] += dot(p.astype(bf), g, NN)
                gk_acc[0:width, pl.ds(lanes, 128)] += dot(ds, q, NN)
                r = dot(kt, ds, NN)
                return jnp.where(sub // 64 == half, r, gq)
            gq = lax.fori_loop(0, 2, one, jnp.zeros((128, 256), f32))
            gq = gq.T * 0.125
            cosine = cos_ref[low:low + 256, :]; sine = sin_ref[low:low + 256, :]
            gm_ref[low:low + 256, pl.ds(lanes, 128)] = turn(gq, cosine, -sine).astype(bf)
    @pl.loop(0, n // 256)
    def _(i):
        rows = pl.ds(pl.multiple_of(i * 256, 256), 256)
        cosine = cos_ref[rows, :]; sine = sin_ref[rows, :]
        gm_ref[rows, 256:512] = turn(gk_acc[rows, :], cosine, -sine).astype(bf)
        gm_ref[rows, 512:768] = gv_acc[rows, :].astype(bf)

def attend_back(mixed, ga, total, cosine, sine, id_col, id_row):
    n = ga.shape[0]
    vm = pl.BlockSpec(memory_space=pltpu.VMEM)
    return pl.pallas_call(
        attend_back_kernel,
        out_shape=jax.ShapeDtypeStruct((n, 768), bf),
        in_specs=[vm] * 7, out_specs=vm,
        scratch_shapes=[pltpu.VMEM((n, 256), f32), pltpu.VMEM((n, 256), f32), pltpu.VMEM((256, n), bf)],
        compiler_params=pltpu.CompilerParams(vmem_limit_bytes=48 << 20),
        cost_estimate=pl.CostEstimate(flops=6 << 30, bytes_accessed=6 << 20, transcendentals=4 << 20),
        name="attend_back",
    )(mixed, ga, total, cosine, sine, id_col, id_row)

def project_kernel(place_ref, gm_ref, weight_hbm, normed_ref, gn_ref, gw_hbm, weight, gw, sems, osems):
    copies = []
    for p in range(8):
        copies.append(pltpu.make_async_copy(
            weight_hbm.at[pl.ds(128 * p, 128)],
            weight.at[pl.ds(pl.multiple_of(place_ref[p] * 128, 128), 128)], sems.at[p]))
        copies[-1].start()
    for c in copies: c.wait()
    n = gm_ref.shape[0]
    @pl.loop(0, n // 256)
    def _(i):
        rows = pl.ds(pl.multiple_of(i * 256, 256), 256)
        gn_ref[rows, :] = dot(gm_ref[rows, :], weight[...], NT).astype(bf)
    out = []
    @pl.loop(0, 4)
    def _(i):
        cols = pl.ds(pl.multiple_of(i * 256, 256), 256)
        gw[cols, :] = dot(normed_ref[:, cols], gm_ref[...], TN).astype(bf)
    for p in range(8):
        c = pltpu.make_async_copy(
            gw.at[pl.ds(pl.multiple_of(place_ref[p] * 128, 128), 128)],
            gw_hbm.at[pl.ds(128 * p, 128)], osems.at[p])
        c.start(); out.append(c)
    for c in out: c.wait()

def project_heads(place, gm, weight, normed):
    n = gm.shape[0]
    vm = pl.BlockSpec(memory_space=pltpu.VMEM)
    any_ = pl.BlockSpec(memory_space=pl.ANY)
    return pl.pallas_call(
        project_kernel,
        out_shape=(jax.ShapeDtypeStruct((n, 1024), bf), jax.ShapeDtypeStruct((1024, 768), bf)),
        in_specs=[pl.BlockSpec(memory_space=pltpu.SMEM), vm, any_, vm], out_specs=(vm, any_),
        scratch_shapes=[pltpu.VMEM((1024, 768), bf), pltpu.VMEM((1024, 768), bf),
                        pltpu.SemaphoreType.DMA((8,)), pltpu.SemaphoreType.DMA((8,))],
        compiler_params=pltpu.CompilerParams(vmem_limit_bytes=48 << 20),
        cost_estimate=pl.CostEstimate(flops=3 << 30, bytes_accessed=10 << 20, transcendentals=0),
        name="project_heads",
    )(place, gm, weight, normed)


FF2=1408; FFP=1536
def layer_norm(x):
    c = x - jnp.mean(x, axis=-1, keepdims=True)
    v = jnp.mean(c * c, axis=-1, keepdims=True)
    return c * lax.rsqrt(v + NORM_EPS)

FLIPS_A=((0,0),(1,0),(0,1),(1,1))
FLIPS_B=((0,0),(0,1),(1,0),(1,1))

def aligned(i, m): return pl.ds(pl.multiple_of(i * m, m), m)

def feed_kernel(me_ref, att_ref, attp_ref, act_ref, actp_ref, cot_ref, cotp_ref,
                a0, a1, a2, a3, b0, b1, b2, b3, da0, da1, da2, da3, db0, db1, db2, db3, outs,
                part_ref, outown_ref, gnown_ref, res_ref, wo_hbm,
                ga_keep, ga_send, gb_keep, gb_send, gda_keep, gda_send, gdb_keep, gdb_send,
                wg, wu, wd, wo, n2, n2t, cot, out_acc, gn_acc, dg, du, dd, sems, osem):
    me = me_ref[0]
    core = me % 2
    yx = me // 2
    small = []; big = []
    def start(lst, src, dst):
        k = len(small) + len(big)
        c = pltpu.make_async_copy(src, dst, sems.at[k]); c.start(); lst.append(c)
    for p in range(4):
        fa = FLIPS_A[p]; fb = FLIPS_B[p]
        ja = yx ^ (fa[0] + 2 * fa[1]); jb = yx ^ (fb[0] + 2 * fb[1])
        for which, src, j, col in ((0, (a0, a1, a2, a3)[p], ja, 0), (1, (b0, b1, b2, b3)[p], jb, 512)):
            for half in range(2):
                lo = col + 256 * half
                start(small, src.at[pl.ds(128 * half, 128), pl.ds(FF2, 256)],
                      wo.at[aligned(j * 2 + core, 128), pl.ds(lo, 256)])
                start(small, outs.at[4 * which + p, pl.ds(128 * half, 128)],
                      wo.at[aligned(j * 2 + 1 - core, 128), pl.ds(lo, 256)])
    for p in range(4):
        fa = FLIPS_A[p]; fb = FLIPS_B[p]
        ja = yx ^ (fa[0] + 2 * fa[1]); jb = yx ^ (fb[0] + 2 * fb[1])
        a = (a0, a1, a2, a3)[p]; b = (b0, b1, b2, b3)[p]
        for src, dst, j in ((a, wg, ja), (b, wu, jb)):
            start(big, src.at[pl.ds(0, 128), pl.ds(0, FF2)], dst.at[aligned(j * 2 + core, 128), pl.ds(0, FF2)])
            start(big, src.at[pl.ds(128, 128), pl.ds(0, FF2)], dst.at[aligned(j * 2 + 1 - core, 128), pl.ds(0, FF2)])
        start(big, (da0, da1, da2, da3)[p], wd.at[aligned(ja, 352), pl.ds(0, 512)])
        start(big, (db0, db1, db2, db3)[p], wd.at[aligned(jb, 352), pl.ds(512, 512)])
    wg[:, FF2:FFP] = jnp.zeros((1024, FFP - FF2), bf)
    wu[:, FF2:FFP] = jnp.zeros((1024, FFP - FF2), bf)
    wd[FF2:FFP, :] = jnp.zeros((FFP - FF2, 1024), bf)
    cot[0:256, :] = cot_ref[...]
    cot[256:512, :] = cotp_ref[...]
    for c in small: c.wait()
    keep = pltpu.make_async_copy(wo, wo_hbm, osem.at[16]); keep.start()
    def first(att, act, base, own):
        joined = jnp.concatenate([att[i] for i in range(4)], axis=1)
        res = act[...].astype(f32) + dot(joined, wo[...], NN)
        if own:
            res_ref[...] = res
        n = layer_norm(res)
        n2[base:base + 256, :] = n.astype(bf)
        n2t[:, base:base + 256] = n.T.astype(bf)
    first(att_ref, act_ref, 0, True)
    first(attp_ref, actp_ref, 256, False)
    out_acc[...] = jnp.zeros_like(out_acc)
    gn_acc[...] = jnp.zeros_like(gn_acc)
    for c in big: c.wait()
    @pl.loop(0, FFP // 256)
    def _(t):
        cols = aligned(t, 256)
        g = dot(n2[...], wg[:, cols], NN)
        u = dot(n2[...], wu[:, cols], NN)
        gh = dot(cot[...], wd[cols, :], NT)
        sig = 1.0 / (1.0 + jnp.exp(-g))
        act_ = g * sig
        h = (act_ * u).astype(bf)
        gu = (gh * act_).astype(bf)
        gg = (gh * u * (sig + act_ * (1.0 - sig))).astype(bf)
        out_acc[...] += dot(h, wd[cols, :], NN)
        gn_acc[...] += dot(gg, wg[:, cols], NT) + dot(gu, wu[:, cols], NT)
        dg[:, cols] = dot(n2t[...], gg, NN).astype(bf)
        du[:, cols] = dot(n2t[...], gu, NN).astype(bf)
        dd[cols, :] = dot(h, cot[...], TN).astype(bf)
    done = []
    def put(src, dst):
        c = pltpu.make_async_copy(src, dst, osem.at[len(done)]); c.start(); done.append(c)
    for q in range(4):
        fx, fy = FLIPS_A[q]
        j = yx ^ (fx + 2 * fy)
        rows = aligned(j, 256)
        put(dg.at[rows, pl.ds(0, FF2)], (ga_send if fx else ga_keep).at[pl.ds(256 * fy, 256)])
        put(du.at[rows, pl.ds(0, FF2)], (gb_send if fy else gb_keep).at[pl.ds(256 * fx, 256)])
        rows = aligned(j, 352)
        put(dd.at[rows, pl.ds(0, 512)], (gda_send if fx else gda_keep).at[pl.ds(352 * fy, 352)])
        put(dd.at[rows, pl.ds(512, 512)], (gdb_send if fy else gdb_keep).at[pl.ds(352 * fx, 352)])
    outown_ref[...] = out_acc[0:256, :]
    gnown_ref[...] = gn_acc[0:256, :]
    part_ref[0:256, :] = out_acc[256:512, :].astype(bf)
    part_ref[256:512, :] = gn_acc[256:512, :].astype(bf)
    keep.wait()
    for c in done: c.wait()

def feed(me, att, attp, act, actp, cot, cotp, a, b, da, db, outs):
    vm = pl.BlockSpec(memory_space=pltpu.VMEM)
    any_ = pl.BlockSpec(memory_space=pl.ANY)
    S = jax.ShapeDtypeStruct
    return pl.pallas_call(
        feed_kernel,
        out_shape=(S((512, 1024), bf), S((256, 1024), f32), S((256, 1024), f32), S((256, 1024), f32), S((1024, 1024), bf),
                   *[S((512, FF2), bf)] * 4, *[S((704, 512), bf)] * 4),
        in_specs=[pl.BlockSpec(memory_space=pltpu.SMEM)] + [vm] * 6 + [any_] * 17,
        out_specs=(vm,) * 4 + (any_,) * 9,
        scratch_shapes=[pltpu.VMEM((1024, FFP), bf), pltpu.VMEM((1024, FFP), bf), pltpu.VMEM((FFP, 1024), bf),
                        pltpu.VMEM((1024, 1024), bf), pltpu.VMEM((512, 1024), bf), pltpu.VMEM((1024, 512), bf),
                        pltpu.VMEM((512, 1024), bf), pltpu.VMEM((512, 1024), f32), pltpu.VMEM((512, 1024), f32),
                        pltpu.VMEM((1024, FFP), bf), pltpu.VMEM((1024, FFP), bf), pltpu.VMEM((FFP, 1024), bf),
                        pltpu.SemaphoreType.DMA((56,)), pltpu.SemaphoreType.DMA((17,))],
        compiler_params=pltpu.CompilerParams(vmem_limit_bytes=50 << 20),
        cost_estimate=pl.CostEstimate(flops=15 << 30, bytes_accessed=30 << 20, transcendentals=1 << 20),
        name="feed",
    )(me, att, attp, act, actp, cot, cotp, *a, *b, *da, *db, outs)

def branch_kernel(me_ref, part_ref, outown_ref, gnown_ref, res_ref, cot_ref, att_ref, wo_ref,
                  layer_ref, gres_ref, gatt_ref, keep_hbm, send_hbm, gw, osem):
    me = me_ref[0]
    core = me % 2
    yx = me // 2
    res = res_ref[...]
    layer_ref[...] = (res + (outown_ref[...] + part_ref[0:256, :].astype(f32))).astype(bf)
    g = gnown_ref[...] + part_ref[256:512, :].astype(f32)
    c = res - jnp.mean(res, axis=-1, keepdims=True)
    r = lax.rsqrt(jnp.mean(c * c, axis=-1, keepdims=True) + NORM_EPS)
    xh = c * r
    d = r * (g - jnp.mean(g, axis=-1, keepdims=True) - xh * jnp.mean(g * xh, axis=-1, keepdims=True))
    gres = cot_ref[...].astype(f32) + d
    gres_ref[...] = gres
    low = gres.astype(bf)
    for i in range(4):
        gw[256 * i : 256 * i + 256, :] = dot(att_ref[i], low, TN).astype(bf)
    done = []
    def put(src, dst):
        cc = pltpu.make_async_copy(src, dst, osem.at[len(done)]); cc.start(); done.append(cc)
    for q in range(4):
        fx, fy = FLIPS_A[q]
        j = yx ^ (fx + 2 * fy)
        for other, dst in ((0, keep_hbm), (1, send_hbm)):
            cc = 1 - core if other else core
            rows = aligned(j * 2 + cc, 128)
            put(gw.at[rows, pl.ds(0, 512)], dst.at[pl.ds(128 * (2 * fx + fy), 128), pl.ds(0, 512)])
            put(gw.at[rows, pl.ds(512, 512)], dst.at[pl.ds(128 * (2 * fy + fx), 128), pl.ds(512, 512)])
    ga = dot(low, wo_ref[...], NT).astype(bf)
    for z in range(4):
        gatt_ref[z] = ga[:, 256 * z:256 * z + 256]
    for cc in done: cc.wait()

def branch(me, part, outown, gnown, res, cot, att, wo):
    vm = pl.BlockSpec(memory_space=pltpu.VMEM)
    any_ = pl.BlockSpec(memory_space=pl.ANY)
    S = jax.ShapeDtypeStruct
    return pl.pallas_call(
        branch_kernel,
        out_shape=(S((256, 1024), bf), S((256, 1024), f32), S((4, 256, 256), bf), S((512, 1024), bf), S((512, 1024), bf)),
        in_specs=[pl.BlockSpec(memory_space=pltpu.SMEM)] + [vm] * 7,
        out_specs=(vm, vm, vm, any_, any_),
        scratch_shapes=[pltpu.VMEM((1024, 1024), bf), pltpu.SemaphoreType.DMA((16,))],
        compiler_params=pltpu.CompilerParams(vmem_limit_bytes=40 << 20),
        cost_estimate=pl.CostEstimate(flops=1 << 30, bytes_accessed=10 << 20, transcendentals=0),
        name="branch",
    )(me, part, outown, gnown, res, cot, att, wo)


def swap(array, bit):
    return lax.ppermute(array, "dp", [(i, i ^ bit) for i in range(8)])


def shift(array, bits):
    return lax.ppermute(array, "ctx", [(i, i ^ bits) for i in range(4)])


def add_low(left, right):
    return (left.astype(f32) + right.astype(f32)).astype(bf)


def split_even(matrix):
    n = matrix.shape[1] // 8
    parts = [matrix[:, n * i : n * i + n] for i in range(8)]
    return jnp.concatenate(parts[0::2], axis=1), jnp.concatenate(parts[1::2], axis=1)


def join_even(even, odd):
    n = even.shape[1] // 4
    parts = []
    for i in range(4):
        parts += [even[:, n * i : n * i + n], odd[:, n * i : n * i + n]]
    return jnp.concatenate(parts, axis=1)


def tie(value, anchor):
    return lax.optimization_barrier((value, anchor))[0]


def fast_device(
    activations,
    block_ids,
    cotangent,
    w_query,
    w_key,
    w_value,
    w_out,
    w_gate,
    w_up,
    w_down,
    m_query,
    m_key,
    m_value,
    m_out,
    m_gate,
    m_up,
    m_down,
    clip_threshold,
    momentum_coeff,
):
    me = lax.axis_index("dp")
    z = lax.axis_index("ctx")
    core = me % 2
    me_ref = me.astype(jnp.int32).reshape(1)
    _, span, width = activations.shape
    length = block_ids.shape[1]
    act = activations.reshape(span, width)
    cot = cotangent.reshape(span, width)
    g0, g1 = split_even(w_gate)
    u0, u1 = split_even(w_up)
    wide = jnp.concatenate([g0, u0, g1, u1, w_out], axis=1)
    wide = lax.all_gather(wide, "ctx", axis=0, tiled=True)
    act_all = lax.all_gather(act, "ctx", axis=0, tiled=True)
    heads = jnp.stack(
        [
            jnp.concatenate([w[:, 256 * i : 256 * i + 256] for w in (w_query, w_key, w_value)], 1)
            for i in range(4)
        ]
    )
    heads = lax.all_to_all(heads, "ctx", 0, 0, tiled=True).reshape(128, 768)
    hx = swap(heads, 2)
    hy = swap(jnp.concatenate([heads, hx], axis=0), 4)
    four = jnp.concatenate([heads, hy[:128], hx, hy[128:]], axis=0)
    heads_rel = jnp.concatenate([four, swap(four, 1)], axis=0)
    places = jnp.arange(8, dtype=jnp.int32)
    places = ((places >> 2 & 1) | (places >> 1 & 1) << 1 | (places & 1) << 2) ^ me
    mine = lax.dynamic_slice_in_dim(wide, core * 2 * FF2, 2 * FF2, 1)
    other = swap(lax.dynamic_slice_in_dim(wide, (1 - core) * 2 * FF2, 2 * FF2, 1), 1)
    out_rows = wide[:, 4 * FF2 :]

    def group(lo, col):
        gate = jnp.concatenate([mine[:, lo : lo + FF2], other[:, lo : lo + FF2]], axis=0)
        out = jnp.concatenate(
            [out_rows[:, col : col + 256], out_rows[:, col + 256 : col + 512]], axis=0
        )
        return jnp.concatenate([gate, out], axis=1)

    def spread(own, first, second):
        near = swap(own, first)
        return [own, near, swap(own, second), swap(near, second)]

    piece_a = spread(group(0, 0), 2, 4)
    piece_b = spread(group(FF2, 512), 4, 2)
    outs = swap(jnp.stack([p[:, FF2:] for p in piece_a + piece_b]), 1)
    down = tie(w_down, act_all)
    downs = jnp.stack([down] + [shift(down, d) for d in (1, 2, 3)])
    down = jnp.concatenate(
        [lax.dynamic_index_in_dim(downs, z ^ i, 0, keepdims=False) for i in range(4)], axis=0
    )
    piece_da = spread(down[:, :512], 2, 4)
    piece_db = spread(down[:, 512:], 4, 2)
    act_other = swap(act, 1)
    cot_other = swap(cot, 1)
    cosine, sine = rotary_tables(jnp.arange(length, dtype=jnp.int32), HEAD_DIM)
    cosine = jnp.concatenate([cosine] * 4, axis=1)
    sine = jnp.concatenate([-sine, sine, -sine, sine], axis=1)
    id_row = jnp.broadcast_to(block_ids, (8, length))
    id_col = jnp.broadcast_to(block_ids.reshape(length, 1), (length, 128))
    normed, mixed, attended, totals, peaks = attend(
        places, act_all, heads_rel, cosine, sine, id_col, id_row
    )
    attended = lax.all_to_all(attended.reshape(4, span, 256), "ctx", 0, 0, tiled=True)
    attended_other = swap(attended, 1)
    (part, out_own, back_own, residual, full_out, *grads) = feed(
        me_ref, attended, attended_other, act, act_other, cot, cot_other,
        piece_a, piece_b, piece_da, piece_db, outs,
    )
    ga_keep, ga_send, gb_keep, gb_send, gda_keep, gda_send, gdb_keep, gdb_send = grads
    part = swap(part, 1)
    layer_out, grad_residual, grad_attended, go_keep, go_send = branch(
        me_ref, part, out_own, back_own, residual, cot, attended, full_out
    )
    grad_attended = lax.all_to_all(grad_attended, "ctx", 0, 0, tiled=True).reshape(length, 256)
    grad_a = add_low(ga_keep, swap(ga_send, 2))
    grad_b = add_low(gb_keep, swap(gb_send, 4))
    grad_da = add_low(gda_keep, swap(gda_send, 2))
    grad_db = add_low(gdb_keep, swap(gdb_send, 4))
    grad_a = add_low(grad_a[:256], swap(grad_a[256:], 4))
    grad_b = add_low(grad_b[:256], swap(grad_b[256:], 2))
    grad_da = add_low(grad_da[:352], swap(grad_da[352:], 4))
    grad_db = add_low(grad_db[:352], swap(grad_db[352:], 2))
    grad_out = add_low(go_keep, swap(go_send, 1))
    grad_oa = add_low(grad_out[:256, :512], swap(grad_out[256:, :512], 2))
    grad_ob = add_low(grad_out[:256, 512:], swap(grad_out[256:, 512:], 4))
    grad_oa = add_low(grad_oa[:128], swap(grad_oa[128:], 4))
    grad_ob = add_low(grad_ob[:128], swap(grad_ob[128:], 2))

    def core_rows(which):
        return jnp.concatenate(
            [lax.dynamic_slice_in_dim(g, which * 128, 128, 0) for g in (grad_a, grad_b)], axis=1
        )

    own_half = core_rows(core)
    other_half = swap(core_rows(1 - core), 1)
    flip = core == 1
    grad_wide = jnp.concatenate(
        [
            jnp.where(flip, other_half, own_half),
            jnp.where(flip, own_half, other_half),
            grad_oa,
            grad_ob,
        ],
        axis=1,
    )
    grad_wide = lax.psum_scatter(grad_wide, "ctx", scatter_dimension=0, tiled=True).astype(f32)
    grad_d = jnp.concatenate([grad_da, grad_db], axis=1)
    grad_d = lax.psum_scatter(grad_d, "ctx", scatter_dimension=0, tiled=True).astype(f32)
    grad_mixed = attend_back(mixed, grad_attended, totals, cosine, sine, id_col, id_row)
    grad_normed, grad_heads = project_heads(places, grad_mixed, heads_rel, normed)
    grad_normed = lax.psum_scatter(grad_normed, "ctx", scatter_dimension=0, tiled=True)
    tokens_wide = act.astype(f32)
    unused, first_pull = jax.vjp(normalize, tokens_wide)
    input_grad = grad_residual + first_pull(grad_normed.astype(f32))[0]
    grad_heads = add_low(grad_heads[:512], swap(grad_heads[512:], 1))
    grad_heads = add_low(grad_heads[:256], swap(grad_heads[256:], 2))
    grad_heads = add_low(grad_heads[:128], swap(grad_heads[128:], 4))
    grad_heads = lax.all_to_all(grad_heads.reshape(4, 32, 768), "ctx", 0, 0, tiled=True)
    grad_heads = grad_heads.astype(f32)
    grad_qkv = [
        jnp.concatenate([grad_heads[i, :, 256 * k : 256 * k + 256] for i in range(4)], axis=1)
        for k in range(3)
    ]
    for bit in (1, 2, 4):
        peaks = jnp.maximum(peaks, swap(peaks, bit))
    peak_list = jnp.stack([peaks] + [shift(peaks, d) for d in (1, 2, 3)])[:, :4, 0]
    head_peaks = jnp.concatenate(
        [lax.dynamic_index_in_dim(peak_list, z ^ i, 0, keepdims=False) for i in range(4)]
    )
    weight_grads = (
        *grad_qkv,
        grad_wide[:, 4 * FF2 :],
        join_even(grad_wide[:, :FF2], grad_wide[:, 2 * FF2 : 3 * FF2]),
        join_even(grad_wide[:, FF2 : 2 * FF2], grad_wide[:, 3 * FF2 : 4 * FF2]),
        grad_d,
    )
    moments = (m_query, m_key, m_value, m_out, m_gate, m_up, m_down)
    new_moments = tuple(
        (momentum_coeff * moment + gradient for moment, gradient in zip(moments, weight_grads))
    )
    head_scale = jnp.sqrt(clip_threshold / jnp.maximum(head_peaks, clip_threshold))
    column_scale = jnp.repeat(head_scale, HEAD_DIM)
    rates = (LEARN_RATE, LEARN_RATE, LEARN_RATE, OUT_RATE, LEARN_RATE, LEARN_RATE, LEARN_RATE)
    shard_list = (w_query, w_key, w_value, w_out, w_gate, w_up, w_down)
    updated = [
        matrix.astype(jnp.float32) - rate * moment
        for matrix, moment, rate in zip(shard_list, new_moments, rates)
    ]
    updated[0] = updated[0] * column_scale[None, :]
    updated[1] = updated[1] * column_scale[None, :]
    updated = [matrix.astype(bf) for matrix in updated]
    return (
        layer_out[None],
        input_grad[None],
        *weight_grads,
        *new_moments,
        *updated,
        head_peaks,
        head_scale,
    )


def solution(mesh):
    placed = (
        P("dp", "ctx", None),
        P("dp", None),
        P("dp", "ctx", None),
        P(("dp", "ctx"), None),
        P(("dp", "ctx"), None),
        P(("dp", "ctx"), None),
        P(("dp", "ctx"), None),
        P(("dp", "ctx"), None),
        P(("dp", "ctx"), None),
        P(("dp", "ctx"), None),
        P(("dp", "ctx"), None),
        P(("dp", "ctx"), None),
        P(("dp", "ctx"), None),
        P(("dp", "ctx"), None),
        P(("dp", "ctx"), None),
        P(("dp", "ctx"), None),
        P(("dp", "ctx"), None),
        P(),
        P(),
    )
    fits = mesh.shape["dp"] == 8 and mesh.shape["ctx"] == 4
    return jax.shard_map(
        fast_device if fits else per_device,
        mesh=mesh,
        in_specs=placed,
        out_specs=(
            P("dp", "ctx", None),
            P("dp", "ctx", None),
            P(("dp", "ctx"), None),
            P(("dp", "ctx"), None),
            P(("dp", "ctx"), None),
            P(("dp", "ctx"), None),
            P(("dp", "ctx"), None),
            P(("dp", "ctx"), None),
            P(("dp", "ctx"), None),
            P(("dp", "ctx"), None),
            P(("dp", "ctx"), None),
            P(("dp", "ctx"), None),
            P(("dp", "ctx"), None),
            P(("dp", "ctx"), None),
            P(("dp", "ctx"), None),
            P(("dp", "ctx"), None),
            P(("dp", "ctx"), None),
            P(("dp", "ctx"), None),
            P(("dp", "ctx"), None),
            P(("dp", "ctx"), None),
            P(("dp", "ctx"), None),
            P(("dp", "ctx"), None),
            P(("dp", "ctx"), None),
            P(),
            P(),
        ),
        check_vma=False,
    )
```

```python
import math

import jax
import jax.numpy as jnp
from jax import lax
from jax.experimental import pallas as pl
from jax.experimental.pallas import tpu as pltpu
from jax.sharding import PartitionSpec as P

HEADS = 16
HEAD_DIM = 64


NORM_EPS = 1e-05
ROPE_BASE = 10000.0
LEARN_RATE = 0.0001
OUT_RATE = 0.0016
MASK_FILL = -1e30


def normalize(values):
    centred = values - jnp.mean(values, axis=-1, keepdims=True)
    spread = jnp.mean(centred * centred, axis=-1, keepdims=True)
    return centred * lax.rsqrt(spread + NORM_EPS)


def rotary_tables(positions, head_width):
    half_width = head_width // 2
    frequency = ROPE_BASE ** (-(jnp.arange(half_width, dtype=jnp.float32) * 2.0 / head_width))
    angles = positions.astype(jnp.float32)[:, None] * frequency[None, :]
    return (jnp.cos(angles), jnp.sin(angles))


def rotate(vectors, cosine, sine_table):
    half_width = vectors.shape[-1] // 2
    first_half = vectors[..., :half_width]
    second = vectors[..., half_width:]
    cos_wide = cosine[:, None, :]
    sin_wide = sine_table[:, None, :]
    return jnp.concatenate(
        [first_half * cos_wide - second * sin_wide, second * cos_wide + first_half * sin_wide],
        axis=-1,
    )


def swiglu(gate_proj, up_proj):
    return jax.nn.silu(gate_proj) * up_proj


def project(left_rows, matrix):
    return jnp.dot(left_rows, matrix, preferred_element_type=jnp.float32)


def project_back(grad_rows, matrix):
    return lax.dot_general(
        grad_rows, matrix, (((1,), (1,)), ((), ())), preferred_element_type=jnp.float32
    )


def shard_gradient(left_rows, right_rows):
    return lax.psum_scatter(
        lax.dot_general(
            left_rows, right_rows, (((0,), (0,)), ((), ())), preferred_element_type=jnp.float32
        ),
        ("dp", "ctx"),
        scatter_dimension=0,
        tiled=True,
    )


def per_device(
    activations,
    block_ids,
    cotangent,
    w_query,
    w_key,
    w_value,
    w_out,
    w_gate,
    w_up,
    w_down,
    m_query,
    m_key,
    m_value,
    m_out,
    m_gate,
    m_up,
    m_down,
    clip_threshold,
    momentum_coeff,
):
    shard_list = (w_query, w_key, w_value, w_out, w_gate, w_up, w_down)
    gathered = (
        lax.all_gather(shard_list[0], ("dp", "ctx"), axis=0, tiled=True),
        lax.all_gather(shard_list[1], ("dp", "ctx"), axis=0, tiled=True),
        lax.all_gather(shard_list[2], ("dp", "ctx"), axis=0, tiled=True),
        lax.all_gather(shard_list[3], ("dp", "ctx"), axis=0, tiled=True),
        lax.all_gather(shard_list[4], ("dp", "ctx"), axis=0, tiled=True),
        lax.all_gather(shard_list[5], ("dp", "ctx"), axis=0, tiled=True),
        lax.all_gather(shard_list[6], ("dp", "ctx"), axis=0, tiled=True),
    )
    full_query, full_key, full_value, full_out, full_gate, full_up, full_down = gathered
    seq_count, span_len, model_width = activations.shape
    ctx_place = lax.axis_index("ctx")
    positions = ctx_place * span_len + jnp.arange(span_len, dtype=jnp.int32)
    cosine, sine_table = rotary_tables(positions, HEAD_DIM)
    score_scale = 1.0 / math.sqrt(HEAD_DIM)

    def split_heads(matrix):
        return matrix.reshape(seq_count, span_len, HEADS, HEAD_DIM)

    tokens_flat = activations.astype(jnp.float32).reshape(-1, model_width)
    normed = normalize(tokens_flat).astype(jnp.bfloat16)
    queries = rotate(split_heads(project(normed, full_query)), cosine, sine_table).astype(
        jnp.bfloat16
    )
    key_rot = rotate(split_heads(project(normed, full_key)), cosine, sine_table).astype(
        jnp.bfloat16
    )
    value_rot = split_heads(project(normed, full_value)).astype(jnp.bfloat16)
    key_all, value_all = (
        lax.all_gather(key_rot, "ctx", axis=1, tiled=True),
        lax.all_gather(value_rot, "ctx", axis=1, tiled=True),
    )
    query_ids = lax.dynamic_slice_in_dim(block_ids, ctx_place * span_len, span_len, 1)
    allowed = (block_ids[:, None, :] <= query_ids[:, :, None])[:, None]

    def masked_scores():
        scores = (
            jnp.einsum("sqhd,skhd->shqk", queries, key_all, preferred_element_type=jnp.float32)
            * score_scale
        )
        return jnp.where(allowed, scores, MASK_FILL)

    masked = masked_scores()
    local_peaks = jnp.max(masked, axis=(0, 2, 3))
    row_top = jnp.max(masked, axis=-1, keepdims=True)
    log_total = row_top + jnp.log(jnp.sum(jnp.exp(masked - row_top), axis=-1, keepdims=True))
    probs_low = jnp.exp(masked - log_total).astype(jnp.bfloat16)
    attended = jnp.einsum(
        "shqk,skhd->sqhd", probs_low, value_all, preferred_element_type=jnp.float32
    )
    attended_low = attended.reshape(-1, model_width).astype(jnp.bfloat16)
    head_peaks = lax.pmax(local_peaks, ("dp", "ctx"))
    residual = tokens_flat + project(attended_low, full_out)
    normed2 = normalize(residual).astype(jnp.bfloat16)
    gate_proj = project(normed2, full_gate)
    up_proj = project(normed2, full_up)
    hidden_low = swiglu(gate_proj, up_proj).astype(jnp.bfloat16)
    layer_out = (
        (residual + project(hidden_low, full_down))
        .astype(jnp.bfloat16)
        .reshape(seq_count, span_len, model_width)
    )
    back_weights = (
        lax.all_gather(shard_list[0], ("dp", "ctx"), axis=0, tiled=True),
        lax.all_gather(shard_list[1], ("dp", "ctx"), axis=0, tiled=True),
        lax.all_gather(shard_list[2], ("dp", "ctx"), axis=0, tiled=True),
        lax.all_gather(shard_list[3], ("dp", "ctx"), axis=0, tiled=True),
        lax.all_gather(shard_list[4], ("dp", "ctx"), axis=0, tiled=True),
        lax.all_gather(shard_list[5], ("dp", "ctx"), axis=0, tiled=True),
        lax.all_gather(shard_list[6], ("dp", "ctx"), axis=0, tiled=True),
    )
    back_query, back_key, back_value, back_out, back_gate, back_up, back_down = back_weights
    grad_rows = cotangent.reshape(-1, model_width)
    grad_hidden = project_back(grad_rows, back_down)
    unused, gate_pull = jax.vjp(swiglu, gate_proj, up_proj)
    grad_gate_wide, grad_up_wide = gate_pull(grad_hidden)
    grad_gate_low = grad_gate_wide.astype(jnp.bfloat16)
    grad_up_low = grad_up_wide.astype(jnp.bfloat16)
    grad_normed2 = project_back(grad_gate_low, back_gate) + project_back(grad_up_low, back_up)
    unused, second_pull = jax.vjp(normalize, residual)
    grad_residual = grad_rows.astype(jnp.float32) + second_pull(grad_normed2)[0]
    grad_branch = grad_residual.astype(jnp.bfloat16)
    grad_attended = split_heads(project_back(grad_branch, back_out).astype(jnp.bfloat16))
    masked = masked_scores()
    probs = jnp.exp(masked - log_total)
    probs_again = probs.astype(jnp.bfloat16)
    grad_values_all = jnp.einsum(
        "shqk,sqhd->skhd", probs_again, grad_attended, preferred_element_type=jnp.float32
    )
    grad_probs = jnp.einsum(
        "sqhd,skhd->shqk", grad_attended, value_all, preferred_element_type=jnp.float32
    )
    score_grad = (
        probs * (grad_probs - jnp.sum(probs * grad_probs, axis=-1, keepdims=True))
    ).astype(jnp.bfloat16)
    grad_queries = (
        jnp.einsum("shqk,skhd->sqhd", score_grad, key_all, preferred_element_type=jnp.float32)
        * score_scale
    )
    grad_keys_all = (
        jnp.einsum("shqk,sqhd->skhd", score_grad, queries, preferred_element_type=jnp.float32)
        * score_scale
    )
    grad_keys, grad_values = (
        lax.psum_scatter(
            grad_keys_all.astype(jnp.bfloat16), "ctx", scatter_dimension=1, tiled=True
        ).astype(jnp.float32),
        lax.psum_scatter(
            grad_values_all.astype(jnp.bfloat16), "ctx", scatter_dimension=1, tiled=True
        ).astype(jnp.float32),
    )
    grad_query_low = (
        rotate(grad_queries, cosine, -sine_table).reshape(-1, model_width).astype(jnp.bfloat16)
    )
    grad_key_low = (
        rotate(grad_keys, cosine, -sine_table).reshape(-1, model_width).astype(jnp.bfloat16)
    )
    grad_value_low = grad_values.reshape(-1, model_width).astype(jnp.bfloat16)
    grad_normed = (
        project_back(grad_query_low, back_query)
        + project_back(grad_key_low, back_key)
        + project_back(grad_value_low, back_value)
    )
    unused, first_pull = jax.vjp(normalize, tokens_flat)
    input_grad = (grad_residual + first_pull(grad_normed)[0]).reshape(
        seq_count, span_len, model_width
    )
    weight_grads = (
        shard_gradient(normed, grad_query_low),
        shard_gradient(normed, grad_key_low),
        shard_gradient(normed, grad_value_low),
        shard_gradient(attended_low, grad_branch),
        shard_gradient(normed2, grad_gate_low),
        shard_gradient(normed2, grad_up_low),
        shard_gradient(hidden_low, grad_rows),
    )
    moments = (m_query, m_key, m_value, m_out, m_gate, m_up, m_down)
    new_moments = tuple(
        (momentum_coeff * moment + gradient for moment, gradient in zip(moments, weight_grads))
    )
    head_scale = jnp.sqrt(clip_threshold / jnp.maximum(head_peaks, clip_threshold))
    column_scale = jnp.repeat(head_scale, HEAD_DIM)
    rates = (LEARN_RATE, LEARN_RATE, LEARN_RATE, OUT_RATE, LEARN_RATE, LEARN_RATE, LEARN_RATE)
    updated = [
        matrix.astype(jnp.float32) - rate * moment
        for matrix, moment, rate in zip(shard_list, new_moments, rates)
    ]
    updated[0] = updated[0] * column_scale[None, :]
    updated[1] = updated[1] * column_scale[None, :]
    updated = [matrix.astype(jnp.bfloat16) for matrix in updated]
    return (
        layer_out,
        input_grad,
        weight_grads[0],
        weight_grads[1],
        weight_grads[2],
        weight_grads[3],
        weight_grads[4],
        weight_grads[5],
        weight_grads[6],
        new_moments[0],
        new_moments[1],
        new_moments[2],
        new_moments[3],
        new_moments[4],
        new_moments[5],
        new_moments[6],
        updated[0],
        updated[1],
        updated[2],
        updated[3],
        updated[4],
        updated[5],
        updated[6],
        head_peaks,
        head_scale,
    )


f32=jnp.float32; bf=jnp.bfloat16
NT=(((1,),(1,)),((),())); TN=(((0,),(0,)),((),())); NN=(((1,),(0,)),((),()))
def dot(a,b,dims): return lax.dot_general(a,b,dims,preferred_element_type=f32)

def turn(values, cosine, signed_sine):
    lane = lax.broadcasted_iota(jnp.int32, cosine.shape, 1)
    first = lane % 64 < 32
    parts = []
    for j in range(values.shape[1] // 128):
        part = values[:, 128 * j : 128 * j + 128]
        partner = jnp.where(first, pltpu.roll(part, 96, 1), pltpu.roll(part, 32, 1))
        parts.append(part * cosine + partner * signed_sine)
    return jnp.concatenate(parts, axis=1)

def attend_kernel(place_ref, act_ref, weight_hbm, cos_ref, sin_ref, id_col, id_row,
                  normed_ref, mixed_ref, attended_ref, total_ref, peak_ref,
                  weight, value_t, sems):
    copies = []
    for p in range(8):
        copies.append(pltpu.make_async_copy(
            weight_hbm.at[pl.ds(128 * p, 128)],
            weight.at[pl.ds(pl.multiple_of(place_ref[p] * 128, 128), 128)], sems.at[p]))
        copies[-1].start()
    n = normed_ref.shape[0]
    @pl.loop(0, n // 128)
    def _(i):
        rows = pl.ds(pl.multiple_of(i * 128, 128), 128)
        x = act_ref[pl.ds(pl.multiple_of(i // 2 * 352 + i % 2 * 128, 32), 128), :].astype(f32)
        c = x - jnp.mean(x, axis=-1, keepdims=True)
        v = jnp.mean(c * c, axis=-1, keepdims=True)
        normed_ref[rows, :] = (c * lax.rsqrt(v + NORM_EPS)).astype(bf)
    for c in copies: c.wait()
    @pl.loop(0, n // 256)
    def _(i):
        rows = pl.ds(pl.multiple_of(i * 256, 256), 256)
        mixed = dot(normed_ref[rows, :], weight[...], NN)
        cosine = cos_ref[rows, :]; sine = sin_ref[rows, :]
        mixed_ref[rows, 0:256] = (turn(mixed[:, 0:256], cosine, sine).astype(bf).astype(f32) * 0.125).astype(bf)
        mixed_ref[rows, 256:512] = turn(mixed[:, 256:512], cosine, sine).astype(bf)
        val = mixed[:, 512:768].astype(bf)
        mixed_ref[rows, 512:768] = val
        value_t[:, rows] = val.astype(f32).T.astype(bf)
    peak_ref[...] = jnp.zeros_like(peak_ref)
    @pl.loop(0, 4)
    def _(h):
        pair = h // 2
        lanes = pl.multiple_of(pair * 128, 128)
        lane = lax.broadcasted_iota(jnp.int32, (256, 128), 1)
        mine = lane // 64 == h % 2
        best = None
        for i in range(4):
            width = min(256 * (i + 2), 1024)
            low = 256 * i
            q = mixed_ref[low:low + 256, pl.ds(lanes, 128)]
            q = jnp.where(mine, q, jnp.zeros_like(q))
            s = dot(mixed_ref[0:width, pl.ds(pl.multiple_of(256 + lanes, 128), 128)], q, NT)
            ok = id_col[low:width, :][:, 0:1] <= id_row[0:1, low:low + 256]
            tail = jnp.where(ok, s[low:width], MASK_FILL)
            top = jnp.max(tail, axis=0, keepdims=True)
            if i:
                head = s[0:low]
                top = jnp.maximum(top, jnp.max(head, axis=0, keepdims=True))
                s = jnp.concatenate([head, tail], axis=0)
            else:
                s = tail
            e = jnp.exp(s - top)
            total = jnp.sum(e, axis=0, keepdims=True)
            o = dot(value_t[pl.ds(lanes, 128), 0:width], e.astype(bf), NN)
            o = o * (1.0 / total)
            o = o.T.astype(bf)
            old = attended_ref[low:low + 256, pl.ds(lanes, 128)]
            attended_ref[low:low + 256, pl.ds(lanes, 128)] = jnp.where(mine, o, old)
            total_ref[pl.ds(h, 1), low:low + 256] = top + jnp.log(total)
            m = jnp.max(top, axis=1, keepdims=True)
            best = m if best is None else jnp.maximum(best, m)
        peak_ref[pl.ds(h, 1), :] = jnp.broadcast_to(best, (1, 128))

def attend(place, act, weight, cosine, sine, id_col, id_row):
    n = cosine.shape[0]
    vm = pl.BlockSpec(memory_space=pltpu.VMEM)
    return pl.pallas_call(
        attend_kernel,
        out_shape=(jax.ShapeDtypeStruct((n, 1024), bf), jax.ShapeDtypeStruct((n, 768), bf),
                   jax.ShapeDtypeStruct((n, 256), bf), jax.ShapeDtypeStruct((8, n), f32),
                   jax.ShapeDtypeStruct((8, 128), f32)),
        in_specs=[pl.BlockSpec(memory_space=pltpu.SMEM), vm, pl.BlockSpec(memory_space=pl.ANY), vm, vm, vm, vm],
        out_specs=(vm,) * 5,
        scratch_shapes=[pltpu.VMEM((1024, 768), bf), pltpu.VMEM((256, n), bf), pltpu.SemaphoreType.DMA((8,))],
        compiler_params=pltpu.CompilerParams(vmem_limit_bytes=28 << 20),
        cost_estimate=pl.CostEstimate(flops=4294967296, bytes_accessed=10485760, transcendentals=0),
        name="attend",
    )(place, act, weight, cosine, sine, id_col, id_row)

def attend_back_kernel(mixed_ref, ga_ref, total_ref, cos_ref, sin_ref, id_col, id_row,
                       gm_ref, gk_acc, gv_acc, key_t):
    n = ga_ref.shape[0]
    gk_acc[...] = jnp.zeros_like(gk_acc)
    gv_acc[...] = jnp.zeros_like(gv_acc)
    @pl.loop(0, n // 256)
    def _(i):
        rows = pl.ds(pl.multiple_of(i * 256, 256), 256)
        key_t[:, rows] = mixed_ref[rows, 256:512].astype(f32).T.astype(bf)
    @pl.loop(0, 2)
    def _(pair):
        lanes = pl.multiple_of(pair * 128, 128)
        lane = lax.broadcasted_iota(jnp.int32, (256, 128), 1)
        sub = lax.broadcasted_iota(jnp.int32, (128, 256), 0)
        for i in range(4):
            width = min(256 * (i + 2), 1024)
            low = 256 * i
            k = mixed_ref[0:width, pl.ds(pl.multiple_of(256 + lanes, 128), 128)]
            v = mixed_ref[0:width, pl.ds(pl.multiple_of(512 + lanes, 128), 128)]
            q_all = mixed_ref[low:low + 256, pl.ds(lanes, 128)]
            g_all = ga_ref[low:low + 256, pl.ds(lanes, 128)]
            kt = key_t[pl.ds(lanes, 128), 0:width]
            ok = id_col[low:width, :][:, 0:1] <= id_row[0:1, low:low + 256]
            def one(half, gq):
                mine = lane // 64 == half
                q = jnp.where(mine, q_all, jnp.zeros_like(q_all))
                g = jnp.where(mine, g_all, jnp.zeros_like(g_all))
                s = dot(k, q, NT) - total_ref[pl.ds(pair * 2 + half, 1), low:low + 256]
                tail = jnp.where(ok, s[low:width], MASK_FILL)
                s = jnp.concatenate([s[0:low], tail], axis=0) if i else tail
                p = jnp.exp(s)
                gp = dot(v, g, NT)
                t = p * gp
                delta = jnp.sum(t, axis=0, keepdims=True)
                ds = (t - p * delta).astype(bf)
                gv_acc[0:width, pl.ds(lanes, 128)] += dot(p.astype(bf), g, NN)
                gk_acc[0:width, pl.ds(lanes, 128)] += dot(ds, q, NN)
                r = dot(kt, ds, NN)
                return jnp.where(sub // 64 == half, r, gq)
            gq = lax.fori_loop(0, 2, one, jnp.zeros((128, 256), f32))
            gq = gq.T * 0.125
            cosine = cos_ref[low:low + 256, :]; sine = sin_ref[low:low + 256, :]
            gm_ref[low:low + 256, pl.ds(lanes, 128)] = turn(gq, cosine, -sine).astype(bf)
    @pl.loop(0, n // 256)
    def _(i):
        rows = pl.ds(pl.multiple_of(i * 256, 256), 256)
        cosine = cos_ref[rows, :]; sine = sin_ref[rows, :]
        gm_ref[rows, 256:512] = turn(gk_acc[rows, :], cosine, -sine).astype(bf)
        gm_ref[rows, 512:768] = gv_acc[rows, :].astype(bf)

def attend_back(mixed, ga, total, cosine, sine, id_col, id_row):
    n = ga.shape[0]
    vm = pl.BlockSpec(memory_space=pltpu.VMEM)
    return pl.pallas_call(
        attend_back_kernel,
        out_shape=jax.ShapeDtypeStruct((n, 768), bf),
        in_specs=[vm] * 7, out_specs=vm,
        scratch_shapes=[pltpu.VMEM((n, 256), f32), pltpu.VMEM((n, 256), f32), pltpu.VMEM((256, n), bf)],
        compiler_params=pltpu.CompilerParams(vmem_limit_bytes=28 << 20),
        cost_estimate=pl.CostEstimate(flops=6442450944, bytes_accessed=6291456, transcendentals=0),
        name="attend_back",
    )(mixed, ga, total, cosine, sine, id_col, id_row)

def tokens_kernel(place_ref, gm_ref, weight_hbm, gn_ref, weight, sems):
    copies = []
    for p in range(8):
        copies.append(pltpu.make_async_copy(
            weight_hbm.at[pl.ds(128 * p, 128)],
            weight.at[pl.ds(pl.multiple_of(place_ref[p] * 128, 128), 128)], sems.at[p]))
        copies[-1].start()
    for c in copies: c.wait()
    @pl.loop(0, gm_ref.shape[0] // 256)
    def _(i):
        rows = pl.ds(pl.multiple_of(i * 256, 256), 256)
        gn_ref[rows, :] = dot(gm_ref[rows, :], weight[...], NT).astype(bf)

def project_tokens(place, gm, weight):
    n = gm.shape[0]
    vm = pl.BlockSpec(memory_space=pltpu.VMEM)
    return pl.pallas_call(
        tokens_kernel,
        out_shape=jax.ShapeDtypeStruct((n, 1024), bf),
        in_specs=[pl.BlockSpec(memory_space=pltpu.SMEM), vm, pl.BlockSpec(memory_space=pl.ANY)], out_specs=vm,
        scratch_shapes=[pltpu.VMEM((1024, 768), bf), pltpu.SemaphoreType.DMA((8,))],
        compiler_params=pltpu.CompilerParams(vmem_limit_bytes=28 << 20),
        cost_estimate=pl.CostEstimate(flops=1073741824, bytes_accessed=4194304, transcendentals=0),
        name="project_tokens",
    )(place, gm, weight)

def weights_kernel(place_ref, gm_ref, normed_ref, keep_hbm, send_hbm, gw, osems):
    @pl.loop(0, 4)
    def _(i):
        cols = pl.ds(pl.multiple_of(i * 256, 256), 256)
        gw[cols, :] = dot(normed_ref[:, cols], gm_ref[...], TN).astype(bf)
    out = []
    for p in range(8):
        c = pltpu.make_async_copy(
            gw.at[pl.ds(pl.multiple_of(place_ref[p] * 128, 128), 128)],
            (keep_hbm if p < 4 else send_hbm).at[pl.ds(128 * (p % 4), 128)], osems.at[p])
        c.start(); out.append(c)
    for c in out: c.wait()

def project_weights(place, gm, normed):
    vm = pl.BlockSpec(memory_space=pltpu.VMEM)
    any_ = pl.BlockSpec(memory_space=pl.ANY)
    return pl.pallas_call(
        weights_kernel,
        out_shape=(jax.ShapeDtypeStruct((512, 768), bf),) * 2,
        in_specs=[pl.BlockSpec(memory_space=pltpu.SMEM), vm, vm], out_specs=(any_,) * 2,
        scratch_shapes=[pltpu.VMEM((1024, 768), bf), pltpu.SemaphoreType.DMA((8,))],
        compiler_params=pltpu.CompilerParams(vmem_limit_bytes=28 << 20),
        cost_estimate=pl.CostEstimate(flops=1073741824, bytes_accessed=4194304, transcendentals=0),
        name="project_weights",
    )(place, gm, normed)


FF2=1408; FFP=1536
def layer_norm(x):
    c = x - jnp.mean(x, axis=-1, keepdims=True)
    v = jnp.mean(c * c, axis=-1, keepdims=True)
    return c * lax.rsqrt(v + NORM_EPS)

FLIPS_A=((0,0),(1,0),(0,1),(1,1))
FLIPS_B=((0,0),(0,1),(1,0),(1,1))

def aligned(i, m): return pl.ds(pl.multiple_of(i * m, m), m)

def feed_kernel(me_ref, att_ref, attp_ref, act_ref, actp_ref, cot_ref, cotp_ref,
                a0, a1, a2, a3, b0, b1, b2, b3, da0, da1, da2, da3, db0, db1, db2, db3, outs,
                part_ref, outown_ref, gnown_ref, res_ref, wo_hbm,
                ga_keep, ga_send, gb_keep, gb_send, gda_keep, gda_send, gdb_keep, gdb_send,
                wg, wu, wd, wo, n2, n2t, cot, out_acc, gn_acc, dg, du, dd, sems, osem):
    me = me_ref[0]
    core = me % 2
    yx = me // 2
    small = []; big = []
    def start(lst, src, dst):
        k = len(small) + len(big)
        c = pltpu.make_async_copy(src, dst, sems.at[k]); c.start(); lst.append(c)
    for p in range(4):
        fa = FLIPS_A[p]; fb = FLIPS_B[p]
        ja = yx ^ (fa[0] + 2 * fa[1]); jb = yx ^ (fb[0] + 2 * fb[1])
        for which, src, j, col in ((0, (a0, a1, a2, a3)[p], ja, 0), (1, (b0, b1, b2, b3)[p], jb, 512)):
            for half in range(2):
                lo = col + 256 * half
                start(small, src.at[pl.ds(128 * half, 128), pl.ds(FF2, 256)],
                      wo.at[aligned(j * 2 + core, 128), pl.ds(lo, 256)])
                start(small, outs.at[4 * which + p, pl.ds(128 * half, 128)],
                      wo.at[aligned(j * 2 + 1 - core, 128), pl.ds(lo, 256)])
    for p in range(4):
        fa = FLIPS_A[p]; fb = FLIPS_B[p]
        ja = yx ^ (fa[0] + 2 * fa[1]); jb = yx ^ (fb[0] + 2 * fb[1])
        a = (a0, a1, a2, a3)[p]; b = (b0, b1, b2, b3)[p]
        for src, dst, j in ((a, wg, ja), (b, wu, jb)):
            start(big, src.at[pl.ds(0, 128), pl.ds(0, FF2)], dst.at[aligned(j * 2 + core, 128), pl.ds(0, FF2)])
            start(big, src.at[pl.ds(128, 128), pl.ds(0, FF2)], dst.at[aligned(j * 2 + 1 - core, 128), pl.ds(0, FF2)])
        start(big, (da0, da1, da2, da3)[p], wd.at[aligned(ja, 352), pl.ds(0, 512)])
        start(big, (db0, db1, db2, db3)[p], wd.at[aligned(jb, 352), pl.ds(512, 512)])
    wg[:, FF2:FFP] = jnp.zeros((1024, FFP - FF2), bf)
    wu[:, FF2:FFP] = jnp.zeros((1024, FFP - FF2), bf)
    wd[FF2:FFP, :] = jnp.zeros((FFP - FF2, 1024), bf)
    cot[0:256, :] = cot_ref[...]
    cot[256:512, :] = cotp_ref[...]
    for c in small: c.wait()
    keep = pltpu.make_async_copy(wo, wo_hbm, osem.at[16]); keep.start()
    def first(att, act, base, own):
        joined = jnp.concatenate([att[i] for i in range(4)], axis=1)
        res = act[...].astype(f32) + dot(joined, wo[...], NN)
        if own:
            res_ref[...] = res
        n = layer_norm(res)
        n2[base:base + 256, :] = n.astype(bf)
        n2t[:, base:base + 256] = n.T.astype(bf)
    first(att_ref, act_ref, 0, True)
    first(attp_ref, actp_ref, 256, False)
    out_acc[...] = jnp.zeros_like(out_acc)
    gn_acc[...] = jnp.zeros_like(gn_acc)
    for c in big: c.wait()
    @pl.loop(0, FFP // 256)
    def _(t):
        cols = aligned(t, 256)
        g = dot(n2[...], wg[:, cols], NN)
        u = dot(n2[...], wu[:, cols], NN)
        gh = dot(cot[...], wd[cols, :], NT)
        sig = 1.0 / (1.0 + jnp.exp(-g))
        act_ = g * sig
        h = (act_ * u).astype(bf)
        gu = (gh * act_).astype(bf)
        gg = (gh * u * (sig + act_ * (1.0 - sig))).astype(bf)
        out_acc[...] += dot(h, wd[cols, :], NN)
        gn_acc[...] += dot(gg, wg[:, cols], NT) + dot(gu, wu[:, cols], NT)
        dg[:, cols] = dot(n2t[...], gg, NN).astype(bf)
        du[:, cols] = dot(n2t[...], gu, NN).astype(bf)
        dd[cols, :] = dot(h, cot[...], TN).astype(bf)
    done = []
    def put(src, dst):
        c = pltpu.make_async_copy(src, dst, osem.at[len(done)]); c.start(); done.append(c)
    for q in range(4):
        fx, fy = FLIPS_A[q]
        j = yx ^ (fx + 2 * fy)
        rows = aligned(j, 256)
        put(dg.at[rows, pl.ds(0, FF2)], (ga_send if fx else ga_keep).at[pl.ds(256 * fy, 256)])
        put(du.at[rows, pl.ds(0, FF2)], (gb_send if fy else gb_keep).at[pl.ds(256 * fx, 256)])
        rows = aligned(j, 352)
        put(dd.at[rows, pl.ds(0, 512)], (gda_send if fx else gda_keep).at[pl.ds(352 * fy, 352)])
        put(dd.at[rows, pl.ds(512, 512)], (gdb_send if fy else gdb_keep).at[pl.ds(352 * fx, 352)])
    outown_ref[...] = out_acc[0:256, :]
    gnown_ref[...] = gn_acc[0:256, :]
    part_ref[0:256, :] = out_acc[256:512, :].astype(bf)
    part_ref[256:512, :] = gn_acc[256:512, :].astype(bf)
    keep.wait()
    for c in done: c.wait()

def feed(me, att, attp, act, actp, cot, cotp, a, b, da, db, outs):
    vm = pl.BlockSpec(memory_space=pltpu.VMEM)
    any_ = pl.BlockSpec(memory_space=pl.ANY)
    S = jax.ShapeDtypeStruct
    return pl.pallas_call(
        feed_kernel,
        out_shape=(S((512, 1024), bf), S((256, 1024), f32), S((256, 1024), f32), S((256, 1024), f32), S((1024, 1024), bf),
                   *[S((512, FF2), bf)] * 4, *[S((704, 512), bf)] * 4),
        in_specs=[pl.BlockSpec(memory_space=pltpu.SMEM)] + [vm] * 6 + [any_] * 17,
        out_specs=(vm,) * 4 + (any_,) * 9,
        scratch_shapes=[pltpu.VMEM((1024, FFP), bf), pltpu.VMEM((1024, FFP), bf), pltpu.VMEM((FFP, 1024), bf),
                        pltpu.VMEM((1024, 1024), bf), pltpu.VMEM((512, 1024), bf), pltpu.VMEM((1024, 512), bf),
                        pltpu.VMEM((512, 1024), bf), pltpu.VMEM((512, 1024), f32), pltpu.VMEM((512, 1024), f32),
                        pltpu.VMEM((1024, FFP), bf), pltpu.VMEM((1024, FFP), bf), pltpu.VMEM((FFP, 1024), bf),
                        pltpu.SemaphoreType.DMA((56,)), pltpu.SemaphoreType.DMA((17,))],
        compiler_params=pltpu.CompilerParams(vmem_limit_bytes=50 << 20),
        cost_estimate=pl.CostEstimate(flops=16106127360, bytes_accessed=31457280, transcendentals=0),
        name="feed",
    )(me, att, attp, act, actp, cot, cotp, *a, *b, *da, *db, outs)

def branch_kernel(me_ref, part_ref, outown_ref, gnown_ref, res_ref, cot_ref, att_ref, wo_ref,
                  layer_ref, gres_ref, gatt_ref, keep_hbm, send_hbm, gw, osem):
    me = me_ref[0]
    core = me % 2
    yx = me // 2
    res = res_ref[...]
    layer_ref[...] = (res + (outown_ref[...] + part_ref[0:256, :].astype(f32))).astype(bf)
    g = gnown_ref[...] + part_ref[256:512, :].astype(f32)
    c = res - jnp.mean(res, axis=-1, keepdims=True)
    r = lax.rsqrt(jnp.mean(c * c, axis=-1, keepdims=True) + NORM_EPS)
    xh = c * r
    d = r * (g - jnp.mean(g, axis=-1, keepdims=True) - xh * jnp.mean(g * xh, axis=-1, keepdims=True))
    gres = cot_ref[...].astype(f32) + d
    gres_ref[...] = gres
    low = gres.astype(bf)
    for i in range(4):
        gw[256 * i : 256 * i + 256, :] = dot(att_ref[i], low, TN).astype(bf)
    done = []
    def put(src, dst):
        cc = pltpu.make_async_copy(src, dst, osem.at[len(done)]); cc.start(); done.append(cc)
    for q in range(4):
        fx, fy = FLIPS_A[q]
        j = yx ^ (fx + 2 * fy)
        for other, dst in ((0, keep_hbm), (1, send_hbm)):
            cc = 1 - core if other else core
            rows = aligned(j * 2 + cc, 128)
            put(gw.at[rows, pl.ds(0, 512)], dst.at[pl.ds(128 * (2 * fx + fy), 128), pl.ds(0, 512)])
            put(gw.at[rows, pl.ds(512, 512)], dst.at[pl.ds(128 * (2 * fy + fx), 128), pl.ds(512, 512)])
    ga = dot(low, wo_ref[...], NT).astype(bf)
    for z in range(4):
        gatt_ref[z] = ga[:, 256 * z:256 * z + 256]
    for cc in done: cc.wait()

def branch(me, part, outown, gnown, res, cot, att, wo):
    vm = pl.BlockSpec(memory_space=pltpu.VMEM)
    any_ = pl.BlockSpec(memory_space=pl.ANY)
    S = jax.ShapeDtypeStruct
    return pl.pallas_call(
        branch_kernel,
        out_shape=(S((256, 1024), bf), S((256, 1024), f32), S((4, 256, 256), bf), S((512, 1024), bf), S((512, 1024), bf)),
        in_specs=[pl.BlockSpec(memory_space=pltpu.SMEM)] + [vm] * 7,
        out_specs=(vm, vm, vm, any_, any_),
        scratch_shapes=[pltpu.VMEM((1024, 1024), bf), pltpu.SemaphoreType.DMA((16,))],
        compiler_params=pltpu.CompilerParams(vmem_limit_bytes=40 << 20),
        cost_estimate=pl.CostEstimate(flops=1073741824, bytes_accessed=10485760, transcendentals=0),
        name="branch",
    )(me, part, outown, gnown, res, cot, att, wo)


def swap(array, bit):
    return lax.ppermute(array, "dp", [(i, i ^ bit) for i in range(8)])


def shift(array, bits):
    return lax.ppermute(array, "ctx", [(i, i ^ bits) for i in range(4)])


def add_low(left, right):
    return (left.astype(f32) + right.astype(f32)).astype(bf)


def split_even(matrix):
    n = matrix.shape[1] // 8
    parts = [matrix[:, n * i : n * i + n] for i in range(8)]
    return jnp.concatenate(parts[0::2], axis=1), jnp.concatenate(parts[1::2], axis=1)


def join_even(even, odd):
    n = even.shape[1] // 4
    parts = []
    for i in range(4):
        parts += [even[:, n * i : n * i + n], odd[:, n * i : n * i + n]]
    return jnp.concatenate(parts, axis=1)


def tie(value, *anchors):
    return lax.optimization_barrier((value, *anchors))[0]


def fast_device(
    activations,
    block_ids,
    cotangent,
    w_query,
    w_key,
    w_value,
    w_out,
    w_gate,
    w_up,
    w_down,
    m_query,
    m_key,
    m_value,
    m_out,
    m_gate,
    m_up,
    m_down,
    clip_threshold,
    momentum_coeff,
):
    me = lax.axis_index("dp")
    z = lax.axis_index("ctx")
    core = me % 2
    me_ref = me.astype(jnp.int32).reshape(1)
    _, span, width = activations.shape
    length = block_ids.shape[1]
    act = activations.reshape(span, width)
    cot = cotangent.reshape(span, width)
    act_other = swap(act, 1)
    cot_other = swap(cot, 1)
    g0, g1 = split_even(w_gate)
    u0, u1 = split_even(w_up)
    even = jnp.stack([g0, u0])
    odd = jnp.stack([g1, u1])
    flip = core == 1
    mine = jnp.where(flip, odd, even)
    other = swap(jnp.where(flip, even, odd), 1)
    out_rows = jnp.stack([w_out[:, :512], w_out[:, 512:]]).reshape(2, 32, 2, 256)
    wide = jnp.stack([mine, other], axis=1)
    wide = jnp.concatenate([wide, out_rows.transpose(0, 2, 1, 3)], axis=3)
    wide = lax.all_gather(wide, "ctx", axis=2, tiled=True).reshape(2, 256, FF2 + 256)
    padded = jnp.concatenate([act, w_down, jnp.zeros((8, width), bf)], axis=0)
    rows_all = lax.all_gather(padded, "ctx", axis=0, tiled=True)
    heads = jnp.stack(
        [
            jnp.concatenate([w[:, 256 * i : 256 * i + 256] for w in (w_query, w_key, w_value)], 1)
            for i in range(4)
        ]
    )
    heads = lax.all_to_all(heads, "ctx", 0, 0, tiled=True).reshape(128, 768)
    hx = swap(heads, 2)
    hy = swap(jnp.concatenate([heads, hx], axis=0), 4)
    four = jnp.concatenate([heads, hy[:128], hx, hy[128:]], axis=0)
    heads_rel = jnp.concatenate([four, swap(four, 1)], axis=0)
    places = jnp.arange(8, dtype=jnp.int32)
    places = ((places >> 2 & 1) | (places >> 1 & 1) << 1 | (places & 1) << 2) ^ me
    wide, act_other, cot_other = lax.optimization_barrier((wide, act_other, cot_other))

    def spread(own, first, second):
        near = swap(own, first)
        return [own, near, swap(own, second), swap(near, second)]

    piece_a = spread(wide[0], 2, 4)
    piece_b = spread(wide[1], 4, 2)
    outs = swap(jnp.stack([p[:, FF2:] for p in piece_a + piece_b]), 1)
    down = jnp.concatenate(
        [rows_all[352 * i + 256 : 352 * i + 344] for i in range(4)], axis=0
    )
    piece_da = spread(down[:, :512], 2, 4)
    piece_db = spread(down[:, 512:], 4, 2)
    cosine, sine = rotary_tables(jnp.arange(length, dtype=jnp.int32), HEAD_DIM)
    cosine = jnp.concatenate([cosine] * 4, axis=1)
    sine = jnp.concatenate([-sine, sine, -sine, sine], axis=1)
    id_row = jnp.broadcast_to(block_ids, (8, length))
    id_col = jnp.broadcast_to(block_ids.reshape(length, 1), (length, 128))
    normed, mixed, attended, totals, peaks = attend(
        places, tie(rows_all, *piece_a, *piece_b), heads_rel, cosine, sine, id_col, id_row
    )
    attended = tie(attended, *piece_da[1:3], *piece_db[1:3])
    attended = lax.all_to_all(attended.reshape(4, span, 256), "ctx", 0, 0, tiled=True)
    attended_other = swap(attended, 1)
    (part, out_own, back_own, residual, full_out, *grads) = feed(
        me_ref, attended, attended_other, act, act_other, cot, cot_other,
        piece_a, piece_b, piece_da, piece_db, outs,
    )
    ga_keep, ga_send, gb_keep, gb_send, gda_keep, gda_send, gdb_keep, gdb_send = grads
    part = swap(part, 1)
    gda_send, gdb_send, part = lax.optimization_barrier((gda_send, gdb_send, part))
    layer_out, grad_residual, grad_attended, go_keep, go_send = branch(
        me_ref, part, out_own, back_own, residual, cot, attended, full_out
    )
    grad_attended = lax.all_to_all(grad_attended, "ctx", 0, 0, tiled=True).reshape(length, 256)
    grad_da = add_low(gda_keep, swap(gda_send, 2))
    grad_db = add_low(gdb_keep, swap(gdb_send, 4))
    ga_send, gb_send, grad_da, grad_db, grad_attended = lax.optimization_barrier(
        (ga_send, gb_send, grad_da, grad_db, grad_attended)
    )
    grad_a = add_low(ga_keep, swap(ga_send, 2))
    grad_b = add_low(gb_keep, swap(gb_send, 4))
    grad_a = add_low(grad_a[:256], swap(grad_a[256:], 4))
    grad_b = add_low(grad_b[:256], swap(grad_b[256:], 2))
    grad_da = add_low(grad_da[:352], swap(grad_da[352:], 4))
    grad_db = add_low(grad_db[:352], swap(grad_db[352:], 2))
    grad_out = add_low(go_keep, swap(go_send, 1))
    grad_oa = add_low(grad_out[:256, :512], swap(grad_out[256:, :512], 2))
    grad_ob = add_low(grad_out[:256, 512:], swap(grad_out[256:, 512:], 4))
    grad_oa = add_low(grad_oa[:128], swap(grad_oa[128:], 4))
    grad_ob = add_low(grad_ob[:128], swap(grad_ob[128:], 2))

    def core_rows(which):
        return jnp.concatenate(
            [lax.dynamic_slice_in_dim(g, which * 128, 128, 0) for g in (grad_a, grad_b)], axis=1
        )

    own_half = core_rows(core)
    other_half = swap(core_rows(1 - core), 1)
    grad_wide = jnp.concatenate(
        [
            jnp.where(flip, other_half, own_half),
            jnp.where(flip, own_half, other_half),
            grad_oa,
            grad_ob,
        ],
        axis=1,
    )
    grad_wide = lax.psum_scatter(grad_wide, "ctx", scatter_dimension=0, tiled=True).astype(f32)
    grad_d = jnp.concatenate([grad_da, grad_db], axis=1)
    grad_d = lax.psum_scatter(grad_d, "ctx", scatter_dimension=0, tiled=True).astype(f32)
    grad_mixed = attend_back(mixed, grad_attended, totals, cosine, sine, id_col, id_row)
    grad_normed = project_tokens(places, grad_mixed, heads_rel)
    grad_heads = project_weights(places, tie(grad_mixed, grad_normed), normed)
    peaks = tie(peaks, grad_normed)
    grad_normed = lax.psum_scatter(grad_normed, "ctx", scatter_dimension=0, tiled=True)
    tokens_wide = act.astype(f32)
    unused, first_pull = jax.vjp(normalize, tokens_wide)
    input_grad = grad_residual + first_pull(grad_normed.astype(f32))[0]
    grad_heads = add_low(grad_heads[0], swap(grad_heads[1], 1))
    grad_heads = add_low(grad_heads[:256], swap(grad_heads[256:], 2))
    grad_heads = add_low(grad_heads[:128], swap(grad_heads[128:], 4))
    grad_heads = lax.all_to_all(grad_heads.reshape(4, 32, 768), "ctx", 0, 0, tiled=True)
    grad_heads = grad_heads.astype(f32)
    grad_qkv = [
        jnp.concatenate([grad_heads[i, :, 256 * k : 256 * k + 256] for i in range(4)], axis=1)
        for k in range(3)
    ]
    for bit in (1, 2, 4):
        peaks = jnp.maximum(peaks, swap(peaks, bit))
    peaks = jnp.concatenate([peaks, shift(peaks, 1)], axis=0)
    peaks = jnp.concatenate([peaks, shift(peaks, 2)], axis=0)
    peak_list = peaks.reshape(4, 8, 128)[:, :4, 0]
    head_peaks = jnp.concatenate(
        [lax.dynamic_index_in_dim(peak_list, z ^ i, 0, keepdims=False) for i in range(4)]
    )
    weight_grads = (
        *grad_qkv,
        grad_wide[:, 4 * FF2 :],
        join_even(grad_wide[:, :FF2], grad_wide[:, 2 * FF2 : 3 * FF2]),
        join_even(grad_wide[:, FF2 : 2 * FF2], grad_wide[:, 3 * FF2 : 4 * FF2]),
        grad_d,
    )
    moments = (m_query, m_key, m_value, m_out, m_gate, m_up, m_down)
    new_moments = tuple(
        (momentum_coeff * moment + gradient for moment, gradient in zip(moments, weight_grads))
    )
    head_scale = jnp.sqrt(clip_threshold / jnp.maximum(head_peaks, clip_threshold))
    column_scale = jnp.repeat(head_scale, HEAD_DIM)
    rates = (LEARN_RATE, LEARN_RATE, LEARN_RATE, OUT_RATE, LEARN_RATE, LEARN_RATE, LEARN_RATE)
    shard_list = (w_query, w_key, w_value, w_out, w_gate, w_up, w_down)
    updated = [
        matrix.astype(jnp.float32) - rate * moment
        for matrix, moment, rate in zip(shard_list, new_moments, rates)
    ]
    updated[0] = updated[0] * column_scale[None, :]
    updated[1] = updated[1] * column_scale[None, :]
    updated = [matrix.astype(bf) for matrix in updated]
    return (
        layer_out[None],
        input_grad[None],
        *weight_grads,
        *new_moments,
        *updated,
        head_peaks,
        head_scale,
    )


def solution(mesh):
    placed = (
        P("dp", "ctx", None),
        P("dp", None),
        P("dp", "ctx", None),
        P(("dp", "ctx"), None),
        P(("dp", "ctx"), None),
        P(("dp", "ctx"), None),
        P(("dp", "ctx"), None),
        P(("dp", "ctx"), None),
        P(("dp", "ctx"), None),
        P(("dp", "ctx"), None),
        P(("dp", "ctx"), None),
        P(("dp", "ctx"), None),
        P(("dp", "ctx"), None),
        P(("dp", "ctx"), None),
        P(("dp", "ctx"), None),
        P(("dp", "ctx"), None),
        P(("dp", "ctx"), None),
        P(),
        P(),
    )
    fits = mesh.shape["dp"] == 8 and mesh.shape["ctx"] == 4
    return jax.shard_map(
        fast_device if fits else per_device,
        mesh=mesh,
        in_specs=placed,
        out_specs=(
            P("dp", "ctx", None),
            P("dp", "ctx", None),
            P(("dp", "ctx"), None),
            P(("dp", "ctx"), None),
            P(("dp", "ctx"), None),
            P(("dp", "ctx"), None),
            P(("dp", "ctx"), None),
            P(("dp", "ctx"), None),
            P(("dp", "ctx"), None),
            P(("dp", "ctx"), None),
            P(("dp", "ctx"), None),
            P(("dp", "ctx"), None),
            P(("dp", "ctx"), None),
            P(("dp", "ctx"), None),
            P(("dp", "ctx"), None),
            P(("dp", "ctx"), None),
            P(("dp", "ctx"), None),
            P(("dp", "ctx"), None),
            P(("dp", "ctx"), None),
            P(("dp", "ctx"), None),
            P(("dp", "ctx"), None),
            P(("dp", "ctx"), None),
            P(("dp", "ctx"), None),
            P(),
            P(),
        ),
        check_vma=False,
    )
```

```python
import math

import jax
import jax.numpy as jnp
from jax import lax
from jax.experimental import pallas as pl
from jax.experimental.pallas import tpu as pltpu
from jax.sharding import PartitionSpec as P

HEADS = 16
HEAD_DIM = 64


NORM_EPS = 1e-05
ROPE_BASE = 10000.0
LEARN_RATE = 0.0001
OUT_RATE = 0.0016
MASK_FILL = -1e30


def normalize(values):
    centred = values - jnp.mean(values, axis=-1, keepdims=True)
    spread = jnp.mean(centred * centred, axis=-1, keepdims=True)
    return centred * lax.rsqrt(spread + NORM_EPS)


def rotary_tables(positions, head_width):
    half_width = head_width // 2
    frequency = ROPE_BASE ** (-(jnp.arange(half_width, dtype=jnp.float32) * 2.0 / head_width))
    angles = positions.astype(jnp.float32)[:, None] * frequency[None, :]
    return (jnp.cos(angles), jnp.sin(angles))


def rotate(vectors, cosine, sine_table):
    half_width = vectors.shape[-1] // 2
    first_half = vectors[..., :half_width]
    second = vectors[..., half_width:]
    cos_wide = cosine[:, None, :]
    sin_wide = sine_table[:, None, :]
    return jnp.concatenate(
        [first_half * cos_wide - second * sin_wide, second * cos_wide + first_half * sin_wide],
        axis=-1,
    )


def swiglu(gate_proj, up_proj):
    return jax.nn.silu(gate_proj) * up_proj


def project(left_rows, matrix):
    return jnp.dot(left_rows, matrix, preferred_element_type=jnp.float32)


def project_back(grad_rows, matrix):
    return lax.dot_general(
        grad_rows, matrix, (((1,), (1,)), ((), ())), preferred_element_type=jnp.float32
    )


def shard_gradient(left_rows, right_rows):
    return lax.psum_scatter(
        lax.dot_general(
            left_rows, right_rows, (((0,), (0,)), ((), ())), preferred_element_type=jnp.float32
        ),
        ("dp", "ctx"),
        scatter_dimension=0,
        tiled=True,
    )


def per_device(
    activations,
    block_ids,
    cotangent,
    w_query,
    w_key,
    w_value,
    w_out,
    w_gate,
    w_up,
    w_down,
    m_query,
    m_key,
    m_value,
    m_out,
    m_gate,
    m_up,
    m_down,
    clip_threshold,
    momentum_coeff,
):
    shard_list = (w_query, w_key, w_value, w_out, w_gate, w_up, w_down)
    gathered = (
        lax.all_gather(shard_list[0], ("dp", "ctx"), axis=0, tiled=True),
        lax.all_gather(shard_list[1], ("dp", "ctx"), axis=0, tiled=True),
        lax.all_gather(shard_list[2], ("dp", "ctx"), axis=0, tiled=True),
        lax.all_gather(shard_list[3], ("dp", "ctx"), axis=0, tiled=True),
        lax.all_gather(shard_list[4], ("dp", "ctx"), axis=0, tiled=True),
        lax.all_gather(shard_list[5], ("dp", "ctx"), axis=0, tiled=True),
        lax.all_gather(shard_list[6], ("dp", "ctx"), axis=0, tiled=True),
    )
    full_query, full_key, full_value, full_out, full_gate, full_up, full_down = gathered
    seq_count, span_len, model_width = activations.shape
    ctx_place = lax.axis_index("ctx")
    positions = ctx_place * span_len + jnp.arange(span_len, dtype=jnp.int32)
    cosine, sine_table = rotary_tables(positions, HEAD_DIM)
    score_scale = 1.0 / math.sqrt(HEAD_DIM)

    def split_heads(matrix):
        return matrix.reshape(seq_count, span_len, HEADS, HEAD_DIM)

    tokens_flat = activations.astype(jnp.float32).reshape(-1, model_width)
    normed = normalize(tokens_flat).astype(jnp.bfloat16)
    queries = rotate(split_heads(project(normed, full_query)), cosine, sine_table).astype(
        jnp.bfloat16
    )
    key_rot = rotate(split_heads(project(normed, full_key)), cosine, sine_table).astype(
        jnp.bfloat16
    )
    value_rot = split_heads(project(normed, full_value)).astype(jnp.bfloat16)
    key_all, value_all = (
        lax.all_gather(key_rot, "ctx", axis=1, tiled=True),
        lax.all_gather(value_rot, "ctx", axis=1, tiled=True),
    )
    query_ids = lax.dynamic_slice_in_dim(block_ids, ctx_place * span_len, span_len, 1)
    allowed = (block_ids[:, None, :] <= query_ids[:, :, None])[:, None]

    def masked_scores():
        scores = (
            jnp.einsum("sqhd,skhd->shqk", queries, key_all, preferred_element_type=jnp.float32)
            * score_scale
        )
        return jnp.where(allowed, scores, MASK_FILL)

    masked = masked_scores()
    local_peaks = jnp.max(masked, axis=(0, 2, 3))
    row_top = jnp.max(masked, axis=-1, keepdims=True)
    log_total = row_top + jnp.log(jnp.sum(jnp.exp(masked - row_top), axis=-1, keepdims=True))
    probs_low = jnp.exp(masked - log_total).astype(jnp.bfloat16)
    attended = jnp.einsum(
        "shqk,skhd->sqhd", probs_low, value_all, preferred_element_type=jnp.float32
    )
    attended_low = attended.reshape(-1, model_width).astype(jnp.bfloat16)
    head_peaks = lax.pmax(local_peaks, ("dp", "ctx"))
    residual = tokens_flat + project(attended_low, full_out)
    normed2 = normalize(residual).astype(jnp.bfloat16)
    gate_proj = project(normed2, full_gate)
    up_proj = project(normed2, full_up)
    hidden_low = swiglu(gate_proj, up_proj).astype(jnp.bfloat16)
    layer_out = (
        (residual + project(hidden_low, full_down))
        .astype(jnp.bfloat16)
        .reshape(seq_count, span_len, model_width)
    )
    back_weights = (
        lax.all_gather(shard_list[0], ("dp", "ctx"), axis=0, tiled=True),
        lax.all_gather(shard_list[1], ("dp", "ctx"), axis=0, tiled=True),
        lax.all_gather(shard_list[2], ("dp", "ctx"), axis=0, tiled=True),
        lax.all_gather(shard_list[3], ("dp", "ctx"), axis=0, tiled=True),
        lax.all_gather(shard_list[4], ("dp", "ctx"), axis=0, tiled=True),
        lax.all_gather(shard_list[5], ("dp", "ctx"), axis=0, tiled=True),
        lax.all_gather(shard_list[6], ("dp", "ctx"), axis=0, tiled=True),
    )
    back_query, back_key, back_value, back_out, back_gate, back_up, back_down = back_weights
    grad_rows = cotangent.reshape(-1, model_width)
    grad_hidden = project_back(grad_rows, back_down)
    unused, gate_pull = jax.vjp(swiglu, gate_proj, up_proj)
    grad_gate_wide, grad_up_wide = gate_pull(grad_hidden)
    grad_gate_low = grad_gate_wide.astype(jnp.bfloat16)
    grad_up_low = grad_up_wide.astype(jnp.bfloat16)
    grad_normed2 = project_back(grad_gate_low, back_gate) + project_back(grad_up_low, back_up)
    unused, second_pull = jax.vjp(normalize, residual)
    grad_residual = grad_rows.astype(jnp.float32) + second_pull(grad_normed2)[0]
    grad_branch = grad_residual.astype(jnp.bfloat16)
    grad_attended = split_heads(project_back(grad_branch, back_out).astype(jnp.bfloat16))
    masked = masked_scores()
    probs = jnp.exp(masked - log_total)
    probs_again = probs.astype(jnp.bfloat16)
    grad_values_all = jnp.einsum(
        "shqk,sqhd->skhd", probs_again, grad_attended, preferred_element_type=jnp.float32
    )
    grad_probs = jnp.einsum(
        "sqhd,skhd->shqk", grad_attended, value_all, preferred_element_type=jnp.float32
    )
    score_grad = (
        probs * (grad_probs - jnp.sum(probs * grad_probs, axis=-1, keepdims=True))
    ).astype(jnp.bfloat16)
    grad_queries = (
        jnp.einsum("shqk,skhd->sqhd", score_grad, key_all, preferred_element_type=jnp.float32)
        * score_scale
    )
    grad_keys_all = (
        jnp.einsum("shqk,sqhd->skhd", score_grad, queries, preferred_element_type=jnp.float32)
        * score_scale
    )
    grad_keys, grad_values = (
        lax.psum_scatter(
            grad_keys_all.astype(jnp.bfloat16), "ctx", scatter_dimension=1, tiled=True
        ).astype(jnp.float32),
        lax.psum_scatter(
            grad_values_all.astype(jnp.bfloat16), "ctx", scatter_dimension=1, tiled=True
        ).astype(jnp.float32),
    )
    grad_query_low = (
        rotate(grad_queries, cosine, -sine_table).reshape(-1, model_width).astype(jnp.bfloat16)
    )
    grad_key_low = (
        rotate(grad_keys, cosine, -sine_table).reshape(-1, model_width).astype(jnp.bfloat16)
    )
    grad_value_low = grad_values.reshape(-1, model_width).astype(jnp.bfloat16)
    grad_normed = (
        project_back(grad_query_low, back_query)
        + project_back(grad_key_low, back_key)
        + project_back(grad_value_low, back_value)
    )
    unused, first_pull = jax.vjp(normalize, tokens_flat)
    input_grad = (grad_residual + first_pull(grad_normed)[0]).reshape(
        seq_count, span_len, model_width
    )
    weight_grads = (
        shard_gradient(normed, grad_query_low),
        shard_gradient(normed, grad_key_low),
        shard_gradient(normed, grad_value_low),
        shard_gradient(attended_low, grad_branch),
        shard_gradient(normed2, grad_gate_low),
        shard_gradient(normed2, grad_up_low),
        shard_gradient(hidden_low, grad_rows),
    )
    moments = (m_query, m_key, m_value, m_out, m_gate, m_up, m_down)
    new_moments = tuple(
        (momentum_coeff * moment + gradient for moment, gradient in zip(moments, weight_grads))
    )
    head_scale = jnp.sqrt(clip_threshold / jnp.maximum(head_peaks, clip_threshold))
    column_scale = jnp.repeat(head_scale, HEAD_DIM)
    rates = (LEARN_RATE, LEARN_RATE, LEARN_RATE, OUT_RATE, LEARN_RATE, LEARN_RATE, LEARN_RATE)
    updated = [
        matrix.astype(jnp.float32) - rate * moment
        for matrix, moment, rate in zip(shard_list, new_moments, rates)
    ]
    updated[0] = updated[0] * column_scale[None, :]
    updated[1] = updated[1] * column_scale[None, :]
    updated = [matrix.astype(jnp.bfloat16) for matrix in updated]
    return (
        layer_out,
        input_grad,
        weight_grads[0],
        weight_grads[1],
        weight_grads[2],
        weight_grads[3],
        weight_grads[4],
        weight_grads[5],
        weight_grads[6],
        new_moments[0],
        new_moments[1],
        new_moments[2],
        new_moments[3],
        new_moments[4],
        new_moments[5],
        new_moments[6],
        updated[0],
        updated[1],
        updated[2],
        updated[3],
        updated[4],
        updated[5],
        updated[6],
        head_peaks,
        head_scale,
    )


f32=jnp.float32; bf=jnp.bfloat16
NT=(((1,),(1,)),((),())); TN=(((0,),(0,)),((),())); NN=(((1,),(0,)),((),()))
FF2=1408
FFP=1536
FLIPS_A=((0,0),(1,0),(0,1),(1,1))
FLIPS_B=((0,0),(0,1),(1,0),(1,1))
MAIN=pl.BlockSpec(memory_space=pltpu.HBM)
S=jax.ShapeDtypeStruct


def dot(a, b, dims):
    return lax.dot_general(a, b, dims, preferred_element_type=f32)


def aligned(i, m):
    return pl.ds(pl.multiple_of(i * m, m), m)


class Copies:
    def __init__(self, sems):
        self.sems = sems
        self.count = 0

    def start(self, source, target):
        copy = pltpu.make_async_copy(source, target, self.sems.at[self.count])
        self.count += 1
        copy.start()
        return copy


def wait_all(copies):
    for copy in copies:
        copy.wait()


def call(kernel, name, outs, scratch, sems, flops, args, limit):
    return pl.pallas_call(
        kernel,
        out_shape=tuple(pltpu.HBM(*o) for o in outs),
        in_specs=[MAIN] * len(args),
        out_specs=(MAIN,) * len(outs),
        scratch_shapes=[pltpu.VMEM(*s) for s in scratch] + [pltpu.SemaphoreType.DMA(n if isinstance(n, tuple) else (n,)) for n in sems],
        compiler_params=pltpu.CompilerParams(vmem_limit_bytes=limit << 20),
        cost_estimate=pl.CostEstimate(flops=flops << 30, bytes_accessed=8 << 20, transcendentals=0),
        name=name,
    )(*(pltpu.with_memory_space_constraint(arg, pltpu.HBM) for arg in args))


def place_of(p):
    return lax.axis_index("dp") ^ ((p >> 2 & 1) | (p >> 1 & 1) << 1 | (p & 1) << 2)


def turn(values, cosine, signed_sine):
    lane = lax.broadcasted_iota(jnp.int32, cosine.shape, 1)
    first = lane % 64 < 32
    parts = []
    for j in range(values.shape[1] // 128):
        part = values[:, 128 * j : 128 * j + 128]
        partner = jnp.where(first, pltpu.roll(part, 96, 1), pltpu.roll(part, 32, 1))
        parts.append(part * cosine + partner * signed_sine)
    return jnp.concatenate(parts, axis=1)


def layer_norm(x):
    c = x - jnp.mean(x, axis=-1, keepdims=True)
    v = jnp.mean(c * c, axis=-1, keepdims=True)
    return c * lax.rsqrt(v + NORM_EPS)


def attend_kernel(*refs):
    (rows_hbm, weight_hbm, cos_hbm, sin_hbm, id_hbm, *pieces) = refs[:13]
    normed_hbm, mixed_hbm, attended_hbm, total_hbm, peak_hbm, outs_hbm = refs[13:19]
    (act, weight, cos_ref, sin_ref, ids, id_col, normed, mixed_ref, attended, value_t, total_ref,
     peak_ref, outs, sems) = refs[19:]
    n = normed.shape[0]
    go = Copies(sems)
    early = [go.start(rows_hbm.at[pl.ds(352 * i, 256)], act.at[pl.ds(256 * i, 256)]) for i in range(4)]
    middle = [
        go.start(weight_hbm.at[pl.ds(128 * p, 128)], weight.at[aligned(place_of(p), 128)])
        for p in range(8)
    ]
    middle += [go.start(cos_hbm, cos_ref), go.start(sin_hbm, sin_ref), go.start(id_hbm, ids)]
    packs = [go.start(piece.at[:, pl.ds(FF2, 256)], outs.at[i]) for i, piece in enumerate(pieces)]
    wait_all(early)

    @pl.loop(0, n // 128)
    def _(i):
        rows = aligned(i, 128)
        normed[rows, :] = layer_norm(act[rows, :].astype(f32)).astype(bf)

    late = [go.start(normed, normed_hbm)]
    wait_all(middle)
    wait_all(packs)
    late.append(go.start(outs, outs_hbm))
    id_col[...] = jnp.broadcast_to(ids[0:1, :], (128, n)).T

    @pl.loop(0, n // 256)
    def _(i):
        rows = aligned(i, 256)
        mixed = dot(normed[rows, :], weight[...], NN)
        cosine = cos_ref[rows, :]
        sine = sin_ref[rows, :]
        queries = turn(mixed[:, 0:256], cosine, sine).astype(bf)
        mixed_ref[rows, 0:256] = (queries.astype(f32) * 0.125).astype(bf)
        mixed_ref[rows, 256:512] = turn(mixed[:, 256:512], cosine, sine).astype(bf)
        value = mixed[:, 512:768]
        mixed_ref[rows, 512:768] = value.astype(bf)
        value_t[:, rows] = value.T.astype(bf)

    late.append(go.start(mixed_ref, mixed_hbm))
    peak_ref[...] = jnp.zeros_like(peak_ref)
    total_ref[...] = jnp.zeros_like(total_ref)

    @pl.loop(0, 4)
    def _(h):
        lanes = pl.multiple_of(h // 2 * 128, 128)
        lane = lax.broadcasted_iota(jnp.int32, (256, 128), 1)
        mine = lane // 64 == h % 2
        best = None
        for i in range(4):
            width = min(256 * (i + 2), 1024)
            low = 256 * i
            q = mixed_ref[low : low + 256, pl.ds(lanes, 128)]
            q = jnp.where(mine, q, jnp.zeros_like(q))
            s = dot(mixed_ref[0:width, pl.ds(pl.multiple_of(256 + lanes, 128), 128)], q, NT)
            ok = id_col[low:width, 0:1] <= ids[0:1, low : low + 256]
            tail = jnp.where(ok, s[low:width], MASK_FILL)
            top = jnp.max(tail, axis=0, keepdims=True)
            if i:
                top = jnp.maximum(top, jnp.max(s[0:low], axis=0, keepdims=True))
                s = jnp.concatenate([s[0:low], tail], axis=0)
            else:
                s = tail
            e = jnp.exp(s - top)
            total = jnp.sum(e, axis=0, keepdims=True)
            o = dot(value_t[pl.ds(lanes, 128), 0:width], e.astype(bf), NN)
            o = (o * (1.0 / total)).T.astype(bf)
            old = attended[low : low + 256, pl.ds(lanes, 128)]
            attended[low : low + 256, pl.ds(lanes, 128)] = jnp.where(mine, o, old)
            total_ref[pl.ds(h, 1), low : low + 256] = top + jnp.log(total)
            m = jnp.max(top, axis=1, keepdims=True)
            best = m if best is None else jnp.maximum(best, m)
        peak_ref[pl.ds(h, 1), :] = jnp.broadcast_to(best, (1, 128))

    late.append(go.start(attended, attended_hbm))
    late.append(go.start(total_ref, total_hbm))
    late.append(go.start(peak_ref, peak_hbm))
    wait_all(late)


def attend(rows_all, weight, cosine, sine, ids, pieces):
    n = cosine.shape[0]
    return call(
        attend_kernel, "attend",
        [((n, 1024), bf), ((n, 768), bf), ((n, 256), bf), ((8, n), f32), ((8, 128), f32),
         ((8, 256, 256), bf)],
        [((n, 1024), bf), ((1024, 768), bf), ((n, 128), f32), ((n, 128), f32), ((8, n), f32),
         ((n, 128), f32), ((n, 1024), bf), ((n, 768), bf), ((n, 256), bf), ((256, n), bf),
         ((8, n), f32), ((8, 128), f32), ((8, 256, 256), bf)],
        [29], 4, (rows_all, weight, cosine, sine, ids, *pieces), 28,
    )


def attend_back_kernel(mixed_hbm, ga_hbm, total_hbm, cos_hbm, sin_hbm, id_hbm, weight_hbm,
                       gm_hbm, gn_hbm,
                       mixed_ref, ga_ref, total_ref, cos_ref, sin_ref, ids, weight,
                       gm_ref, gn_ref, gk_acc, gv_acc, key_t, id_col, sems):
    n = ga_ref.shape[0]
    go = Copies(sems)
    early = [
        go.start(a, b)
        for a, b in ((mixed_hbm, mixed_ref), (ga_hbm, ga_ref), (total_hbm, total_ref),
                     (id_hbm, ids), (cos_hbm, cos_ref), (sin_hbm, sin_ref))
    ]
    late = [
        go.start(weight_hbm.at[pl.ds(128 * p, 128)], weight.at[aligned(place_of(p), 128)])
        for p in range(8)
    ]
    gk_acc[...] = jnp.zeros_like(gk_acc)
    gv_acc[...] = jnp.zeros_like(gv_acc)
    wait_all(early)
    id_col[...] = jnp.broadcast_to(ids[0:1, :], (128, n)).T

    @pl.loop(0, n // 256)
    def _(i):
        rows = aligned(i, 256)
        key_t[:, rows] = mixed_ref[rows, 256:512].astype(f32).T.astype(bf)

    @pl.loop(0, 2)
    def _(pair):
        lanes = pl.multiple_of(pair * 128, 128)
        lane = lax.broadcasted_iota(jnp.int32, (256, 128), 1)
        sub = lax.broadcasted_iota(jnp.int32, (128, 256), 0)
        for i in range(4):
            width = min(256 * (i + 2), 1024)
            low = 256 * i
            k = mixed_ref[0:width, pl.ds(pl.multiple_of(256 + lanes, 128), 128)]
            v = mixed_ref[0:width, pl.ds(pl.multiple_of(512 + lanes, 128), 128)]
            q_all = mixed_ref[low : low + 256, pl.ds(lanes, 128)]
            g_all = ga_ref[low : low + 256, pl.ds(lanes, 128)]
            kt = key_t[pl.ds(lanes, 128), 0:width]
            ok = id_col[low:width, 0:1] <= ids[0:1, low : low + 256]

            def one(half, gq):
                mine = lane // 64 == half
                q = jnp.where(mine, q_all, jnp.zeros_like(q_all))
                g = jnp.where(mine, g_all, jnp.zeros_like(g_all))
                s = dot(k, q, NT) - total_ref[pl.ds(pair * 2 + half, 1), low : low + 256]
                tail = jnp.where(ok, s[low:width], MASK_FILL)
                s = jnp.concatenate([s[0:low], tail], axis=0) if i else tail
                p = jnp.exp(s)
                t = p * dot(v, g, NT)
                delta = jnp.sum(t, axis=0, keepdims=True)
                ds = (t - p * delta).astype(bf)
                gv_acc[0:width, pl.ds(lanes, 128)] += dot(p.astype(bf), g, NN)
                gk_acc[0:width, pl.ds(lanes, 128)] += dot(ds, q, NN)
                return jnp.where(sub // 64 == half, dot(kt, ds, NN), gq)

            gq = lax.fori_loop(0, 2, one, jnp.zeros((128, 256), f32))
            gq = gq.T * 0.125
            cosine = cos_ref[low : low + 256, :]
            sine = sin_ref[low : low + 256, :]
            gm_ref[low : low + 256, pl.ds(lanes, 128)] = turn(gq, cosine, -sine).astype(bf)

    wait_all(late)

    @pl.loop(0, n // 256)
    def _(i):
        rows = aligned(i, 256)
        cosine = cos_ref[rows, :]
        sine = sin_ref[rows, :]
        gm_ref[rows, 256:512] = turn(gk_acc[rows, :], cosine, -sine).astype(bf)
        gm_ref[rows, 512:768] = gv_acc[rows, :].astype(bf)
        gn_ref[rows, :] = dot(gm_ref[rows, :], weight[...], NT).astype(bf)
        copy = pltpu.make_async_copy(gn_ref.at[rows], gn_hbm.at[rows], sems.at[14 + i])
        copy.start()

    out = pltpu.make_async_copy(gm_ref, gm_hbm, sems.at[18])
    out.start()
    for i in range(4):
        rows = pl.ds(256 * i, 256)
        pltpu.make_async_copy(gn_ref.at[rows], gn_hbm.at[rows], sems.at[14 + i]).wait()
    out.wait()


def attend_back(mixed, ga, total, cosine, sine, ids, weight):
    n = ga.shape[0]
    return call(
        attend_back_kernel, "attend_back",
        [((n, 768), bf), ((n, 1024), bf)],
        [((n, 768), bf), ((n, 256), bf), ((8, n), f32), ((n, 128), f32), ((n, 128), f32),
         ((8, n), f32), ((1024, 768), bf), ((n, 768), bf), ((n, 1024), bf), ((n, 256), f32),
         ((n, 256), f32), ((256, n), bf), ((n, 128), f32)],
        [19], 7, (mixed, ga, total, cosine, sine, ids, weight), 32,
    )


def weights_kernel(gm_hbm, normed_hbm, keep_hbm, send_hbm, gm_ref, normed_ref, gw, sems):
    go = Copies(sems)
    wait_all([go.start(gm_hbm, gm_ref), go.start(normed_hbm, normed_ref)])

    @pl.loop(0, 4)
    def _(i):
        cols = aligned(i, 256)
        gw[cols, :] = dot(normed_ref[:, cols], gm_ref[...], TN).astype(bf)

    wait_all([
        go.start(gw.at[aligned(place_of(p), 128)],
                 (keep_hbm if p < 4 else send_hbm).at[pl.ds(128 * (p % 4), 128)])
        for p in range(8)
    ])


def project_weights(gm, normed):
    n = gm.shape[0]
    return call(
        weights_kernel, "project_weights", [((512, 768), bf)] * 2,
        [((n, 768), bf), ((n, 1024), bf), ((1024, 768), bf)], [10], 1, (gm, normed), 24,
    )


def feed_kernel(*refs):
    att_hbm, attp_hbm, act_hbm, actp_hbm, cot_hbm, cotp_hbm = refs[:6]
    a_in, b_in, da_in, db_in, outs = refs[6:10], refs[10:14], refs[14:18], refs[18:22], refs[22]
    part_hbm, outown_hbm, gnown_hbm, res_hbm, wo_hbm = refs[23:28]
    (ga_keep, ga_send, gb_keep, gb_send, gda_keep, gda_send, gdb_keep, gdb_send) = refs[28:36]
    (wg, wu, wd, wo, att, act, n2, n2t, cot, res_ref, out_acc, gn_acc, part, dg, du, dd,
     sems, osem, tsem) = refs[36:]
    me = lax.axis_index("dp")
    core = me % 2
    yx = me // 2
    go = Copies(sems)
    small = []
    for base, src, own in ((0, att_hbm, act_hbm), (256, attp_hbm, actp_hbm)):
        rows = pl.ds(base, 256)
        small += [go.start(src.at[i], att.at[rows, pl.ds(256 * i, 256)]) for i in range(4)]
        small.append(go.start(own, act.at[rows]))
    places = []
    for p in range(4):
        (ax, ay), (bx, by) = FLIPS_A[p], FLIPS_B[p]
        places.append((yx ^ (ax + 2 * ay), yx ^ (bx + 2 * by)))
    for p, (ja, jb) in enumerate(places):
        for which, src, j, col in ((0, a_in[p], ja, 0), (1, b_in[p], jb, 512)):
            for half in range(2):
                cols = pl.ds(col + 256 * half, 256)
                rows = pl.ds(128 * half, 128)
                small.append(go.start(src.at[rows, pl.ds(FF2, 256)], wo.at[aligned(j * 2 + core, 128), cols]))
                small.append(go.start(outs.at[4 * which + p, rows], wo.at[aligned(j * 2 + 1 - core, 128), cols]))
    big = []
    for p, (ja, jb) in enumerate(places):
        for src, dst, j in ((a_in[p], wg, ja), (b_in[p], wu, jb)):
            for half, c in ((0, core), (1, 1 - core)):
                big.append(go.start(src.at[pl.ds(128 * half, 128), pl.ds(0, FF2)],
                                    dst.at[aligned(j * 2 + c, 128), pl.ds(0, FF2)]))
    big += [go.start(cot_hbm, cot.at[pl.ds(0, 256)]), go.start(cotp_hbm, cot.at[pl.ds(256, 256)])]
    for p, (ja, jb) in enumerate(places):
        big.append(go.start(da_in[p], wd.at[aligned(ja, 352), pl.ds(0, 512)]))
        big.append(go.start(db_in[p], wd.at[aligned(jb, 352), pl.ds(512, 512)]))
    wg[:, FF2:FFP] = jnp.zeros((1024, FFP - FF2), bf)
    wu[:, FF2:FFP] = jnp.zeros((1024, FFP - FF2), bf)
    wd[FF2:FFP, :] = jnp.zeros((FFP - FF2, 1024), bf)
    out_acc[...] = jnp.zeros_like(out_acc)
    gn_acc[...] = jnp.zeros_like(gn_acc)
    wait_all(small)
    ogo = Copies(osem)
    done = [ogo.start(wo, wo_hbm)]

    @pl.loop(0, 2)
    def _(i):
        rows = aligned(i, 256)
        res = act[rows, :].astype(f32) + dot(att[rows, :], wo[...], NN)
        res_ref[rows, :] = res
        n = layer_norm(res)
        n2[rows, :] = n.astype(bf)
        n2t[:, rows] = n.T.astype(bf)

    done.append(ogo.start(res_ref.at[pl.ds(0, 256)], res_hbm))
    wait_all(big)

    def tile_copies(t, width):
        copies = []
        cols = pl.ds(pl.multiple_of(t * 256, 256), width)
        for q in range(4):
            fx, fy = FLIPS_A[q]
            rows = aligned(yx ^ (fx + 2 * fy), 256)
            for k, src, dst, slot in ((0, dg, ga_send if fx else ga_keep, fy), (1, du, gb_send if fy else gb_keep, fx)):
                copies.append(pltpu.make_async_copy(
                    src.at[rows, cols], dst.at[pl.ds(256 * slot, 256), cols], tsem.at[t, 2 * q + k]))
        return copies

    last = FFP // 256 - 1

    @pl.loop(0, last + 1)
    def _(t):
        cols = aligned(t, 256)
        g = dot(n2[...], wg[:, cols], NN)
        u = dot(n2[...], wu[:, cols], NN)
        gh = dot(cot[...], wd[cols, :], NT)
        sig = 1.0 / (1.0 + jnp.exp(-g))
        silu = g * sig
        h = (silu * u).astype(bf)
        gu = (gh * silu).astype(bf)
        gg = (gh * u * (sig + silu * (1.0 - sig))).astype(bf)
        dg[:, cols] = dot(n2t[...], gg, NN).astype(bf)
        du[:, cols] = dot(n2t[...], gu, NN).astype(bf)

        @pl.when(t < last)
        def _():
            for copy in tile_copies(t, 256):
                copy.start()

        dd[cols, :] = dot(h, cot[...], TN).astype(bf)
        gn_acc[...] += dot(gg, wg[:, cols], NT) + dot(gu, wu[:, cols], NT)
        out_acc[...] += dot(h, wd[cols, :], NN)

    ends = tile_copies(last, FF2 - 256 * last)
    for copy in ends:
        copy.start()
    part[0:256, :] = out_acc[256:512, :].astype(bf)
    part[256:512, :] = gn_acc[256:512, :].astype(bf)
    done.append(ogo.start(part, part_hbm))
    done.append(ogo.start(gn_acc.at[pl.ds(0, 256)], gnown_hbm))
    done.append(ogo.start(out_acc.at[pl.ds(0, 256)], outown_hbm))
    for q in range(4):
        fx, fy = FLIPS_A[q]
        rows = aligned(yx ^ (fx + 2 * fy), 352)
        done.append(ogo.start(dd.at[rows, pl.ds(0, 512)], (gda_send if fx else gda_keep).at[pl.ds(352 * fy, 352)]))
        done.append(ogo.start(dd.at[rows, pl.ds(512, 512)], (gdb_send if fy else gdb_keep).at[pl.ds(352 * fx, 352)]))
    for t in range(last):
        wait_all(tile_copies(t, 256))
    wait_all(ends)
    wait_all(done)


def feed(att, attp, act, actp, cot, cotp, a, b, da, db, outs):
    big = [((1024, FFP), bf), ((1024, FFP), bf), ((FFP, 1024), bf)]
    return call(
        feed_kernel, "feed",
        [((512, 1024), bf), ((256, 1024), f32), ((256, 1024), f32), ((256, 1024), f32), ((1024, 1024), bf)]
        + [((512, FF2), bf)] * 4 + [((704, 512), bf)] * 4,
        big + [((1024, 1024), bf), ((512, 1024), bf), ((512, 1024), bf), ((512, 1024), bf), ((1024, 512), bf),
               ((512, 1024), bf), ((512, 1024), f32), ((512, 1024), f32), ((512, 1024), f32), ((512, 1024), bf)] + big,
        [68, 13, (6, 8)], 15, (att, attp, act, actp, cot, cotp, *a, *b, *da, *db, outs), 50,
    )


def branch_kernel(part_hbm, outown_hbm, gnown_hbm, res_hbm, cot_hbm, att_hbm, wo_hbm,
                  layer_hbm, gres_hbm, gatt_hbm, keep_hbm, send_hbm,
                  part, outown, gnown, res_ref, cot, att, wo, layer, gres_ref, gatt, gw, sems):
    me = lax.axis_index("dp")
    core = me % 2
    yx = me // 2
    go = Copies(sems)
    first = [
        go.start(a, b)
        for a, b in ((part_hbm, part), (gnown_hbm, gnown), (res_hbm, res_ref), (cot_hbm, cot))
    ]
    late = [go.start(wo_hbm, wo), go.start(outown_hbm, outown)]
    late += [go.start(att_hbm.at[i], att.at[:, pl.ds(256 * i, 256)]) for i in range(4)]
    wait_all(first)
    res = res_ref[...]
    g = gnown[...] + part[256:512, :].astype(f32)
    c = res - jnp.mean(res, axis=-1, keepdims=True)
    r = lax.rsqrt(jnp.mean(c * c, axis=-1, keepdims=True) + NORM_EPS)
    xh = c * r
    d = r * (g - jnp.mean(g, axis=-1, keepdims=True) - xh * jnp.mean(g * xh, axis=-1, keepdims=True))
    gres = cot[...].astype(f32) + d
    gres_ref[...] = gres
    low = gres.astype(bf)
    wait_all(late)
    done = [go.start(gres_ref, gres_hbm)]
    ga = dot(low, wo[...], NT).astype(bf)
    for z in range(4):
        gatt[z] = ga[:, 256 * z : 256 * z + 256]
    done.append(go.start(gatt, gatt_hbm))
    layer[...] = (res + (outown[...] + part[0:256, :].astype(f32))).astype(bf)
    done.append(go.start(layer, layer_hbm))
    gw[...] = dot(att[...], low, TN).astype(bf)
    for q in range(4):
        fx, fy = FLIPS_A[q]
        j = yx ^ (fx + 2 * fy)
        for dst, c in ((keep_hbm, core), (send_hbm, 1 - core)):
            rows = aligned(j * 2 + c, 128)
            done.append(go.start(gw.at[rows, pl.ds(0, 512)], dst.at[pl.ds(128 * (2 * fx + fy), 128), pl.ds(0, 512)]))
            done.append(go.start(gw.at[rows, pl.ds(512, 512)], dst.at[pl.ds(128 * (2 * fy + fx), 128), pl.ds(512, 512)]))
    wait_all(done)


def branch(part, outown, gnown, res, cot, att, wo):
    tall = ((256, 1024), f32)
    low = ((256, 1024), bf)
    return call(
        branch_kernel, "branch",
        [low, tall, ((4, 256, 256), bf), ((512, 1024), bf), ((512, 1024), bf)],
        [((512, 1024), bf), tall, tall, tall, low, low, ((1024, 1024), bf), low, tall, ((4, 256, 256), bf),
         ((1024, 1024), bf)],
        [29], 1, (part, outown, gnown, res, cot, att, wo), 32,
    )


def swap(array, bit):
    return lax.ppermute(array, "dp", [(i, i ^ bit) for i in range(8)])


def shift(array, bits):
    return lax.ppermute(array, "ctx", [(i, i ^ bits) for i in range(4)])


def add_low(left, right):
    return (left.astype(f32) + right.astype(f32)).astype(bf)


def split_even(matrix):
    n = matrix.shape[1] // 8
    parts = [matrix[:, n * i : n * i + n] for i in range(8)]
    return jnp.concatenate(parts[0::2], axis=1), jnp.concatenate(parts[1::2], axis=1)


def join_even(even, odd):
    n = even.shape[1] // 4
    parts = []
    for i in range(4):
        parts += [even[:, n * i : n * i + n], odd[:, n * i : n * i + n]]
    return jnp.concatenate(parts, axis=1)


def tie(value, *anchors):
    return lax.optimization_barrier((value, *anchors))[0]


def fast_device(
    activations,
    block_ids,
    cotangent,
    w_query,
    w_key,
    w_value,
    w_out,
    w_gate,
    w_up,
    w_down,
    m_query,
    m_key,
    m_value,
    m_out,
    m_gate,
    m_up,
    m_down,
    clip_threshold,
    momentum_coeff,
):
    me = lax.axis_index("dp")
    z = lax.axis_index("ctx")
    core = me % 2
    _, span, width = activations.shape
    length = block_ids.shape[1]
    act = activations.reshape(span, width)
    cot = cotangent.reshape(span, width)
    act_other = swap(act, 1)
    cot_other = swap(cot, 1)
    g0, g1 = split_even(w_gate)
    u0, u1 = split_even(w_up)
    even = jnp.stack([g0, u0])
    odd = jnp.stack([g1, u1])
    flip = core == 1
    mine = jnp.where(flip, odd, even)
    other = swap(jnp.where(flip, even, odd), 1)
    out_rows = jnp.stack([w_out[:, :512], w_out[:, 512:]]).reshape(2, 32, 2, 256)
    wide = jnp.stack([mine, other], axis=1)
    wide = jnp.concatenate([wide, out_rows.transpose(0, 2, 1, 3)], axis=3)
    wide = lax.all_gather(wide, "ctx", axis=2, tiled=True).reshape(2, 256, FF2 + 256)
    padded = jnp.concatenate([act, w_down, jnp.zeros((8, width), bf)], axis=0)
    rows_all = lax.all_gather(padded, "ctx", axis=0, tiled=True)
    heads = jnp.stack(
        [
            jnp.concatenate([w[:, 256 * i : 256 * i + 256] for w in (w_query, w_key, w_value)], 1)
            for i in range(4)
        ]
    )
    heads = lax.all_to_all(heads, "ctx", 0, 0, tiled=True).reshape(128, 768)
    hx = swap(heads, 2)
    hy = swap(jnp.concatenate([heads, hx], axis=0), 4)
    four = jnp.concatenate([heads, hy[:128], hx, hy[128:]], axis=0)
    heads_rel = jnp.concatenate([four, swap(four, 1)], axis=0)
    wide, act_other, cot_other = lax.optimization_barrier((wide, act_other, cot_other))

    def spread(own, first, second):
        near = swap(own, first)
        return [own, near, swap(own, second), swap(near, second)]

    piece_a = spread(wide[0], 2, 4)
    piece_b = spread(wide[1], 4, 2)
    down = jnp.concatenate(
        [rows_all[352 * i + 256 : 352 * i + 344] for i in range(4)], axis=0
    )
    piece_da = spread(down[:, :512], 2, 4)
    piece_db = spread(down[:, 512:], 4, 2)
    cosine, sine = rotary_tables(jnp.arange(length, dtype=jnp.int32), HEAD_DIM)
    cosine = jnp.concatenate([cosine] * 4, axis=1)
    sine = jnp.concatenate([-sine, sine, -sine, sine], axis=1)
    ids = jnp.broadcast_to(block_ids, (8, length)).astype(f32)
    pieces = lax.optimization_barrier((rows_all, *piece_a, *piece_b))
    normed, mixed, attended, totals, peaks, outs = attend(
        pieces[0], heads_rel, cosine, sine, ids, pieces[1:]
    )
    piece_a, piece_b = pieces[1:5], pieces[5:]
    outs = swap(outs, 1)
    attended = tie(attended, *piece_da[1:3], *piece_db[1:3])
    attended = lax.all_to_all(attended.reshape(4, span, 256), "ctx", 0, 0, tiled=True)
    attended_other = swap(tie(attended, piece_da[3], piece_db[3]), 1)
    (part, out_own, back_own, residual, full_out, *grads) = feed(
        attended, attended_other, act, act_other, cot, cot_other,
        piece_a, piece_b, piece_da, piece_db, outs,
    )
    ga_keep, ga_send, gb_keep, gb_send, gda_keep, gda_send, gdb_keep, gdb_send = grads
    part = swap(part, 1)
    gda_send, gdb_send, part = lax.optimization_barrier((gda_send, gdb_send, part))
    layer_out, grad_residual, grad_attended, go_keep, go_send = branch(
        part, out_own, back_own, residual, cot, attended, full_out
    )
    grad_attended = lax.all_to_all(grad_attended, "ctx", 0, 0, tiled=True).reshape(length, 256)
    gda_other = swap(gda_send, 2)
    gdb_other = swap(gdb_send, 4)
    grad_da = add_low(gda_keep, gda_other)
    grad_db = add_low(gdb_keep, gdb_other)
    ga_send, gb_send, grad_da, grad_db = lax.optimization_barrier(
        (ga_send, gb_send, grad_da, grad_db)
    )
    ga_other = swap(ga_send, 2)
    gb_other = swap(gb_send, 4)
    grad_a = add_low(ga_keep, ga_other)
    grad_b = add_low(gb_keep, gb_other)
    grad_a = add_low(grad_a[:256], swap(grad_a[256:], 4))
    grad_b = add_low(grad_b[:256], swap(grad_b[256:], 2))
    grad_da = add_low(grad_da[:352], swap(grad_da[352:], 4))
    grad_db = add_low(grad_db[:352], swap(grad_db[352:], 2))
    go_keep, ga_later = lax.optimization_barrier((go_keep, ga_other))
    grad_out = add_low(go_keep, swap(go_send, 1))
    grad_oa = add_low(grad_out[:256, :512], swap(grad_out[256:, :512], 2))
    grad_ob = add_low(grad_out[:256, 512:], swap(grad_out[256:, 512:], 4))
    grad_oa = add_low(grad_oa[:128], swap(grad_oa[128:], 4))
    grad_ob = add_low(grad_ob[:128], swap(grad_ob[128:], 2))

    def core_rows(which):
        return jnp.concatenate(
            [lax.dynamic_slice_in_dim(g, which * 128, 128, 0) for g in (grad_a, grad_b)], axis=1
        )

    own_half = core_rows(core)
    other_half = swap(core_rows(1 - core), 1)
    grad_d = jnp.concatenate([grad_da, grad_db], axis=1).reshape(4, 88, width)
    grad_d = jnp.pad(grad_d, ((0, 0), (0, 8), (0, 0))).reshape(4, 3, 32, width)
    grad_d = grad_d.transpose(0, 2, 1, 3).reshape(128, 3 * width)
    grad_wide = jnp.concatenate(
        [
            jnp.where(flip, other_half, own_half),
            jnp.where(flip, own_half, other_half),
            grad_oa,
            grad_ob,
            grad_d,
        ],
        axis=1,
    )
    grad_wide = lax.psum_scatter(grad_wide, "ctx", scatter_dimension=0, tiled=True).astype(f32)
    grad_mixed, grad_normed = attend_back(
        mixed, grad_attended, totals, cosine, sine, ids, heads_rel
    )
    grad_heads = project_weights(tie(grad_mixed, ga_other, gb_other), normed)
    peaks = tie(peaks, ga_other)
    peaks = lax.all_to_all(
        jnp.broadcast_to(peaks[None], (32, 8, 128)), ("dp", "ctx"), 0, 0, tiled=True
    )
    head_peaks = jnp.max(peaks.reshape(8, 4, 8, 128), axis=0)[:, :4, 0].reshape(HEADS)
    grad_normed = lax.psum_scatter(grad_normed, "ctx", scatter_dimension=0, tiled=True)
    tokens_wide = act.astype(f32)
    unused, first_pull = jax.vjp(normalize, tokens_wide)
    input_grad = grad_residual + first_pull(grad_normed.astype(f32))[0]
    grad_heads = add_low(grad_heads[0], swap(grad_heads[1], 1))
    grad_heads = add_low(grad_heads[:256], swap(grad_heads[256:], 2))
    grad_heads = add_low(grad_heads[:128], swap(grad_heads[128:], 4))
    grad_heads = lax.all_to_all(grad_heads.reshape(4, 32, 768), "ctx", 0, 0, tiled=True)
    grad_heads = grad_heads.astype(f32)
    grad_qkv = [
        jnp.concatenate([grad_heads[i, :, 256 * k : 256 * k + 256] for i in range(4)], axis=1)
        for k in range(3)
    ]
    grad_d_sum = grad_wide[:, 4 * FF2 + width :].reshape(32, 3, width).transpose(1, 0, 2)
    grad_d_sum = grad_d_sum.reshape(96, width)[:88]
    weight_grads = (
        *grad_qkv,
        grad_wide[:, 4 * FF2 : 4 * FF2 + width],
        join_even(grad_wide[:, :FF2], grad_wide[:, 2 * FF2 : 3 * FF2]),
        join_even(grad_wide[:, FF2 : 2 * FF2], grad_wide[:, 3 * FF2 : 4 * FF2]),
        grad_d_sum,
    )
    moments = (m_query, m_key, m_value, m_out, m_gate, m_up, m_down)
    new_moments = tuple(
        (momentum_coeff * moment + gradient for moment, gradient in zip(moments, weight_grads))
    )
    head_scale = jnp.sqrt(clip_threshold / jnp.maximum(head_peaks, clip_threshold))
    column_scale = jnp.repeat(head_scale, HEAD_DIM)
    rates = (LEARN_RATE, LEARN_RATE, LEARN_RATE, OUT_RATE, LEARN_RATE, LEARN_RATE, LEARN_RATE)
    shard_list = (w_query, w_key, w_value, w_out, w_gate, w_up, w_down)
    updated = [
        matrix.astype(jnp.float32) - rate * moment
        for matrix, moment, rate in zip(shard_list, new_moments, rates)
    ]
    updated[0] = updated[0] * column_scale[None, :]
    updated[1] = updated[1] * column_scale[None, :]
    updated = [matrix.astype(bf) for matrix in updated]
    return (
        layer_out[None],
        input_grad[None],
        *weight_grads,
        *new_moments,
        *updated,
        head_peaks,
        head_scale,
    )


def solution(mesh):
    placed = (
        P("dp", "ctx", None),
        P("dp", None),
        P("dp", "ctx", None),
        P(("dp", "ctx"), None),
        P(("dp", "ctx"), None),
        P(("dp", "ctx"), None),
        P(("dp", "ctx"), None),
        P(("dp", "ctx"), None),
        P(("dp", "ctx"), None),
        P(("dp", "ctx"), None),
        P(("dp", "ctx"), None),
        P(("dp", "ctx"), None),
        P(("dp", "ctx"), None),
        P(("dp", "ctx"), None),
        P(("dp", "ctx"), None),
        P(("dp", "ctx"), None),
        P(("dp", "ctx"), None),
        P(),
        P(),
    )
    fits = mesh.shape["dp"] == 8 and mesh.shape["ctx"] == 4
    return jax.shard_map(
        fast_device if fits else per_device,
        mesh=mesh,
        in_specs=placed,
        out_specs=(
            P("dp", "ctx", None),
            P("dp", "ctx", None),
            P(("dp", "ctx"), None),
            P(("dp", "ctx"), None),
            P(("dp", "ctx"), None),
            P(("dp", "ctx"), None),
            P(("dp", "ctx"), None),
            P(("dp", "ctx"), None),
            P(("dp", "ctx"), None),
            P(("dp", "ctx"), None),
            P(("dp", "ctx"), None),
            P(("dp", "ctx"), None),
            P(("dp", "ctx"), None),
            P(("dp", "ctx"), None),
            P(("dp", "ctx"), None),
            P(("dp", "ctx"), None),
            P(("dp", "ctx"), None),
            P(("dp", "ctx"), None),
            P(("dp", "ctx"), None),
            P(("dp", "ctx"), None),
            P(("dp", "ctx"), None),
            P(("dp", "ctx"), None),
            P(("dp", "ctx"), None),
            P(),
            P(),
        ),
        check_vma=False,
    )
```

```python
import math

import jax
import jax.numpy as jnp
from jax import lax
from jax.experimental import pallas as pl
from jax.experimental.pallas import tpu as pltpu
from jax.sharding import PartitionSpec as P

HEADS = 16
HEAD_DIM = 64


NORM_EPS = 1e-05
ROPE_BASE = 10000.0
LEARN_RATE = 0.0001
OUT_RATE = 0.0016
MASK_FILL = -1e30


def normalize(values):
    centred = values - jnp.mean(values, axis=-1, keepdims=True)
    spread = jnp.mean(centred * centred, axis=-1, keepdims=True)
    return centred * lax.rsqrt(spread + NORM_EPS)


def rotary_tables(positions, head_width):
    half_width = head_width // 2
    frequency = ROPE_BASE ** (-(jnp.arange(half_width, dtype=jnp.float32) * 2.0 / head_width))
    angles = positions.astype(jnp.float32)[:, None] * frequency[None, :]
    return (jnp.cos(angles), jnp.sin(angles))


def rotate(vectors, cosine, sine_table):
    half_width = vectors.shape[-1] // 2
    first_half = vectors[..., :half_width]
    second = vectors[..., half_width:]
    cos_wide = cosine[:, None, :]
    sin_wide = sine_table[:, None, :]
    return jnp.concatenate(
        [first_half * cos_wide - second * sin_wide, second * cos_wide + first_half * sin_wide],
        axis=-1,
    )


def swiglu(gate_proj, up_proj):
    return jax.nn.silu(gate_proj) * up_proj


def project(left_rows, matrix):
    return jnp.dot(left_rows, matrix, preferred_element_type=jnp.float32)


def project_back(grad_rows, matrix):
    return lax.dot_general(
        grad_rows, matrix, (((1,), (1,)), ((), ())), preferred_element_type=jnp.float32
    )


def shard_gradient(left_rows, right_rows):
    return lax.psum_scatter(
        lax.dot_general(
            left_rows, right_rows, (((0,), (0,)), ((), ())), preferred_element_type=jnp.float32
        ),
        ("dp", "ctx"),
        scatter_dimension=0,
        tiled=True,
    )


def per_device(
    activations,
    block_ids,
    cotangent,
    w_query,
    w_key,
    w_value,
    w_out,
    w_gate,
    w_up,
    w_down,
    m_query,
    m_key,
    m_value,
    m_out,
    m_gate,
    m_up,
    m_down,
    clip_threshold,
    momentum_coeff,
):
    shard_list = (w_query, w_key, w_value, w_out, w_gate, w_up, w_down)
    gathered = (
        lax.all_gather(shard_list[0], ("dp", "ctx"), axis=0, tiled=True),
        lax.all_gather(shard_list[1], ("dp", "ctx"), axis=0, tiled=True),
        lax.all_gather(shard_list[2], ("dp", "ctx"), axis=0, tiled=True),
        lax.all_gather(shard_list[3], ("dp", "ctx"), axis=0, tiled=True),
        lax.all_gather(shard_list[4], ("dp", "ctx"), axis=0, tiled=True),
        lax.all_gather(shard_list[5], ("dp", "ctx"), axis=0, tiled=True),
        lax.all_gather(shard_list[6], ("dp", "ctx"), axis=0, tiled=True),
    )
    full_query, full_key, full_value, full_out, full_gate, full_up, full_down = gathered
    seq_count, span_len, model_width = activations.shape
    ctx_place = lax.axis_index("ctx")
    positions = ctx_place * span_len + jnp.arange(span_len, dtype=jnp.int32)
    cosine, sine_table = rotary_tables(positions, HEAD_DIM)
    score_scale = 1.0 / math.sqrt(HEAD_DIM)

    def split_heads(matrix):
        return matrix.reshape(seq_count, span_len, HEADS, HEAD_DIM)

    tokens_flat = activations.astype(jnp.float32).reshape(-1, model_width)
    normed = normalize(tokens_flat).astype(jnp.bfloat16)
    queries = rotate(split_heads(project(normed, full_query)), cosine, sine_table).astype(
        jnp.bfloat16
    )
    key_rot = rotate(split_heads(project(normed, full_key)), cosine, sine_table).astype(
        jnp.bfloat16
    )
    value_rot = split_heads(project(normed, full_value)).astype(jnp.bfloat16)
    key_all, value_all = (
        lax.all_gather(key_rot, "ctx", axis=1, tiled=True),
        lax.all_gather(value_rot, "ctx", axis=1, tiled=True),
    )
    query_ids = lax.dynamic_slice_in_dim(block_ids, ctx_place * span_len, span_len, 1)
    allowed = (block_ids[:, None, :] <= query_ids[:, :, None])[:, None]

    def masked_scores():
        scores = (
            jnp.einsum("sqhd,skhd->shqk", queries, key_all, preferred_element_type=jnp.float32)
            * score_scale
        )
        return jnp.where(allowed, scores, MASK_FILL)

    masked = masked_scores()
    local_peaks = jnp.max(masked, axis=(0, 2, 3))
    row_top = jnp.max(masked, axis=-1, keepdims=True)
    log_total = row_top + jnp.log(jnp.sum(jnp.exp(masked - row_top), axis=-1, keepdims=True))
    probs_low = jnp.exp(masked - log_total).astype(jnp.bfloat16)
    attended = jnp.einsum(
        "shqk,skhd->sqhd", probs_low, value_all, preferred_element_type=jnp.float32
    )
    attended_low = attended.reshape(-1, model_width).astype(jnp.bfloat16)
    head_peaks = lax.pmax(local_peaks, ("dp", "ctx"))
    residual = tokens_flat + project(attended_low, full_out)
    normed2 = normalize(residual).astype(jnp.bfloat16)
    gate_proj = project(normed2, full_gate)
    up_proj = project(normed2, full_up)
    hidden_low = swiglu(gate_proj, up_proj).astype(jnp.bfloat16)
    layer_out = (
        (residual + project(hidden_low, full_down))
        .astype(jnp.bfloat16)
        .reshape(seq_count, span_len, model_width)
    )
    back_weights = (
        lax.all_gather(shard_list[0], ("dp", "ctx"), axis=0, tiled=True),
        lax.all_gather(shard_list[1], ("dp", "ctx"), axis=0, tiled=True),
        lax.all_gather(shard_list[2], ("dp", "ctx"), axis=0, tiled=True),
        lax.all_gather(shard_list[3], ("dp", "ctx"), axis=0, tiled=True),
        lax.all_gather(shard_list[4], ("dp", "ctx"), axis=0, tiled=True),
        lax.all_gather(shard_list[5], ("dp", "ctx"), axis=0, tiled=True),
        lax.all_gather(shard_list[6], ("dp", "ctx"), axis=0, tiled=True),
    )
    back_query, back_key, back_value, back_out, back_gate, back_up, back_down = back_weights
    grad_rows = cotangent.reshape(-1, model_width)
    grad_hidden = project_back(grad_rows, back_down)
    unused, gate_pull = jax.vjp(swiglu, gate_proj, up_proj)
    grad_gate_wide, grad_up_wide = gate_pull(grad_hidden)
    grad_gate_low = grad_gate_wide.astype(jnp.bfloat16)
    grad_up_low = grad_up_wide.astype(jnp.bfloat16)
    grad_normed2 = project_back(grad_gate_low, back_gate) + project_back(grad_up_low, back_up)
    unused, second_pull = jax.vjp(normalize, residual)
    grad_residual = grad_rows.astype(jnp.float32) + second_pull(grad_normed2)[0]
    grad_branch = grad_residual.astype(jnp.bfloat16)
    grad_attended = split_heads(project_back(grad_branch, back_out).astype(jnp.bfloat16))
    masked = masked_scores()
    probs = jnp.exp(masked - log_total)
    probs_again = probs.astype(jnp.bfloat16)
    grad_values_all = jnp.einsum(
        "shqk,sqhd->skhd", probs_again, grad_attended, preferred_element_type=jnp.float32
    )
    grad_probs = jnp.einsum(
        "sqhd,skhd->shqk", grad_attended, value_all, preferred_element_type=jnp.float32
    )
    score_grad = (
        probs * (grad_probs - jnp.sum(probs * grad_probs, axis=-1, keepdims=True))
    ).astype(jnp.bfloat16)
    grad_queries = (
        jnp.einsum("shqk,skhd->sqhd", score_grad, key_all, preferred_element_type=jnp.float32)
        * score_scale
    )
    grad_keys_all = (
        jnp.einsum("shqk,sqhd->skhd", score_grad, queries, preferred_element_type=jnp.float32)
        * score_scale
    )
    grad_keys, grad_values = (
        lax.psum_scatter(
            grad_keys_all.astype(jnp.bfloat16), "ctx", scatter_dimension=1, tiled=True
        ).astype(jnp.float32),
        lax.psum_scatter(
            grad_values_all.astype(jnp.bfloat16), "ctx", scatter_dimension=1, tiled=True
        ).astype(jnp.float32),
    )
    grad_query_low = (
        rotate(grad_queries, cosine, -sine_table).reshape(-1, model_width).astype(jnp.bfloat16)
    )
    grad_key_low = (
        rotate(grad_keys, cosine, -sine_table).reshape(-1, model_width).astype(jnp.bfloat16)
    )
    grad_value_low = grad_values.reshape(-1, model_width).astype(jnp.bfloat16)
    grad_normed = (
        project_back(grad_query_low, back_query)
        + project_back(grad_key_low, back_key)
        + project_back(grad_value_low, back_value)
    )
    unused, first_pull = jax.vjp(normalize, tokens_flat)
    input_grad = (grad_residual + first_pull(grad_normed)[0]).reshape(
        seq_count, span_len, model_width
    )
    weight_grads = (
        shard_gradient(normed, grad_query_low),
        shard_gradient(normed, grad_key_low),
        shard_gradient(normed, grad_value_low),
        shard_gradient(attended_low, grad_branch),
        shard_gradient(normed2, grad_gate_low),
        shard_gradient(normed2, grad_up_low),
        shard_gradient(hidden_low, grad_rows),
    )
    moments = (m_query, m_key, m_value, m_out, m_gate, m_up, m_down)
    new_moments = tuple(
        (momentum_coeff * moment + gradient for moment, gradient in zip(moments, weight_grads))
    )
    head_scale = jnp.sqrt(clip_threshold / jnp.maximum(head_peaks, clip_threshold))
    column_scale = jnp.repeat(head_scale, HEAD_DIM)
    rates = (LEARN_RATE, LEARN_RATE, LEARN_RATE, OUT_RATE, LEARN_RATE, LEARN_RATE, LEARN_RATE)
    updated = [
        matrix.astype(jnp.float32) - rate * moment
        for matrix, moment, rate in zip(shard_list, new_moments, rates)
    ]
    updated[0] = updated[0] * column_scale[None, :]
    updated[1] = updated[1] * column_scale[None, :]
    updated = [matrix.astype(jnp.bfloat16) for matrix in updated]
    return (
        layer_out,
        input_grad,
        weight_grads[0],
        weight_grads[1],
        weight_grads[2],
        weight_grads[3],
        weight_grads[4],
        weight_grads[5],
        weight_grads[6],
        new_moments[0],
        new_moments[1],
        new_moments[2],
        new_moments[3],
        new_moments[4],
        new_moments[5],
        new_moments[6],
        updated[0],
        updated[1],
        updated[2],
        updated[3],
        updated[4],
        updated[5],
        updated[6],
        head_peaks,
        head_scale,
    )


f32=jnp.float32; bf=jnp.bfloat16
NT=(((1,),(1,)),((),())); TN=(((0,),(0,)),((),())); NN=(((1,),(0,)),((),()))
FF2=1408
FFP=1536
FLIPS_A=((0,0),(1,0),(0,1),(1,1))
FLIPS_B=((0,0),(0,1),(1,0),(1,1))
MAIN=pl.BlockSpec(memory_space=pltpu.HBM)
S=jax.ShapeDtypeStruct


def dot(a, b, dims):
    return lax.dot_general(a, b, dims, preferred_element_type=f32)


def aligned(i, m):
    return pl.ds(pl.multiple_of(i * m, m), m)


class Copies:
    def __init__(self, sems):
        self.sems = sems
        self.count = 0

    def start(self, source, target):
        copy = pltpu.make_async_copy(source, target, self.sems.at[self.count])
        self.count += 1
        copy.start()
        return copy


def wait_all(copies):
    for copy in copies:
        copy.wait()


def call(kernel, name, outs, scratch, sems, flops, args, limit):
    return pl.pallas_call(
        kernel,
        out_shape=tuple(pltpu.HBM(*o) for o in outs),
        in_specs=[MAIN] * len(args),
        out_specs=(MAIN,) * len(outs),
        scratch_shapes=[pltpu.VMEM(*s) for s in scratch] + [pltpu.SemaphoreType.DMA(n if isinstance(n, tuple) else (n,)) for n in sems],
        compiler_params=pltpu.CompilerParams(vmem_limit_bytes=limit << 20),
        cost_estimate=pl.CostEstimate(flops=flops << 30, bytes_accessed=8 << 20, transcendentals=0),
        name=name,
    )(*(pltpu.with_memory_space_constraint(arg, pltpu.HBM) for arg in args))


def place_of(p):
    return lax.axis_index("dp") ^ ((p >> 2 & 1) | (p >> 1 & 1) << 1 | (p & 1) << 2)


def turn(values, cosine, signed_sine):
    lane = lax.broadcasted_iota(jnp.int32, cosine.shape, 1)
    first = lane % 64 < 32
    parts = []
    for j in range(values.shape[1] // 128):
        part = values[:, 128 * j : 128 * j + 128]
        partner = jnp.where(first, pltpu.roll(part, 96, 1), pltpu.roll(part, 32, 1))
        parts.append(part * cosine + partner * signed_sine)
    return jnp.concatenate(parts, axis=1)


def layer_norm(x):
    c = x - jnp.mean(x, axis=-1, keepdims=True)
    v = jnp.mean(c * c, axis=-1, keepdims=True)
    return c * lax.rsqrt(v + NORM_EPS)


def attend_kernel(*refs):
    (rows_hbm, weight_hbm, cos_hbm, sin_hbm, id_hbm, *pieces) = refs[:13]
    normed_hbm, mixed_hbm, attended_hbm, total_hbm, peak_hbm, outs_hbm = refs[13:19]
    (act, weight, cos_ref, sin_ref, ids, id_col, normed, mixed_ref, attended, value_t, total_ref,
     peak_ref, outs, sems) = refs[19:]
    n = normed.shape[0]
    go = Copies(sems)
    early = [go.start(rows_hbm.at[pl.ds(352 * i, 256)], act.at[pl.ds(256 * i, 256)]) for i in range(4)]
    middle = [
        go.start(weight_hbm.at[pl.ds(128 * p, 128)], weight.at[aligned(place_of(p), 128)])
        for p in range(8)
    ]
    middle += [go.start(cos_hbm, cos_ref), go.start(sin_hbm, sin_ref), go.start(id_hbm, ids)]
    packs = [go.start(piece.at[:, pl.ds(FF2, 256)], outs.at[i]) for i, piece in enumerate(pieces)]
    wait_all(early)

    @pl.loop(0, n // 128)
    def _(i):
        rows = aligned(i, 128)
        normed[rows, :] = layer_norm(act[rows, :].astype(f32)).astype(bf)

    late = [go.start(normed, normed_hbm)]
    wait_all(middle)
    wait_all(packs)
    late.append(go.start(outs, outs_hbm))
    id_col[...] = jnp.broadcast_to(ids[0:1, :], (128, n)).T

    @pl.loop(0, n // 256)
    def _(i):
        rows = aligned(i, 256)
        mixed = dot(normed[rows, :], weight[...], NN)
        cosine = cos_ref[rows, :]
        sine = sin_ref[rows, :]
        queries = turn(mixed[:, 0:256], cosine, sine).astype(bf)
        mixed_ref[rows, 0:256] = (queries.astype(f32) * 0.125).astype(bf)
        mixed_ref[rows, 256:512] = turn(mixed[:, 256:512], cosine, sine).astype(bf)
        value = mixed[:, 512:768]
        mixed_ref[rows, 512:768] = value.astype(bf)
        value_t[:, rows] = value.T.astype(bf)

    late.append(go.start(mixed_ref, mixed_hbm))
    peak_ref[...] = jnp.zeros_like(peak_ref)
    total_ref[...] = jnp.zeros_like(total_ref)

    @pl.loop(0, 4)
    def _(h):
        lanes = pl.multiple_of(h // 2 * 128, 128)
        lane = lax.broadcasted_iota(jnp.int32, (256, 128), 1)
        mine = lane // 64 == h % 2
        best = None
        for i in range(4):
            width = min(256 * (i + 2), 1024)
            low = 256 * i
            q = mixed_ref[low : low + 256, pl.ds(lanes, 128)]
            q = jnp.where(mine, q, jnp.zeros_like(q))
            s = dot(mixed_ref[0:width, pl.ds(pl.multiple_of(256 + lanes, 128), 128)], q, NT)
            ok = id_col[low:width, 0:1] <= ids[0:1, low : low + 256]
            tail = jnp.where(ok, s[low:width], MASK_FILL)
            top = jnp.max(tail, axis=0, keepdims=True)
            if i:
                top = jnp.maximum(top, jnp.max(s[0:low], axis=0, keepdims=True))
                s = jnp.concatenate([s[0:low], tail], axis=0)
            else:
                s = tail
            e = jnp.exp(s - top)
            total = jnp.sum(e, axis=0, keepdims=True)
            o = dot(value_t[pl.ds(lanes, 128), 0:width], e.astype(bf), NN)
            o = (o * (1.0 / total)).T.astype(bf)
            old = attended[low : low + 256, pl.ds(lanes, 128)]
            attended[low : low + 256, pl.ds(lanes, 128)] = jnp.where(mine, o, old)
            total_ref[pl.ds(h, 1), low : low + 256] = top + jnp.log(total)
            m = jnp.max(top, axis=1, keepdims=True)
            best = m if best is None else jnp.maximum(best, m)
        peak_ref[pl.ds(h, 1), :] = jnp.broadcast_to(best, (1, 128))

    late.append(go.start(attended, attended_hbm))
    late.append(go.start(total_ref, total_hbm))
    late.append(go.start(peak_ref, peak_hbm))
    wait_all(late)


def attend(rows_all, weight, cosine, sine, ids, pieces):
    n = cosine.shape[0]
    return call(
        attend_kernel, "attend",
        [((n, 1024), bf), ((n, 768), bf), ((n, 256), bf), ((8, n), f32), ((8, 128), f32),
         ((8, 256, 256), bf)],
        [((n, 1024), bf), ((1024, 768), bf), ((n, 128), f32), ((n, 128), f32), ((8, n), f32),
         ((n, 128), f32), ((n, 1024), bf), ((n, 768), bf), ((n, 256), bf), ((256, n), bf),
         ((8, n), f32), ((8, 128), f32), ((8, 256, 256), bf)],
        [29], 4, (rows_all, weight, cosine, sine, ids, *pieces), 28,
    )


def attend_back_kernel(mixed_hbm, ga_hbm, total_hbm, cos_hbm, sin_hbm, id_hbm, weight_hbm,
                       gm_hbm, gn_hbm,
                       mixed_ref, ga_ref, total_ref, cos_ref, sin_ref, ids, weight,
                       gm_ref, gn_ref, gk_acc, gv_acc, key_t, id_col, sems):
    n = ga_ref.shape[0]
    go = Copies(sems)
    early = [
        go.start(a, b)
        for a, b in ((mixed_hbm, mixed_ref), (ga_hbm, ga_ref), (total_hbm, total_ref),
                     (id_hbm, ids), (cos_hbm, cos_ref), (sin_hbm, sin_ref))
    ]
    late = [
        go.start(weight_hbm.at[pl.ds(128 * p, 128)], weight.at[aligned(place_of(p), 128)])
        for p in range(8)
    ]
    gk_acc[...] = jnp.zeros_like(gk_acc)
    gv_acc[...] = jnp.zeros_like(gv_acc)
    wait_all(early)
    id_col[...] = jnp.broadcast_to(ids[0:1, :], (128, n)).T

    @pl.loop(0, n // 256)
    def _(i):
        rows = aligned(i, 256)
        key_t[:, rows] = mixed_ref[rows, 256:512].astype(f32).T.astype(bf)

    @pl.loop(0, 2)
    def _(pair):
        lanes = pl.multiple_of(pair * 128, 128)
        lane = lax.broadcasted_iota(jnp.int32, (256, 128), 1)
        sub = lax.broadcasted_iota(jnp.int32, (128, 256), 0)
        for i in range(4):
            width = min(256 * (i + 2), 1024)
            low = 256 * i
            k = mixed_ref[0:width, pl.ds(pl.multiple_of(256 + lanes, 128), 128)]
            v = mixed_ref[0:width, pl.ds(pl.multiple_of(512 + lanes, 128), 128)]
            q_all = mixed_ref[low : low + 256, pl.ds(lanes, 128)]
            g_all = ga_ref[low : low + 256, pl.ds(lanes, 128)]
            kt = key_t[pl.ds(lanes, 128), 0:width]
            ok = id_col[low:width, 0:1] <= ids[0:1, low : low + 256]

            def one(half, gq):
                mine = lane // 64 == half
                q = jnp.where(mine, q_all, jnp.zeros_like(q_all))
                g = jnp.where(mine, g_all, jnp.zeros_like(g_all))
                s = dot(k, q, NT) - total_ref[pl.ds(pair * 2 + half, 1), low : low + 256]
                tail = jnp.where(ok, s[low:width], MASK_FILL)
                s = jnp.concatenate([s[0:low], tail], axis=0) if i else tail
                p = jnp.exp(s)
                t = p * dot(v, g, NT)
                delta = jnp.sum(t, axis=0, keepdims=True)
                ds = (t - p * delta).astype(bf)
                gv_acc[0:width, pl.ds(lanes, 128)] += dot(p.astype(bf), g, NN)
                gk_acc[0:width, pl.ds(lanes, 128)] += dot(ds, q, NN)
                return jnp.where(sub // 64 == half, dot(kt, ds, NN), gq)

            gq = lax.fori_loop(0, 2, one, jnp.zeros((128, 256), f32))
            gq = gq.T * 0.125
            cosine = cos_ref[low : low + 256, :]
            sine = sin_ref[low : low + 256, :]
            gm_ref[low : low + 256, pl.ds(lanes, 128)] = turn(gq, cosine, -sine).astype(bf)

    wait_all(late)

    @pl.loop(0, n // 256)
    def _(i):
        rows = aligned(i, 256)
        cosine = cos_ref[rows, :]
        sine = sin_ref[rows, :]
        gm_ref[rows, 256:512] = turn(gk_acc[rows, :], cosine, -sine).astype(bf)
        gm_ref[rows, 512:768] = gv_acc[rows, :].astype(bf)
        gn_ref[rows, :] = dot(gm_ref[rows, :], weight[...], NT).astype(bf)
        copy = pltpu.make_async_copy(gn_ref.at[rows], gn_hbm.at[rows], sems.at[14 + i])
        copy.start()

    out = pltpu.make_async_copy(gm_ref, gm_hbm, sems.at[18])
    out.start()
    for i in range(4):
        rows = pl.ds(256 * i, 256)
        pltpu.make_async_copy(gn_ref.at[rows], gn_hbm.at[rows], sems.at[14 + i]).wait()
    out.wait()


def attend_back(mixed, ga, total, cosine, sine, ids, weight):
    n = ga.shape[0]
    return call(
        attend_back_kernel, "attend_back",
        [((n, 768), bf), ((n, 1024), bf)],
        [((n, 768), bf), ((n, 256), bf), ((8, n), f32), ((n, 128), f32), ((n, 128), f32),
         ((8, n), f32), ((1024, 768), bf), ((n, 768), bf), ((n, 1024), bf), ((n, 256), f32),
         ((n, 256), f32), ((256, n), bf), ((n, 128), f32)],
        [19], 0, (mixed, ga, total, cosine, sine, ids, weight), 32,
    )


def weights_kernel(gm_hbm, normed_hbm, okeep_hbm, osend_hbm, keep_hbm, send_hbm,
                   gm_ref, normed_ref, gw, okeep, osend, sems):
    go = Copies(sems)
    first = [go.start(gm_hbm, gm_ref), go.start(normed_hbm, normed_ref)]
    second = [go.start(okeep_hbm, okeep), go.start(osend_hbm, osend)]
    wait_all(first + second)
    cols = pl.ds(768, 1024)
    late = [go.start(okeep, keep_hbm.at[:, cols]), go.start(osend, send_hbm.at[:, cols])]

    @pl.loop(0, 4)
    def _(i):
        cols = aligned(i, 256)
        gw[cols, :] = dot(normed_ref[:, cols], gm_ref[...], TN).astype(bf)

    late += [
        go.start(gw.at[aligned(place_of(p), 128)],
                 (keep_hbm if p < 4 else send_hbm).at[pl.ds(128 * (p % 4), 128), pl.ds(0, 768)])
        for p in range(8)
    ]
    wait_all(late)


def project_weights(gm, normed, okeep, osend):
    n = gm.shape[0]
    return call(
        weights_kernel, "project_weights", [((512, 1792), bf)] * 2,
        [((n, 768), bf), ((n, 1024), bf), ((1024, 768), bf), ((512, 1024), bf), ((512, 1024), bf)],
        [14], 1, (gm, normed, okeep, osend), 24,
    )


def feed_kernel(*refs):
    att_hbm, attp_hbm, act_hbm, actp_hbm, cot_hbm, cotp_hbm = refs[:6]
    a_in, b_in, da_in, db_in, outs = refs[6:10], refs[10:14], refs[14:18], refs[18:22], refs[22]
    part_hbm, outown_hbm, gnown_hbm, res_hbm, wo_hbm = refs[23:28]
    (ga_keep, ga_send, gb_keep, gb_send, gda_keep, gda_send, gdb_keep, gdb_send) = refs[28:36]
    (wg, wu, wd, wo, att, act, n2, n2t, cot, res_ref, out_acc, gn_acc, part, dg, du, dd,
     sems, osem, tsem) = refs[36:]
    me = lax.axis_index("dp")
    core = me % 2
    yx = me // 2
    go = Copies(sems)
    small = []
    for base, src, own in ((0, att_hbm, act_hbm), (256, attp_hbm, actp_hbm)):
        rows = pl.ds(base, 256)
        small += [go.start(src.at[i], att.at[rows, pl.ds(256 * i, 256)]) for i in range(4)]
        small.append(go.start(own, act.at[rows]))
    places = []
    for p in range(4):
        (ax, ay), (bx, by) = FLIPS_A[p], FLIPS_B[p]
        places.append((yx ^ (ax + 2 * ay), yx ^ (bx + 2 * by)))
    for p, (ja, jb) in enumerate(places):
        for which, src, j, col in ((0, a_in[p], ja, 0), (1, b_in[p], jb, 512)):
            for half in range(2):
                cols = pl.ds(col + 256 * half, 256)
                rows = pl.ds(128 * half, 128)
                small.append(go.start(src.at[rows, pl.ds(FF2, 256)], wo.at[aligned(j * 2 + core, 128), cols]))
                small.append(go.start(outs.at[4 * which + p, rows], wo.at[aligned(j * 2 + 1 - core, 128), cols]))
    big = []
    for p, (ja, jb) in enumerate(places):
        for src, dst, j in ((a_in[p], wg, ja), (b_in[p], wu, jb)):
            for half, c in ((0, core), (1, 1 - core)):
                big.append(go.start(src.at[pl.ds(128 * half, 128), pl.ds(0, FF2)],
                                    dst.at[aligned(j * 2 + c, 128), pl.ds(0, FF2)]))
    big += [go.start(cot_hbm, cot.at[pl.ds(0, 256)]), go.start(cotp_hbm, cot.at[pl.ds(256, 256)])]
    for p, (ja, jb) in enumerate(places):
        big.append(go.start(da_in[p], wd.at[aligned(ja, 352), pl.ds(0, 512)]))
        big.append(go.start(db_in[p], wd.at[aligned(jb, 352), pl.ds(512, 512)]))
    wg[:, FF2:FFP] = jnp.zeros((1024, FFP - FF2), bf)
    wu[:, FF2:FFP] = jnp.zeros((1024, FFP - FF2), bf)
    wd[FF2:FFP, :] = jnp.zeros((FFP - FF2, 1024), bf)
    out_acc[...] = jnp.zeros_like(out_acc)
    gn_acc[...] = jnp.zeros_like(gn_acc)
    wait_all(small)
    ogo = Copies(osem)
    done = [ogo.start(wo, wo_hbm)]

    @pl.loop(0, 2)
    def _(i):
        rows = aligned(i, 256)
        res = act[rows, :].astype(f32) + dot(att[rows, :], wo[...], NN)
        res_ref[rows, :] = res
        n = layer_norm(res)
        n2[rows, :] = n.astype(bf)
        n2t[:, rows] = n.T.astype(bf)

    done.append(ogo.start(res_ref.at[pl.ds(0, 256)], res_hbm))
    wait_all(big)

    def tile_copies(t, width):
        copies = []
        cols = pl.ds(pl.multiple_of(t * 256, 256), width)
        for q in range(4):
            fx, fy = FLIPS_A[q]
            rows = aligned(yx ^ (fx + 2 * fy), 256)
            for k, src, dst, slot in ((0, dg, ga_send if fx else ga_keep, fy), (1, du, gb_send if fy else gb_keep, fx)):
                copies.append(pltpu.make_async_copy(
                    src.at[rows, cols], dst.at[pl.ds(256 * slot, 256), cols], tsem.at[t, 2 * q + k]))
        return copies

    last = FFP // 256 - 1

    @pl.loop(0, last + 1)
    def _(t):
        cols = aligned(t, 256)
        g = dot(n2[...], wg[:, cols], NN)
        u = dot(n2[...], wu[:, cols], NN)
        gh = dot(cot[...], wd[cols, :], NT)
        sig = 1.0 / (1.0 + jnp.exp(-g))
        silu = g * sig
        h = (silu * u).astype(bf)
        gu = (gh * silu).astype(bf)
        gg = (gh * u * (sig + silu * (1.0 - sig))).astype(bf)
        dg[:, cols] = dot(n2t[...], gg, NN).astype(bf)
        du[:, cols] = dot(n2t[...], gu, NN).astype(bf)

        @pl.when(t < last)
        def _():
            for copy in tile_copies(t, 256):
                copy.start()

        dd[cols, :] = dot(h, cot[...], TN).astype(bf)
        gn_acc[...] += dot(gg, wg[:, cols], NT) + dot(gu, wu[:, cols], NT)
        out_acc[...] += dot(h, wd[cols, :], NN)

    ends = tile_copies(last, FF2 - 256 * last)
    for copy in ends:
        copy.start()
    part[0:256, :] = out_acc[256:512, :].astype(bf)
    part[256:512, :] = gn_acc[256:512, :].astype(bf)
    done.append(ogo.start(part, part_hbm))
    done.append(ogo.start(gn_acc.at[pl.ds(0, 256)], gnown_hbm))
    done.append(ogo.start(out_acc.at[pl.ds(0, 256)], outown_hbm))
    for q in range(4):
        fx, fy = FLIPS_A[q]
        rows = aligned(yx ^ (fx + 2 * fy), 352)
        done.append(ogo.start(dd.at[rows, pl.ds(0, 512)], (gda_send if fx else gda_keep).at[pl.ds(352 * fy, 352)]))
        done.append(ogo.start(dd.at[rows, pl.ds(512, 512)], (gdb_send if fy else gdb_keep).at[pl.ds(352 * fx, 352)]))
    for t in range(last):
        wait_all(tile_copies(t, 256))
    wait_all(ends)
    wait_all(done)


def feed(att, attp, act, actp, cot, cotp, a, b, da, db, outs):
    big = [((1024, FFP), bf), ((1024, FFP), bf), ((FFP, 1024), bf)]
    return call(
        feed_kernel, "feed",
        [((512, 1024), bf), ((256, 1024), f32), ((256, 1024), f32), ((256, 1024), f32), ((1024, 1024), bf)]
        + [((512, FF2), bf)] * 4 + [((704, 512), bf)] * 4,
        big + [((1024, 1024), bf), ((512, 1024), bf), ((512, 1024), bf), ((512, 1024), bf), ((1024, 512), bf),
               ((512, 1024), bf), ((512, 1024), f32), ((512, 1024), f32), ((512, 1024), f32), ((512, 1024), bf)] + big,
        [68, 13, (6, 8)], 15, (att, attp, act, actp, cot, cotp, *a, *b, *da, *db, outs), 50,
    )


def branch_kernel(part_hbm, outown_hbm, gnown_hbm, res_hbm, cot_hbm, att_hbm, wo_hbm,
                  layer_hbm, gres_hbm, gatt_hbm, keep_hbm, send_hbm,
                  part, outown, gnown, res_ref, cot, att, wo, layer, gres_ref, gatt, gw, sems):
    me = lax.axis_index("dp")
    core = me % 2
    yx = me // 2
    go = Copies(sems)
    first = [
        go.start(a, b)
        for a, b in ((part_hbm, part), (gnown_hbm, gnown), (res_hbm, res_ref), (cot_hbm, cot))
    ]
    late = [go.start(wo_hbm, wo), go.start(outown_hbm, outown)]
    late += [go.start(att_hbm.at[i], att.at[:, pl.ds(256 * i, 256)]) for i in range(4)]
    wait_all(first)
    res = res_ref[...]
    g = gnown[...] + part[256:512, :].astype(f32)
    c = res - jnp.mean(res, axis=-1, keepdims=True)
    r = lax.rsqrt(jnp.mean(c * c, axis=-1, keepdims=True) + NORM_EPS)
    xh = c * r
    d = r * (g - jnp.mean(g, axis=-1, keepdims=True) - xh * jnp.mean(g * xh, axis=-1, keepdims=True))
    gres = cot[...].astype(f32) + d
    gres_ref[...] = gres
    low = gres.astype(bf)
    wait_all(late)
    done = [go.start(gres_ref, gres_hbm)]
    ga = dot(low, wo[...], NT).astype(bf)
    for z in range(4):
        gatt[z] = ga[:, 256 * z : 256 * z + 256]
    done.append(go.start(gatt, gatt_hbm))
    layer[...] = (res + (outown[...] + part[0:256, :].astype(f32))).astype(bf)
    done.append(go.start(layer, layer_hbm))
    gw[...] = dot(att[...], low, TN).astype(bf)
    for q in range(4):
        fx, fy = FLIPS_A[q]
        j = yx ^ (fx + 2 * fy)
        for dst, c in ((keep_hbm, core), (send_hbm, 1 - core)):
            rows = aligned(j * 2 + c, 128)
            done.append(go.start(gw.at[rows], dst.at[pl.ds(128 * (2 * fx + fy), 128)]))
    wait_all(done)


def branch(part, outown, gnown, res, cot, att, wo):
    tall = ((256, 1024), f32)
    low = ((256, 1024), bf)
    return call(
        branch_kernel, "branch",
        [low, tall, ((4, 256, 256), bf), ((512, 1024), bf), ((512, 1024), bf)],
        [((512, 1024), bf), tall, tall, tall, low, low, ((1024, 1024), bf), low, tall, ((4, 256, 256), bf),
         ((1024, 1024), bf)],
        [21], 1, (part, outown, gnown, res, cot, att, wo), 32,
    )


def swap(array, bit):
    return lax.ppermute(array, "dp", [(i, i ^ bit) for i in range(8)])


def shift(array, bits):
    return lax.ppermute(array, "ctx", [(i, i ^ bits) for i in range(4)])


def add_low(left, right):
    return (left.astype(f32) + right.astype(f32)).astype(bf)


def split_even(matrix):
    n = matrix.shape[1] // 8
    parts = [matrix[:, n * i : n * i + n] for i in range(8)]
    return jnp.concatenate(parts[0::2], axis=1), jnp.concatenate(parts[1::2], axis=1)


def join_even(even, odd):
    n = even.shape[1] // 4
    parts = []
    for i in range(4):
        parts += [even[:, n * i : n * i + n], odd[:, n * i : n * i + n]]
    return jnp.concatenate(parts, axis=1)


def tie(value, *anchors):
    return lax.optimization_barrier((value, *anchors))[0]


def fast_device(
    activations,
    block_ids,
    cotangent,
    w_query,
    w_key,
    w_value,
    w_out,
    w_gate,
    w_up,
    w_down,
    m_query,
    m_key,
    m_value,
    m_out,
    m_gate,
    m_up,
    m_down,
    clip_threshold,
    momentum_coeff,
):
    me = lax.axis_index("dp")
    z = lax.axis_index("ctx")
    core = me % 2
    _, span, width = activations.shape
    length = block_ids.shape[1]
    act = activations.reshape(span, width)
    cot = cotangent.reshape(span, width)
    act_other = swap(act, 1)
    cot_other = swap(cot, 1)
    g0, g1 = split_even(w_gate)
    u0, u1 = split_even(w_up)
    even = jnp.stack([g0, u0])
    odd = jnp.stack([g1, u1])
    flip = core == 1
    mine = jnp.where(flip, odd, even)
    other = swap(jnp.where(flip, even, odd), 1)
    out_rows = jnp.stack([w_out[:, :512], w_out[:, 512:]]).reshape(2, 32, 2, 256)
    wide = jnp.stack([mine, other], axis=1)
    wide = jnp.concatenate([wide, out_rows.transpose(0, 2, 1, 3)], axis=3)
    wide = lax.all_gather(wide, "ctx", axis=2, tiled=True).reshape(2, 256, FF2 + 256)
    padded = jnp.concatenate([act, w_down, jnp.zeros((8, width), bf)], axis=0)
    rows_all = lax.all_gather(padded, "ctx", axis=0, tiled=True)
    heads = jnp.stack(
        [
            jnp.concatenate([w[:, 256 * i : 256 * i + 256] for w in (w_query, w_key, w_value)], 1)
            for i in range(4)
        ]
    )
    heads = lax.all_to_all(heads, "ctx", 0, 0, tiled=True).reshape(128, 768)
    hx = swap(heads, 2)
    hy = swap(jnp.concatenate([heads, hx], axis=0), 4)
    four = jnp.concatenate([heads, hy[:128], hx, hy[128:]], axis=0)
    heads_rel = jnp.concatenate([four, swap(four, 1)], axis=0)
    wide, act_other, cot_other = lax.optimization_barrier((wide, act_other, cot_other))

    def spread(own, first, second):
        near = swap(own, first)
        return [own, near, swap(own, second), swap(near, second)]

    piece_a = spread(wide[0], 2, 4)
    piece_b = spread(wide[1], 4, 2)
    down = jnp.concatenate(
        [rows_all[352 * i + 256 : 352 * i + 344] for i in range(4)], axis=0
    )
    piece_da = spread(down[:, :512], 2, 4)
    piece_db = spread(down[:, 512:], 4, 2)
    cosine, sine = rotary_tables(jnp.arange(length, dtype=jnp.int32), HEAD_DIM)
    cosine = jnp.concatenate([cosine] * 4, axis=1)
    sine = jnp.concatenate([-sine, sine, -sine, sine], axis=1)
    ids = jnp.broadcast_to(block_ids, (8, length)).astype(f32)
    pieces = lax.optimization_barrier((rows_all, *piece_a, *piece_b))
    normed, mixed, attended, totals, peaks, outs = attend(
        pieces[0], heads_rel, cosine, sine, ids, pieces[1:]
    )
    piece_a, piece_b = pieces[1:5], pieces[5:]
    outs = swap(outs, 1)
    attended = tie(attended, *piece_da[1:3], *piece_db[1:3])
    attended = lax.all_to_all(attended.reshape(4, span, 256), "ctx", 0, 0, tiled=True)
    attended_other = swap(tie(attended, piece_da[3], piece_db[3]), 1)
    (part, out_own, back_own, residual, full_out, *grads) = feed(
        attended, attended_other, act, act_other, cot, cot_other,
        piece_a, piece_b, piece_da, piece_db, outs,
    )
    ga_keep, ga_send, gb_keep, gb_send, gda_keep, gda_send, gdb_keep, gdb_send = grads
    part = swap(part, 1)
    ga_send, gb_send, gda_send, gdb_send, part = lax.optimization_barrier(
        (ga_send, gb_send, gda_send, gdb_send, part)
    )
    gda_other = swap(gda_send, 2)
    gdb_other = swap(gdb_send, 4)
    ga_other = swap(ga_send, 2)
    gb_other = swap(gb_send, 4)
    layer_out, grad_residual, grad_attended, go_keep, go_send = branch(
        part, out_own, back_own, residual, cot, attended, full_out
    )
    grad_attended = lax.all_to_all(grad_attended, "ctx", 0, 0, tiled=True).reshape(length, 256)
    grad_mixed, grad_normed = attend_back(
        mixed, grad_attended, totals, cosine, sine, ids, heads_rel
    )
    grad_mixed = tie(grad_mixed, ga_other, gb_other, gda_other, gdb_other)
    grad_heads = project_weights(grad_mixed, normed, go_keep, go_send)
    ga_keep, gb_keep, gda_keep, gdb_keep, grad_heads = lax.optimization_barrier(
        (ga_keep, gb_keep, gda_keep, gdb_keep, grad_heads)
    )
    grad_da = add_low(gda_keep, gda_other)
    grad_db = add_low(gdb_keep, gdb_other)
    grad_a = add_low(ga_keep, ga_other)
    grad_b = add_low(gb_keep, gb_other)
    grad_a = add_low(grad_a[:256], swap(grad_a[256:], 4))
    grad_b = add_low(grad_b[:256], swap(grad_b[256:], 2))
    grad_da = add_low(grad_da[:352], swap(grad_da[352:], 4))
    grad_db = add_low(grad_db[:352], swap(grad_db[352:], 2))
    def core_rows(which):
        return jnp.concatenate(
            [lax.dynamic_slice_in_dim(g, which * 128, 128, 0) for g in (grad_a, grad_b)], axis=1
        )

    own_half = core_rows(core)
    other_half = swap(core_rows(1 - core), 1)
    grad_d = jnp.concatenate([grad_da, grad_db], axis=1).reshape(4, 88, width)
    grad_d = jnp.pad(grad_d, ((0, 0), (0, 8), (0, 0))).reshape(4, 3, 32, width)
    grad_d = grad_d.transpose(0, 2, 1, 3).reshape(128, 3 * width)
    grad_wide = jnp.concatenate(
        [
            jnp.where(flip, other_half, own_half),
            jnp.where(flip, own_half, other_half),
            grad_d,
        ],
        axis=1,
    )
    grad_wide = lax.psum_scatter(grad_wide, "ctx", scatter_dimension=0, tiled=True).astype(f32)
    peaks = tie(peaks, ga_other)
    peaks = lax.all_to_all(
        jnp.broadcast_to(peaks[None], (32, 8, 128)), ("dp", "ctx"), 0, 0, tiled=True
    )
    head_peaks = jnp.max(peaks.reshape(8, 4, 8, 128), axis=0)[:, :4, 0].reshape(HEADS)
    grad_normed = lax.psum_scatter(grad_normed, "ctx", scatter_dimension=0, tiled=True)
    tokens_wide = act.astype(f32)
    unused, first_pull = jax.vjp(normalize, tokens_wide)
    input_grad = grad_residual + first_pull(grad_normed.astype(f32))[0]
    grad_heads = add_low(grad_heads[0], swap(grad_heads[1], 1))
    grad_heads = add_low(grad_heads[:256], swap(grad_heads[256:], 2))
    grad_heads = add_low(grad_heads[:128], swap(grad_heads[128:], 4))
    grad_heads = lax.all_to_all(grad_heads.reshape(4, 32, 768 + width), "ctx", 0, 0, tiled=True)
    grad_heads = grad_heads.astype(f32)
    parts = grad_heads[:, :, 768:]
    grad_out = parts[0] + parts[1] + (parts[2] + parts[3])
    grad_qkv = [
        jnp.concatenate([grad_heads[i, :, 256 * k : 256 * k + 256] for i in range(4)], axis=1)
        for k in range(3)
    ]
    grad_d_sum = grad_wide[:, 4 * FF2 :].reshape(32, 3, width).transpose(1, 0, 2)
    grad_d_sum = grad_d_sum.reshape(96, width)[:88]
    weight_grads = (
        *grad_qkv,
        grad_out,
        join_even(grad_wide[:, :FF2], grad_wide[:, 2 * FF2 : 3 * FF2]),
        join_even(grad_wide[:, FF2 : 2 * FF2], grad_wide[:, 3 * FF2 : 4 * FF2]),
        grad_d_sum,
    )
    moments = (m_query, m_key, m_value, m_out, m_gate, m_up, m_down)
    new_moments = tuple(
        (momentum_coeff * moment + gradient for moment, gradient in zip(moments, weight_grads))
    )
    head_scale = jnp.sqrt(clip_threshold / jnp.maximum(head_peaks, clip_threshold))
    column_scale = jnp.repeat(head_scale, HEAD_DIM)
    rates = (LEARN_RATE, LEARN_RATE, LEARN_RATE, OUT_RATE, LEARN_RATE, LEARN_RATE, LEARN_RATE)
    shard_list = (w_query, w_key, w_value, w_out, w_gate, w_up, w_down)
    updated = [
        matrix.astype(jnp.float32) - rate * moment
        for matrix, moment, rate in zip(shard_list, new_moments, rates)
    ]
    updated[0] = updated[0] * column_scale[None, :]
    updated[1] = updated[1] * column_scale[None, :]
    updated = [matrix.astype(bf) for matrix in updated]
    return (
        layer_out[None],
        input_grad[None],
        *weight_grads,
        *new_moments,
        *updated,
        head_peaks,
        head_scale,
    )


def solution(mesh):
    placed = (
        P("dp", "ctx", None),
        P("dp", None),
        P("dp", "ctx", None),
        P(("dp", "ctx"), None),
        P(("dp", "ctx"), None),
        P(("dp", "ctx"), None),
        P(("dp", "ctx"), None),
        P(("dp", "ctx"), None),
        P(("dp", "ctx"), None),
        P(("dp", "ctx"), None),
        P(("dp", "ctx"), None),
        P(("dp", "ctx"), None),
        P(("dp", "ctx"), None),
        P(("dp", "ctx"), None),
        P(("dp", "ctx"), None),
        P(("dp", "ctx"), None),
        P(("dp", "ctx"), None),
        P(),
        P(),
    )
    fits = mesh.shape["dp"] == 8 and mesh.shape["ctx"] == 4
    return jax.shard_map(
        fast_device if fits else per_device,
        mesh=mesh,
        in_specs=placed,
        out_specs=(
            P("dp", "ctx", None),
            P("dp", "ctx", None),
            P(("dp", "ctx"), None),
            P(("dp", "ctx"), None),
            P(("dp", "ctx"), None),
            P(("dp", "ctx"), None),
            P(("dp", "ctx"), None),
            P(("dp", "ctx"), None),
            P(("dp", "ctx"), None),
            P(("dp", "ctx"), None),
            P(("dp", "ctx"), None),
            P(("dp", "ctx"), None),
            P(("dp", "ctx"), None),
            P(("dp", "ctx"), None),
            P(("dp", "ctx"), None),
            P(("dp", "ctx"), None),
            P(("dp", "ctx"), None),
            P(("dp", "ctx"), None),
            P(("dp", "ctx"), None),
            P(("dp", "ctx"), None),
            P(("dp", "ctx"), None),
            P(("dp", "ctx"), None),
            P(("dp", "ctx"), None),
            P(),
            P(),
        ),
        check_vma=False,
    )
```

```python
import math

import jax
import jax.numpy as jnp
from jax import lax
from jax.experimental import pallas as pl
from jax.experimental.pallas import tpu as pltpu
from jax.sharding import PartitionSpec as P

HEADS = 16
HEAD_DIM = 64


NORM_EPS = 1e-05
ROPE_BASE = 10000.0
LEARN_RATE = 0.0001
OUT_RATE = 0.0016
MASK_FILL = -1e30


def normalize(values):
    centred = values - jnp.mean(values, axis=-1, keepdims=True)
    spread = jnp.mean(centred * centred, axis=-1, keepdims=True)
    return centred * lax.rsqrt(spread + NORM_EPS)


def rotary_tables(positions, head_width):
    half_width = head_width // 2
    frequency = ROPE_BASE ** (-(jnp.arange(half_width, dtype=jnp.float32) * 2.0 / head_width))
    angles = positions.astype(jnp.float32)[:, None] * frequency[None, :]
    return (jnp.cos(angles), jnp.sin(angles))


def rotate(vectors, cosine, sine_table):
    half_width = vectors.shape[-1] // 2
    first_half = vectors[..., :half_width]
    second = vectors[..., half_width:]
    cos_wide = cosine[:, None, :]
    sin_wide = sine_table[:, None, :]
    return jnp.concatenate(
        [first_half * cos_wide - second * sin_wide, second * cos_wide + first_half * sin_wide],
        axis=-1,
    )


def swiglu(gate_proj, up_proj):
    return jax.nn.silu(gate_proj) * up_proj


def project(left_rows, matrix):
    return jnp.dot(left_rows, matrix, preferred_element_type=jnp.float32)


def project_back(grad_rows, matrix):
    return lax.dot_general(
        grad_rows, matrix, (((1,), (1,)), ((), ())), preferred_element_type=jnp.float32
    )


def shard_gradient(left_rows, right_rows):
    return lax.psum_scatter(
        lax.dot_general(
            left_rows, right_rows, (((0,), (0,)), ((), ())), preferred_element_type=jnp.float32
        ),
        ("dp", "ctx"),
        scatter_dimension=0,
        tiled=True,
    )


def per_device(
    activations,
    block_ids,
    cotangent,
    w_query,
    w_key,
    w_value,
    w_out,
    w_gate,
    w_up,
    w_down,
    m_query,
    m_key,
    m_value,
    m_out,
    m_gate,
    m_up,
    m_down,
    clip_threshold,
    momentum_coeff,
):
    shard_list = (w_query, w_key, w_value, w_out, w_gate, w_up, w_down)
    gathered = (
        lax.all_gather(shard_list[0], ("dp", "ctx"), axis=0, tiled=True),
        lax.all_gather(shard_list[1], ("dp", "ctx"), axis=0, tiled=True),
        lax.all_gather(shard_list[2], ("dp", "ctx"), axis=0, tiled=True),
        lax.all_gather(shard_list[3], ("dp", "ctx"), axis=0, tiled=True),
        lax.all_gather(shard_list[4], ("dp", "ctx"), axis=0, tiled=True),
        lax.all_gather(shard_list[5], ("dp", "ctx"), axis=0, tiled=True),
        lax.all_gather(shard_list[6], ("dp", "ctx"), axis=0, tiled=True),
    )
    full_query, full_key, full_value, full_out, full_gate, full_up, full_down = gathered
    seq_count, span_len, model_width = activations.shape
    ctx_place = lax.axis_index("ctx")
    positions = ctx_place * span_len + jnp.arange(span_len, dtype=jnp.int32)
    cosine, sine_table = rotary_tables(positions, HEAD_DIM)
    score_scale = 1.0 / math.sqrt(HEAD_DIM)

    def split_heads(matrix):
        return matrix.reshape(seq_count, span_len, HEADS, HEAD_DIM)

    tokens_flat = activations.astype(jnp.float32).reshape(-1, model_width)
    normed = normalize(tokens_flat).astype(jnp.bfloat16)
    queries = rotate(split_heads(project(normed, full_query)), cosine, sine_table).astype(
        jnp.bfloat16
    )
    key_rot = rotate(split_heads(project(normed, full_key)), cosine, sine_table).astype(
        jnp.bfloat16
    )
    value_rot = split_heads(project(normed, full_value)).astype(jnp.bfloat16)
    key_all, value_all = (
        lax.all_gather(key_rot, "ctx", axis=1, tiled=True),
        lax.all_gather(value_rot, "ctx", axis=1, tiled=True),
    )
    query_ids = lax.dynamic_slice_in_dim(block_ids, ctx_place * span_len, span_len, 1)
    allowed = (block_ids[:, None, :] <= query_ids[:, :, None])[:, None]

    def masked_scores():
        scores = (
            jnp.einsum("sqhd,skhd->shqk", queries, key_all, preferred_element_type=jnp.float32)
            * score_scale
        )
        return jnp.where(allowed, scores, MASK_FILL)

    masked = masked_scores()
    local_peaks = jnp.max(masked, axis=(0, 2, 3))
    row_top = jnp.max(masked, axis=-1, keepdims=True)
    log_total = row_top + jnp.log(jnp.sum(jnp.exp(masked - row_top), axis=-1, keepdims=True))
    probs_low = jnp.exp(masked - log_total).astype(jnp.bfloat16)
    attended = jnp.einsum(
        "shqk,skhd->sqhd", probs_low, value_all, preferred_element_type=jnp.float32
    )
    attended_low = attended.reshape(-1, model_width).astype(jnp.bfloat16)
    head_peaks = lax.pmax(local_peaks, ("dp", "ctx"))
    residual = tokens_flat + project(attended_low, full_out)
    normed2 = normalize(residual).astype(jnp.bfloat16)
    gate_proj = project(normed2, full_gate)
    up_proj = project(normed2, full_up)
    hidden_low = swiglu(gate_proj, up_proj).astype(jnp.bfloat16)
    layer_out = (
        (residual + project(hidden_low, full_down))
        .astype(jnp.bfloat16)
        .reshape(seq_count, span_len, model_width)
    )
    back_weights = (
        lax.all_gather(shard_list[0], ("dp", "ctx"), axis=0, tiled=True),
        lax.all_gather(shard_list[1], ("dp", "ctx"), axis=0, tiled=True),
        lax.all_gather(shard_list[2], ("dp", "ctx"), axis=0, tiled=True),
        lax.all_gather(shard_list[3], ("dp", "ctx"), axis=0, tiled=True),
        lax.all_gather(shard_list[4], ("dp", "ctx"), axis=0, tiled=True),
        lax.all_gather(shard_list[5], ("dp", "ctx"), axis=0, tiled=True),
        lax.all_gather(shard_list[6], ("dp", "ctx"), axis=0, tiled=True),
    )
    back_query, back_key, back_value, back_out, back_gate, back_up, back_down = back_weights
    grad_rows = cotangent.reshape(-1, model_width)
    grad_hidden = project_back(grad_rows, back_down)
    unused, gate_pull = jax.vjp(swiglu, gate_proj, up_proj)
    grad_gate_wide, grad_up_wide = gate_pull(grad_hidden)
    grad_gate_low = grad_gate_wide.astype(jnp.bfloat16)
    grad_up_low = grad_up_wide.astype(jnp.bfloat16)
    grad_normed2 = project_back(grad_gate_low, back_gate) + project_back(grad_up_low, back_up)
    unused, second_pull = jax.vjp(normalize, residual)
    grad_residual = grad_rows.astype(jnp.float32) + second_pull(grad_normed2)[0]
    grad_branch = grad_residual.astype(jnp.bfloat16)
    grad_attended = split_heads(project_back(grad_branch, back_out).astype(jnp.bfloat16))
    masked = masked_scores()
    probs = jnp.exp(masked - log_total)
    probs_again = probs.astype(jnp.bfloat16)
    grad_values_all = jnp.einsum(
        "shqk,sqhd->skhd", probs_again, grad_attended, preferred_element_type=jnp.float32
    )
    grad_probs = jnp.einsum(
        "sqhd,skhd->shqk", grad_attended, value_all, preferred_element_type=jnp.float32
    )
    score_grad = (
        probs * (grad_probs - jnp.sum(probs * grad_probs, axis=-1, keepdims=True))
    ).astype(jnp.bfloat16)
    grad_queries = (
        jnp.einsum("shqk,skhd->sqhd", score_grad, key_all, preferred_element_type=jnp.float32)
        * score_scale
    )
    grad_keys_all = (
        jnp.einsum("shqk,sqhd->skhd", score_grad, queries, preferred_element_type=jnp.float32)
        * score_scale
    )
    grad_keys, grad_values = (
        lax.psum_scatter(
            grad_keys_all.astype(jnp.bfloat16), "ctx", scatter_dimension=1, tiled=True
        ).astype(jnp.float32),
        lax.psum_scatter(
            grad_values_all.astype(jnp.bfloat16), "ctx", scatter_dimension=1, tiled=True
        ).astype(jnp.float32),
    )
    grad_query_low = (
        rotate(grad_queries, cosine, -sine_table).reshape(-1, model_width).astype(jnp.bfloat16)
    )
    grad_key_low = (
        rotate(grad_keys, cosine, -sine_table).reshape(-1, model_width).astype(jnp.bfloat16)
    )
    grad_value_low = grad_values.reshape(-1, model_width).astype(jnp.bfloat16)
    grad_normed = (
        project_back(grad_query_low, back_query)
        + project_back(grad_key_low, back_key)
        + project_back(grad_value_low, back_value)
    )
    unused, first_pull = jax.vjp(normalize, tokens_flat)
    input_grad = (grad_residual + first_pull(grad_normed)[0]).reshape(
        seq_count, span_len, model_width
    )
    weight_grads = (
        shard_gradient(normed, grad_query_low),
        shard_gradient(normed, grad_key_low),
        shard_gradient(normed, grad_value_low),
        shard_gradient(attended_low, grad_branch),
        shard_gradient(normed2, grad_gate_low),
        shard_gradient(normed2, grad_up_low),
        shard_gradient(hidden_low, grad_rows),
    )
    moments = (m_query, m_key, m_value, m_out, m_gate, m_up, m_down)
    new_moments = tuple(
        (momentum_coeff * moment + gradient for moment, gradient in zip(moments, weight_grads))
    )
    head_scale = jnp.sqrt(clip_threshold / jnp.maximum(head_peaks, clip_threshold))
    column_scale = jnp.repeat(head_scale, HEAD_DIM)
    rates = (LEARN_RATE, LEARN_RATE, LEARN_RATE, OUT_RATE, LEARN_RATE, LEARN_RATE, LEARN_RATE)
    updated = [
        matrix.astype(jnp.float32) - rate * moment
        for matrix, moment, rate in zip(shard_list, new_moments, rates)
    ]
    updated[0] = updated[0] * column_scale[None, :]
    updated[1] = updated[1] * column_scale[None, :]
    updated = [matrix.astype(jnp.bfloat16) for matrix in updated]
    return (
        layer_out,
        input_grad,
        weight_grads[0],
        weight_grads[1],
        weight_grads[2],
        weight_grads[3],
        weight_grads[4],
        weight_grads[5],
        weight_grads[6],
        new_moments[0],
        new_moments[1],
        new_moments[2],
        new_moments[3],
        new_moments[4],
        new_moments[5],
        new_moments[6],
        updated[0],
        updated[1],
        updated[2],
        updated[3],
        updated[4],
        updated[5],
        updated[6],
        head_peaks,
        head_scale,
    )


f32=jnp.float32; bf=jnp.bfloat16
NT=(((1,),(1,)),((),())); TN=(((0,),(0,)),((),())); NN=(((1,),(0,)),((),()))
FF2=1408
FFP=1536
FLIPS_A=((0,0),(1,0),(0,1),(1,1))
FLIPS_B=((0,0),(0,1),(1,0),(1,1))
MAIN=pl.BlockSpec(memory_space=pltpu.HBM)
S=jax.ShapeDtypeStruct


def dot(a, b, dims):
    return lax.dot_general(a, b, dims, preferred_element_type=f32)


def aligned(i, m):
    return pl.ds(pl.multiple_of(i * m, m), m)


class Copies:
    def __init__(self, sems):
        self.sems = sems
        self.count = 0

    def start(self, source, target):
        copy = pltpu.make_async_copy(source, target, self.sems.at[self.count])
        self.count += 1
        copy.start()
        return copy


def wait_all(copies):
    for copy in copies:
        copy.wait()


def call(kernel, name, outs, scratch, sems, flops, args, limit):
    return pl.pallas_call(
        kernel,
        out_shape=tuple(pltpu.HBM(*o) for o in outs),
        in_specs=[MAIN] * len(args),
        out_specs=(MAIN,) * len(outs),
        scratch_shapes=[pltpu.VMEM(*s) for s in scratch] + [pltpu.SemaphoreType.DMA(n if isinstance(n, tuple) else (n,)) for n in sems],
        compiler_params=pltpu.CompilerParams(vmem_limit_bytes=limit << 20),
        cost_estimate=pl.CostEstimate(flops=flops << 30, bytes_accessed=8 << 20, transcendentals=0),
        name=name,
    )(*(pltpu.with_memory_space_constraint(arg, pltpu.HBM) for arg in args))


def place_of(p):
    return lax.axis_index("dp") ^ ((p >> 2 & 1) | (p >> 1 & 1) << 1 | (p & 1) << 2)


def turn(values, cosine, signed_sine):
    lane = lax.broadcasted_iota(jnp.int32, cosine.shape, 1)
    first = lane % 64 < 32
    parts = []
    for j in range(values.shape[1] // 128):
        part = values[:, 128 * j : 128 * j + 128]
        partner = jnp.where(first, pltpu.roll(part, 96, 1), pltpu.roll(part, 32, 1))
        parts.append(part * cosine + partner * signed_sine)
    return jnp.concatenate(parts, axis=1)


def layer_norm(x):
    c = x - jnp.mean(x, axis=-1, keepdims=True)
    v = jnp.mean(c * c, axis=-1, keepdims=True)
    return c * lax.rsqrt(v + NORM_EPS)


def attend_kernel(*refs):
    (rows_hbm, weight_hbm, cos_hbm, sin_hbm, id_hbm, *pieces) = refs[:13]
    normed_hbm, mixed_hbm, attended_hbm, total_hbm, peak_hbm, outs_hbm = refs[13:19]
    (act, weight, cos_ref, sin_ref, ids, id_col, normed, mixed_ref, attended, value_t, total_ref,
     peak_ref, outs, sems) = refs[19:]
    n = normed.shape[0]
    go = Copies(sems)
    early = [go.start(rows_hbm.at[pl.ds(352 * i, 256)], act.at[pl.ds(256 * i, 256)]) for i in range(4)]
    middle = [
        go.start(weight_hbm.at[pl.ds(128 * p, 128)], weight.at[aligned(place_of(p), 128)])
        for p in range(8)
    ]
    middle += [go.start(cos_hbm, cos_ref), go.start(sin_hbm, sin_ref), go.start(id_hbm, ids)]
    packs = [go.start(piece.at[:, pl.ds(FF2, 256)], outs.at[i]) for i, piece in enumerate(pieces)]
    wait_all(early)

    @pl.loop(0, n // 128)
    def _(i):
        rows = aligned(i, 128)
        normed[rows, :] = layer_norm(act[rows, :].astype(f32)).astype(bf)

    late = [go.start(normed, normed_hbm)]
    wait_all(middle)
    wait_all(packs)
    late.append(go.start(outs, outs_hbm))
    id_col[...] = jnp.broadcast_to(ids[0:1, :], (128, n)).T

    @pl.loop(0, n // 256)
    def _(i):
        rows = aligned(i, 256)
        mixed = dot(normed[rows, :], weight[...], NN)
        cosine = cos_ref[rows, :]
        sine = sin_ref[rows, :]
        queries = turn(mixed[:, 0:256], cosine, sine).astype(bf)
        mixed_ref[rows, 0:256] = (queries.astype(f32) * 0.125).astype(bf)
        mixed_ref[rows, 256:512] = turn(mixed[:, 256:512], cosine, sine).astype(bf)
        value = mixed[:, 512:768]
        mixed_ref[rows, 512:768] = value.astype(bf)
        value_t[:, rows] = value.T.astype(bf)

    late.append(go.start(mixed_ref, mixed_hbm))
    peak_ref[...] = jnp.zeros_like(peak_ref)
    total_ref[...] = jnp.zeros_like(total_ref)

    @pl.loop(0, 2)
    def _(pair):
        lanes = pl.multiple_of(pair * 128, 128)
        lane = lax.broadcasted_iota(jnp.int32, (256, 128), 1)
        best = [None, None]
        for i in range(4):
            width = min(256 * (i + 2), 1024)
            low = 256 * i
            both = mixed_ref[low : low + 256, pl.ds(lanes, 128)]
            keys = mixed_ref[0:width, pl.ds(pl.multiple_of(256 + lanes, 128), 128)]
            values = value_t[pl.ds(lanes, 128), 0:width]
            ok = id_col[low:width, 0:1] <= ids[0:1, low : low + 256]
            outs = []
            for half in range(2):
                q = jnp.where(lane // 64 == half, both, jnp.zeros_like(both))
                s = dot(keys, q, NT)
                tail = jnp.where(ok, s[low:width], MASK_FILL)
                top = jnp.max(tail, axis=0, keepdims=True)
                if i:
                    top = jnp.maximum(top, jnp.max(s[0:low], axis=0, keepdims=True))
                    s = jnp.concatenate([s[0:low], tail], axis=0)
                else:
                    s = tail
                e = jnp.exp(s - top)
                total = jnp.sum(e, axis=0, keepdims=True)
                o = dot(values, e.astype(bf), NN)
                outs.append(o[64 * half : 64 * half + 64] * (1.0 / total))
                total_ref[pl.ds(pair * 2 + half, 1), low : low + 256] = top + jnp.log(total)
                m = jnp.max(top, axis=1, keepdims=True)
                best[half] = m if best[half] is None else jnp.maximum(best[half], m)
            o = jnp.concatenate(outs, axis=0).T.astype(bf)
            attended[low : low + 256, pl.ds(lanes, 128)] = o
        for half in range(2):
            peak_ref[pl.ds(pair * 2 + half, 1), :] = jnp.broadcast_to(best[half], (1, 128))

    late.append(go.start(attended, attended_hbm))
    late.append(go.start(total_ref, total_hbm))
    late.append(go.start(peak_ref, peak_hbm))
    wait_all(late)


def attend(rows_all, weight, cosine, sine, ids, pieces):
    n = cosine.shape[0]
    return call(
        attend_kernel, "attend",
        [((n, 1024), bf), ((n, 768), bf), ((n, 256), bf), ((8, n), f32), ((8, 128), f32),
         ((8, 256, 256), bf)],
        [((n, 1024), bf), ((1024, 768), bf), ((n, 128), f32), ((n, 128), f32), ((8, n), f32),
         ((n, 128), f32), ((n, 1024), bf), ((n, 768), bf), ((n, 256), bf), ((256, n), bf),
         ((8, n), f32), ((8, 128), f32), ((8, 256, 256), bf)],
        [29], 4, (rows_all, weight, cosine, sine, ids, *pieces), 28,
    )


def attend_back_kernel(mixed_hbm, ga_hbm, total_hbm, cos_hbm, sin_hbm, id_hbm, weight_hbm,
                       gm_hbm, gn_hbm,
                       mixed_ref, ga_ref, total_ref, cos_ref, sin_ref, ids, weight,
                       gm_ref, gn_ref, gk_acc, gv_acc, key_t, id_col, sems):
    n = ga_ref.shape[0]
    go = Copies(sems)
    early = [
        go.start(a, b)
        for a, b in ((mixed_hbm, mixed_ref), (ga_hbm, ga_ref), (total_hbm, total_ref),
                     (id_hbm, ids), (cos_hbm, cos_ref), (sin_hbm, sin_ref))
    ]
    late = [
        go.start(weight_hbm.at[pl.ds(128 * p, 128)], weight.at[aligned(place_of(p), 128)])
        for p in range(8)
    ]
    gk_acc[...] = jnp.zeros_like(gk_acc)
    gv_acc[...] = jnp.zeros_like(gv_acc)
    wait_all(early)
    id_col[...] = jnp.broadcast_to(ids[0:1, :], (128, n)).T

    @pl.loop(0, n // 256)
    def _(i):
        rows = aligned(i, 256)
        key_t[:, rows] = mixed_ref[rows, 256:512].astype(f32).T.astype(bf)

    @pl.loop(0, 2)
    def _(pair):
        lanes = pl.multiple_of(pair * 128, 128)
        lane = lax.broadcasted_iota(jnp.int32, (256, 128), 1)
        sub = lax.broadcasted_iota(jnp.int32, (128, 256), 0)
        for i in range(4):
            width = min(256 * (i + 2), 1024)
            low = 256 * i
            k = mixed_ref[0:width, pl.ds(pl.multiple_of(256 + lanes, 128), 128)]
            v = mixed_ref[0:width, pl.ds(pl.multiple_of(512 + lanes, 128), 128)]
            q_all = mixed_ref[low : low + 256, pl.ds(lanes, 128)]
            g_all = ga_ref[low : low + 256, pl.ds(lanes, 128)]
            kt = key_t[pl.ds(lanes, 128), 0:width]
            ok = id_col[low:width, 0:1] <= ids[0:1, low : low + 256]

            def one(half, gq):
                mine = lane // 64 == half
                q = jnp.where(mine, q_all, jnp.zeros_like(q_all))
                g = jnp.where(mine, g_all, jnp.zeros_like(g_all))
                s = dot(k, q, NT) - total_ref[pl.ds(pair * 2 + half, 1), low : low + 256]
                tail = jnp.where(ok, s[low:width], MASK_FILL)
                s = jnp.concatenate([s[0:low], tail], axis=0) if i else tail
                p = jnp.exp(s)
                t = p * dot(v, g, NT)
                delta = jnp.sum(t, axis=0, keepdims=True)
                ds = (t - p * delta).astype(bf)
                gv_acc[0:width, pl.ds(lanes, 128)] += dot(p.astype(bf), g, NN)
                gk_acc[0:width, pl.ds(lanes, 128)] += dot(ds, q, NN)
                return jnp.where(sub // 64 == half, dot(kt, ds, NN), gq)

            gq = one(1, one(0, jnp.zeros((128, 256), f32)))
            gq = gq.T * 0.125
            cosine = cos_ref[low : low + 256, :]
            sine = sin_ref[low : low + 256, :]
            gm_ref[low : low + 256, pl.ds(lanes, 128)] = turn(gq, cosine, -sine).astype(bf)

    wait_all(late)

    @pl.loop(0, n // 256)
    def _(i):
        rows = aligned(i, 256)
        cosine = cos_ref[rows, :]
        sine = sin_ref[rows, :]
        gm_ref[rows, 256:512] = turn(gk_acc[rows, :], cosine, -sine).astype(bf)
        gm_ref[rows, 512:768] = gv_acc[rows, :].astype(bf)
        gn_ref[rows, :] = dot(gm_ref[rows, :], weight[...], NT).astype(bf)
        copy = pltpu.make_async_copy(gn_ref.at[rows], gn_hbm.at[rows], sems.at[14 + i])
        copy.start()

    out = pltpu.make_async_copy(gm_ref, gm_hbm, sems.at[18])
    out.start()
    for i in range(4):
        rows = pl.ds(256 * i, 256)
        pltpu.make_async_copy(gn_ref.at[rows], gn_hbm.at[rows], sems.at[14 + i]).wait()
    out.wait()


def attend_back(mixed, ga, total, cosine, sine, ids, weight):
    n = ga.shape[0]
    return call(
        attend_back_kernel, "attend_back",
        [((n, 768), bf), ((n, 1024), bf)],
        [((n, 768), bf), ((n, 256), bf), ((8, n), f32), ((n, 128), f32), ((n, 128), f32),
         ((8, n), f32), ((1024, 768), bf), ((n, 768), bf), ((n, 1024), bf), ((n, 256), f32),
         ((n, 256), f32), ((256, n), bf), ((n, 128), f32)],
        [19], 0, (mixed, ga, total, cosine, sine, ids, weight), 32,
    )


def weights_kernel(gm_hbm, normed_hbm, okeep_hbm, osend_hbm, keep_hbm, send_hbm,
                   gm_ref, normed_ref, gw, okeep, osend, sems):
    go = Copies(sems)
    first = [go.start(gm_hbm, gm_ref), go.start(normed_hbm, normed_ref)]
    second = [go.start(okeep_hbm, okeep), go.start(osend_hbm, osend)]
    wait_all(first + second)
    cols = pl.ds(768, 1024)
    late = [go.start(okeep, keep_hbm.at[:, cols]), go.start(osend, send_hbm.at[:, cols])]

    @pl.loop(0, 4)
    def _(i):
        cols = aligned(i, 256)
        gw[cols, :] = dot(normed_ref[:, cols], gm_ref[...], TN).astype(bf)

    late += [
        go.start(gw.at[aligned(place_of(p), 128)],
                 (keep_hbm if p < 4 else send_hbm).at[pl.ds(128 * (p % 4), 128), pl.ds(0, 768)])
        for p in range(8)
    ]
    wait_all(late)


def project_weights(gm, normed, okeep, osend):
    n = gm.shape[0]
    return call(
        weights_kernel, "project_weights", [((512, 1792), bf)] * 2,
        [((n, 768), bf), ((n, 1024), bf), ((1024, 768), bf), ((512, 1024), bf), ((512, 1024), bf)],
        [14], 1, (gm, normed, okeep, osend), 24,
    )


def feed_kernel(*refs):
    att_hbm, attp_hbm, act_hbm, actp_hbm, cot_hbm, cotp_hbm = refs[:6]
    a_in, b_in, da_in, db_in, outs = refs[6:10], refs[10:14], refs[14:18], refs[18:22], refs[22]
    part_hbm, outown_hbm, gnown_hbm, res_hbm, wo_hbm = refs[23:28]
    (ga_keep, ga_send, gb_keep, gb_send, gda_keep, gda_send, gdb_keep, gdb_send) = refs[28:36]
    (wg, wu, wd, wo, att, act, n2, n2t, cot, res_ref, out_acc, gn_acc, part, dg, du, dd,
     sems, osem, tsem) = refs[36:]
    me = lax.axis_index("dp")
    core = me % 2
    yx = me // 2
    go = Copies(sems)
    small = []
    for base, src, own in ((0, att_hbm, act_hbm), (256, attp_hbm, actp_hbm)):
        rows = pl.ds(base, 256)
        small += [go.start(src.at[i], att.at[rows, pl.ds(256 * i, 256)]) for i in range(4)]
        small.append(go.start(own, act.at[rows]))
    places = []
    for p in range(4):
        (ax, ay), (bx, by) = FLIPS_A[p], FLIPS_B[p]
        places.append((yx ^ (ax + 2 * ay), yx ^ (bx + 2 * by)))
    for p, (ja, jb) in enumerate(places):
        for which, src, j, col in ((0, a_in[p], ja, 0), (1, b_in[p], jb, 512)):
            for half in range(2):
                cols = pl.ds(col + 256 * half, 256)
                rows = pl.ds(128 * half, 128)
                small.append(go.start(src.at[rows, pl.ds(FF2, 256)], wo.at[aligned(j * 2 + core, 128), cols]))
                small.append(go.start(outs.at[4 * which + p, rows], wo.at[aligned(j * 2 + 1 - core, 128), cols]))
    big = []
    for p, (ja, jb) in enumerate(places):
        for src, dst, j in ((a_in[p], wg, ja), (b_in[p], wu, jb)):
            for half, c in ((0, core), (1, 1 - core)):
                big.append(go.start(src.at[pl.ds(128 * half, 128), pl.ds(0, FF2)],
                                    dst.at[aligned(j * 2 + c, 128), pl.ds(0, FF2)]))
    big += [go.start(cot_hbm, cot.at[pl.ds(0, 256)]), go.start(cotp_hbm, cot.at[pl.ds(256, 256)])]
    for p, (ja, jb) in enumerate(places):
        big.append(go.start(da_in[p], wd.at[aligned(ja, 352), pl.ds(0, 512)]))
        big.append(go.start(db_in[p], wd.at[aligned(jb, 352), pl.ds(512, 512)]))
    wg[:, FF2:FFP] = jnp.zeros((1024, FFP - FF2), bf)
    wu[:, FF2:FFP] = jnp.zeros((1024, FFP - FF2), bf)
    wd[FF2:FFP, :] = jnp.zeros((FFP - FF2, 1024), bf)
    out_acc[...] = jnp.zeros_like(out_acc)
    gn_acc[...] = jnp.zeros_like(gn_acc)
    wait_all(small)
    ogo = Copies(osem)
    done = [ogo.start(wo, wo_hbm)]

    @pl.loop(0, 2)
    def _(i):
        rows = aligned(i, 256)
        res = act[rows, :].astype(f32) + dot(att[rows, :], wo[...], NN)
        res_ref[rows, :] = res
        n = layer_norm(res)
        n2[rows, :] = n.astype(bf)
        n2t[:, rows] = n.T.astype(bf)

    done.append(ogo.start(res_ref.at[pl.ds(0, 256)], res_hbm))
    wait_all(big)

    def tile_copies(t, width):
        copies = []
        cols = pl.ds(pl.multiple_of(t * 256, 256), width)
        for q in range(4):
            fx, fy = FLIPS_A[q]
            rows = aligned(yx ^ (fx + 2 * fy), 256)
            for k, src, dst, slot in ((0, dg, ga_send if fx else ga_keep, fy), (1, du, gb_send if fy else gb_keep, fx)):
                copies.append(pltpu.make_async_copy(
                    src.at[rows, cols], dst.at[pl.ds(256 * slot, 256), cols], tsem.at[t, 2 * q + k]))
        return copies

    last = FFP // 256 - 1

    @pl.loop(0, last + 1)
    def _(t):
        cols = aligned(t, 256)
        g = dot(n2[...], wg[:, cols], NN)
        u = dot(n2[...], wu[:, cols], NN)
        gh = dot(cot[...], wd[cols, :], NT)
        sig = 1.0 / (1.0 + jnp.exp(-g))
        silu = g * sig
        h = (silu * u).astype(bf)
        gu = (gh * silu).astype(bf)
        gg = (gh * u * (sig + silu * (1.0 - sig))).astype(bf)
        dg[:, cols] = dot(n2t[...], gg, NN).astype(bf)
        du[:, cols] = dot(n2t[...], gu, NN).astype(bf)

        @pl.when(t < last)
        def _():
            for copy in tile_copies(t, 256):
                copy.start()

        dd[cols, :] = dot(h, cot[...], TN).astype(bf)
        gn_acc[...] += dot(gg, wg[:, cols], NT) + dot(gu, wu[:, cols], NT)
        out_acc[...] += dot(h, wd[cols, :], NN)

    ends = tile_copies(last, FF2 - 256 * last)
    for copy in ends:
        copy.start()
    part[0:256, :] = out_acc[256:512, :].astype(bf)
    part[256:512, :] = gn_acc[256:512, :].astype(bf)
    done.append(ogo.start(part, part_hbm))
    done.append(ogo.start(gn_acc.at[pl.ds(0, 256)], gnown_hbm))
    done.append(ogo.start(out_acc.at[pl.ds(0, 256)], outown_hbm))
    for q in range(4):
        fx, fy = FLIPS_A[q]
        rows = aligned(yx ^ (fx + 2 * fy), 352)
        done.append(ogo.start(dd.at[rows, pl.ds(0, 512)], (gda_send if fx else gda_keep).at[pl.ds(352 * fy, 352)]))
        done.append(ogo.start(dd.at[rows, pl.ds(512, 512)], (gdb_send if fy else gdb_keep).at[pl.ds(352 * fx, 352)]))
    for t in range(last):
        wait_all(tile_copies(t, 256))
    wait_all(ends)
    wait_all(done)


def feed(att, attp, act, actp, cot, cotp, a, b, da, db, outs):
    big = [((1024, FFP), bf), ((1024, FFP), bf), ((FFP, 1024), bf)]
    return call(
        feed_kernel, "feed",
        [((512, 1024), bf), ((256, 1024), f32), ((256, 1024), f32), ((256, 1024), f32), ((1024, 1024), bf)]
        + [((512, FF2), bf)] * 4 + [((704, 512), bf)] * 4,
        big + [((1024, 1024), bf), ((512, 1024), bf), ((512, 1024), bf), ((512, 1024), bf), ((1024, 512), bf),
               ((512, 1024), bf), ((512, 1024), f32), ((512, 1024), f32), ((512, 1024), f32), ((512, 1024), bf)] + big,
        [68, 13, (6, 8)], 15, (att, attp, act, actp, cot, cotp, *a, *b, *da, *db, outs), 50,
    )


def branch_kernel(part_hbm, outown_hbm, gnown_hbm, res_hbm, cot_hbm, att_hbm, wo_hbm,
                  layer_hbm, gres_hbm, gatt_hbm, keep_hbm, send_hbm,
                  part, outown, gnown, res_ref, cot, att, wo, layer, gres_ref, gatt, gw, sems):
    me = lax.axis_index("dp")
    core = me % 2
    yx = me // 2
    go = Copies(sems)
    first = [
        go.start(a, b)
        for a, b in ((part_hbm, part), (gnown_hbm, gnown), (res_hbm, res_ref), (cot_hbm, cot))
    ]
    late = [go.start(wo_hbm, wo), go.start(outown_hbm, outown)]
    late += [go.start(att_hbm.at[i], att.at[:, pl.ds(256 * i, 256)]) for i in range(4)]
    wait_all(first)
    res = res_ref[...]
    g = gnown[...] + part[256:512, :].astype(f32)
    c = res - jnp.mean(res, axis=-1, keepdims=True)
    r = lax.rsqrt(jnp.mean(c * c, axis=-1, keepdims=True) + NORM_EPS)
    xh = c * r
    d = r * (g - jnp.mean(g, axis=-1, keepdims=True) - xh * jnp.mean(g * xh, axis=-1, keepdims=True))
    gres = cot[...].astype(f32) + d
    gres_ref[...] = gres
    low = gres.astype(bf)
    wait_all(late)
    done = [go.start(gres_ref, gres_hbm)]
    ga = dot(low, wo[...], NT).astype(bf)
    for z in range(4):
        gatt[z] = ga[:, 256 * z : 256 * z + 256]
    done.append(go.start(gatt, gatt_hbm))
    layer[...] = (res + (outown[...] + part[0:256, :].astype(f32))).astype(bf)
    done.append(go.start(layer, layer_hbm))
    gw[...] = dot(att[...], low, TN).astype(bf)
    for q in range(4):
        fx, fy = FLIPS_A[q]
        j = yx ^ (fx + 2 * fy)
        for dst, c in ((keep_hbm, core), (send_hbm, 1 - core)):
            rows = aligned(j * 2 + c, 128)
            done.append(go.start(gw.at[rows], dst.at[pl.ds(128 * (2 * fx + fy), 128)]))
    wait_all(done)


def branch(part, outown, gnown, res, cot, att, wo):
    tall = ((256, 1024), f32)
    low = ((256, 1024), bf)
    return call(
        branch_kernel, "branch",
        [low, tall, ((4, 256, 256), bf), ((512, 1024), bf), ((512, 1024), bf)],
        [((512, 1024), bf), tall, tall, tall, low, low, ((1024, 1024), bf), low, tall, ((4, 256, 256), bf),
         ((1024, 1024), bf)],
        [21], 1, (part, outown, gnown, res, cot, att, wo), 32,
    )


def update_kernel(coeff_ref, wide_ref, mg, mu, md, wg, wu, wd, *refs):
    outs, (gg, gu, gd, ng, nu, nd, og, ou, od), sems = refs[:9], refs[9:18], refs[18]
    coeff = coeff_ref[0]
    go = Copies(sems)
    done = []
    part = FF2 // 4

    def finish(i, grad, moment, weight, new_moment, new_weight):
        done.append(go.start(grad, outs[i]))
        moved = coeff * moment[...] + grad[...]
        new_moment[...] = moved
        done.append(go.start(new_moment, outs[3 + i]))
        new_weight[...] = (weight[...].astype(f32) - LEARN_RATE * moved).astype(bf)
        done.append(go.start(new_weight, outs[6 + i]))

    for i, (grad, moment, weight, nm, nw) in enumerate(((gg, mg, wg, ng, og), (gu, mu, wu, nu, ou))):
        for side in range(2):
            columns = wide_ref[:, FF2 * (2 * side + i) : FF2 * (2 * side + i + 1)].astype(f32)
            for j in range(4):
                low = part * (2 * j + side)
                grad[:, low : low + part] = columns[:, part * j : part * j + part]
        finish(i, grad, moment, weight, nm, nw)
    for j in range(3):
        rows = min(32, 88 - 32 * j)
        low = 4 * FF2 + 1024 * j
        gd[32 * j : 32 * j + rows, :] = wide_ref[:, low : low + 1024].astype(f32)[0:rows]
    finish(2, gd, md, wd, nd, od)
    wait_all(done)


def update(coeff, wide, moments, weights):
    shapes = [(32, 2 * FF2), (32, 2 * FF2), (88, 1024)]
    outs = [(s, f32) for s in shapes] * 2 + [(s, bf) for s in shapes]
    vmem = pl.BlockSpec(memory_space=pltpu.VMEM)
    return pl.pallas_call(
        update_kernel,
        out_shape=tuple(pltpu.HBM(*o) for o in outs),
        in_specs=[pl.BlockSpec(memory_space=pltpu.SMEM)] + [vmem] * 7,
        out_specs=(MAIN,) * 9,
        scratch_shapes=[pltpu.VMEM(*o) for o in outs] + [pltpu.SemaphoreType.DMA((9,))],
        compiler_params=pltpu.CompilerParams(vmem_limit_bytes=16 << 20),
        cost_estimate=pl.CostEstimate(flops=1 << 20, bytes_accessed=6 << 20, transcendentals=0),
        name="update",
    )(coeff, wide, *moments, *weights)


def swap(array, bit):
    return lax.ppermute(array, "dp", [(i, i ^ bit) for i in range(8)])


def shift(array, bits):
    return lax.ppermute(array, "ctx", [(i, i ^ bits) for i in range(4)])


def add_low(left, right):
    return (left.astype(f32) + right.astype(f32)).astype(bf)


def split_even(matrix):
    n = matrix.shape[1] // 8
    parts = [matrix[:, n * i : n * i + n] for i in range(8)]
    return jnp.concatenate(parts[0::2], axis=1), jnp.concatenate(parts[1::2], axis=1)


def tie(value, *anchors):
    return lax.optimization_barrier((value, *anchors))[0]


def fast_device(
    activations,
    block_ids,
    cotangent,
    w_query,
    w_key,
    w_value,
    w_out,
    w_gate,
    w_up,
    w_down,
    m_query,
    m_key,
    m_value,
    m_out,
    m_gate,
    m_up,
    m_down,
    clip_threshold,
    momentum_coeff,
):
    me = lax.axis_index("dp")
    z = lax.axis_index("ctx")
    core = me % 2
    _, span, width = activations.shape
    length = block_ids.shape[1]
    act = activations.reshape(span, width)
    cot = cotangent.reshape(span, width)
    act_other = swap(act, 1)
    cot_other = swap(cot, 1)
    g0, g1 = split_even(w_gate)
    u0, u1 = split_even(w_up)
    even = jnp.stack([g0, u0])
    odd = jnp.stack([g1, u1])
    flip = core == 1
    mine = jnp.where(flip, odd, even)
    other = swap(jnp.where(flip, even, odd), 1)
    out_rows = jnp.stack([w_out[:, :512], w_out[:, 512:]]).reshape(2, 32, 2, 256)
    wide = jnp.stack([mine, other], axis=1)
    wide = jnp.concatenate([wide, out_rows.transpose(0, 2, 1, 3)], axis=3)
    wide = lax.all_gather(wide, "ctx", axis=2, tiled=True).reshape(2, 256, FF2 + 256)
    padded = jnp.concatenate([act, w_down, jnp.zeros((8, width), bf)], axis=0)
    rows_all = lax.all_gather(padded, "ctx", axis=0, tiled=True)
    heads = jnp.stack(
        [
            jnp.concatenate([w[:, 256 * i : 256 * i + 256] for w in (w_query, w_key, w_value)], 1)
            for i in range(4)
        ]
    )
    heads = lax.all_to_all(heads, "ctx", 0, 0, tiled=True).reshape(128, 768)
    hx = swap(heads, 2)
    hy = swap(jnp.concatenate([heads, hx], axis=0), 4)
    four = jnp.concatenate([heads, hy[:128], hx, hy[128:]], axis=0)
    heads_rel = jnp.concatenate([four, swap(four, 1)], axis=0)
    wide, act_other, cot_other = lax.optimization_barrier((wide, act_other, cot_other))

    def spread(own, first, second):
        near = swap(own, first)
        return [own, near, swap(own, second), swap(near, second)]

    piece_a = spread(wide[0], 2, 4)
    piece_b = spread(wide[1], 4, 2)
    down = jnp.concatenate(
        [rows_all[352 * i + 256 : 352 * i + 344] for i in range(4)], axis=0
    )
    piece_da = spread(down[:, :512], 2, 4)
    piece_db = spread(down[:, 512:], 4, 2)
    cosine, sine = rotary_tables(jnp.arange(length, dtype=jnp.int32), HEAD_DIM)
    cosine = jnp.concatenate([cosine] * 4, axis=1)
    sine = jnp.concatenate([-sine, sine, -sine, sine], axis=1)
    ids = jnp.broadcast_to(block_ids, (8, length)).astype(f32)
    pieces = lax.optimization_barrier((rows_all, *piece_a, *piece_b))
    normed, mixed, attended, totals, peaks, outs = attend(
        pieces[0], heads_rel, cosine, sine, ids, pieces[1:]
    )
    piece_a, piece_b = pieces[1:5], pieces[5:]
    outs = swap(outs, 1)
    attended = tie(attended, *piece_da[1:3], *piece_db[1:3])
    attended = lax.all_to_all(attended.reshape(4, span, 256), "ctx", 0, 0, tiled=True)
    attended_other = swap(tie(attended, piece_da[3], piece_db[3]), 1)
    (part, out_own, back_own, residual, full_out, *grads) = feed(
        attended, attended_other, act, act_other, cot, cot_other,
        piece_a, piece_b, piece_da, piece_db, outs,
    )
    ga_keep, ga_send, gb_keep, gb_send, gda_keep, gda_send, gdb_keep, gdb_send = grads
    part = swap(part, 1)
    ga_send, gb_send, gda_send, gdb_send, part = lax.optimization_barrier(
        (ga_send, gb_send, gda_send, gdb_send, part)
    )
    gda_other = swap(gda_send, 2)
    gdb_other = swap(gdb_send, 4)
    ga_other = swap(ga_send, 2)
    gb_other = swap(gb_send, 4)
    layer_out, grad_residual, grad_attended, go_keep, go_send = branch(
        part, out_own, back_own, residual, cot, attended, full_out
    )
    grad_attended = lax.all_to_all(grad_attended, "ctx", 0, 0, tiled=True).reshape(length, 256)
    grad_mixed, grad_normed = attend_back(
        mixed, grad_attended, totals, cosine, sine, ids, heads_rel
    )
    (ga_keep, gb_keep, gda_keep, gdb_keep, ga_other, gb_other, gda_other, gdb_other, grad_mixed) = (
        lax.optimization_barrier(
            (ga_keep, gb_keep, gda_keep, gdb_keep, ga_other, gb_other, gda_other, gdb_other,
             grad_mixed)
        )
    )
    grad_a = add_low(ga_keep, ga_other)
    grad_b = add_low(gb_keep, gb_other)
    grad_da = add_low(gda_keep, gda_other)
    grad_db = add_low(gdb_keep, gdb_other)
    grad_heads = project_weights(
        tie(grad_mixed, grad_a, grad_b, grad_da, grad_db), normed, go_keep, go_send
    )
    grad_a = add_low(grad_a[:256], swap(grad_a[256:], 4))
    grad_b = add_low(grad_b[:256], swap(grad_b[256:], 2))
    grad_da = add_low(grad_da[:352], swap(grad_da[352:], 4))
    grad_db = add_low(grad_db[:352], swap(grad_db[352:], 2))
    def core_rows(which):
        return jnp.concatenate(
            [lax.dynamic_slice_in_dim(g, which * 128, 128, 0) for g in (grad_a, grad_b)], axis=1
        )

    own_half = core_rows(core)
    other_half = swap(core_rows(1 - core), 1)
    grad_d = jnp.concatenate([grad_da, grad_db], axis=1).reshape(4, 88, width)
    grad_d = jnp.pad(grad_d, ((0, 0), (0, 8), (0, 0))).reshape(4, 3, 32, width)
    grad_d = grad_d.transpose(0, 2, 1, 3).reshape(128, 3 * width)
    grad_wide = jnp.concatenate(
        [
            jnp.where(flip, other_half, own_half),
            jnp.where(flip, own_half, other_half),
            grad_d,
        ],
        axis=1,
    )
    grad_wide = lax.psum_scatter(grad_wide, "ctx", scatter_dimension=0, tiled=True)
    peaks = tie(peaks, ga_other)
    peaks = lax.all_to_all(
        jnp.broadcast_to(peaks[None], (32, 8, 128)), ("dp", "ctx"), 0, 0, tiled=True
    )
    head_peaks = jnp.max(peaks.reshape(8, 4, 8, 128), axis=0)[:, :4, 0].reshape(HEADS)
    grad_normed = lax.psum_scatter(grad_normed, "ctx", scatter_dimension=0, tiled=True)
    tokens_wide = act.astype(f32)
    unused, first_pull = jax.vjp(normalize, tokens_wide)
    input_grad = grad_residual + first_pull(grad_normed.astype(f32))[0]
    grad_heads = add_low(grad_heads[0], swap(grad_heads[1], 1))
    grad_heads = add_low(grad_heads[:256], swap(grad_heads[256:], 2))
    grad_heads = add_low(grad_heads[:128], swap(grad_heads[128:], 4))
    grad_heads = lax.all_to_all(grad_heads.reshape(4, 32, 768 + width), "ctx", 0, 0, tiled=True)
    grad_heads = grad_heads.astype(f32)
    parts = grad_heads[:, :, 768:]
    grad_out = parts[0] + parts[1] + (parts[2] + parts[3])
    grad_qkv = [
        jnp.concatenate([grad_heads[i, :, 256 * k : 256 * k + 256] for i in range(4)], axis=1)
        for k in range(3)
    ]
    big = update(
        momentum_coeff.reshape(1), grad_wide, (m_gate, m_up, m_down), (w_gate, w_up, w_down)
    )
    weight_grads = (*grad_qkv, grad_out)
    moments = (m_query, m_key, m_value, m_out)
    new_moments = tuple(
        (momentum_coeff * moment + gradient for moment, gradient in zip(moments, weight_grads))
    )
    head_scale = jnp.sqrt(clip_threshold / jnp.maximum(head_peaks, clip_threshold))
    column_scale = jnp.repeat(head_scale, HEAD_DIM)
    rates = (LEARN_RATE, LEARN_RATE, LEARN_RATE, OUT_RATE)
    shard_list = (w_query, w_key, w_value, w_out)
    updated = [
        matrix.astype(jnp.float32) - rate * moment
        for matrix, moment, rate in zip(shard_list, new_moments, rates)
    ]
    updated[0] = updated[0] * column_scale[None, :]
    updated[1] = updated[1] * column_scale[None, :]
    updated = [matrix.astype(bf) for matrix in updated]
    return (
        layer_out[None],
        input_grad[None],
        *weight_grads,
        *big[:3],
        *new_moments,
        *big[3:6],
        *updated,
        *big[6:],
        head_peaks,
        head_scale,
    )


def solution(mesh):
    placed = (
        P("dp", "ctx", None),
        P("dp", None),
        P("dp", "ctx", None),
        P(("dp", "ctx"), None),
        P(("dp", "ctx"), None),
        P(("dp", "ctx"), None),
        P(("dp", "ctx"), None),
        P(("dp", "ctx"), None),
        P(("dp", "ctx"), None),
        P(("dp", "ctx"), None),
        P(("dp", "ctx"), None),
        P(("dp", "ctx"), None),
        P(("dp", "ctx"), None),
        P(("dp", "ctx"), None),
        P(("dp", "ctx"), None),
        P(("dp", "ctx"), None),
        P(("dp", "ctx"), None),
        P(),
        P(),
    )
    fits = mesh.shape["dp"] == 8 and mesh.shape["ctx"] == 4
    return jax.shard_map(
        fast_device if fits else per_device,
        mesh=mesh,
        in_specs=placed,
        out_specs=(
            P("dp", "ctx", None),
            P("dp", "ctx", None),
            P(("dp", "ctx"), None),
            P(("dp", "ctx"), None),
            P(("dp", "ctx"), None),
            P(("dp", "ctx"), None),
            P(("dp", "ctx"), None),
            P(("dp", "ctx"), None),
            P(("dp", "ctx"), None),
            P(("dp", "ctx"), None),
            P(("dp", "ctx"), None),
            P(("dp", "ctx"), None),
            P(("dp", "ctx"), None),
            P(("dp", "ctx"), None),
            P(("dp", "ctx"), None),
            P(("dp", "ctx"), None),
            P(("dp", "ctx"), None),
            P(("dp", "ctx"), None),
            P(("dp", "ctx"), None),
            P(("dp", "ctx"), None),
            P(("dp", "ctx"), None),
            P(("dp", "ctx"), None),
            P(("dp", "ctx"), None),
            P(),
            P(),
        ),
        check_vma=False,
    )
```

```python
import math

import jax
import jax.numpy as jnp
from jax import lax
from jax.experimental import pallas as pl
from jax.experimental.pallas import tpu as pltpu
from jax.sharding import PartitionSpec as P

HEADS = 16
HEAD_DIM = 64


NORM_EPS = 1e-05
ROPE_BASE = 10000.0
LEARN_RATE = 0.0001
OUT_RATE = 0.0016
MASK_FILL = -1e30


def normalize(values):
    centred = values - jnp.mean(values, axis=-1, keepdims=True)
    spread = jnp.mean(centred * centred, axis=-1, keepdims=True)
    return centred * lax.rsqrt(spread + NORM_EPS)


def rotary_tables(positions, head_width):
    half_width = head_width // 2
    frequency = ROPE_BASE ** (-(jnp.arange(half_width, dtype=jnp.float32) * 2.0 / head_width))
    angles = positions.astype(jnp.float32)[:, None] * frequency[None, :]
    return (jnp.cos(angles), jnp.sin(angles))


def rotate(vectors, cosine, sine_table):
    half_width = vectors.shape[-1] // 2
    first_half = vectors[..., :half_width]
    second = vectors[..., half_width:]
    cos_wide = cosine[:, None, :]
    sin_wide = sine_table[:, None, :]
    return jnp.concatenate(
        [first_half * cos_wide - second * sin_wide, second * cos_wide + first_half * sin_wide],
        axis=-1,
    )


def swiglu(gate_proj, up_proj):
    return jax.nn.silu(gate_proj) * up_proj


def project(left_rows, matrix):
    return jnp.dot(left_rows, matrix, preferred_element_type=jnp.float32)


def project_back(grad_rows, matrix):
    return lax.dot_general(
        grad_rows, matrix, (((1,), (1,)), ((), ())), preferred_element_type=jnp.float32
    )


def shard_gradient(left_rows, right_rows):
    return lax.psum_scatter(
        lax.dot_general(
            left_rows, right_rows, (((0,), (0,)), ((), ())), preferred_element_type=jnp.float32
        ),
        ("dp", "ctx"),
        scatter_dimension=0,
        tiled=True,
    )


def per_device(
    activations,
    block_ids,
    cotangent,
    w_query,
    w_key,
    w_value,
    w_out,
    w_gate,
    w_up,
    w_down,
    m_query,
    m_key,
    m_value,
    m_out,
    m_gate,
    m_up,
    m_down,
    clip_threshold,
    momentum_coeff,
):
    shard_list = (w_query, w_key, w_value, w_out, w_gate, w_up, w_down)
    gathered = (
        lax.all_gather(shard_list[0], ("dp", "ctx"), axis=0, tiled=True),
        lax.all_gather(shard_list[1], ("dp", "ctx"), axis=0, tiled=True),
        lax.all_gather(shard_list[2], ("dp", "ctx"), axis=0, tiled=True),
        lax.all_gather(shard_list[3], ("dp", "ctx"), axis=0, tiled=True),
        lax.all_gather(shard_list[4], ("dp", "ctx"), axis=0, tiled=True),
        lax.all_gather(shard_list[5], ("dp", "ctx"), axis=0, tiled=True),
        lax.all_gather(shard_list[6], ("dp", "ctx"), axis=0, tiled=True),
    )
    full_query, full_key, full_value, full_out, full_gate, full_up, full_down = gathered
    seq_count, span_len, model_width = activations.shape
    ctx_place = lax.axis_index("ctx")
    positions = ctx_place * span_len + jnp.arange(span_len, dtype=jnp.int32)
    cosine, sine_table = rotary_tables(positions, HEAD_DIM)
    score_scale = 1.0 / math.sqrt(HEAD_DIM)

    def split_heads(matrix):
        return matrix.reshape(seq_count, span_len, HEADS, HEAD_DIM)

    tokens_flat = activations.astype(jnp.float32).reshape(-1, model_width)
    normed = normalize(tokens_flat).astype(jnp.bfloat16)
    queries = rotate(split_heads(project(normed, full_query)), cosine, sine_table).astype(
        jnp.bfloat16
    )
    key_rot = rotate(split_heads(project(normed, full_key)), cosine, sine_table).astype(
        jnp.bfloat16
    )
    value_rot = split_heads(project(normed, full_value)).astype(jnp.bfloat16)
    key_all, value_all = (
        lax.all_gather(key_rot, "ctx", axis=1, tiled=True),
        lax.all_gather(value_rot, "ctx", axis=1, tiled=True),
    )
    query_ids = lax.dynamic_slice_in_dim(block_ids, ctx_place * span_len, span_len, 1)
    allowed = (block_ids[:, None, :] <= query_ids[:, :, None])[:, None]

    def masked_scores():
        scores = (
            jnp.einsum("sqhd,skhd->shqk", queries, key_all, preferred_element_type=jnp.float32)
            * score_scale
        )
        return jnp.where(allowed, scores, MASK_FILL)

    masked = masked_scores()
    local_peaks = jnp.max(masked, axis=(0, 2, 3))
    row_top = jnp.max(masked, axis=-1, keepdims=True)
    log_total = row_top + jnp.log(jnp.sum(jnp.exp(masked - row_top), axis=-1, keepdims=True))
    probs_low = jnp.exp(masked - log_total).astype(jnp.bfloat16)
    attended = jnp.einsum(
        "shqk,skhd->sqhd", probs_low, value_all, preferred_element_type=jnp.float32
    )
    attended_low = attended.reshape(-1, model_width).astype(jnp.bfloat16)
    head_peaks = lax.pmax(local_peaks, ("dp", "ctx"))
    residual = tokens_flat + project(attended_low, full_out)
    normed2 = normalize(residual).astype(jnp.bfloat16)
    gate_proj = project(normed2, full_gate)
    up_proj = project(normed2, full_up)
    hidden_low = swiglu(gate_proj, up_proj).astype(jnp.bfloat16)
    layer_out = (
        (residual + project(hidden_low, full_down))
        .astype(jnp.bfloat16)
        .reshape(seq_count, span_len, model_width)
    )
    back_weights = (
        lax.all_gather(shard_list[0], ("dp", "ctx"), axis=0, tiled=True),
        lax.all_gather(shard_list[1], ("dp", "ctx"), axis=0, tiled=True),
        lax.all_gather(shard_list[2], ("dp", "ctx"), axis=0, tiled=True),
        lax.all_gather(shard_list[3], ("dp", "ctx"), axis=0, tiled=True),
        lax.all_gather(shard_list[4], ("dp", "ctx"), axis=0, tiled=True),
        lax.all_gather(shard_list[5], ("dp", "ctx"), axis=0, tiled=True),
        lax.all_gather(shard_list[6], ("dp", "ctx"), axis=0, tiled=True),
    )
    back_query, back_key, back_value, back_out, back_gate, back_up, back_down = back_weights
    grad_rows = cotangent.reshape(-1, model_width)
    grad_hidden = project_back(grad_rows, back_down)
    unused, gate_pull = jax.vjp(swiglu, gate_proj, up_proj)
    grad_gate_wide, grad_up_wide = gate_pull(grad_hidden)
    grad_gate_low = grad_gate_wide.astype(jnp.bfloat16)
    grad_up_low = grad_up_wide.astype(jnp.bfloat16)
    grad_normed2 = project_back(grad_gate_low, back_gate) + project_back(grad_up_low, back_up)
    unused, second_pull = jax.vjp(normalize, residual)
    grad_residual = grad_rows.astype(jnp.float32) + second_pull(grad_normed2)[0]
    grad_branch = grad_residual.astype(jnp.bfloat16)
    grad_attended = split_heads(project_back(grad_branch, back_out).astype(jnp.bfloat16))
    masked = masked_scores()
    probs = jnp.exp(masked - log_total)
    probs_again = probs.astype(jnp.bfloat16)
    grad_values_all = jnp.einsum(
        "shqk,sqhd->skhd", probs_again, grad_attended, preferred_element_type=jnp.float32
    )
    grad_probs = jnp.einsum(
        "sqhd,skhd->shqk", grad_attended, value_all, preferred_element_type=jnp.float32
    )
    score_grad = (
        probs * (grad_probs - jnp.sum(probs * grad_probs, axis=-1, keepdims=True))
    ).astype(jnp.bfloat16)
    grad_queries = (
        jnp.einsum("shqk,skhd->sqhd", score_grad, key_all, preferred_element_type=jnp.float32)
        * score_scale
    )
    grad_keys_all = (
        jnp.einsum("shqk,sqhd->skhd", score_grad, queries, preferred_element_type=jnp.float32)
        * score_scale
    )
    grad_keys, grad_values = (
        lax.psum_scatter(
            grad_keys_all.astype(jnp.bfloat16), "ctx", scatter_dimension=1, tiled=True
        ).astype(jnp.float32),
        lax.psum_scatter(
            grad_values_all.astype(jnp.bfloat16), "ctx", scatter_dimension=1, tiled=True
        ).astype(jnp.float32),
    )
    grad_query_low = (
        rotate(grad_queries, cosine, -sine_table).reshape(-1, model_width).astype(jnp.bfloat16)
    )
    grad_key_low = (
        rotate(grad_keys, cosine, -sine_table).reshape(-1, model_width).astype(jnp.bfloat16)
    )
    grad_value_low = grad_values.reshape(-1, model_width).astype(jnp.bfloat16)
    grad_normed = (
        project_back(grad_query_low, back_query)
        + project_back(grad_key_low, back_key)
        + project_back(grad_value_low, back_value)
    )
    unused, first_pull = jax.vjp(normalize, tokens_flat)
    input_grad = (grad_residual + first_pull(grad_normed)[0]).reshape(
        seq_count, span_len, model_width
    )
    weight_grads = (
        shard_gradient(normed, grad_query_low),
        shard_gradient(normed, grad_key_low),
        shard_gradient(normed, grad_value_low),
        shard_gradient(attended_low, grad_branch),
        shard_gradient(normed2, grad_gate_low),
        shard_gradient(normed2, grad_up_low),
        shard_gradient(hidden_low, grad_rows),
    )
    moments = (m_query, m_key, m_value, m_out, m_gate, m_up, m_down)
    new_moments = tuple(
        (momentum_coeff * moment + gradient for moment, gradient in zip(moments, weight_grads))
    )
    head_scale = jnp.sqrt(clip_threshold / jnp.maximum(head_peaks, clip_threshold))
    column_scale = jnp.repeat(head_scale, HEAD_DIM)
    rates = (LEARN_RATE, LEARN_RATE, LEARN_RATE, OUT_RATE, LEARN_RATE, LEARN_RATE, LEARN_RATE)
    updated = [
        matrix.astype(jnp.float32) - rate * moment
        for matrix, moment, rate in zip(shard_list, new_moments, rates)
    ]
    updated[0] = updated[0] * column_scale[None, :]
    updated[1] = updated[1] * column_scale[None, :]
    updated = [matrix.astype(jnp.bfloat16) for matrix in updated]
    return (
        layer_out,
        input_grad,
        weight_grads[0],
        weight_grads[1],
        weight_grads[2],
        weight_grads[3],
        weight_grads[4],
        weight_grads[5],
        weight_grads[6],
        new_moments[0],
        new_moments[1],
        new_moments[2],
        new_moments[3],
        new_moments[4],
        new_moments[5],
        new_moments[6],
        updated[0],
        updated[1],
        updated[2],
        updated[3],
        updated[4],
        updated[5],
        updated[6],
        head_peaks,
        head_scale,
    )


f32=jnp.float32; bf=jnp.bfloat16
NT=(((1,),(1,)),((),())); TN=(((0,),(0,)),((),())); NN=(((1,),(0,)),((),()))
FF2=1408
FFP=1536
FLIPS_A=((0,0),(1,0),(0,1),(1,1))
FLIPS_B=((0,0),(0,1),(1,0),(1,1))
MAIN=pl.BlockSpec(memory_space=pltpu.HBM)
S=jax.ShapeDtypeStruct


def dot(a, b, dims):
    return lax.dot_general(a, b, dims, preferred_element_type=f32)


def aligned(i, m):
    return pl.ds(pl.multiple_of(i * m, m), m)


class Copies:
    def __init__(self, sems):
        self.sems = sems
        self.count = 0

    def start(self, source, target):
        copy = pltpu.make_async_copy(source, target, self.sems.at[self.count])
        self.count += 1
        copy.start()
        return copy


def wait_all(copies):
    for copy in copies:
        copy.wait()


def call(kernel, name, outs, scratch, sems, flops, args, limit):
    return pl.pallas_call(
        kernel,
        out_shape=tuple(pltpu.HBM(*o) for o in outs),
        in_specs=[MAIN] * len(args),
        out_specs=(MAIN,) * len(outs),
        scratch_shapes=[pltpu.VMEM(*s) for s in scratch] + [pltpu.SemaphoreType.DMA(n if isinstance(n, tuple) else (n,)) for n in sems],
        compiler_params=pltpu.CompilerParams(vmem_limit_bytes=limit << 20),
        cost_estimate=pl.CostEstimate(flops=flops << 30, bytes_accessed=8 << 20, transcendentals=0),
        name=name,
    )(*(pltpu.with_memory_space_constraint(arg, pltpu.HBM) for arg in args))


def place_of(p):
    return lax.axis_index("dp") ^ ((p >> 2 & 1) | (p >> 1 & 1) << 1 | (p & 1) << 2)


def turn(values, cosine, signed_sine):
    lane = lax.broadcasted_iota(jnp.int32, cosine.shape, 1)
    first = lane % 64 < 32
    parts = []
    for j in range(values.shape[1] // 128):
        part = values[:, 128 * j : 128 * j + 128]
        partner = jnp.where(first, pltpu.roll(part, 96, 1), pltpu.roll(part, 32, 1))
        parts.append(part * cosine + partner * signed_sine)
    return jnp.concatenate(parts, axis=1)


def layer_norm(x):
    c = x - jnp.mean(x, axis=-1, keepdims=True)
    v = jnp.mean(c * c, axis=-1, keepdims=True)
    return c * lax.rsqrt(v + NORM_EPS)


def attend_kernel(*refs):
    (rows_hbm, weight_hbm, cos_hbm, sin_hbm, id_hbm, *pieces) = refs[:13]
    normed_hbm, mixed_hbm, attended_hbm, total_hbm, peak_hbm, outs_hbm = refs[13:19]
    (act, weight, cos_ref, sin_ref, ids, id_col, normed, mixed_ref, attended, value_t, total_ref,
     peak_ref, outs, sems) = refs[19:]
    n = normed.shape[0]
    go = Copies(sems)
    early = [go.start(rows_hbm.at[pl.ds(352 * i, 256)], act.at[pl.ds(256 * i, 256)]) for i in range(4)]
    middle = [
        go.start(weight_hbm.at[pl.ds(128 * p, 128)], weight.at[aligned(place_of(p), 128)])
        for p in range(8)
    ]
    middle += [go.start(cos_hbm, cos_ref), go.start(sin_hbm, sin_ref), go.start(id_hbm, ids)]
    packs = [go.start(piece.at[:, pl.ds(FF2, 256)], outs.at[i]) for i, piece in enumerate(pieces)]
    wait_all(early)

    @pl.loop(0, n // 128)
    def _(i):
        rows = aligned(i, 128)
        normed[rows, :] = layer_norm(act[rows, :].astype(f32)).astype(bf)

    late = [go.start(normed, normed_hbm)]
    wait_all(middle)
    wait_all(packs)
    late.append(go.start(outs, outs_hbm))
    id_col[...] = jnp.broadcast_to(ids[0:1, :], (128, n)).T

    @pl.loop(0, n // 256)
    def _(i):
        rows = aligned(i, 256)
        mixed = dot(normed[rows, :], weight[...], NN)
        cosine = cos_ref[rows, :]
        sine = sin_ref[rows, :]
        queries = turn(mixed[:, 0:256], cosine, sine).astype(bf)
        mixed_ref[rows, 0:256] = (queries.astype(f32) * 0.125).astype(bf)
        mixed_ref[rows, 256:512] = turn(mixed[:, 256:512], cosine, sine).astype(bf)
        value = mixed[:, 512:768]
        mixed_ref[rows, 512:768] = value.astype(bf)
        value_t[:, rows] = value.T.astype(bf)

    late.append(go.start(mixed_ref, mixed_hbm))
    peak_ref[...] = jnp.zeros_like(peak_ref)
    total_ref[...] = jnp.zeros_like(total_ref)

    @pl.loop(0, 2)
    def _(pair):
        lanes = pl.multiple_of(pair * 128, 128)
        lane = lax.broadcasted_iota(jnp.int32, (256, 128), 1)
        best = [None, None]
        for i in range(4):
            width = min(256 * (i + 2), 1024)
            low = 256 * i
            both = mixed_ref[low : low + 256, pl.ds(lanes, 128)]
            keys = mixed_ref[0:width, pl.ds(pl.multiple_of(256 + lanes, 128), 128)]
            values = value_t[pl.ds(lanes, 128), 0:width]
            ok = id_col[low:width, 0:1] <= ids[0:1, low : low + 256]
            outs = []
            for half in range(2):
                q = jnp.where(lane // 64 == half, both, jnp.zeros_like(both))
                s = dot(keys, q, NT)
                tail = jnp.where(ok, s[low:width], MASK_FILL)
                top = jnp.max(tail, axis=0, keepdims=True)
                if i:
                    top = jnp.maximum(top, jnp.max(s[0:low], axis=0, keepdims=True))
                    s = jnp.concatenate([s[0:low], tail], axis=0)
                else:
                    s = tail
                e = jnp.exp(s - top)
                total = jnp.sum(e, axis=0, keepdims=True)
                o = dot(values, e.astype(bf), NN)
                outs.append(o[64 * half : 64 * half + 64] * (1.0 / total))
                total_ref[pl.ds(pair * 2 + half, 1), low : low + 256] = top + jnp.log(total)
                m = jnp.max(top, axis=1, keepdims=True)
                best[half] = m if best[half] is None else jnp.maximum(best[half], m)
            o = jnp.concatenate(outs, axis=0).T.astype(bf)
            attended[low : low + 256, pl.ds(lanes, 128)] = o
        for half in range(2):
            peak_ref[pl.ds(pair * 2 + half, 1), :] = jnp.broadcast_to(best[half], (1, 128))

    late.append(go.start(attended, attended_hbm))
    late.append(go.start(total_ref, total_hbm))
    late.append(go.start(peak_ref, peak_hbm))
    wait_all(late)


def attend(rows_all, weight, cosine, sine, ids, pieces):
    n = cosine.shape[0]
    return call(
        attend_kernel, "attend",
        [((n, 1024), bf), ((n, 768), bf), ((n, 256), bf), ((8, n), f32), ((8, 128), f32),
         ((8, 256, 256), bf)],
        [((n, 1024), bf), ((1024, 768), bf), ((n, 128), f32), ((n, 128), f32), ((8, n), f32),
         ((n, 128), f32), ((n, 1024), bf), ((n, 768), bf), ((n, 256), bf), ((256, n), bf),
         ((8, n), f32), ((8, 128), f32), ((8, 256, 256), bf)],
        [29], 4, (rows_all, weight, cosine, sine, ids, *pieces), 28,
    )


def attend_back_kernel(mixed_hbm, ga_hbm, total_hbm, cos_hbm, sin_hbm, id_hbm, weight_hbm,
                       gm_hbm, gn_hbm,
                       mixed_ref, ga_ref, total_ref, cos_ref, sin_ref, ids, weight,
                       gm_ref, gn_ref, gk_acc, gv_acc, key_t, id_col, sems):
    n = ga_ref.shape[0]
    go = Copies(sems)
    early = [
        go.start(a, b)
        for a, b in ((mixed_hbm, mixed_ref), (ga_hbm, ga_ref), (total_hbm, total_ref),
                     (id_hbm, ids), (cos_hbm, cos_ref), (sin_hbm, sin_ref))
    ]
    late = [
        go.start(weight_hbm.at[pl.ds(128 * p, 128)], weight.at[aligned(place_of(p), 128)])
        for p in range(8)
    ]
    gk_acc[...] = jnp.zeros_like(gk_acc)
    gv_acc[...] = jnp.zeros_like(gv_acc)
    wait_all(early)
    id_col[...] = jnp.broadcast_to(ids[0:1, :], (128, n)).T

    @pl.loop(0, n // 256)
    def _(i):
        rows = aligned(i, 256)
        key_t[:, rows] = mixed_ref[rows, 256:512].astype(f32).T.astype(bf)

    @pl.loop(0, 2)
    def _(pair):
        lanes = pl.multiple_of(pair * 128, 128)
        lane = lax.broadcasted_iota(jnp.int32, (256, 128), 1)
        sub = lax.broadcasted_iota(jnp.int32, (128, 256), 0)
        for i in range(4):
            width = min(256 * (i + 2), 1024)
            low = 256 * i
            k = mixed_ref[0:width, pl.ds(pl.multiple_of(256 + lanes, 128), 128)]
            v = mixed_ref[0:width, pl.ds(pl.multiple_of(512 + lanes, 128), 128)]
            q_all = mixed_ref[low : low + 256, pl.ds(lanes, 128)]
            g_all = ga_ref[low : low + 256, pl.ds(lanes, 128)]
            kt = key_t[pl.ds(lanes, 128), 0:width]
            ok = id_col[low:width, 0:1] <= ids[0:1, low : low + 256]

            def one(half, gq):
                mine = lane // 64 == half
                q = jnp.where(mine, q_all, jnp.zeros_like(q_all))
                g = jnp.where(mine, g_all, jnp.zeros_like(g_all))
                s = dot(k, q, NT) - total_ref[pl.ds(pair * 2 + half, 1), low : low + 256]
                tail = jnp.where(ok, s[low:width], MASK_FILL)
                s = jnp.concatenate([s[0:low], tail], axis=0) if i else tail
                p = jnp.exp(s)
                t = p * dot(v, g, NT)
                delta = jnp.sum(t, axis=0, keepdims=True)
                ds = (t - p * delta).astype(bf)
                gv_acc[0:width, pl.ds(lanes, 128)] += dot(p.astype(bf), g, NN)
                gk_acc[0:width, pl.ds(lanes, 128)] += dot(ds, q, NN)
                return jnp.where(sub // 64 == half, dot(kt, ds, NN), gq)

            gq = one(1, one(0, jnp.zeros((128, 256), f32)))
            gq = gq.T * 0.125
            cosine = cos_ref[low : low + 256, :]
            sine = sin_ref[low : low + 256, :]
            gm_ref[low : low + 256, pl.ds(lanes, 128)] = turn(gq, cosine, -sine).astype(bf)

    wait_all(late)

    @pl.loop(0, n // 256)
    def _(i):
        rows = aligned(i, 256)
        cosine = cos_ref[rows, :]
        sine = sin_ref[rows, :]
        gm_ref[rows, 256:512] = turn(gk_acc[rows, :], cosine, -sine).astype(bf)
        gm_ref[rows, 512:768] = gv_acc[rows, :].astype(bf)
        gn_ref[rows, :] = dot(gm_ref[rows, :], weight[...], NT).astype(bf)
        copy = pltpu.make_async_copy(gn_ref.at[rows], gn_hbm.at[rows], sems.at[14 + i])
        copy.start()

    out = pltpu.make_async_copy(gm_ref, gm_hbm, sems.at[18])
    out.start()
    for i in range(4):
        rows = pl.ds(256 * i, 256)
        pltpu.make_async_copy(gn_ref.at[rows], gn_hbm.at[rows], sems.at[14 + i]).wait()
    out.wait()


def attend_back(mixed, ga, total, cosine, sine, ids, weight):
    n = ga.shape[0]
    return call(
        attend_back_kernel, "attend_back",
        [((n, 768), bf), ((n, 1024), bf)],
        [((n, 768), bf), ((n, 256), bf), ((8, n), f32), ((n, 128), f32), ((n, 128), f32),
         ((8, n), f32), ((1024, 768), bf), ((n, 768), bf), ((n, 1024), bf), ((n, 256), f32),
         ((n, 256), f32), ((256, n), bf), ((n, 128), f32)],
        [19], 0, (mixed, ga, total, cosine, sine, ids, weight), 32,
    )


def weights_kernel(gm_hbm, normed_hbm, okeep_hbm, osend_hbm, keep_hbm, send_hbm,
                   gm_ref, normed_ref, gw, okeep, osend, sems):
    go = Copies(sems)
    first = [go.start(gm_hbm, gm_ref), go.start(normed_hbm, normed_ref)]
    second = [go.start(okeep_hbm, okeep), go.start(osend_hbm, osend)]
    wait_all(first + second)
    cols = pl.ds(768, 1024)
    late = [go.start(okeep, keep_hbm.at[:, cols]), go.start(osend, send_hbm.at[:, cols])]

    @pl.loop(0, 4)
    def _(i):
        cols = aligned(i, 256)
        gw[cols, :] = dot(normed_ref[:, cols], gm_ref[...], TN).astype(bf)

    late += [
        go.start(gw.at[aligned(place_of(p), 128)],
                 (keep_hbm if p < 4 else send_hbm).at[pl.ds(128 * (p % 4), 128), pl.ds(0, 768)])
        for p in range(8)
    ]
    wait_all(late)


def project_weights(gm, normed, okeep, osend):
    n = gm.shape[0]
    return call(
        weights_kernel, "project_weights", [((512, 1792), bf)] * 2,
        [((n, 768), bf), ((n, 1024), bf), ((1024, 768), bf), ((512, 1024), bf), ((512, 1024), bf)],
        [14], 1, (gm, normed, okeep, osend), 24,
    )


def feed_kernel(*refs):
    att_hbm, attp_hbm, act_hbm, actp_hbm, cot_hbm, cotp_hbm = refs[:6]
    a_in, b_in, da_in, db_in, outs = refs[6:10], refs[10:14], refs[14:18], refs[18:22], refs[22]
    part_hbm, gnown_hbm, res_hbm, wo_hbm, h_hbm = refs[23:28]
    ga_keep, ga_send, gb_keep, gb_send = refs[28:32]
    (wg, wu, wd, wo, att, act, n2, n2t, cot, res_ref, gn_acc, part, dg, du, hidden,
     sems, osem, tsem) = refs[32:]
    me = lax.axis_index("dp")
    core = me % 2
    yx = me // 2
    go = Copies(sems)
    small = []
    for base, src, own in ((0, att_hbm, act_hbm), (256, attp_hbm, actp_hbm)):
        rows = pl.ds(base, 256)
        small += [go.start(src.at[i], att.at[rows, pl.ds(256 * i, 256)]) for i in range(4)]
        small.append(go.start(own, act.at[rows]))
    places = []
    for p in range(4):
        (ax, ay), (bx, by) = FLIPS_A[p], FLIPS_B[p]
        places.append((yx ^ (ax + 2 * ay), yx ^ (bx + 2 * by)))
    for p, (ja, jb) in enumerate(places):
        for which, src, j, col in ((0, a_in[p], ja, 0), (1, b_in[p], jb, 512)):
            for half in range(2):
                cols = pl.ds(col + 256 * half, 256)
                rows = pl.ds(128 * half, 128)
                small.append(go.start(src.at[rows, pl.ds(FF2, 256)], wo.at[aligned(j * 2 + core, 128), cols]))
                small.append(go.start(outs.at[4 * which + p, rows], wo.at[aligned(j * 2 + 1 - core, 128), cols]))
    big = []
    for p, (ja, jb) in enumerate(places):
        for src, dst, j in ((a_in[p], wg, ja), (b_in[p], wu, jb)):
            for half, c in ((0, core), (1, 1 - core)):
                big.append(go.start(src.at[pl.ds(128 * half, 128), pl.ds(0, FF2)],
                                    dst.at[aligned(j * 2 + c, 128), pl.ds(0, FF2)]))
    big += [go.start(cot_hbm, cot.at[pl.ds(0, 256)]), go.start(cotp_hbm, cot.at[pl.ds(256, 256)])]
    for p, (ja, jb) in enumerate(places):
        big.append(go.start(da_in[p], wd.at[aligned(ja, 352), pl.ds(0, 512)]))
        big.append(go.start(db_in[p], wd.at[aligned(jb, 352), pl.ds(512, 512)]))
    wg[:, FF2:FFP] = jnp.zeros((1024, FFP - FF2), bf)
    wu[:, FF2:FFP] = jnp.zeros((1024, FFP - FF2), bf)
    wd[FF2:FFP, :] = jnp.zeros((FFP - FF2, 1024), bf)
    gn_acc[...] = jnp.zeros_like(gn_acc)
    wait_all(small)
    ogo = Copies(osem)
    done = [ogo.start(wo, wo_hbm)]

    @pl.loop(0, 2)
    def _(i):
        rows = aligned(i, 256)
        res = act[rows, :].astype(f32) + dot(att[rows, :], wo[...], NN)
        res_ref[rows, :] = res
        n = layer_norm(res)
        n2[rows, :] = n.astype(bf)
        n2t[:, rows] = n.T.astype(bf)

    done.append(ogo.start(res_ref.at[pl.ds(0, 256)], res_hbm))
    wait_all(big)

    def tile_copies(t, width):
        copies = []
        cols = pl.ds(pl.multiple_of(t * 256, 256), width)
        for q in range(4):
            fx, fy = FLIPS_A[q]
            rows = aligned(yx ^ (fx + 2 * fy), 256)
            for k, src, dst, slot in ((0, dg, ga_send if fx else ga_keep, fy), (1, du, gb_send if fy else gb_keep, fx)):
                copies.append(pltpu.make_async_copy(
                    src.at[rows, cols], dst.at[pl.ds(256 * slot, 256), cols], tsem.at[t, 2 * q + k]))
        copies.append(pltpu.make_async_copy(hidden.at[:, cols], h_hbm.at[:, cols], tsem.at[t, 8]))
        return copies

    last = FFP // 256 - 1

    @pl.loop(0, last + 1)
    def _(t):
        cols = aligned(t, 256)
        g = dot(n2[...], wg[:, cols], NN)
        u = dot(n2[...], wu[:, cols], NN)
        gh = dot(cot[...], wd[cols, :], NT)
        sig = 1.0 / (1.0 + jnp.exp(-g))
        silu = g * sig
        hidden[:, cols] = (silu * u).astype(bf)
        gu = (gh * silu).astype(bf)
        gg = (gh * u * (sig + silu * (1.0 - sig))).astype(bf)
        dg[:, cols] = dot(n2t[...], gg, NN).astype(bf)
        du[:, cols] = dot(n2t[...], gu, NN).astype(bf)

        @pl.when(t < last)
        def _():
            for copy in tile_copies(t, 256):
                copy.start()

        gn_acc[...] += dot(gg, wg[:, cols], NT) + dot(gu, wu[:, cols], NT)

    ends = tile_copies(last, FF2 - 256 * last)
    for copy in ends:
        copy.start()
    part[...] = gn_acc[256:512, :].astype(bf)
    done.append(ogo.start(part, part_hbm))
    done.append(ogo.start(gn_acc.at[pl.ds(0, 256)], gnown_hbm))
    for t in range(last):
        wait_all(tile_copies(t, 256))
    wait_all(ends)
    wait_all(done)


def feed(att, attp, act, actp, cot, cotp, a, b, da, db, outs):
    big = [((1024, FFP), bf), ((1024, FFP), bf), ((FFP, 1024), bf)]
    return call(
        feed_kernel, "feed",
        [((256, 1024), bf), ((256, 1024), f32), ((256, 1024), f32), ((1024, 1024), bf), ((512, FF2), bf)]
        + [((512, FF2), bf)] * 4,
        big + [((1024, 1024), bf), ((512, 1024), bf), ((512, 1024), bf), ((512, 1024), bf), ((1024, 512), bf),
               ((512, 1024), bf), ((512, 1024), f32), ((512, 1024), f32), ((256, 1024), bf)]
        + big[:2] + [((512, FFP), bf)],
        [68, 4, (6, 9)], 12, (att, attp, act, actp, cot, cotp, *a, *b, *da, *db, outs), 50,
    )


def finish_kernel(*refs):
    h_hbm, cot_hbm, cotp_hbm, att_hbm, gres_hbm = refs[:5]
    da_in, db_in = refs[5:9], refs[9:13]
    part_hbm, own_hbm, gda_keep, gda_send, gdb_keep, gdb_send, keep_hbm, send_hbm = refs[13:21]
    hidden, cot, att, gres, wd, out, part, dd, gw, sems = refs[21:]
    me = lax.axis_index("dp")
    core = me % 2
    yx = me // 2
    go = Copies(sems)
    first = [go.start(h_hbm, hidden), go.start(cot_hbm, cot.at[pl.ds(0, 256)]),
             go.start(cotp_hbm, cot.at[pl.ds(256, 256)])]
    second = []
    for p in range(4):
        (ax, ay), (bx, by) = FLIPS_A[p], FLIPS_B[p]
        second.append(go.start(da_in[p], wd.at[aligned(yx ^ (ax + 2 * ay), 352), pl.ds(0, 512)]))
        second.append(go.start(db_in[p], wd.at[aligned(yx ^ (bx + 2 * by), 352), pl.ds(512, 512)]))
    third = [go.start(gres_hbm, gres)]
    third += [go.start(att_hbm.at[i], att.at[:, pl.ds(256 * i, 256)]) for i in range(4)]
    wait_all(first)
    done = []

    @pl.loop(0, FF2 // 128)
    def _(t):
        cols = aligned(t, 128)
        dd[cols, :] = dot(hidden[:, cols], cot[...], TN).astype(bf)

    for q in range(4):
        fx, fy = FLIPS_A[q]
        rows = aligned(yx ^ (fx + 2 * fy), 352)
        done.append(go.start(dd.at[rows, pl.ds(0, 512)], (gda_send if fx else gda_keep).at[pl.ds(352 * fy, 352)]))
        done.append(go.start(dd.at[rows, pl.ds(512, 512)], (gdb_send if fy else gdb_keep).at[pl.ds(352 * fx, 352)]))
    wait_all(second)
    part[...] = dot(hidden[256:512, :], wd[...], NN).astype(bf)
    done.append(go.start(part, part_hbm))
    out[...] = dot(hidden[0:256, :], wd[...], NN)
    done.append(go.start(out, own_hbm))
    wait_all(third)
    low = gres[...].astype(bf)

    @pl.loop(0, 4)
    def _(i):
        cols = aligned(i, 256)
        gw[cols, :] = dot(att[:, cols], low, TN).astype(bf)

    for q in range(4):
        fx, fy = FLIPS_A[q]
        j = yx ^ (fx + 2 * fy)
        for dst, c in ((keep_hbm, core), (send_hbm, 1 - core)):
            done.append(go.start(gw.at[aligned(j * 2 + c, 128)], dst.at[pl.ds(128 * (2 * fx + fy), 128)]))
    wait_all(done)


def finish(hidden, cot, cotp, att, gres, da, db):
    tall = ((256, 1024), f32)
    low = ((256, 1024), bf)
    half = ((512, 1024), bf)
    return call(
        finish_kernel, "finish",
        [low, tall] + [((704, 512), bf)] * 4 + [half] * 2,
        [((512, FF2), bf), half, low, tall, ((FF2, 1024), bf), tall, low, ((FF2, 1024), bf), ((1024, 1024), bf)],
        [34], 60, (hidden, cot, cotp, att, gres, *da, *db), 32,
    )


def branch_kernel(part_hbm, gnown_hbm, res_hbm, cot_hbm, wo_hbm, gres_hbm, gatt_hbm,
                  part, gnown, res_ref, cot, wo, gres_ref, gatt, sems):
    go = Copies(sems)
    first = [
        go.start(a, b)
        for a, b in ((res_hbm, res_ref), (gnown_hbm, gnown), (part_hbm, part), (cot_hbm, cot))
    ]
    late = go.start(wo_hbm, wo)
    wait_all(first)
    res = res_ref[...]
    g = gnown[...] + part[...].astype(f32)
    c = res - jnp.mean(res, axis=-1, keepdims=True)
    r = lax.rsqrt(jnp.mean(c * c, axis=-1, keepdims=True) + NORM_EPS)
    xh = c * r
    d = r * (g - jnp.mean(g, axis=-1, keepdims=True) - xh * jnp.mean(g * xh, axis=-1, keepdims=True))
    gres = cot[...].astype(f32) + d
    gres_ref[...] = gres
    low = gres.astype(bf)
    done = [go.start(gres_ref, gres_hbm)]
    late.wait()
    ga = dot(low, wo[...], NT).astype(bf)
    for z in range(4):
        gatt[z] = ga[:, 256 * z : 256 * z + 256]
    done.append(go.start(gatt, gatt_hbm))
    wait_all(done)


def branch(part, gnown, res, cot, wo):
    tall = ((256, 1024), f32)
    low = ((256, 1024), bf)
    return call(
        branch_kernel, "branch", [tall, ((4, 256, 256), bf)],
        [low, tall, tall, low, ((1024, 1024), bf), tall, ((4, 256, 256), bf)],
        [7], 1, (part, gnown, res, cot, wo), 32,
    )


def update_kernel(coeff_ref, wide_ref, mg, mu, md, wg, wu, wd, *refs):
    outs, (gg, gu, gd, ng, nu, nd, og, ou, od), sems = refs[:9], refs[9:18], refs[18]
    coeff = coeff_ref[0]
    go = Copies(sems)
    done = []
    part = FF2 // 4

    def finish(i, grad, moment, weight, new_moment, new_weight):
        done.append(go.start(grad, outs[i]))
        moved = coeff * moment[...] + grad[...]
        new_moment[...] = moved
        done.append(go.start(new_moment, outs[3 + i]))
        new_weight[...] = (weight[...].astype(f32) - LEARN_RATE * moved).astype(bf)
        done.append(go.start(new_weight, outs[6 + i]))

    for i, (grad, moment, weight, nm, nw) in enumerate(((gg, mg, wg, ng, og), (gu, mu, wu, nu, ou))):
        for side in range(2):
            columns = wide_ref[:, FF2 * (2 * side + i) : FF2 * (2 * side + i + 1)].astype(f32)
            for j in range(4):
                low = part * (2 * j + side)
                grad[:, low : low + part] = columns[:, part * j : part * j + part]
        finish(i, grad, moment, weight, nm, nw)
    for j in range(3):
        rows = min(32, 88 - 32 * j)
        low = 4 * FF2 + 1024 * j
        gd[32 * j : 32 * j + rows, :] = wide_ref[:, low : low + 1024].astype(f32)[0:rows]
    finish(2, gd, md, wd, nd, od)
    wait_all(done)


def update(coeff, wide, moments, weights):
    shapes = [(32, 2 * FF2), (32, 2 * FF2), (88, 1024)]
    outs = [(s, f32) for s in shapes] * 2 + [(s, bf) for s in shapes]
    vmem = pl.BlockSpec(memory_space=pltpu.VMEM)
    return pl.pallas_call(
        update_kernel,
        out_shape=tuple(pltpu.HBM(*o) for o in outs),
        in_specs=[pl.BlockSpec(memory_space=pltpu.SMEM)] + [vmem] * 7,
        out_specs=(MAIN,) * 9,
        scratch_shapes=[pltpu.VMEM(*o) for o in outs] + [pltpu.SemaphoreType.DMA((9,))],
        compiler_params=pltpu.CompilerParams(vmem_limit_bytes=16 << 20),
        cost_estimate=pl.CostEstimate(flops=1 << 20, bytes_accessed=6 << 20, transcendentals=0),
        name="update",
    )(coeff, wide, *moments, *weights)


def swap(array, bit):
    return lax.ppermute(array, "dp", [(i, i ^ bit) for i in range(8)])


def shift(array, bits):
    return lax.ppermute(array, "ctx", [(i, i ^ bits) for i in range(4)])


def add_low(left, right):
    return (left.astype(f32) + right.astype(f32)).astype(bf)


def split_even(matrix):
    n = matrix.shape[1] // 8
    parts = [matrix[:, n * i : n * i + n] for i in range(8)]
    return jnp.concatenate(parts[0::2], axis=1), jnp.concatenate(parts[1::2], axis=1)


def tie(value, *anchors):
    return lax.optimization_barrier((value, *anchors))[0]


def fast_device(
    activations,
    block_ids,
    cotangent,
    w_query,
    w_key,
    w_value,
    w_out,
    w_gate,
    w_up,
    w_down,
    m_query,
    m_key,
    m_value,
    m_out,
    m_gate,
    m_up,
    m_down,
    clip_threshold,
    momentum_coeff,
):
    me = lax.axis_index("dp")
    z = lax.axis_index("ctx")
    core = me % 2
    _, span, width = activations.shape
    length = block_ids.shape[1]
    act = activations.reshape(span, width)
    cot = cotangent.reshape(span, width)
    act_other = swap(act, 1)
    cot_other = swap(cot, 1)
    g0, g1 = split_even(w_gate)
    u0, u1 = split_even(w_up)
    even = jnp.stack([g0, u0])
    odd = jnp.stack([g1, u1])
    flip = core == 1
    mine = jnp.where(flip, odd, even)
    other = swap(jnp.where(flip, even, odd), 1)
    out_rows = jnp.stack([w_out[:, :512], w_out[:, 512:]]).reshape(2, 32, 2, 256)
    wide = jnp.stack([mine, other], axis=1)
    wide = jnp.concatenate([wide, out_rows.transpose(0, 2, 1, 3)], axis=3)
    wide = lax.all_gather(wide, "ctx", axis=2, tiled=True).reshape(2, 256, FF2 + 256)
    padded = jnp.concatenate([act, w_down, jnp.zeros((8, width), bf)], axis=0)
    rows_all = lax.all_gather(padded, "ctx", axis=0, tiled=True)
    heads = jnp.stack(
        [
            jnp.concatenate([w[:, 256 * i : 256 * i + 256] for w in (w_query, w_key, w_value)], 1)
            for i in range(4)
        ]
    )
    heads = lax.all_to_all(heads, "ctx", 0, 0, tiled=True).reshape(128, 768)
    hx = swap(heads, 2)
    hy = swap(jnp.concatenate([heads, hx], axis=0), 4)
    four = jnp.concatenate([heads, hy[:128], hx, hy[128:]], axis=0)
    heads_rel = jnp.concatenate([four, swap(four, 1)], axis=0)
    wide, act_other, cot_other = lax.optimization_barrier((wide, act_other, cot_other))

    def spread(own, first, second):
        near = swap(own, first)
        return [own, near, swap(own, second), swap(near, second)]

    piece_a = spread(wide[0], 2, 4)
    piece_b = spread(wide[1], 4, 2)
    down = jnp.concatenate(
        [rows_all[352 * i + 256 : 352 * i + 344] for i in range(4)], axis=0
    )
    piece_da = spread(down[:, :512], 2, 4)
    piece_db = spread(down[:, 512:], 4, 2)
    cosine, sine = rotary_tables(jnp.arange(length, dtype=jnp.int32), HEAD_DIM)
    cosine = jnp.concatenate([cosine] * 4, axis=1)
    sine = jnp.concatenate([-sine, sine, -sine, sine], axis=1)
    ids = jnp.broadcast_to(block_ids, (8, length)).astype(f32)
    pieces = lax.optimization_barrier((rows_all, *piece_a, *piece_b))
    normed, mixed, attended, totals, peaks, outs = attend(
        pieces[0], heads_rel, cosine, sine, ids, pieces[1:]
    )
    piece_a, piece_b = pieces[1:5], pieces[5:]
    outs = swap(outs, 1)
    attended = tie(attended, *piece_da[1:3], *piece_db[1:3])
    attended = lax.all_to_all(attended.reshape(4, span, 256), "ctx", 0, 0, tiled=True)
    attended_other = swap(tie(attended, piece_da[3], piece_db[3]), 1)
    part, back_own, residual, full_out, hidden, ga_keep, ga_send, gb_keep, gb_send = feed(
        attended, attended_other, act, act_other, cot, cot_other,
        piece_a, piece_b, piece_da, piece_db, outs,
    )
    part = swap(part, 1)
    ga_send, gb_send, part = lax.optimization_barrier((ga_send, gb_send, part))
    ga_other = swap(ga_send, 2)
    gb_other = swap(gb_send, 4)
    grad_residual, grad_attended = branch(part, back_own, residual, cot, full_out)
    grad_attended = lax.all_to_all(grad_attended, "ctx", 0, 0, tiled=True).reshape(length, 256)
    (out_part, out_own, gda_keep, gda_send, gdb_keep, gdb_send, go_keep, go_send) = finish(
        hidden, cot, cot_other, attended, grad_residual, piece_da, piece_db
    )
    gda_other = swap(gda_send, 2)
    gdb_other = swap(gdb_send, 4)
    grad_attended, out_part = lax.optimization_barrier((grad_attended, out_part))
    layer_out = (residual + (out_own + swap(out_part, 1).astype(f32))).astype(bf)
    grad_mixed, grad_normed = attend_back(
        mixed, grad_attended, totals, cosine, sine, ids, heads_rel
    )
    grad_mixed = tie(grad_mixed, ga_other, gb_other)
    grad_heads = project_weights(grad_mixed, normed, go_keep, go_send)
    ga_keep, gb_keep, gda_keep, gdb_keep, grad_heads = lax.optimization_barrier(
        (ga_keep, gb_keep, gda_keep, gdb_keep, grad_heads)
    )
    grad_a = add_low(ga_keep, ga_other)
    grad_b = add_low(gb_keep, gb_other)
    grad_da = add_low(gda_keep, gda_other)
    grad_db = add_low(gdb_keep, gdb_other)
    grad_a = add_low(grad_a[:256], swap(grad_a[256:], 4))
    grad_b = add_low(grad_b[:256], swap(grad_b[256:], 2))
    grad_da = add_low(grad_da[:352], swap(grad_da[352:], 4))
    grad_db = add_low(grad_db[:352], swap(grad_db[352:], 2))
    def core_rows(which):
        return jnp.concatenate(
            [lax.dynamic_slice_in_dim(g, which * 128, 128, 0) for g in (grad_a, grad_b)], axis=1
        )

    own_half = core_rows(core)
    other_half = swap(core_rows(1 - core), 1)
    grad_d = jnp.concatenate([grad_da, grad_db], axis=1).reshape(4, 88, width)
    grad_d = jnp.pad(grad_d, ((0, 0), (0, 8), (0, 0))).reshape(4, 3, 32, width)
    grad_d = grad_d.transpose(0, 2, 1, 3).reshape(128, 3 * width)
    grad_wide = jnp.concatenate(
        [
            jnp.where(flip, other_half, own_half),
            jnp.where(flip, own_half, other_half),
            grad_d,
        ],
        axis=1,
    )
    grad_wide = lax.psum_scatter(grad_wide, "ctx", scatter_dimension=0, tiled=True)
    peaks = tie(peaks, ga_other)
    peaks = lax.all_to_all(
        jnp.broadcast_to(peaks[None], (32, 8, 128)), ("dp", "ctx"), 0, 0, tiled=True
    )
    head_peaks = jnp.max(peaks.reshape(8, 4, 8, 128), axis=0)[:, :4, 0].reshape(HEADS)
    grad_normed = lax.psum_scatter(grad_normed, "ctx", scatter_dimension=0, tiled=True)
    tokens_wide = act.astype(f32)
    unused, first_pull = jax.vjp(normalize, tokens_wide)
    input_grad = grad_residual + first_pull(grad_normed.astype(f32))[0]
    grad_heads = add_low(grad_heads[0], swap(grad_heads[1], 1))
    grad_heads = add_low(grad_heads[:256], swap(grad_heads[256:], 2))
    grad_heads = add_low(grad_heads[:128], swap(grad_heads[128:], 4))
    grad_heads = lax.all_to_all(grad_heads.reshape(4, 32, 768 + width), "ctx", 0, 0, tiled=True)
    grad_heads = grad_heads.astype(f32)
    parts = grad_heads[:, :, 768:]
    grad_out = parts[0] + parts[1] + (parts[2] + parts[3])
    grad_qkv = [
        jnp.concatenate([grad_heads[i, :, 256 * k : 256 * k + 256] for i in range(4)], axis=1)
        for k in range(3)
    ]
    big = update(
        momentum_coeff.reshape(1), grad_wide, (m_gate, m_up, m_down), (w_gate, w_up, w_down)
    )
    weight_grads = (*grad_qkv, grad_out)
    moments = (m_query, m_key, m_value, m_out)
    new_moments = tuple(
        (momentum_coeff * moment + gradient for moment, gradient in zip(moments, weight_grads))
    )
    head_scale = jnp.sqrt(clip_threshold / jnp.maximum(head_peaks, clip_threshold))
    column_scale = jnp.repeat(head_scale, HEAD_DIM)
    rates = (LEARN_RATE, LEARN_RATE, LEARN_RATE, OUT_RATE)
    shard_list = (w_query, w_key, w_value, w_out)
    updated = [
        matrix.astype(jnp.float32) - rate * moment
        for matrix, moment, rate in zip(shard_list, new_moments, rates)
    ]
    updated[0] = updated[0] * column_scale[None, :]
    updated[1] = updated[1] * column_scale[None, :]
    updated = [matrix.astype(bf) for matrix in updated]
    return (
        layer_out[None],
        input_grad[None],
        *weight_grads,
        *big[:3],
        *new_moments,
        *big[3:6],
        *updated,
        *big[6:],
        head_peaks,
        head_scale,
    )


def solution(mesh):
    placed = (
        P("dp", "ctx", None),
        P("dp", None),
        P("dp", "ctx", None),
        P(("dp", "ctx"), None),
        P(("dp", "ctx"), None),
        P(("dp", "ctx"), None),
        P(("dp", "ctx"), None),
        P(("dp", "ctx"), None),
        P(("dp", "ctx"), None),
        P(("dp", "ctx"), None),
        P(("dp", "ctx"), None),
        P(("dp", "ctx"), None),
        P(("dp", "ctx"), None),
        P(("dp", "ctx"), None),
        P(("dp", "ctx"), None),
        P(("dp", "ctx"), None),
        P(("dp", "ctx"), None),
        P(),
        P(),
    )
    fits = mesh.shape["dp"] == 8 and mesh.shape["ctx"] == 4
    return jax.shard_map(
        fast_device if fits else per_device,
        mesh=mesh,
        in_specs=placed,
        out_specs=(
            P("dp", "ctx", None),
            P("dp", "ctx", None),
            P(("dp", "ctx"), None),
            P(("dp", "ctx"), None),
            P(("dp", "ctx"), None),
            P(("dp", "ctx"), None),
            P(("dp", "ctx"), None),
            P(("dp", "ctx"), None),
            P(("dp", "ctx"), None),
            P(("dp", "ctx"), None),
            P(("dp", "ctx"), None),
            P(("dp", "ctx"), None),
            P(("dp", "ctx"), None),
            P(("dp", "ctx"), None),
            P(("dp", "ctx"), None),
            P(("dp", "ctx"), None),
            P(("dp", "ctx"), None),
            P(("dp", "ctx"), None),
            P(("dp", "ctx"), None),
            P(("dp", "ctx"), None),
            P(("dp", "ctx"), None),
            P(("dp", "ctx"), None),
            P(("dp", "ctx"), None),
            P(),
            P(),
        ),
        check_vma=False,
    )
```

```python
import math

import jax
import jax.numpy as jnp
from jax import lax
from jax.experimental import pallas as pl
from jax.experimental.pallas import tpu as pltpu
from jax.sharding import PartitionSpec as P

HEADS = 16
HEAD_DIM = 64


NORM_EPS = 1e-05
ROPE_BASE = 10000.0
LEARN_RATE = 0.0001
OUT_RATE = 0.0016
MASK_FILL = -1e30


def normalize(values):
    centred = values - jnp.mean(values, axis=-1, keepdims=True)
    spread = jnp.mean(centred * centred, axis=-1, keepdims=True)
    return centred * lax.rsqrt(spread + NORM_EPS)


def rotary_tables(positions, head_width):
    half_width = head_width // 2
    frequency = ROPE_BASE ** (-(jnp.arange(half_width, dtype=jnp.float32) * 2.0 / head_width))
    angles = positions.astype(jnp.float32)[:, None] * frequency[None, :]
    return (jnp.cos(angles), jnp.sin(angles))


def rotate(vectors, cosine, sine_table):
    half_width = vectors.shape[-1] // 2
    first_half = vectors[..., :half_width]
    second = vectors[..., half_width:]
    cos_wide = cosine[:, None, :]
    sin_wide = sine_table[:, None, :]
    return jnp.concatenate(
        [first_half * cos_wide - second * sin_wide, second * cos_wide + first_half * sin_wide],
        axis=-1,
    )


def swiglu(gate_proj, up_proj):
    return jax.nn.silu(gate_proj) * up_proj


def project(left_rows, matrix):
    return jnp.dot(left_rows, matrix, preferred_element_type=jnp.float32)


def project_back(grad_rows, matrix):
    return lax.dot_general(
        grad_rows, matrix, (((1,), (1,)), ((), ())), preferred_element_type=jnp.float32
    )


def shard_gradient(left_rows, right_rows):
    return lax.psum_scatter(
        lax.dot_general(
            left_rows, right_rows, (((0,), (0,)), ((), ())), preferred_element_type=jnp.float32
        ),
        ("dp", "ctx"),
        scatter_dimension=0,
        tiled=True,
    )


def per_device(
    activations,
    block_ids,
    cotangent,
    w_query,
    w_key,
    w_value,
    w_out,
    w_gate,
    w_up,
    w_down,
    m_query,
    m_key,
    m_value,
    m_out,
    m_gate,
    m_up,
    m_down,
    clip_threshold,
    momentum_coeff,
):
    shard_list = (w_query, w_key, w_value, w_out, w_gate, w_up, w_down)
    gathered = (
        lax.all_gather(shard_list[0], ("dp", "ctx"), axis=0, tiled=True),
        lax.all_gather(shard_list[1], ("dp", "ctx"), axis=0, tiled=True),
        lax.all_gather(shard_list[2], ("dp", "ctx"), axis=0, tiled=True),
        lax.all_gather(shard_list[3], ("dp", "ctx"), axis=0, tiled=True),
        lax.all_gather(shard_list[4], ("dp", "ctx"), axis=0, tiled=True),
        lax.all_gather(shard_list[5], ("dp", "ctx"), axis=0, tiled=True),
        lax.all_gather(shard_list[6], ("dp", "ctx"), axis=0, tiled=True),
    )
    full_query, full_key, full_value, full_out, full_gate, full_up, full_down = gathered
    seq_count, span_len, model_width = activations.shape
    ctx_place = lax.axis_index("ctx")
    positions = ctx_place * span_len + jnp.arange(span_len, dtype=jnp.int32)
    cosine, sine_table = rotary_tables(positions, HEAD_DIM)
    score_scale = 1.0 / math.sqrt(HEAD_DIM)

    def split_heads(matrix):
        return matrix.reshape(seq_count, span_len, HEADS, HEAD_DIM)

    tokens_flat = activations.astype(jnp.float32).reshape(-1, model_width)
    normed = normalize(tokens_flat).astype(jnp.bfloat16)
    queries = rotate(split_heads(project(normed, full_query)), cosine, sine_table).astype(
        jnp.bfloat16
    )
    key_rot = rotate(split_heads(project(normed, full_key)), cosine, sine_table).astype(
        jnp.bfloat16
    )
    value_rot = split_heads(project(normed, full_value)).astype(jnp.bfloat16)
    key_all, value_all = (
        lax.all_gather(key_rot, "ctx", axis=1, tiled=True),
        lax.all_gather(value_rot, "ctx", axis=1, tiled=True),
    )
    query_ids = lax.dynamic_slice_in_dim(block_ids, ctx_place * span_len, span_len, 1)
    allowed = (block_ids[:, None, :] <= query_ids[:, :, None])[:, None]

    def masked_scores():
        scores = (
            jnp.einsum("sqhd,skhd->shqk", queries, key_all, preferred_element_type=jnp.float32)
            * score_scale
        )
        return jnp.where(allowed, scores, MASK_FILL)

    masked = masked_scores()
    local_peaks = jnp.max(masked, axis=(0, 2, 3))
    row_top = jnp.max(masked, axis=-1, keepdims=True)
    log_total = row_top + jnp.log(jnp.sum(jnp.exp(masked - row_top), axis=-1, keepdims=True))
    probs_low = jnp.exp(masked - log_total).astype(jnp.bfloat16)
    attended = jnp.einsum(
        "shqk,skhd->sqhd", probs_low, value_all, preferred_element_type=jnp.float32
    )
    attended_low = attended.reshape(-1, model_width).astype(jnp.bfloat16)
    head_peaks = lax.pmax(local_peaks, ("dp", "ctx"))
    residual = tokens_flat + project(attended_low, full_out)
    normed2 = normalize(residual).astype(jnp.bfloat16)
    gate_proj = project(normed2, full_gate)
    up_proj = project(normed2, full_up)
    hidden_low = swiglu(gate_proj, up_proj).astype(jnp.bfloat16)
    layer_out = (
        (residual + project(hidden_low, full_down))
        .astype(jnp.bfloat16)
        .reshape(seq_count, span_len, model_width)
    )
    back_weights = (
        lax.all_gather(shard_list[0], ("dp", "ctx"), axis=0, tiled=True),
        lax.all_gather(shard_list[1], ("dp", "ctx"), axis=0, tiled=True),
        lax.all_gather(shard_list[2], ("dp", "ctx"), axis=0, tiled=True),
        lax.all_gather(shard_list[3], ("dp", "ctx"), axis=0, tiled=True),
        lax.all_gather(shard_list[4], ("dp", "ctx"), axis=0, tiled=True),
        lax.all_gather(shard_list[5], ("dp", "ctx"), axis=0, tiled=True),
        lax.all_gather(shard_list[6], ("dp", "ctx"), axis=0, tiled=True),
    )
    back_query, back_key, back_value, back_out, back_gate, back_up, back_down = back_weights
    grad_rows = cotangent.reshape(-1, model_width)
    grad_hidden = project_back(grad_rows, back_down)
    unused, gate_pull = jax.vjp(swiglu, gate_proj, up_proj)
    grad_gate_wide, grad_up_wide = gate_pull(grad_hidden)
    grad_gate_low = grad_gate_wide.astype(jnp.bfloat16)
    grad_up_low = grad_up_wide.astype(jnp.bfloat16)
    grad_normed2 = project_back(grad_gate_low, back_gate) + project_back(grad_up_low, back_up)
    unused, second_pull = jax.vjp(normalize, residual)
    grad_residual = grad_rows.astype(jnp.float32) + second_pull(grad_normed2)[0]
    grad_branch = grad_residual.astype(jnp.bfloat16)
    grad_attended = split_heads(project_back(grad_branch, back_out).astype(jnp.bfloat16))
    masked = masked_scores()
    probs = jnp.exp(masked - log_total)
    probs_again = probs.astype(jnp.bfloat16)
    grad_values_all = jnp.einsum(
        "shqk,sqhd->skhd", probs_again, grad_attended, preferred_element_type=jnp.float32
    )
    grad_probs = jnp.einsum(
        "sqhd,skhd->shqk", grad_attended, value_all, preferred_element_type=jnp.float32
    )
    score_grad = (
        probs * (grad_probs - jnp.sum(probs * grad_probs, axis=-1, keepdims=True))
    ).astype(jnp.bfloat16)
    grad_queries = (
        jnp.einsum("shqk,skhd->sqhd", score_grad, key_all, preferred_element_type=jnp.float32)
        * score_scale
    )
    grad_keys_all = (
        jnp.einsum("shqk,sqhd->skhd", score_grad, queries, preferred_element_type=jnp.float32)
        * score_scale
    )
    grad_keys, grad_values = (
        lax.psum_scatter(
            grad_keys_all.astype(jnp.bfloat16), "ctx", scatter_dimension=1, tiled=True
        ).astype(jnp.float32),
        lax.psum_scatter(
            grad_values_all.astype(jnp.bfloat16), "ctx", scatter_dimension=1, tiled=True
        ).astype(jnp.float32),
    )
    grad_query_low = (
        rotate(grad_queries, cosine, -sine_table).reshape(-1, model_width).astype(jnp.bfloat16)
    )
    grad_key_low = (
        rotate(grad_keys, cosine, -sine_table).reshape(-1, model_width).astype(jnp.bfloat16)
    )
    grad_value_low = grad_values.reshape(-1, model_width).astype(jnp.bfloat16)
    grad_normed = (
        project_back(grad_query_low, back_query)
        + project_back(grad_key_low, back_key)
        + project_back(grad_value_low, back_value)
    )
    unused, first_pull = jax.vjp(normalize, tokens_flat)
    input_grad = (grad_residual + first_pull(grad_normed)[0]).reshape(
        seq_count, span_len, model_width
    )
    weight_grads = (
        shard_gradient(normed, grad_query_low),
        shard_gradient(normed, grad_key_low),
        shard_gradient(normed, grad_value_low),
        shard_gradient(attended_low, grad_branch),
        shard_gradient(normed2, grad_gate_low),
        shard_gradient(normed2, grad_up_low),
        shard_gradient(hidden_low, grad_rows),
    )
    moments = (m_query, m_key, m_value, m_out, m_gate, m_up, m_down)
    new_moments = tuple(
        (momentum_coeff * moment + gradient for moment, gradient in zip(moments, weight_grads))
    )
    head_scale = jnp.sqrt(clip_threshold / jnp.maximum(head_peaks, clip_threshold))
    column_scale = jnp.repeat(head_scale, HEAD_DIM)
    rates = (LEARN_RATE, LEARN_RATE, LEARN_RATE, OUT_RATE, LEARN_RATE, LEARN_RATE, LEARN_RATE)
    updated = [
        matrix.astype(jnp.float32) - rate * moment
        for matrix, moment, rate in zip(shard_list, new_moments, rates)
    ]
    updated[0] = updated[0] * column_scale[None, :]
    updated[1] = updated[1] * column_scale[None, :]
    updated = [matrix.astype(jnp.bfloat16) for matrix in updated]
    return (
        layer_out,
        input_grad,
        weight_grads[0],
        weight_grads[1],
        weight_grads[2],
        weight_grads[3],
        weight_grads[4],
        weight_grads[5],
        weight_grads[6],
        new_moments[0],
        new_moments[1],
        new_moments[2],
        new_moments[3],
        new_moments[4],
        new_moments[5],
        new_moments[6],
        updated[0],
        updated[1],
        updated[2],
        updated[3],
        updated[4],
        updated[5],
        updated[6],
        head_peaks,
        head_scale,
    )


f32=jnp.float32; bf=jnp.bfloat16
NT=(((1,),(1,)),((),())); TN=(((0,),(0,)),((),())); NN=(((1,),(0,)),((),()))
FF2=1408
FFP=1536
FLIPS_A=((0,0),(1,0),(0,1),(1,1))
FLIPS_B=((0,0),(0,1),(1,0),(1,1))
MAIN=pl.BlockSpec(memory_space=pltpu.HBM)
S=jax.ShapeDtypeStruct


def dot(a, b, dims):
    return lax.dot_general(a, b, dims, preferred_element_type=f32)


def aligned(i, m):
    return pl.ds(pl.multiple_of(i * m, m), m)


class Copies:
    def __init__(self, sems):
        self.sems = sems
        self.count = 0

    def start(self, source, target):
        copy = pltpu.make_async_copy(source, target, self.sems.at[self.count])
        self.count += 1
        copy.start()
        return copy


def wait_all(copies):
    for copy in copies:
        copy.wait()


def call(kernel, name, outs, scratch, sems, flops, args, limit):
    return pl.pallas_call(
        kernel,
        out_shape=tuple(pltpu.HBM(*o) for o in outs),
        in_specs=[MAIN] * len(args),
        out_specs=(MAIN,) * len(outs),
        scratch_shapes=[pltpu.VMEM(*s) for s in scratch] + [pltpu.SemaphoreType.DMA(n if isinstance(n, tuple) else (n,)) for n in sems],
        compiler_params=pltpu.CompilerParams(vmem_limit_bytes=limit << 20),
        cost_estimate=pl.CostEstimate(flops=flops << 30, bytes_accessed=8 << 20, transcendentals=0),
        name=name,
    )(*(pltpu.with_memory_space_constraint(arg, pltpu.HBM) for arg in args))


def place_of(p):
    return lax.axis_index("dp") ^ ((p >> 2 & 1) | (p >> 1 & 1) << 1 | (p & 1) << 2)


def turn(values, cosine, signed_sine):
    lane = lax.broadcasted_iota(jnp.int32, cosine.shape, 1)
    first = lane % 64 < 32
    parts = []
    for j in range(values.shape[1] // 128):
        part = values[:, 128 * j : 128 * j + 128]
        partner = jnp.where(first, pltpu.roll(part, 96, 1), pltpu.roll(part, 32, 1))
        parts.append(part * cosine + partner * signed_sine)
    return jnp.concatenate(parts, axis=1)


def layer_norm(x):
    c = x - jnp.mean(x, axis=-1, keepdims=True)
    v = jnp.mean(c * c, axis=-1, keepdims=True)
    return c * lax.rsqrt(v + NORM_EPS)


def attend_kernel(*refs):
    (rows_hbm, weight_hbm, cos_hbm, sin_hbm, id_hbm, *pieces) = refs[:13]
    normed_hbm, mixed_hbm, attended_hbm, total_hbm, peak_hbm, outs_hbm = refs[13:19]
    (act, weight, cos_ref, sin_ref, ids, id_col, normed, mixed_ref, attended, value_t, total_ref,
     peak_ref, outs, sems) = refs[19:]
    n = normed.shape[0]
    go = Copies(sems)
    early = [go.start(rows_hbm.at[pl.ds(344 * i, 256)], act.at[pl.ds(256 * i, 256)]) for i in range(4)]
    middle = [
        go.start(weight_hbm.at[pl.ds(128 * p, 128)], weight.at[aligned(place_of(p), 128)])
        for p in range(8)
    ]
    middle += [go.start(cos_hbm, cos_ref), go.start(sin_hbm, sin_ref), go.start(id_hbm, ids)]
    packs = [go.start(piece.at[:, pl.ds(FF2, 256)], outs.at[i]) for i, piece in enumerate(pieces)]
    wait_all(early)

    def norm(i):
        rows = aligned(i, 256)
        normed[rows, :] = layer_norm(act[rows, :].astype(f32)).astype(bf)

    def mix(i):
        rows = aligned(i, 256)
        mixed = dot(normed[rows, :], weight[...], NN)
        cosine = cos_ref[rows, :]
        sine = sin_ref[rows, :]
        queries = turn(mixed[:, 0:256], cosine, sine).astype(bf)
        mixed_ref[rows, 0:256] = (queries.astype(f32) * 0.125).astype(bf)
        mixed_ref[rows, 256:512] = turn(mixed[:, 256:512], cosine, sine).astype(bf)
        value = mixed[:, 512:768]
        mixed_ref[rows, 512:768] = value.astype(bf)
        value_t[:, rows] = value.T.astype(bf)

    norm(0)
    wait_all(middle)
    wait_all(packs)
    id_col[...] = jnp.broadcast_to(ids[0:1, :], (128, n)).T

    @pl.loop(0, n // 256 - 1)
    def _(i):
        mix(i)
        norm(i + 1)

    mix(n // 256 - 1)
    late = [go.start(normed, normed_hbm), go.start(outs, outs_hbm)]
    late.append(go.start(mixed_ref, mixed_hbm))
    peak_ref[...] = jnp.zeros_like(peak_ref)
    total_ref[...] = jnp.zeros_like(total_ref)

    @pl.loop(0, 2)
    def _(pair):
        lanes = pl.multiple_of(pair * 128, 128)
        lane = lax.broadcasted_iota(jnp.int32, (256, 128), 1)
        best = [None, None]
        for i in range(4):
            width = min(256 * (i + 2), 1024)
            low = 256 * i
            both = mixed_ref[low : low + 256, pl.ds(lanes, 128)]
            keys = mixed_ref[0:width, pl.ds(pl.multiple_of(256 + lanes, 128), 128)]
            values = value_t[pl.ds(lanes, 128), 0:width]
            ok = id_col[low:width, 0:1] <= ids[0:1, low : low + 256]
            outs = []
            for half in range(2):
                q = jnp.where(lane // 64 == half, both, jnp.zeros_like(both))
                s = dot(keys, q, NT)
                tail = jnp.where(ok, s[low:width], MASK_FILL)
                top = jnp.max(tail, axis=0, keepdims=True)
                if i:
                    top = jnp.maximum(top, jnp.max(s[0:low], axis=0, keepdims=True))
                    s = jnp.concatenate([s[0:low], tail], axis=0)
                else:
                    s = tail
                e = jnp.exp(s - top)
                total = jnp.sum(e, axis=0, keepdims=True)
                o = dot(values, e.astype(bf), NN)
                outs.append(o[64 * half : 64 * half + 64] * (1.0 / total))
                total_ref[pl.ds(pair * 2 + half, 1), low : low + 256] = top + jnp.log(total)
                m = jnp.max(top, axis=1, keepdims=True)
                best[half] = m if best[half] is None else jnp.maximum(best[half], m)
            o = jnp.concatenate(outs, axis=0).T.astype(bf)
            attended[low : low + 256, pl.ds(lanes, 128)] = o
        for half in range(2):
            peak_ref[pl.ds(pair * 2 + half, 1), :] = jnp.broadcast_to(best[half], (1, 128))

    late.append(go.start(attended, attended_hbm))
    late.append(go.start(total_ref, total_hbm))
    late.append(go.start(peak_ref, peak_hbm))
    wait_all(late)


def attend(rows_all, weight, cosine, sine, ids, pieces):
    n = cosine.shape[0]
    return call(
        attend_kernel, "attend",
        [((n, 1024), bf), ((n, 768), bf), ((n, 256), bf), ((8, n), f32), ((8, 128), f32),
         ((8, 256, 256), bf)],
        [((n, 1024), bf), ((1024, 768), bf), ((n, 128), f32), ((n, 128), f32), ((8, n), f32),
         ((n, 128), f32), ((n, 1024), bf), ((n, 768), bf), ((n, 256), bf), ((256, n), bf),
         ((8, n), f32), ((8, 128), f32), ((8, 256, 256), bf)],
        [29], 4, (rows_all, weight, cosine, sine, ids, *pieces), 28,
    )


def attend_back_kernel(mixed_hbm, ga_hbm, total_hbm, cos_hbm, sin_hbm, id_hbm, weight_hbm,
                       gm_hbm, gn_hbm,
                       mixed_ref, ga_ref, total_ref, cos_ref, sin_ref, ids, weight,
                       gm_ref, gn_ref, gk_acc, gv_acc, key_t, id_col, sems):
    n = ga_ref.shape[0]
    go = Copies(sems)
    early = [
        go.start(a, b)
        for a, b in ((mixed_hbm, mixed_ref), (ga_hbm, ga_ref), (total_hbm, total_ref),
                     (id_hbm, ids), (cos_hbm, cos_ref), (sin_hbm, sin_ref))
    ]
    late = [
        go.start(weight_hbm.at[pl.ds(128 * p, 128)], weight.at[aligned(place_of(p), 128)])
        for p in range(8)
    ]
    gk_acc[...] = jnp.zeros_like(gk_acc)
    gv_acc[...] = jnp.zeros_like(gv_acc)
    wait_all(early)
    id_col[...] = jnp.broadcast_to(ids[0:1, :], (128, n)).T

    @pl.loop(0, n // 256)
    def _(i):
        rows = aligned(i, 256)
        key_t[:, rows] = mixed_ref[rows, 256:512].astype(f32).T.astype(bf)

    @pl.loop(0, 2)
    def _(pair):
        lanes = pl.multiple_of(pair * 128, 128)
        lane = lax.broadcasted_iota(jnp.int32, (256, 128), 1)
        sub = lax.broadcasted_iota(jnp.int32, (128, 256), 0)
        for i in range(4):
            width = min(256 * (i + 2), 1024)
            low = 256 * i
            k = mixed_ref[0:width, pl.ds(pl.multiple_of(256 + lanes, 128), 128)]
            v = mixed_ref[0:width, pl.ds(pl.multiple_of(512 + lanes, 128), 128)]
            q_all = mixed_ref[low : low + 256, pl.ds(lanes, 128)]
            g_all = ga_ref[low : low + 256, pl.ds(lanes, 128)]
            kt = key_t[pl.ds(lanes, 128), 0:width]
            ok = id_col[low:width, 0:1] <= ids[0:1, low : low + 256]

            def one(half, gq):
                mine = lane // 64 == half
                q = jnp.where(mine, q_all, jnp.zeros_like(q_all))
                g = jnp.where(mine, g_all, jnp.zeros_like(g_all))
                s = dot(k, q, NT) - total_ref[pl.ds(pair * 2 + half, 1), low : low + 256]
                tail = jnp.where(ok, s[low:width], MASK_FILL)
                s = jnp.concatenate([s[0:low], tail], axis=0) if i else tail
                p = jnp.exp(s)
                t = p * dot(v, g, NT)
                delta = jnp.sum(t, axis=0, keepdims=True)
                ds = (t - p * delta).astype(bf)
                gv_acc[0:width, pl.ds(lanes, 128)] += dot(p.astype(bf), g, NN)
                gk_acc[0:width, pl.ds(lanes, 128)] += dot(ds, q, NN)
                return jnp.where(sub // 64 == half, dot(kt, ds, NN), gq)

            gq = one(1, one(0, jnp.zeros((128, 256), f32)))
            gq = gq.T * 0.125
            cosine = cos_ref[low : low + 256, :]
            sine = sin_ref[low : low + 256, :]
            gm_ref[low : low + 256, pl.ds(lanes, 128)] = turn(gq, cosine, -sine).astype(bf)

    wait_all(late)

    @pl.loop(0, n // 256)
    def _(i):
        rows = aligned(i, 256)
        cosine = cos_ref[rows, :]
        sine = sin_ref[rows, :]
        gm_ref[rows, 256:512] = turn(gk_acc[rows, :], cosine, -sine).astype(bf)
        gm_ref[rows, 512:768] = gv_acc[rows, :].astype(bf)
        gn_ref[rows, :] = dot(gm_ref[rows, :], weight[...], NT).astype(bf)
        copy = pltpu.make_async_copy(gn_ref.at[rows], gn_hbm.at[rows], sems.at[14 + i])
        copy.start()

    out = pltpu.make_async_copy(gm_ref, gm_hbm, sems.at[18])
    out.start()
    for i in range(4):
        rows = pl.ds(256 * i, 256)
        pltpu.make_async_copy(gn_ref.at[rows], gn_hbm.at[rows], sems.at[14 + i]).wait()
    out.wait()


def attend_back(mixed, ga, total, cosine, sine, ids, weight):
    n = ga.shape[0]
    return call(
        attend_back_kernel, "attend_back",
        [((n, 768), bf), ((n, 1024), bf)],
        [((n, 768), bf), ((n, 256), bf), ((8, n), f32), ((n, 128), f32), ((n, 128), f32),
         ((8, n), f32), ((1024, 768), bf), ((n, 768), bf), ((n, 1024), bf), ((n, 256), f32),
         ((n, 256), f32), ((256, n), bf), ((n, 128), f32)],
        [19], 0, (mixed, ga, total, cosine, sine, ids, weight), 32,
    )


def weights_kernel(gm_hbm, normed_hbm, okeep_hbm, osend_hbm, keep_hbm, send_hbm,
                   gm_ref, normed_ref, gw, okeep, osend, sems):
    go = Copies(sems)
    first = [go.start(gm_hbm, gm_ref), go.start(normed_hbm, normed_ref)]
    second = [go.start(okeep_hbm, okeep), go.start(osend_hbm, osend)]
    wait_all(first + second)
    cols = pl.ds(768, 1024)
    late = [go.start(okeep, keep_hbm.at[:, cols]), go.start(osend, send_hbm.at[:, cols])]

    @pl.loop(0, 4)
    def _(i):
        cols = aligned(i, 256)
        gw[cols, :] = dot(normed_ref[:, cols], gm_ref[...], TN).astype(bf)

    late += [
        go.start(gw.at[aligned(place_of(p), 128)],
                 (keep_hbm if p < 4 else send_hbm).at[pl.ds(128 * (p % 4), 128), pl.ds(0, 768)])
        for p in range(8)
    ]
    wait_all(late)


def project_weights(gm, normed, okeep, osend):
    n = gm.shape[0]
    return call(
        weights_kernel, "project_weights", [((512, 1792), bf)] * 2,
        [((n, 768), bf), ((n, 1024), bf), ((1024, 768), bf), ((512, 1024), bf), ((512, 1024), bf)],
        [14], 1, (gm, normed, okeep, osend), 24,
    )


def feed_kernel(*refs):
    att_hbm, attp_hbm, act_hbm, actp_hbm, cot_hbm, cotp_hbm = refs[:6]
    a_in, b_in, da_in, db_in, outs = refs[6:10], refs[10:14], refs[14:18], refs[18:22], refs[22]
    part_hbm, gnown_hbm, res_hbm, wo_hbm, h_hbm = refs[23:28]
    ga_keep, ga_send, gb_keep, gb_send = refs[28:32]
    (wg, wu, wd, wo, att, act, n2, n2t, cot, res_ref, gn_acc, part, dg, du, hidden,
     sems, osem, tsem) = refs[32:]
    me = lax.axis_index("dp")
    core = me % 2
    yx = me // 2
    go = Copies(sems)
    small = []
    for base, src, own in ((0, att_hbm, act_hbm), (256, attp_hbm, actp_hbm)):
        rows = pl.ds(base, 256)
        small += [go.start(src.at[i], att.at[rows, pl.ds(256 * i, 256)]) for i in range(4)]
        small.append(go.start(own, act.at[rows]))
    places = []
    for p in range(4):
        (ax, ay), (bx, by) = FLIPS_A[p], FLIPS_B[p]
        places.append((yx ^ (ax + 2 * ay), yx ^ (bx + 2 * by)))
    for p, (ja, jb) in enumerate(places):
        for which, src, j, col in ((0, a_in[p], ja, 0), (1, b_in[p], jb, 512)):
            for half in range(2):
                cols = pl.ds(col + 256 * half, 256)
                rows = pl.ds(128 * half, 128)
                small.append(go.start(src.at[rows, pl.ds(FF2, 256)], wo.at[aligned(j * 2 + core, 128), cols]))
                small.append(go.start(outs.at[4 * which + p, rows], wo.at[aligned(j * 2 + 1 - core, 128), cols]))
    big = []
    for p, (ja, jb) in enumerate(places):
        for src, dst, j in ((a_in[p], wg, ja), (b_in[p], wu, jb)):
            for half, c in ((0, core), (1, 1 - core)):
                big.append(go.start(src.at[pl.ds(128 * half, 128), pl.ds(0, FF2)],
                                    dst.at[aligned(j * 2 + c, 128), pl.ds(0, FF2)]))
    big += [go.start(cot_hbm, cot.at[pl.ds(0, 256)]), go.start(cotp_hbm, cot.at[pl.ds(256, 256)])]
    for p, (ja, jb) in enumerate(places):
        big.append(go.start(da_in[p], wd.at[aligned(ja, 352), pl.ds(0, 512)]))
        big.append(go.start(db_in[p], wd.at[aligned(jb, 352), pl.ds(512, 512)]))
    wg[:, FF2:FFP] = jnp.zeros((1024, FFP - FF2), bf)
    wu[:, FF2:FFP] = jnp.zeros((1024, FFP - FF2), bf)
    wd[FF2:FFP, :] = jnp.zeros((FFP - FF2, 1024), bf)
    gn_acc[...] = jnp.zeros_like(gn_acc)
    wait_all(small)
    ogo = Copies(osem)
    done = [ogo.start(wo, wo_hbm)]

    @pl.loop(0, 2)
    def _(i):
        rows = aligned(i, 256)
        res = act[rows, :].astype(f32) + dot(att[rows, :], wo[...], NN)
        res_ref[rows, :] = res
        n = layer_norm(res)
        n2[rows, :] = n.astype(bf)
        n2t[:, rows] = n.T.astype(bf)

    done.append(ogo.start(res_ref.at[pl.ds(0, 256)], res_hbm))
    wait_all(big)

    def tile_copies(t, width):
        copies = []
        cols = pl.ds(pl.multiple_of(t * 256, 256), width)
        for q in range(4):
            fx, fy = FLIPS_A[q]
            rows = aligned(yx ^ (fx + 2 * fy), 256)
            for k, src, dst, slot in ((0, dg, ga_send if fx else ga_keep, fy), (1, du, gb_send if fy else gb_keep, fx)):
                copies.append(pltpu.make_async_copy(
                    src.at[rows, cols], dst.at[pl.ds(256 * slot, 256), cols], tsem.at[t, 2 * q + k]))
        copies.append(pltpu.make_async_copy(hidden.at[:, cols], h_hbm.at[:, cols], tsem.at[t, 8]))
        return copies

    last = FFP // 256 - 1

    @pl.loop(0, last + 1)
    def _(t):
        cols = aligned(t, 256)
        g = dot(n2[...], wg[:, cols], NN)
        u = dot(n2[...], wu[:, cols], NN)
        gh = dot(cot[...], wd[cols, :], NT)
        sig = 1.0 / (1.0 + jnp.exp(-g))
        silu = g * sig
        hidden[:, cols] = (silu * u).astype(bf)
        gu = (gh * silu).astype(bf)
        gg = (gh * u * (sig + silu * (1.0 - sig))).astype(bf)
        dg[:, cols] = dot(n2t[...], gg, NN).astype(bf)
        du[:, cols] = dot(n2t[...], gu, NN).astype(bf)

        @pl.when(t < last)
        def _():
            for copy in tile_copies(t, 256):
                copy.start()

        gn_acc[...] += dot(gg, wg[:, cols], NT) + dot(gu, wu[:, cols], NT)

    ends = tile_copies(last, FF2 - 256 * last)
    for copy in ends:
        copy.start()
    part[...] = gn_acc[256:512, :].astype(bf)
    done.append(ogo.start(part, part_hbm))
    done.append(ogo.start(gn_acc.at[pl.ds(0, 256)], gnown_hbm))
    for t in range(last):
        wait_all(tile_copies(t, 256))
    wait_all(ends)
    wait_all(done)


def feed(att, attp, act, actp, cot, cotp, a, b, da, db, outs):
    big = [((1024, FFP), bf), ((1024, FFP), bf), ((FFP, 1024), bf)]
    return call(
        feed_kernel, "feed",
        [((256, 1024), bf), ((256, 1024), f32), ((256, 1024), f32), ((1024, 1024), bf), ((512, FF2), bf)]
        + [((512, FF2), bf)] * 4,
        big + [((1024, 1024), bf), ((512, 1024), bf), ((512, 1024), bf), ((512, 1024), bf), ((1024, 512), bf),
               ((512, 1024), bf), ((512, 1024), f32), ((512, 1024), f32), ((256, 1024), bf)]
        + big[:2] + [((512, FFP), bf)],
        [68, 4, (6, 9)], 12, (att, attp, act, actp, cot, cotp, *a, *b, *da, *db, outs), 50,
    )


def finish_kernel(*refs):
    h_hbm, cot_hbm, cotp_hbm, att_hbm, gres_hbm = refs[:5]
    da_in, db_in = refs[5:9], refs[9:13]
    part_hbm, own_hbm, gda_keep, gda_send, gdb_keep, gdb_send, keep_hbm, send_hbm = refs[13:21]
    hidden, cot, att, gres, wd, out, part, dd, gw, sems = refs[21:]
    me = lax.axis_index("dp")
    core = me % 2
    yx = me // 2
    go = Copies(sems)
    first = [go.start(h_hbm, hidden), go.start(cot_hbm, cot.at[pl.ds(0, 256)]),
             go.start(cotp_hbm, cot.at[pl.ds(256, 256)])]
    second = []
    for p in range(4):
        (ax, ay), (bx, by) = FLIPS_A[p], FLIPS_B[p]
        second.append(go.start(da_in[p], wd.at[aligned(yx ^ (ax + 2 * ay), 352), pl.ds(0, 512)]))
        second.append(go.start(db_in[p], wd.at[aligned(yx ^ (bx + 2 * by), 352), pl.ds(512, 512)]))
    third = [go.start(gres_hbm, gres)]
    third += [go.start(att_hbm.at[i], att.at[:, pl.ds(256 * i, 256)]) for i in range(4)]
    wait_all(first)
    done = []

    @pl.loop(0, FF2 // 128)
    def _(t):
        cols = aligned(t, 128)
        dd[cols, :] = dot(hidden[:, cols], cot[...], TN).astype(bf)

    for q in range(4):
        fx, fy = FLIPS_A[q]
        rows = aligned(yx ^ (fx + 2 * fy), 352)
        done.append(go.start(dd.at[rows, pl.ds(0, 512)], (gda_send if fx else gda_keep).at[pl.ds(352 * fy, 352)]))
        done.append(go.start(dd.at[rows, pl.ds(512, 512)], (gdb_send if fy else gdb_keep).at[pl.ds(352 * fx, 352)]))
    wait_all(second)
    part[...] = dot(hidden[256:512, :], wd[...], NN).astype(bf)
    done.append(go.start(part, part_hbm))
    out[...] = dot(hidden[0:256, :], wd[...], NN)
    done.append(go.start(out, own_hbm))
    wait_all(third)
    low = gres[...].astype(bf)

    @pl.loop(0, 4)
    def _(i):
        cols = aligned(i, 256)
        gw[cols, :] = dot(att[:, cols], low, TN).astype(bf)

    for q in range(4):
        fx, fy = FLIPS_A[q]
        j = yx ^ (fx + 2 * fy)
        for dst, c in ((keep_hbm, core), (send_hbm, 1 - core)):
            done.append(go.start(gw.at[aligned(j * 2 + c, 128)], dst.at[pl.ds(128 * (2 * fx + fy), 128)]))
    wait_all(done)


def finish(hidden, cot, cotp, att, gres, da, db):
    tall = ((256, 1024), f32)
    low = ((256, 1024), bf)
    half = ((512, 1024), bf)
    return call(
        finish_kernel, "finish",
        [low, tall] + [((704, 512), bf)] * 4 + [half] * 2,
        [((512, FF2), bf), half, low, tall, ((FF2, 1024), bf), tall, low, ((FF2, 1024), bf), ((1024, 1024), bf)],
        [34], 60, (hidden, cot, cotp, att, gres, *da, *db), 32,
    )


def branch_kernel(part_hbm, gnown_hbm, res_hbm, cot_hbm, wo_hbm, gres_hbm, gatt_hbm,
                  part, gnown, res_ref, cot, wo, gres_ref, gatt, sems):
    go = Copies(sems)
    first = [
        go.start(a, b)
        for a, b in ((res_hbm, res_ref), (gnown_hbm, gnown), (part_hbm, part), (cot_hbm, cot))
    ]
    late = go.start(wo_hbm, wo)
    wait_all(first)
    res = res_ref[...]
    g = gnown[...] + part[...].astype(f32)
    c = res - jnp.mean(res, axis=-1, keepdims=True)
    r = lax.rsqrt(jnp.mean(c * c, axis=-1, keepdims=True) + NORM_EPS)
    xh = c * r
    d = r * (g - jnp.mean(g, axis=-1, keepdims=True) - xh * jnp.mean(g * xh, axis=-1, keepdims=True))
    gres = cot[...].astype(f32) + d
    gres_ref[...] = gres
    low = gres.astype(bf)
    done = [go.start(gres_ref, gres_hbm)]
    late.wait()
    ga = dot(low, wo[...], NT).astype(bf)
    for z in range(4):
        gatt[z] = ga[:, 256 * z : 256 * z + 256]
    done.append(go.start(gatt, gatt_hbm))
    wait_all(done)


def branch(part, gnown, res, cot, wo):
    tall = ((256, 1024), f32)
    low = ((256, 1024), bf)
    return call(
        branch_kernel, "branch", [tall, ((4, 256, 256), bf)],
        [low, tall, tall, low, ((1024, 1024), bf), tall, ((4, 256, 256), bf)],
        [7], 1, (part, gnown, res, cot, wo), 32,
    )


def update_kernel(coeff_ref, wide_ref, mg, mu, md, wg, wu, wd, *refs):
    outs, (gg, gu, gd, ng, nu, nd, og, ou, od), sems = refs[:9], refs[9:18], refs[18]
    coeff = coeff_ref[0]
    go = Copies(sems)
    done = []
    part = FF2 // 4

    def finish(i, grad, moment, weight, new_moment, new_weight):
        done.append(go.start(grad, outs[i]))
        moved = coeff * moment[...] + grad[...]
        new_moment[...] = moved
        done.append(go.start(new_moment, outs[3 + i]))
        new_weight[...] = (weight[...].astype(f32) - LEARN_RATE * moved).astype(bf)
        done.append(go.start(new_weight, outs[6 + i]))

    for i, (grad, moment, weight, nm, nw) in enumerate(((gg, mg, wg, ng, og), (gu, mu, wu, nu, ou))):
        for side in range(2):
            columns = wide_ref[:, FF2 * (2 * side + i) : FF2 * (2 * side + i + 1)].astype(f32)
            for j in range(4):
                low = part * (2 * j + side)
                grad[:, low : low + part] = columns[:, part * j : part * j + part]
        finish(i, grad, moment, weight, nm, nw)
    for j in range(3):
        rows = min(32, 88 - 32 * j)
        low = 4 * FF2 + 1024 * j
        gd[32 * j : 32 * j + rows, :] = wide_ref[:, low : low + 1024].astype(f32)[0:rows]
    finish(2, gd, md, wd, nd, od)
    wait_all(done)


def update(coeff, wide, moments, weights):
    shapes = [(32, 2 * FF2), (32, 2 * FF2), (88, 1024)]
    outs = [(s, f32) for s in shapes] * 2 + [(s, bf) for s in shapes]
    vmem = pl.BlockSpec(memory_space=pltpu.VMEM)
    return pl.pallas_call(
        update_kernel,
        out_shape=tuple(pltpu.HBM(*o) for o in outs),
        in_specs=[pl.BlockSpec(memory_space=pltpu.SMEM)] + [vmem] * 7,
        out_specs=(MAIN,) * 9,
        scratch_shapes=[pltpu.VMEM(*o) for o in outs] + [pltpu.SemaphoreType.DMA((9,))],
        compiler_params=pltpu.CompilerParams(vmem_limit_bytes=16 << 20),
        cost_estimate=pl.CostEstimate(flops=1 << 20, bytes_accessed=6 << 20, transcendentals=0),
        name="update",
    )(coeff, wide, *moments, *weights)


def swap(array, bit):
    return lax.ppermute(array, "dp", [(i, i ^ bit) for i in range(8)])


def shift(array, bits):
    return lax.ppermute(array, "ctx", [(i, i ^ bits) for i in range(4)])


def add_low(left, right):
    return (left.astype(f32) + right.astype(f32)).astype(bf)


def split_even(matrix):
    n = matrix.shape[1] // 8
    parts = [matrix[:, n * i : n * i + n] for i in range(8)]
    return jnp.concatenate(parts[0::2], axis=1), jnp.concatenate(parts[1::2], axis=1)


def tie(value, *anchors):
    return lax.optimization_barrier((value, *anchors))[0]


def fast_device(
    activations,
    block_ids,
    cotangent,
    w_query,
    w_key,
    w_value,
    w_out,
    w_gate,
    w_up,
    w_down,
    m_query,
    m_key,
    m_value,
    m_out,
    m_gate,
    m_up,
    m_down,
    clip_threshold,
    momentum_coeff,
):
    me = lax.axis_index("dp")
    z = lax.axis_index("ctx")
    core = me % 2
    _, span, width = activations.shape
    length = block_ids.shape[1]
    act = activations.reshape(span, width)
    cot = cotangent.reshape(span, width)
    act_other = swap(act, 1)
    cot_other = swap(cot, 1)
    g0, g1 = split_even(w_gate)
    u0, u1 = split_even(w_up)
    even = jnp.stack([g0, u0])
    odd = jnp.stack([g1, u1])
    flip = core == 1
    mine = jnp.where(flip, odd, even)
    other = swap(jnp.where(flip, even, odd), 1)
    out_rows = jnp.stack([w_out[:, :512], w_out[:, 512:]]).reshape(2, 32, 2, 256)
    wide = jnp.stack([mine, other], axis=1)
    wide = jnp.concatenate([wide, out_rows.transpose(0, 2, 1, 3)], axis=3)
    wide = lax.all_gather(wide, "ctx", axis=2, tiled=True).reshape(2, 256, FF2 + 256)
    padded = jnp.concatenate([act, w_down], axis=0)
    rows_all = lax.all_gather(padded, "ctx", axis=0, tiled=True)
    heads = jnp.stack(
        [
            jnp.concatenate([w[:, 256 * i : 256 * i + 256] for w in (w_query, w_key, w_value)], 1)
            for i in range(4)
        ]
    )
    heads = lax.all_to_all(heads, "ctx", 0, 0, tiled=True).reshape(128, 768)
    hx = swap(heads, 2)
    hy = swap(jnp.concatenate([heads, hx], axis=0), 4)
    four = jnp.concatenate([heads, hy[:128], hx, hy[128:]], axis=0)
    heads_rel = jnp.concatenate([four, swap(four, 1)], axis=0)
    wide, act_other, cot_other = lax.optimization_barrier((wide, act_other, cot_other))

    def spread(own, first, second):
        near = swap(own, first)
        return [own, near, swap(own, second), swap(near, second)]

    piece_a = spread(wide[0], 2, 4)
    piece_b = spread(wide[1], 4, 2)
    down = jnp.concatenate(
        [rows_all[344 * i + 256 : 344 * i + 344] for i in range(4)], axis=0
    )
    piece_da = spread(down[:, :512], 2, 4)
    piece_db = spread(down[:, 512:], 4, 2)
    cosine, sine = rotary_tables(jnp.arange(length, dtype=jnp.int32), HEAD_DIM)
    cosine = jnp.concatenate([cosine] * 4, axis=1)
    sine = jnp.concatenate([-sine, sine, -sine, sine], axis=1)
    ids = jnp.broadcast_to(block_ids, (8, length)).astype(f32)
    pieces = lax.optimization_barrier((rows_all, *piece_a, *piece_b))
    normed, mixed, attended, totals, peaks, outs = attend(
        pieces[0], heads_rel, cosine, sine, ids, pieces[1:]
    )
    piece_a, piece_b = pieces[1:5], pieces[5:]
    outs = swap(outs, 1)
    attended = tie(attended, *piece_da[1:3], *piece_db[1:3])
    attended = lax.all_to_all(attended.reshape(4, span, 256), "ctx", 0, 0, tiled=True)
    attended_other = swap(tie(attended, piece_da[3], piece_db[3]), 1)
    part, back_own, residual, full_out, hidden, ga_keep, ga_send, gb_keep, gb_send = feed(
        attended, attended_other, act, act_other, cot, cot_other,
        piece_a, piece_b, piece_da, piece_db, outs,
    )
    part = swap(part, 1)
    ga_send, gb_send, part = lax.optimization_barrier((ga_send, gb_send, part))
    ga_other = swap(ga_send, 2)
    gb_other = swap(gb_send, 4)
    grad_residual, grad_attended = branch(part, back_own, residual, cot, full_out)
    grad_attended = lax.all_to_all(grad_attended, "ctx", 0, 0, tiled=True).reshape(length, 256)
    (out_part, out_own, gda_keep, gda_send, gdb_keep, gdb_send, go_keep, go_send) = finish(
        hidden, cot, cot_other, attended, grad_residual, piece_da, piece_db
    )
    gda_other = swap(gda_send, 2)
    gdb_other = swap(gdb_send, 4)
    grad_attended, out_part = lax.optimization_barrier((grad_attended, out_part))
    layer_out = (residual + (out_own + swap(out_part, 1).astype(f32))).astype(bf)
    grad_mixed, grad_normed = attend_back(
        mixed, grad_attended, totals, cosine, sine, ids, heads_rel
    )
    grad_mixed = tie(grad_mixed, ga_other, gb_other)
    grad_heads = project_weights(grad_mixed, normed, go_keep, go_send)
    ga_keep, gb_keep, gda_keep, gdb_keep, grad_heads = lax.optimization_barrier(
        (ga_keep, gb_keep, gda_keep, gdb_keep, grad_heads)
    )
    grad_a = add_low(ga_keep, ga_other)
    grad_b = add_low(gb_keep, gb_other)
    grad_da = add_low(gda_keep, gda_other)
    grad_db = add_low(gdb_keep, gdb_other)
    grad_a = add_low(grad_a[:256], swap(grad_a[256:], 4))
    grad_b = add_low(grad_b[:256], swap(grad_b[256:], 2))
    grad_da = add_low(grad_da[:352], swap(grad_da[352:], 4))
    grad_db = add_low(grad_db[:352], swap(grad_db[352:], 2))
    def core_rows(which):
        return jnp.concatenate(
            [lax.dynamic_slice_in_dim(g, which * 128, 128, 0) for g in (grad_a, grad_b)], axis=1
        )

    own_half = core_rows(core)
    other_half = swap(core_rows(1 - core), 1)
    grad_d = jnp.concatenate([grad_da, grad_db], axis=1).reshape(4, 88, width)
    grad_d = jnp.pad(grad_d, ((0, 0), (0, 8), (0, 0))).reshape(4, 3, 32, width)
    grad_d = grad_d.transpose(0, 2, 1, 3).reshape(128, 3 * width)
    grad_wide = jnp.concatenate(
        [
            jnp.where(flip, other_half, own_half),
            jnp.where(flip, own_half, other_half),
            grad_d,
        ],
        axis=1,
    )
    grad_wide = lax.psum_scatter(grad_wide, "ctx", scatter_dimension=0, tiled=True)
    peaks = tie(peaks, ga_other)
    peaks = lax.all_to_all(
        jnp.broadcast_to(peaks[None], (32, 8, 128)), ("dp", "ctx"), 0, 0, tiled=True
    )
    head_peaks = jnp.max(peaks.reshape(8, 4, 8, 128), axis=0)[:, :4, 0].reshape(HEADS)
    grad_normed = lax.psum_scatter(grad_normed, "ctx", scatter_dimension=0, tiled=True)
    tokens_wide = act.astype(f32)
    unused, first_pull = jax.vjp(normalize, tokens_wide)
    input_grad = grad_residual + first_pull(grad_normed.astype(f32))[0]
    grad_heads = add_low(grad_heads[0], swap(grad_heads[1], 1))
    grad_heads = add_low(grad_heads[:256], swap(grad_heads[256:], 2))
    grad_heads = add_low(grad_heads[:128], swap(grad_heads[128:], 4))
    grad_heads = lax.all_to_all(grad_heads.reshape(4, 32, 768 + width), "ctx", 0, 0, tiled=True)
    big = update(
        momentum_coeff.reshape(1), grad_wide, (m_gate, m_up, m_down), (w_gate, w_up, w_down)
    )
    grad_heads, *big = lax.optimization_barrier((grad_heads, *big))
    grad_heads = grad_heads.astype(f32)
    parts = grad_heads[:, :, 768:]
    grad_out = parts[0] + parts[1] + (parts[2] + parts[3])
    grad_qkv = [
        jnp.concatenate([grad_heads[i, :, 256 * k : 256 * k + 256] for i in range(4)], axis=1)
        for k in range(3)
    ]
    weight_grads = (*grad_qkv, grad_out)
    moments = (m_query, m_key, m_value, m_out)
    new_moments = tuple(
        (momentum_coeff * moment + gradient for moment, gradient in zip(moments, weight_grads))
    )
    head_scale = jnp.sqrt(clip_threshold / jnp.maximum(head_peaks, clip_threshold))
    column_scale = jnp.repeat(head_scale, HEAD_DIM)
    rates = (LEARN_RATE, LEARN_RATE, LEARN_RATE, OUT_RATE)
    shard_list = (w_query, w_key, w_value, w_out)
    updated = [
        matrix.astype(jnp.float32) - rate * moment
        for matrix, moment, rate in zip(shard_list, new_moments, rates)
    ]
    updated[0] = updated[0] * column_scale[None, :]
    updated[1] = updated[1] * column_scale[None, :]
    updated = [matrix.astype(bf) for matrix in updated]
    return (
        layer_out[None],
        input_grad[None],
        *weight_grads,
        *big[:3],
        *new_moments,
        *big[3:6],
        *updated,
        *big[6:],
        head_peaks,
        head_scale,
    )


def solution(mesh):
    placed = (
        P("dp", "ctx", None),
        P("dp", None),
        P("dp", "ctx", None),
        P(("dp", "ctx"), None),
        P(("dp", "ctx"), None),
        P(("dp", "ctx"), None),
        P(("dp", "ctx"), None),
        P(("dp", "ctx"), None),
        P(("dp", "ctx"), None),
        P(("dp", "ctx"), None),
        P(("dp", "ctx"), None),
        P(("dp", "ctx"), None),
        P(("dp", "ctx"), None),
        P(("dp", "ctx"), None),
        P(("dp", "ctx"), None),
        P(("dp", "ctx"), None),
        P(("dp", "ctx"), None),
        P(),
        P(),
    )
    fits = mesh.shape["dp"] == 8 and mesh.shape["ctx"] == 4
    return jax.shard_map(
        fast_device if fits else per_device,
        mesh=mesh,
        in_specs=placed,
        out_specs=(
            P("dp", "ctx", None),
            P("dp", "ctx", None),
            P(("dp", "ctx"), None),
            P(("dp", "ctx"), None),
            P(("dp", "ctx"), None),
            P(("dp", "ctx"), None),
            P(("dp", "ctx"), None),
            P(("dp", "ctx"), None),
            P(("dp", "ctx"), None),
            P(("dp", "ctx"), None),
            P(("dp", "ctx"), None),
            P(("dp", "ctx"), None),
            P(("dp", "ctx"), None),
            P(("dp", "ctx"), None),
            P(("dp", "ctx"), None),
            P(("dp", "ctx"), None),
            P(("dp", "ctx"), None),
            P(("dp", "ctx"), None),
            P(("dp", "ctx"), None),
            P(("dp", "ctx"), None),
            P(("dp", "ctx"), None),
            P(("dp", "ctx"), None),
            P(("dp", "ctx"), None),
            P(),
            P(),
        ),
        check_vma=False,
    )
```

```python
import math

import jax
import jax.numpy as jnp
from jax import lax
from jax.experimental import pallas as pl
from jax.experimental.pallas import tpu as pltpu
from jax.sharding import PartitionSpec as P

HEADS = 16
HEAD_DIM = 64


NORM_EPS = 1e-05
ROPE_BASE = 10000.0
LEARN_RATE = 0.0001
OUT_RATE = 0.0016
MASK_FILL = -1e30


def normalize(values):
    centred = values - jnp.mean(values, axis=-1, keepdims=True)
    spread = jnp.mean(centred * centred, axis=-1, keepdims=True)
    return centred * lax.rsqrt(spread + NORM_EPS)


def rotary_tables(positions, head_width):
    half_width = head_width // 2
    frequency = ROPE_BASE ** (-(jnp.arange(half_width, dtype=jnp.float32) * 2.0 / head_width))
    angles = positions.astype(jnp.float32)[:, None] * frequency[None, :]
    return (jnp.cos(angles), jnp.sin(angles))


def rotate(vectors, cosine, sine_table):
    half_width = vectors.shape[-1] // 2
    first_half = vectors[..., :half_width]
    second = vectors[..., half_width:]
    cos_wide = cosine[:, None, :]
    sin_wide = sine_table[:, None, :]
    return jnp.concatenate(
        [first_half * cos_wide - second * sin_wide, second * cos_wide + first_half * sin_wide],
        axis=-1,
    )


def swiglu(gate_proj, up_proj):
    return jax.nn.silu(gate_proj) * up_proj


def project(left_rows, matrix):
    return jnp.dot(left_rows, matrix, preferred_element_type=jnp.float32)


def project_back(grad_rows, matrix):
    return lax.dot_general(
        grad_rows, matrix, (((1,), (1,)), ((), ())), preferred_element_type=jnp.float32
    )


def shard_gradient(left_rows, right_rows):
    return lax.psum_scatter(
        lax.dot_general(
            left_rows, right_rows, (((0,), (0,)), ((), ())), preferred_element_type=jnp.float32
        ),
        ("dp", "ctx"),
        scatter_dimension=0,
        tiled=True,
    )


def per_device(
    activations,
    block_ids,
    cotangent,
    w_query,
    w_key,
    w_value,
    w_out,
    w_gate,
    w_up,
    w_down,
    m_query,
    m_key,
    m_value,
    m_out,
    m_gate,
    m_up,
    m_down,
    clip_threshold,
    momentum_coeff,
):
    shard_list = (w_query, w_key, w_value, w_out, w_gate, w_up, w_down)
    gathered = (
        lax.all_gather(shard_list[0], ("dp", "ctx"), axis=0, tiled=True),
        lax.all_gather(shard_list[1], ("dp", "ctx"), axis=0, tiled=True),
        lax.all_gather(shard_list[2], ("dp", "ctx"), axis=0, tiled=True),
        lax.all_gather(shard_list[3], ("dp", "ctx"), axis=0, tiled=True),
        lax.all_gather(shard_list[4], ("dp", "ctx"), axis=0, tiled=True),
        lax.all_gather(shard_list[5], ("dp", "ctx"), axis=0, tiled=True),
        lax.all_gather(shard_list[6], ("dp", "ctx"), axis=0, tiled=True),
    )
    full_query, full_key, full_value, full_out, full_gate, full_up, full_down = gathered
    seq_count, span_len, model_width = activations.shape
    ctx_place = lax.axis_index("ctx")
    positions = ctx_place * span_len + jnp.arange(span_len, dtype=jnp.int32)
    cosine, sine_table = rotary_tables(positions, HEAD_DIM)
    score_scale = 1.0 / math.sqrt(HEAD_DIM)

    def split_heads(matrix):
        return matrix.reshape(seq_count, span_len, HEADS, HEAD_DIM)

    tokens_flat = activations.astype(jnp.float32).reshape(-1, model_width)
    normed = normalize(tokens_flat).astype(jnp.bfloat16)
    queries = rotate(split_heads(project(normed, full_query)), cosine, sine_table).astype(
        jnp.bfloat16
    )
    key_rot = rotate(split_heads(project(normed, full_key)), cosine, sine_table).astype(
        jnp.bfloat16
    )
    value_rot = split_heads(project(normed, full_value)).astype(jnp.bfloat16)
    key_all, value_all = (
        lax.all_gather(key_rot, "ctx", axis=1, tiled=True),
        lax.all_gather(value_rot, "ctx", axis=1, tiled=True),
    )
    query_ids = lax.dynamic_slice_in_dim(block_ids, ctx_place * span_len, span_len, 1)
    allowed = (block_ids[:, None, :] <= query_ids[:, :, None])[:, None]

    def masked_scores():
        scores = (
            jnp.einsum("sqhd,skhd->shqk", queries, key_all, preferred_element_type=jnp.float32)
            * score_scale
        )
        return jnp.where(allowed, scores, MASK_FILL)

    masked = masked_scores()
    local_peaks = jnp.max(masked, axis=(0, 2, 3))
    row_top = jnp.max(masked, axis=-1, keepdims=True)
    log_total = row_top + jnp.log(jnp.sum(jnp.exp(masked - row_top), axis=-1, keepdims=True))
    probs_low = jnp.exp(masked - log_total).astype(jnp.bfloat16)
    attended = jnp.einsum(
        "shqk,skhd->sqhd", probs_low, value_all, preferred_element_type=jnp.float32
    )
    attended_low = attended.reshape(-1, model_width).astype(jnp.bfloat16)
    head_peaks = lax.pmax(local_peaks, ("dp", "ctx"))
    residual = tokens_flat + project(attended_low, full_out)
    normed2 = normalize(residual).astype(jnp.bfloat16)
    gate_proj = project(normed2, full_gate)
    up_proj = project(normed2, full_up)
    hidden_low = swiglu(gate_proj, up_proj).astype(jnp.bfloat16)
    layer_out = (
        (residual + project(hidden_low, full_down))
        .astype(jnp.bfloat16)
        .reshape(seq_count, span_len, model_width)
    )
    back_weights = (
        lax.all_gather(shard_list[0], ("dp", "ctx"), axis=0, tiled=True),
        lax.all_gather(shard_list[1], ("dp", "ctx"), axis=0, tiled=True),
        lax.all_gather(shard_list[2], ("dp", "ctx"), axis=0, tiled=True),
        lax.all_gather(shard_list[3], ("dp", "ctx"), axis=0, tiled=True),
        lax.all_gather(shard_list[4], ("dp", "ctx"), axis=0, tiled=True),
        lax.all_gather(shard_list[5], ("dp", "ctx"), axis=0, tiled=True),
        lax.all_gather(shard_list[6], ("dp", "ctx"), axis=0, tiled=True),
    )
    back_query, back_key, back_value, back_out, back_gate, back_up, back_down = back_weights
    grad_rows = cotangent.reshape(-1, model_width)
    grad_hidden = project_back(grad_rows, back_down)
    unused, gate_pull = jax.vjp(swiglu, gate_proj, up_proj)
    grad_gate_wide, grad_up_wide = gate_pull(grad_hidden)
    grad_gate_low = grad_gate_wide.astype(jnp.bfloat16)
    grad_up_low = grad_up_wide.astype(jnp.bfloat16)
    grad_normed2 = project_back(grad_gate_low, back_gate) + project_back(grad_up_low, back_up)
    unused, second_pull = jax.vjp(normalize, residual)
    grad_residual = grad_rows.astype(jnp.float32) + second_pull(grad_normed2)[0]
    grad_branch = grad_residual.astype(jnp.bfloat16)
    grad_attended = split_heads(project_back(grad_branch, back_out).astype(jnp.bfloat16))
    masked = masked_scores()
    probs = jnp.exp(masked - log_total)
    probs_again = probs.astype(jnp.bfloat16)
    grad_values_all = jnp.einsum(
        "shqk,sqhd->skhd", probs_again, grad_attended, preferred_element_type=jnp.float32
    )
    grad_probs = jnp.einsum(
        "sqhd,skhd->shqk", grad_attended, value_all, preferred_element_type=jnp.float32
    )
    score_grad = (
        probs * (grad_probs - jnp.sum(probs * grad_probs, axis=-1, keepdims=True))
    ).astype(jnp.bfloat16)
    grad_queries = (
        jnp.einsum("shqk,skhd->sqhd", score_grad, key_all, preferred_element_type=jnp.float32)
        * score_scale
    )
    grad_keys_all = (
        jnp.einsum("shqk,sqhd->skhd", score_grad, queries, preferred_element_type=jnp.float32)
        * score_scale
    )
    grad_keys, grad_values = (
        lax.psum_scatter(
            grad_keys_all.astype(jnp.bfloat16), "ctx", scatter_dimension=1, tiled=True
        ).astype(jnp.float32),
        lax.psum_scatter(
            grad_values_all.astype(jnp.bfloat16), "ctx", scatter_dimension=1, tiled=True
        ).astype(jnp.float32),
    )
    grad_query_low = (
        rotate(grad_queries, cosine, -sine_table).reshape(-1, model_width).astype(jnp.bfloat16)
    )
    grad_key_low = (
        rotate(grad_keys, cosine, -sine_table).reshape(-1, model_width).astype(jnp.bfloat16)
    )
    grad_value_low = grad_values.reshape(-1, model_width).astype(jnp.bfloat16)
    grad_normed = (
        project_back(grad_query_low, back_query)
        + project_back(grad_key_low, back_key)
        + project_back(grad_value_low, back_value)
    )
    unused, first_pull = jax.vjp(normalize, tokens_flat)
    input_grad = (grad_residual + first_pull(grad_normed)[0]).reshape(
        seq_count, span_len, model_width
    )
    weight_grads = (
        shard_gradient(normed, grad_query_low),
        shard_gradient(normed, grad_key_low),
        shard_gradient(normed, grad_value_low),
        shard_gradient(attended_low, grad_branch),
        shard_gradient(normed2, grad_gate_low),
        shard_gradient(normed2, grad_up_low),
        shard_gradient(hidden_low, grad_rows),
    )
    moments = (m_query, m_key, m_value, m_out, m_gate, m_up, m_down)
    new_moments = tuple(
        (momentum_coeff * moment + gradient for moment, gradient in zip(moments, weight_grads))
    )
    head_scale = jnp.sqrt(clip_threshold / jnp.maximum(head_peaks, clip_threshold))
    column_scale = jnp.repeat(head_scale, HEAD_DIM)
    rates = (LEARN_RATE, LEARN_RATE, LEARN_RATE, OUT_RATE, LEARN_RATE, LEARN_RATE, LEARN_RATE)
    updated = [
        matrix.astype(jnp.float32) - rate * moment
        for matrix, moment, rate in zip(shard_list, new_moments, rates)
    ]
    updated[0] = updated[0] * column_scale[None, :]
    updated[1] = updated[1] * column_scale[None, :]
    updated = [matrix.astype(jnp.bfloat16) for matrix in updated]
    return (
        layer_out,
        input_grad,
        weight_grads[0],
        weight_grads[1],
        weight_grads[2],
        weight_grads[3],
        weight_grads[4],
        weight_grads[5],
        weight_grads[6],
        new_moments[0],
        new_moments[1],
        new_moments[2],
        new_moments[3],
        new_moments[4],
        new_moments[5],
        new_moments[6],
        updated[0],
        updated[1],
        updated[2],
        updated[3],
        updated[4],
        updated[5],
        updated[6],
        head_peaks,
        head_scale,
    )


f32=jnp.float32; bf=jnp.bfloat16
NT=(((1,),(1,)),((),())); TN=(((0,),(0,)),((),())); NN=(((1,),(0,)),((),()))
FF2=1408
FFP=1536
FLIPS_A=((0,0),(1,0),(0,1),(1,1))
FLIPS_B=((0,0),(0,1),(1,0),(1,1))
MAIN=pl.BlockSpec(memory_space=pltpu.HBM)
S=jax.ShapeDtypeStruct


def dot(a, b, dims):
    return lax.dot_general(a, b, dims, preferred_element_type=f32)


def aligned(i, m):
    return pl.ds(pl.multiple_of(i * m, m), m)


class Copies:
    def __init__(self, sems):
        self.sems = sems
        self.count = 0

    def start(self, source, target):
        copy = pltpu.make_async_copy(source, target, self.sems.at[self.count])
        self.count += 1
        copy.start()
        return copy


def wait_all(copies):
    for copy in copies:
        copy.wait()


def call(kernel, name, outs, scratch, sems, flops, args, limit):
    return pl.pallas_call(
        kernel,
        out_shape=tuple(pltpu.HBM(*o) for o in outs),
        in_specs=[MAIN] * len(args),
        out_specs=(MAIN,) * len(outs),
        scratch_shapes=[pltpu.VMEM(*s) for s in scratch] + [pltpu.SemaphoreType.DMA(n if isinstance(n, tuple) else (n,)) for n in sems],
        compiler_params=pltpu.CompilerParams(vmem_limit_bytes=limit << 20),
        cost_estimate=pl.CostEstimate(flops=flops << 30, bytes_accessed=8 << 20, transcendentals=0),
        name=name,
    )(*(pltpu.with_memory_space_constraint(arg, pltpu.HBM) for arg in args))


def place_of(p):
    return lax.axis_index("dp") ^ ((p >> 2 & 1) | (p >> 1 & 1) << 1 | (p & 1) << 2)


def turn(values, cosine, signed_sine):
    lane = lax.broadcasted_iota(jnp.int32, cosine.shape, 1)
    first = lane % 64 < 32
    parts = []
    for j in range(values.shape[1] // 128):
        part = values[:, 128 * j : 128 * j + 128]
        partner = jnp.where(first, pltpu.roll(part, 96, 1), pltpu.roll(part, 32, 1))
        parts.append(part * cosine + partner * signed_sine)
    return jnp.concatenate(parts, axis=1)


def layer_norm(x):
    c = x - jnp.mean(x, axis=-1, keepdims=True)
    v = jnp.mean(c * c, axis=-1, keepdims=True)
    return c * lax.rsqrt(v + NORM_EPS)


def wide_pieces(own, by_x, by_y, a_far, b_far):
    return ([own.at[0], by_x.at[0], by_y.at[0], a_far], [own.at[1], by_y.at[1], by_x.at[1], b_far])


def down_pieces(own, by_x, by_y, a_far, b_far):
    low, high = pl.ds(0, 512), pl.ds(512, 512)
    return ([own.at[:, low], by_x.at[:, low], by_y.at[:, low], a_far],
            [own.at[:, high], by_y.at[:, high], by_x.at[:, high], b_far])


def attend_kernel(*refs):
    rows_hbm, weight_hbm, cos_hbm, sin_hbm, id_hbm = refs[:5]
    pieces = sum(wide_pieces(*refs[5:10]), [])
    normed_hbm, mixed_hbm, attended_hbm, total_hbm, peak_hbm, outs_hbm = refs[10:16]
    (act, weight, cos_ref, sin_ref, ids, id_col, normed, mixed_ref, attended, value_t, total_ref,
     peak_ref, outs, sems) = refs[16:]
    n = normed.shape[0]
    go = Copies(sems)
    early = [go.start(rows_hbm.at[pl.ds(344 * i, 256)], act.at[pl.ds(256 * i, 256)]) for i in range(4)]
    middle = [
        go.start(weight_hbm.at[pl.ds(128 * p, 128)], weight.at[aligned(place_of(p), 128)])
        for p in range(8)
    ]
    middle += [go.start(cos_hbm, cos_ref), go.start(sin_hbm, sin_ref), go.start(id_hbm, ids)]
    packs = [go.start(piece.at[:, pl.ds(FF2, 256)], outs.at[i]) for i, piece in enumerate(pieces)]
    wait_all(early)

    def norm(i):
        rows = aligned(i, 256)
        normed[rows, :] = layer_norm(act[rows, :].astype(f32)).astype(bf)

    def mix(i):
        rows = aligned(i, 256)
        mixed = dot(normed[rows, :], weight[...], NN)
        cosine = cos_ref[rows, :]
        sine = sin_ref[rows, :]
        queries = turn(mixed[:, 0:256], cosine, sine).astype(bf)
        mixed_ref[rows, 0:256] = (queries.astype(f32) * 0.125).astype(bf)
        mixed_ref[rows, 256:512] = turn(mixed[:, 256:512], cosine, sine).astype(bf)
        value = mixed[:, 512:768]
        mixed_ref[rows, 512:768] = value.astype(bf)
        value_t[:, rows] = value.T.astype(bf)

    norm(0)
    wait_all(middle)
    wait_all(packs)
    id_col[...] = jnp.broadcast_to(ids[0:1, :], (128, n)).T

    @pl.loop(0, n // 256 - 1)
    def _(i):
        mix(i)
        norm(i + 1)

    mix(n // 256 - 1)
    late = [go.start(normed, normed_hbm), go.start(outs, outs_hbm)]
    late.append(go.start(mixed_ref, mixed_hbm))
    peak_ref[...] = jnp.zeros_like(peak_ref)
    total_ref[...] = jnp.zeros_like(total_ref)

    @pl.loop(0, 2)
    def _(pair):
        lanes = pl.multiple_of(pair * 128, 128)
        lane = lax.broadcasted_iota(jnp.int32, (256, 128), 1)
        best = [None, None]
        for i in range(4):
            width = min(256 * (i + 2), 1024)
            low = 256 * i
            both = mixed_ref[low : low + 256, pl.ds(lanes, 128)]
            keys = mixed_ref[0:width, pl.ds(pl.multiple_of(256 + lanes, 128), 128)]
            values = value_t[pl.ds(lanes, 128), 0:width]
            ok = id_col[low:width, 0:1] <= ids[0:1, low : low + 256]
            outs = []
            for half in range(2):
                q = jnp.where(lane // 64 == half, both, jnp.zeros_like(both))
                s = dot(keys, q, NT)
                tail = jnp.where(ok, s[low:width], MASK_FILL)
                top = jnp.max(tail, axis=0, keepdims=True)
                if i:
                    top = jnp.maximum(top, jnp.max(s[0:low], axis=0, keepdims=True))
                    s = jnp.concatenate([s[0:low], tail], axis=0)
                else:
                    s = tail
                e = jnp.exp(s - top)
                total = jnp.sum(e, axis=0, keepdims=True)
                o = dot(values, e.astype(bf), NN)
                outs.append(o[64 * half : 64 * half + 64] * (1.0 / total))
                total_ref[pl.ds(pair * 2 + half, 1), low : low + 256] = top + jnp.log(total)
                m = jnp.max(top, axis=1, keepdims=True)
                best[half] = m if best[half] is None else jnp.maximum(best[half], m)
            o = jnp.concatenate(outs, axis=0).T.astype(bf)
            attended[low : low + 256, pl.ds(lanes, 128)] = o
        for half in range(2):
            peak_ref[pl.ds(pair * 2 + half, 1), :] = jnp.broadcast_to(best[half], (1, 128))

    late.append(go.start(attended, attended_hbm))
    late.append(go.start(total_ref, total_hbm))
    late.append(go.start(peak_ref, peak_hbm))
    wait_all(late)


def attend(rows_all, weight, cosine, sine, ids, pieces):
    n = cosine.shape[0]
    return call(
        attend_kernel, "attend",
        [((n, 1024), bf), ((n, 768), bf), ((n, 256), bf), ((8, n), f32), ((8, 128), f32),
         ((8, 256, 256), bf)],
        [((n, 1024), bf), ((1024, 768), bf), ((n, 128), f32), ((n, 128), f32), ((8, n), f32),
         ((n, 128), f32), ((n, 1024), bf), ((n, 768), bf), ((n, 256), bf), ((256, n), bf),
         ((8, n), f32), ((8, 128), f32), ((8, 256, 256), bf)],
        [29], 4, (rows_all, weight, cosine, sine, ids, *pieces), 28,
    )


def attend_back_kernel(mixed_hbm, ga_hbm, total_hbm, cos_hbm, sin_hbm, id_hbm, weight_hbm,
                       gm_hbm, gn_hbm,
                       mixed_ref, ga_ref, total_ref, cos_ref, sin_ref, ids, weight,
                       gm_ref, gn_ref, gk_acc, gv_acc, key_t, id_col, sems):
    n = ga_ref.shape[0]
    go = Copies(sems)
    early = [
        go.start(a, b)
        for a, b in ((mixed_hbm, mixed_ref), (ga_hbm, ga_ref), (total_hbm, total_ref),
                     (id_hbm, ids), (cos_hbm, cos_ref), (sin_hbm, sin_ref))
    ]
    late = [
        go.start(weight_hbm.at[pl.ds(128 * p, 128)], weight.at[aligned(place_of(p), 128)])
        for p in range(8)
    ]
    gk_acc[...] = jnp.zeros_like(gk_acc)
    gv_acc[...] = jnp.zeros_like(gv_acc)
    wait_all(early)
    id_col[...] = jnp.broadcast_to(ids[0:1, :], (128, n)).T

    @pl.loop(0, n // 256)
    def _(i):
        rows = aligned(i, 256)
        key_t[:, rows] = mixed_ref[rows, 256:512].astype(f32).T.astype(bf)

    @pl.loop(0, 2)
    def _(pair):
        lanes = pl.multiple_of(pair * 128, 128)
        lane = lax.broadcasted_iota(jnp.int32, (256, 128), 1)
        sub = lax.broadcasted_iota(jnp.int32, (128, 256), 0)
        for i in range(4):
            width = min(256 * (i + 2), 1024)
            low = 256 * i
            k = mixed_ref[0:width, pl.ds(pl.multiple_of(256 + lanes, 128), 128)]
            v = mixed_ref[0:width, pl.ds(pl.multiple_of(512 + lanes, 128), 128)]
            q_all = mixed_ref[low : low + 256, pl.ds(lanes, 128)]
            g_all = ga_ref[low : low + 256, pl.ds(lanes, 128)]
            kt = key_t[pl.ds(lanes, 128), 0:width]
            ok = id_col[low:width, 0:1] <= ids[0:1, low : low + 256]

            def one(half, gq):
                mine = lane // 64 == half
                q = jnp.where(mine, q_all, jnp.zeros_like(q_all))
                g = jnp.where(mine, g_all, jnp.zeros_like(g_all))
                s = dot(k, q, NT) - total_ref[pl.ds(pair * 2 + half, 1), low : low + 256]
                tail = jnp.where(ok, s[low:width], MASK_FILL)
                s = jnp.concatenate([s[0:low], tail], axis=0) if i else tail
                p = jnp.exp(s)
                t = p * dot(v, g, NT)
                delta = jnp.sum(t, axis=0, keepdims=True)
                ds = (t - p * delta).astype(bf)
                gv_acc[0:width, pl.ds(lanes, 128)] += dot(p.astype(bf), g, NN)
                gk_acc[0:width, pl.ds(lanes, 128)] += dot(ds, q, NN)
                return jnp.where(sub // 64 == half, dot(kt, ds, NN), gq)

            gq = one(1, one(0, jnp.zeros((128, 256), f32)))
            gq = gq.T * 0.125
            cosine = cos_ref[low : low + 256, :]
            sine = sin_ref[low : low + 256, :]
            gm_ref[low : low + 256, pl.ds(lanes, 128)] = turn(gq, cosine, -sine).astype(bf)

    wait_all(late)

    @pl.loop(0, n // 256)
    def _(i):
        rows = aligned(i, 256)
        cosine = cos_ref[rows, :]
        sine = sin_ref[rows, :]
        gm_ref[rows, 256:512] = turn(gk_acc[rows, :], cosine, -sine).astype(bf)
        gm_ref[rows, 512:768] = gv_acc[rows, :].astype(bf)
        gn_ref[rows, :] = dot(gm_ref[rows, :], weight[...], NT).astype(bf)
        copy = pltpu.make_async_copy(gn_ref.at[rows], gn_hbm.at[rows], sems.at[14 + i])
        copy.start()

    out = pltpu.make_async_copy(gm_ref, gm_hbm, sems.at[18])
    out.start()
    for i in range(4):
        rows = pl.ds(256 * i, 256)
        pltpu.make_async_copy(gn_ref.at[rows], gn_hbm.at[rows], sems.at[14 + i]).wait()
    out.wait()


def attend_back(mixed, ga, total, cosine, sine, ids, weight):
    n = ga.shape[0]
    return call(
        attend_back_kernel, "attend_back",
        [((n, 768), bf), ((n, 1024), bf)],
        [((n, 768), bf), ((n, 256), bf), ((8, n), f32), ((n, 128), f32), ((n, 128), f32),
         ((8, n), f32), ((1024, 768), bf), ((n, 768), bf), ((n, 1024), bf), ((n, 256), f32),
         ((n, 256), f32), ((256, n), bf), ((n, 128), f32)],
        [19], 0, (mixed, ga, total, cosine, sine, ids, weight), 32,
    )


def weights_kernel(gm_hbm, normed_hbm, okeep_hbm, osend_hbm, keep_hbm, send_hbm,
                   gm_ref, normed_ref, gw, okeep, osend, sems):
    go = Copies(sems)
    first = [go.start(gm_hbm, gm_ref), go.start(normed_hbm, normed_ref)]
    second = [go.start(okeep_hbm, okeep), go.start(osend_hbm, osend)]
    wait_all(first + second)
    cols = pl.ds(768, 1024)
    late = [go.start(okeep, keep_hbm.at[:, cols]), go.start(osend, send_hbm.at[:, cols])]

    @pl.loop(0, 4)
    def _(i):
        cols = aligned(i, 256)
        gw[cols, :] = dot(normed_ref[:, cols], gm_ref[...], TN).astype(bf)

    late += [
        go.start(gw.at[aligned(place_of(p), 128)],
                 (keep_hbm if p < 4 else send_hbm).at[pl.ds(128 * (p % 4), 128), pl.ds(0, 768)])
        for p in range(8)
    ]
    wait_all(late)


def project_weights(gm, normed, okeep, osend):
    n = gm.shape[0]
    return call(
        weights_kernel, "project_weights", [((512, 1792), bf)] * 2,
        [((n, 768), bf), ((n, 1024), bf), ((1024, 768), bf), ((512, 1024), bf), ((512, 1024), bf)],
        [14], 1, (gm, normed, okeep, osend), 24,
    )


def feed_kernel(*refs):
    att_hbm, attp_hbm, act_hbm, actp_hbm, cot_hbm, cotp_hbm = refs[:6]
    a_in, b_in = wide_pieces(*refs[6:11])
    da_in, db_in = down_pieces(*refs[11:16])
    outs = refs[16]
    part_hbm, gnown_hbm, res_hbm, wo_hbm, h_hbm = refs[17:22]
    ga_keep, ga_send, gb_keep, gb_send = refs[22:26]
    (wg, wu, wd, wo, att, act, n2, n2t, cot, res_ref, gn_acc, part, dg, du, hidden,
     sems, osem, tsem) = refs[26:]
    me = lax.axis_index("dp")
    core = me % 2
    yx = me // 2
    go = Copies(sems)
    small = []
    for base, src, own in ((0, att_hbm, act_hbm), (256, attp_hbm, actp_hbm)):
        rows = pl.ds(base, 256)
        small += [go.start(src.at[i], att.at[rows, pl.ds(256 * i, 256)]) for i in range(4)]
        small.append(go.start(own, act.at[rows]))
    places = []
    for p in range(4):
        (ax, ay), (bx, by) = FLIPS_A[p], FLIPS_B[p]
        places.append((yx ^ (ax + 2 * ay), yx ^ (bx + 2 * by)))
    for p, (ja, jb) in enumerate(places):
        for which, src, j, col in ((0, a_in[p], ja, 0), (1, b_in[p], jb, 512)):
            for half in range(2):
                cols = pl.ds(col + 256 * half, 256)
                rows = pl.ds(128 * half, 128)
                small.append(go.start(src.at[rows, pl.ds(FF2, 256)], wo.at[aligned(j * 2 + core, 128), cols]))
                small.append(go.start(outs.at[4 * which + p, rows], wo.at[aligned(j * 2 + 1 - core, 128), cols]))
    big = []
    for p, (ja, jb) in enumerate(places):
        for src, dst, j in ((a_in[p], wg, ja), (b_in[p], wu, jb)):
            for half, c in ((0, core), (1, 1 - core)):
                big.append(go.start(src.at[pl.ds(128 * half, 128), pl.ds(0, FF2)],
                                    dst.at[aligned(j * 2 + c, 128), pl.ds(0, FF2)]))
    big += [go.start(cot_hbm, cot.at[pl.ds(0, 256)]), go.start(cotp_hbm, cot.at[pl.ds(256, 256)])]
    for p, (ja, jb) in enumerate(places):
        big.append(go.start(da_in[p], wd.at[aligned(ja, 352), pl.ds(0, 512)]))
        big.append(go.start(db_in[p], wd.at[aligned(jb, 352), pl.ds(512, 512)]))
    wg[:, FF2:FFP] = jnp.zeros((1024, FFP - FF2), bf)
    wu[:, FF2:FFP] = jnp.zeros((1024, FFP - FF2), bf)
    wd[FF2:FFP, :] = jnp.zeros((FFP - FF2, 1024), bf)
    gn_acc[...] = jnp.zeros_like(gn_acc)
    wait_all(small)
    ogo = Copies(osem)
    done = [ogo.start(wo, wo_hbm)]

    @pl.loop(0, 2)
    def _(i):
        rows = aligned(i, 256)
        res = act[rows, :].astype(f32) + dot(att[rows, :], wo[...], NN)
        res_ref[rows, :] = res
        n = layer_norm(res)
        n2[rows, :] = n.astype(bf)
        n2t[:, rows] = n.T.astype(bf)

    done.append(ogo.start(res_ref.at[pl.ds(0, 256)], res_hbm))
    wait_all(big)

    def tile_copies(t, width):
        copies = []
        cols = pl.ds(pl.multiple_of(t * 256, 256), width)
        for q in range(4):
            fx, fy = FLIPS_A[q]
            rows = aligned(yx ^ (fx + 2 * fy), 256)
            for k, src, dst, slot in ((0, dg, ga_send if fx else ga_keep, fy), (1, du, gb_send if fy else gb_keep, fx)):
                copies.append(pltpu.make_async_copy(
                    src.at[rows, cols], dst.at[pl.ds(256 * slot, 256), cols], tsem.at[t, 2 * q + k]))
        copies.append(pltpu.make_async_copy(hidden.at[:, cols], h_hbm.at[:, cols], tsem.at[t, 8]))
        return copies

    last = FFP // 256 - 1

    @pl.loop(0, last + 1)
    def _(t):
        cols = aligned(t, 256)
        g = dot(n2[...], wg[:, cols], NN)
        u = dot(n2[...], wu[:, cols], NN)
        gh = dot(cot[...], wd[cols, :], NT)
        sig = 1.0 / (1.0 + jnp.exp(-g))
        silu = g * sig
        hidden[:, cols] = (silu * u).astype(bf)
        gu = (gh * silu).astype(bf)
        gg = (gh * u * (sig + silu * (1.0 - sig))).astype(bf)
        dg[:, cols] = dot(n2t[...], gg, NN).astype(bf)
        du[:, cols] = dot(n2t[...], gu, NN).astype(bf)

        @pl.when(t < last)
        def _():
            for copy in tile_copies(t, 256):
                copy.start()

        gn_acc[...] += dot(gg, wg[:, cols], NT) + dot(gu, wu[:, cols], NT)

    ends = tile_copies(last, FF2 - 256 * last)
    for copy in ends:
        copy.start()
    part[...] = gn_acc[256:512, :].astype(bf)
    done.append(ogo.start(part, part_hbm))
    done.append(ogo.start(gn_acc.at[pl.ds(0, 256)], gnown_hbm))
    for t in range(last):
        wait_all(tile_copies(t, 256))
    wait_all(ends)
    wait_all(done)


def feed(att, attp, act, actp, cot, cotp, wide, down, outs):
    big = [((1024, FFP), bf), ((1024, FFP), bf), ((FFP, 1024), bf)]
    return call(
        feed_kernel, "feed",
        [((256, 1024), bf), ((256, 1024), f32), ((256, 1024), f32), ((1024, 1024), bf), ((512, FF2), bf)]
        + [((512, FF2), bf)] * 4,
        big + [((1024, 1024), bf), ((512, 1024), bf), ((512, 1024), bf), ((512, 1024), bf), ((1024, 512), bf),
               ((512, 1024), bf), ((512, 1024), f32), ((512, 1024), f32), ((256, 1024), bf)]
        + big[:2] + [((512, FFP), bf)],
        [68, 4, (6, 9)], 12, (att, attp, act, actp, cot, cotp, *wide, *down, outs), 50,
    )


def finish_kernel(*refs):
    h_hbm, cot_hbm, cotp_hbm, att_hbm, gres_hbm = refs[:5]
    da_in, db_in = down_pieces(*refs[5:10])
    part_hbm, own_hbm, gda_keep, gda_send, gdb_keep, gdb_send, keep_hbm, send_hbm = refs[10:18]
    hidden, cot, att, gres, wd, out, part, dd, gw, sems = refs[18:]
    me = lax.axis_index("dp")
    core = me % 2
    yx = me // 2
    go = Copies(sems)
    first = [go.start(h_hbm, hidden), go.start(cot_hbm, cot.at[pl.ds(0, 256)]),
             go.start(cotp_hbm, cot.at[pl.ds(256, 256)])]
    second = []
    for p in range(4):
        (ax, ay), (bx, by) = FLIPS_A[p], FLIPS_B[p]
        second.append(go.start(da_in[p], wd.at[aligned(yx ^ (ax + 2 * ay), 352), pl.ds(0, 512)]))
        second.append(go.start(db_in[p], wd.at[aligned(yx ^ (bx + 2 * by), 352), pl.ds(512, 512)]))
    third = [go.start(gres_hbm, gres)]
    third += [go.start(att_hbm.at[i], att.at[:, pl.ds(256 * i, 256)]) for i in range(4)]
    wait_all(first)
    done = []

    @pl.loop(0, FF2 // 128)
    def _(t):
        cols = aligned(t, 128)
        dd[cols, :] = dot(hidden[:, cols], cot[...], TN).astype(bf)

    for q in range(4):
        fx, fy = FLIPS_A[q]
        rows = aligned(yx ^ (fx + 2 * fy), 352)
        done.append(go.start(dd.at[rows, pl.ds(0, 512)], (gda_send if fx else gda_keep).at[pl.ds(352 * fy, 352)]))
        done.append(go.start(dd.at[rows, pl.ds(512, 512)], (gdb_send if fy else gdb_keep).at[pl.ds(352 * fx, 352)]))
    wait_all(second)
    part[...] = dot(hidden[256:512, :], wd[...], NN).astype(bf)
    done.append(go.start(part, part_hbm))
    out[...] = dot(hidden[0:256, :], wd[...], NN)
    done.append(go.start(out, own_hbm))
    wait_all(third)
    low = gres[...].astype(bf)

    @pl.loop(0, 4)
    def _(i):
        cols = aligned(i, 256)
        gw[cols, :] = dot(att[:, cols], low, TN).astype(bf)

    for q in range(4):
        fx, fy = FLIPS_A[q]
        j = yx ^ (fx + 2 * fy)
        for dst, c in ((keep_hbm, core), (send_hbm, 1 - core)):
            done.append(go.start(gw.at[aligned(j * 2 + c, 128)], dst.at[pl.ds(128 * (2 * fx + fy), 128)]))
    wait_all(done)


def finish(hidden, cot, cotp, att, gres, down):
    tall = ((256, 1024), f32)
    low = ((256, 1024), bf)
    half = ((512, 1024), bf)
    return call(
        finish_kernel, "finish",
        [low, tall] + [((704, 512), bf)] * 4 + [half] * 2,
        [((512, FF2), bf), half, low, tall, ((FF2, 1024), bf), tall, low, ((FF2, 1024), bf), ((1024, 1024), bf)],
        [34], 60, (hidden, cot, cotp, att, gres, *down), 32,
    )


def branch_kernel(part_hbm, gnown_hbm, res_hbm, cot_hbm, wo_hbm, gres_hbm, gatt_hbm,
                  part, gnown, res_ref, cot, wo, gres_ref, gatt, sems):
    go = Copies(sems)
    first = [
        go.start(a, b)
        for a, b in ((res_hbm, res_ref), (gnown_hbm, gnown), (part_hbm, part), (cot_hbm, cot))
    ]
    late = go.start(wo_hbm, wo)
    wait_all(first)
    res = res_ref[...]
    g = gnown[...] + part[...].astype(f32)
    c = res - jnp.mean(res, axis=-1, keepdims=True)
    r = lax.rsqrt(jnp.mean(c * c, axis=-1, keepdims=True) + NORM_EPS)
    xh = c * r
    d = r * (g - jnp.mean(g, axis=-1, keepdims=True) - xh * jnp.mean(g * xh, axis=-1, keepdims=True))
    gres = cot[...].astype(f32) + d
    gres_ref[...] = gres
    low = gres.astype(bf)
    done = [go.start(gres_ref, gres_hbm)]
    late.wait()
    ga = dot(low, wo[...], NT).astype(bf)
    for z in range(4):
        gatt[z] = ga[:, 256 * z : 256 * z + 256]
    done.append(go.start(gatt, gatt_hbm))
    wait_all(done)


def branch(part, gnown, res, cot, wo):
    tall = ((256, 1024), f32)
    low = ((256, 1024), bf)
    return call(
        branch_kernel, "branch", [tall, ((4, 256, 256), bf)],
        [low, tall, tall, low, ((1024, 1024), bf), tall, ((4, 256, 256), bf)],
        [7], 1, (part, gnown, res, cot, wo), 32,
    )


def update_kernel(coeff_ref, wide_ref, mg, mu, md, wg, wu, wd, *refs):
    outs, (gg, gu, gd, ng, nu, nd, og, ou, od), sems = refs[:9], refs[9:18], refs[18]
    coeff = coeff_ref[0]
    go = Copies(sems)
    done = []
    part = FF2 // 4

    def finish(i, grad, moment, weight, new_moment, new_weight):
        done.append(go.start(grad, outs[i]))
        moved = coeff * moment[...] + grad[...]
        new_moment[...] = moved
        done.append(go.start(new_moment, outs[3 + i]))
        new_weight[...] = (weight[...].astype(f32) - LEARN_RATE * moved).astype(bf)
        done.append(go.start(new_weight, outs[6 + i]))

    for i, (grad, moment, weight, nm, nw) in enumerate(((gg, mg, wg, ng, og), (gu, mu, wu, nu, ou))):
        for side in range(2):
            columns = wide_ref[:, FF2 * (2 * side + i) : FF2 * (2 * side + i + 1)].astype(f32)
            for j in range(4):
                low = part * (2 * j + side)
                grad[:, low : low + part] = columns[:, part * j : part * j + part]
        finish(i, grad, moment, weight, nm, nw)
    for j in range(3):
        rows = min(32, 88 - 32 * j)
        low = 4 * FF2 + 1024 * j
        gd[32 * j : 32 * j + rows, :] = wide_ref[:, low : low + 1024].astype(f32)[0:rows]
    finish(2, gd, md, wd, nd, od)
    wait_all(done)


def update(coeff, wide, moments, weights):
    shapes = [(32, 2 * FF2), (32, 2 * FF2), (88, 1024)]
    outs = [(s, f32) for s in shapes] * 2 + [(s, bf) for s in shapes]
    vmem = pl.BlockSpec(memory_space=pltpu.VMEM)
    return pl.pallas_call(
        update_kernel,
        out_shape=tuple(pltpu.HBM(*o) for o in outs),
        in_specs=[pl.BlockSpec(memory_space=pltpu.SMEM)] + [vmem] * 7,
        out_specs=(MAIN,) * 9,
        scratch_shapes=[pltpu.VMEM(*o) for o in outs] + [pltpu.SemaphoreType.DMA((9,))],
        compiler_params=pltpu.CompilerParams(vmem_limit_bytes=16 << 20),
        cost_estimate=pl.CostEstimate(flops=1 << 20, bytes_accessed=6 << 20, transcendentals=0),
        name="update",
    )(coeff, wide, *moments, *weights)


def swap(array, bit):
    return lax.ppermute(array, "dp", [(i, i ^ bit) for i in range(8)])


def shift(array, bits):
    return lax.ppermute(array, "ctx", [(i, i ^ bits) for i in range(4)])


def add_low(left, right):
    return (left.astype(f32) + right.astype(f32)).astype(bf)


def split_even(matrix):
    n = matrix.shape[1] // 8
    parts = [matrix[:, n * i : n * i + n] for i in range(8)]
    return jnp.concatenate(parts[0::2], axis=1), jnp.concatenate(parts[1::2], axis=1)


def tie(value, *anchors):
    return lax.optimization_barrier((value, *anchors))[0]


def fast_device(
    activations,
    block_ids,
    cotangent,
    w_query,
    w_key,
    w_value,
    w_out,
    w_gate,
    w_up,
    w_down,
    m_query,
    m_key,
    m_value,
    m_out,
    m_gate,
    m_up,
    m_down,
    clip_threshold,
    momentum_coeff,
):
    me = lax.axis_index("dp")
    z = lax.axis_index("ctx")
    core = me % 2
    _, span, width = activations.shape
    length = block_ids.shape[1]
    act = activations.reshape(span, width)
    cot = cotangent.reshape(span, width)
    act_other = swap(act, 1)
    cot_other = swap(cot, 1)
    g0, g1 = split_even(w_gate)
    u0, u1 = split_even(w_up)
    even = jnp.stack([g0, u0])
    odd = jnp.stack([g1, u1])
    flip = core == 1
    mine = jnp.where(flip, odd, even)
    other = swap(jnp.where(flip, even, odd), 1)
    out_rows = jnp.stack([w_out[:, :512], w_out[:, 512:]]).reshape(2, 32, 2, 256)
    wide = jnp.stack([mine, other], axis=1)
    wide = jnp.concatenate([wide, out_rows.transpose(0, 2, 1, 3)], axis=3)
    wide = lax.all_gather(wide, "ctx", axis=2, tiled=True).reshape(2, 256, FF2 + 256)
    padded = jnp.concatenate([act, w_down], axis=0)
    rows_all = lax.all_gather(padded, "ctx", axis=0, tiled=True)
    heads = jnp.stack(
        [
            jnp.concatenate([w[:, 256 * i : 256 * i + 256] for w in (w_query, w_key, w_value)], 1)
            for i in range(4)
        ]
    )
    heads = lax.all_to_all(heads, "ctx", 0, 0, tiled=True).reshape(128, 768)
    hx = swap(heads, 2)
    hy = swap(jnp.concatenate([heads, hx], axis=0), 4)
    four = jnp.concatenate([heads, hy[:128], hx, hy[128:]], axis=0)
    heads_rel = jnp.concatenate([four, swap(four, 1)], axis=0)
    cosine, sine = rotary_tables(jnp.arange(length, dtype=jnp.int32), HEAD_DIM)
    cosine = jnp.concatenate([cosine] * 4, axis=1)
    sine = jnp.concatenate([-sine, sine, -sine, sine], axis=1)
    ids = jnp.broadcast_to(block_ids, (8, length)).astype(f32)
    wide, act_other, cot_other, heads_rel, cosine, sine, ids = lax.optimization_barrier(
        (wide, act_other, cot_other, heads_rel, cosine, sine, ids)
    )

    wide_x, wide_y = swap(wide, 2), swap(wide, 4)
    wide_all = [wide, wide_x, wide_y, swap(wide_x[0], 4), swap(wide_y[1], 2)]
    down = jnp.concatenate([rows_all[344 * i + 256 : 344 * i + 344] for i in range(4)], axis=0)
    down_x, down_y = swap(down, 2), swap(down, 4)
    rows_all, *wide_all = lax.optimization_barrier((rows_all, *wide_all))
    normed, mixed, attended, totals, peaks, outs = attend(
        rows_all, heads_rel, cosine, sine, ids, wide_all
    )
    outs = swap(outs, 1)
    attended, down_x, down_y = lax.optimization_barrier((attended, down_x, down_y))
    down_all = [down, down_x, down_y, swap(down_x[:, :512], 4), swap(down_y[:, 512:], 2)]
    attended = lax.all_to_all(attended.reshape(4, span, 256), "ctx", 0, 0, tiled=True)
    attended_other = swap(tie(attended, *down_all[3:]), 1)
    part, back_own, residual, full_out, hidden, ga_keep, ga_send, gb_keep, gb_send = feed(
        attended, attended_other, act, act_other, cot, cot_other,
        wide_all, down_all, outs,
    )
    part = swap(part, 1)
    ga_send, gb_send, part = lax.optimization_barrier((ga_send, gb_send, part))
    ga_other = swap(ga_send, 2)
    gb_other = swap(gb_send, 4)
    grad_residual, grad_attended = branch(part, back_own, residual, cot, full_out)
    grad_attended = lax.all_to_all(grad_attended, "ctx", 0, 0, tiled=True).reshape(length, 256)
    (out_part, out_own, gda_keep, gda_send, gdb_keep, gdb_send, go_keep, go_send) = finish(
        hidden, cot, cot_other, attended, grad_residual, down_all
    )
    gda_other = swap(gda_send, 2)
    gdb_other = swap(gdb_send, 4)
    grad_attended, out_part = lax.optimization_barrier((grad_attended, out_part))
    layer_out = (residual + (out_own + swap(out_part, 1).astype(f32))).astype(bf)
    grad_mixed, grad_normed = attend_back(
        mixed, grad_attended, totals, cosine, sine, ids, heads_rel
    )
    grad_mixed = tie(grad_mixed, ga_other, gb_other)
    grad_heads = project_weights(grad_mixed, normed, go_keep, go_send)
    ga_keep, gb_keep, gda_keep, gdb_keep, grad_heads = lax.optimization_barrier(
        (ga_keep, gb_keep, gda_keep, gdb_keep, grad_heads)
    )
    grad_a = add_low(ga_keep, ga_other)
    grad_b = add_low(gb_keep, gb_other)
    grad_da = add_low(gda_keep, gda_other)
    grad_db = add_low(gdb_keep, gdb_other)
    grad_a = add_low(grad_a[:256], swap(grad_a[256:], 4))
    grad_b = add_low(grad_b[:256], swap(grad_b[256:], 2))
    grad_da = add_low(grad_da[:352], swap(grad_da[352:], 4))
    grad_db = add_low(grad_db[:352], swap(grad_db[352:], 2))
    def core_rows(which):
        return jnp.concatenate(
            [lax.dynamic_slice_in_dim(g, which * 128, 128, 0) for g in (grad_a, grad_b)], axis=1
        )

    own_half = core_rows(core)
    other_half = swap(core_rows(1 - core), 1)
    grad_d = jnp.concatenate([grad_da, grad_db], axis=1).reshape(4, 88, width)
    grad_d = jnp.pad(grad_d, ((0, 0), (0, 8), (0, 0))).reshape(4, 3, 32, width)
    grad_d = grad_d.transpose(0, 2, 1, 3).reshape(128, 3 * width)
    grad_wide = jnp.concatenate(
        [
            jnp.where(flip, other_half, own_half),
            jnp.where(flip, own_half, other_half),
            grad_d,
        ],
        axis=1,
    )
    grad_wide = lax.psum_scatter(grad_wide, "ctx", scatter_dimension=0, tiled=True)
    peaks = tie(peaks, ga_other)
    peaks = lax.all_to_all(
        jnp.broadcast_to(peaks[None], (32, 8, 128)), ("dp", "ctx"), 0, 0, tiled=True
    )
    head_peaks = jnp.max(peaks.reshape(8, 4, 8, 128), axis=0)[:, :4, 0].reshape(HEADS)
    grad_normed = lax.psum_scatter(grad_normed, "ctx", scatter_dimension=0, tiled=True)
    tokens_wide = act.astype(f32)
    unused, first_pull = jax.vjp(normalize, tokens_wide)
    input_grad = grad_residual + first_pull(grad_normed.astype(f32))[0]
    grad_heads = add_low(grad_heads[0], swap(grad_heads[1], 1))
    grad_heads = add_low(grad_heads[:256], swap(grad_heads[256:], 2))
    grad_heads = add_low(grad_heads[:128], swap(grad_heads[128:], 4))
    grad_heads = lax.all_to_all(grad_heads.reshape(4, 32, 768 + width), "ctx", 0, 0, tiled=True)
    big = update(
        momentum_coeff.reshape(1), grad_wide, (m_gate, m_up, m_down), (w_gate, w_up, w_down)
    )
    grad_heads, *big = lax.optimization_barrier((grad_heads, *big))
    grad_heads = grad_heads.astype(f32)
    parts = grad_heads[:, :, 768:]
    grad_out = parts[0] + parts[1] + (parts[2] + parts[3])
    grad_qkv = [
        jnp.concatenate([grad_heads[i, :, 256 * k : 256 * k + 256] for i in range(4)], axis=1)
        for k in range(3)
    ]
    weight_grads = (*grad_qkv, grad_out)
    moments = (m_query, m_key, m_value, m_out)
    new_moments = tuple(
        (momentum_coeff * moment + gradient for moment, gradient in zip(moments, weight_grads))
    )
    head_scale = jnp.sqrt(clip_threshold / jnp.maximum(head_peaks, clip_threshold))
    column_scale = jnp.repeat(head_scale, HEAD_DIM)
    rates = (LEARN_RATE, LEARN_RATE, LEARN_RATE, OUT_RATE)
    shard_list = (w_query, w_key, w_value, w_out)
    updated = [
        matrix.astype(jnp.float32) - rate * moment
        for matrix, moment, rate in zip(shard_list, new_moments, rates)
    ]
    updated[0] = updated[0] * column_scale[None, :]
    updated[1] = updated[1] * column_scale[None, :]
    updated = [matrix.astype(bf) for matrix in updated]
    return (
        layer_out[None],
        input_grad[None],
        *weight_grads,
        *big[:3],
        *new_moments,
        *big[3:6],
        *updated,
        *big[6:],
        head_peaks,
        head_scale,
    )


def solution(mesh):
    placed = (
        P("dp", "ctx", None),
        P("dp", None),
        P("dp", "ctx", None),
        P(("dp", "ctx"), None),
        P(("dp", "ctx"), None),
        P(("dp", "ctx"), None),
        P(("dp", "ctx"), None),
        P(("dp", "ctx"), None),
        P(("dp", "ctx"), None),
        P(("dp", "ctx"), None),
        P(("dp", "ctx"), None),
        P(("dp", "ctx"), None),
        P(("dp", "ctx"), None),
        P(("dp", "ctx"), None),
        P(("dp", "ctx"), None),
        P(("dp", "ctx"), None),
        P(("dp", "ctx"), None),
        P(),
        P(),
    )
    fits = mesh.shape["dp"] == 8 and mesh.shape["ctx"] == 4
    return jax.shard_map(
        fast_device if fits else per_device,
        mesh=mesh,
        in_specs=placed,
        out_specs=(
            P("dp", "ctx", None),
            P("dp", "ctx", None),
            P(("dp", "ctx"), None),
            P(("dp", "ctx"), None),
            P(("dp", "ctx"), None),
            P(("dp", "ctx"), None),
            P(("dp", "ctx"), None),
            P(("dp", "ctx"), None),
            P(("dp", "ctx"), None),
            P(("dp", "ctx"), None),
            P(("dp", "ctx"), None),
            P(("dp", "ctx"), None),
            P(("dp", "ctx"), None),
            P(("dp", "ctx"), None),
            P(("dp", "ctx"), None),
            P(("dp", "ctx"), None),
            P(("dp", "ctx"), None),
            P(("dp", "ctx"), None),
            P(("dp", "ctx"), None),
            P(("dp", "ctx"), None),
            P(("dp", "ctx"), None),
            P(("dp", "ctx"), None),
            P(("dp", "ctx"), None),
            P(),
            P(),
        ),
        check_vma=False,
    )
```

```python
import math

import jax
import jax.numpy as jnp
from jax import lax
from jax.experimental import pallas as pl
from jax.experimental.pallas import tpu as pltpu
from jax.sharding import PartitionSpec as P

HEADS = 16
HEAD_DIM = 64


NORM_EPS = 1e-05
ROPE_BASE = 10000.0
LEARN_RATE = 0.0001
OUT_RATE = 0.0016
MASK_FILL = -1e30


def normalize(values):
    centred = values - jnp.mean(values, axis=-1, keepdims=True)
    spread = jnp.mean(centred * centred, axis=-1, keepdims=True)
    return centred * lax.rsqrt(spread + NORM_EPS)


def rotary_tables(positions, head_width):
    half_width = head_width // 2
    frequency = ROPE_BASE ** (-(jnp.arange(half_width, dtype=jnp.float32) * 2.0 / head_width))
    angles = positions.astype(jnp.float32)[:, None] * frequency[None, :]
    return (jnp.cos(angles), jnp.sin(angles))


def rotate(vectors, cosine, sine_table):
    half_width = vectors.shape[-1] // 2
    first_half = vectors[..., :half_width]
    second = vectors[..., half_width:]
    cos_wide = cosine[:, None, :]
    sin_wide = sine_table[:, None, :]
    return jnp.concatenate(
        [first_half * cos_wide - second * sin_wide, second * cos_wide + first_half * sin_wide],
        axis=-1,
    )


def swiglu(gate_proj, up_proj):
    return jax.nn.silu(gate_proj) * up_proj


def project(left_rows, matrix):
    return jnp.dot(left_rows, matrix, preferred_element_type=jnp.float32)


def project_back(grad_rows, matrix):
    return lax.dot_general(
        grad_rows, matrix, (((1,), (1,)), ((), ())), preferred_element_type=jnp.float32
    )


def shard_gradient(left_rows, right_rows):
    return lax.psum_scatter(
        lax.dot_general(
            left_rows, right_rows, (((0,), (0,)), ((), ())), preferred_element_type=jnp.float32
        ),
        ("dp", "ctx"),
        scatter_dimension=0,
        tiled=True,
    )


def per_device(
    activations,
    block_ids,
    cotangent,
    w_query,
    w_key,
    w_value,
    w_out,
    w_gate,
    w_up,
    w_down,
    m_query,
    m_key,
    m_value,
    m_out,
    m_gate,
    m_up,
    m_down,
    clip_threshold,
    momentum_coeff,
):
    shard_list = (w_query, w_key, w_value, w_out, w_gate, w_up, w_down)
    gathered = (
        lax.all_gather(shard_list[0], ("dp", "ctx"), axis=0, tiled=True),
        lax.all_gather(shard_list[1], ("dp", "ctx"), axis=0, tiled=True),
        lax.all_gather(shard_list[2], ("dp", "ctx"), axis=0, tiled=True),
        lax.all_gather(shard_list[3], ("dp", "ctx"), axis=0, tiled=True),
        lax.all_gather(shard_list[4], ("dp", "ctx"), axis=0, tiled=True),
        lax.all_gather(shard_list[5], ("dp", "ctx"), axis=0, tiled=True),
        lax.all_gather(shard_list[6], ("dp", "ctx"), axis=0, tiled=True),
    )
    full_query, full_key, full_value, full_out, full_gate, full_up, full_down = gathered
    seq_count, span_len, model_width = activations.shape
    ctx_place = lax.axis_index("ctx")
    positions = ctx_place * span_len + jnp.arange(span_len, dtype=jnp.int32)
    cosine, sine_table = rotary_tables(positions, HEAD_DIM)
    score_scale = 1.0 / math.sqrt(HEAD_DIM)

    def split_heads(matrix):
        return matrix.reshape(seq_count, span_len, HEADS, HEAD_DIM)

    tokens_flat = activations.astype(jnp.float32).reshape(-1, model_width)
    normed = normalize(tokens_flat).astype(jnp.bfloat16)
    queries = rotate(split_heads(project(normed, full_query)), cosine, sine_table).astype(
        jnp.bfloat16
    )
    key_rot = rotate(split_heads(project(normed, full_key)), cosine, sine_table).astype(
        jnp.bfloat16
    )
    value_rot = split_heads(project(normed, full_value)).astype(jnp.bfloat16)
    key_all, value_all = (
        lax.all_gather(key_rot, "ctx", axis=1, tiled=True),
        lax.all_gather(value_rot, "ctx", axis=1, tiled=True),
    )
    query_ids = lax.dynamic_slice_in_dim(block_ids, ctx_place * span_len, span_len, 1)
    allowed = (block_ids[:, None, :] <= query_ids[:, :, None])[:, None]

    def masked_scores():
        scores = (
            jnp.einsum("sqhd,skhd->shqk", queries, key_all, preferred_element_type=jnp.float32)
            * score_scale
        )
        return jnp.where(allowed, scores, MASK_FILL)

    masked = masked_scores()
    local_peaks = jnp.max(masked, axis=(0, 2, 3))
    row_top = jnp.max(masked, axis=-1, keepdims=True)
    log_total = row_top + jnp.log(jnp.sum(jnp.exp(masked - row_top), axis=-1, keepdims=True))
    probs_low = jnp.exp(masked - log_total).astype(jnp.bfloat16)
    attended = jnp.einsum(
        "shqk,skhd->sqhd", probs_low, value_all, preferred_element_type=jnp.float32
    )
    attended_low = attended.reshape(-1, model_width).astype(jnp.bfloat16)
    head_peaks = lax.pmax(local_peaks, ("dp", "ctx"))
    residual = tokens_flat + project(attended_low, full_out)
    normed2 = normalize(residual).astype(jnp.bfloat16)
    gate_proj = project(normed2, full_gate)
    up_proj = project(normed2, full_up)
    hidden_low = swiglu(gate_proj, up_proj).astype(jnp.bfloat16)
    layer_out = (
        (residual + project(hidden_low, full_down))
        .astype(jnp.bfloat16)
        .reshape(seq_count, span_len, model_width)
    )
    back_weights = (
        lax.all_gather(shard_list[0], ("dp", "ctx"), axis=0, tiled=True),
        lax.all_gather(shard_list[1], ("dp", "ctx"), axis=0, tiled=True),
        lax.all_gather(shard_list[2], ("dp", "ctx"), axis=0, tiled=True),
        lax.all_gather(shard_list[3], ("dp", "ctx"), axis=0, tiled=True),
        lax.all_gather(shard_list[4], ("dp", "ctx"), axis=0, tiled=True),
        lax.all_gather(shard_list[5], ("dp", "ctx"), axis=0, tiled=True),
        lax.all_gather(shard_list[6], ("dp", "ctx"), axis=0, tiled=True),
    )
    back_query, back_key, back_value, back_out, back_gate, back_up, back_down = back_weights
    grad_rows = cotangent.reshape(-1, model_width)
    grad_hidden = project_back(grad_rows, back_down)
    unused, gate_pull = jax.vjp(swiglu, gate_proj, up_proj)
    grad_gate_wide, grad_up_wide = gate_pull(grad_hidden)
    grad_gate_low = grad_gate_wide.astype(jnp.bfloat16)
    grad_up_low = grad_up_wide.astype(jnp.bfloat16)
    grad_normed2 = project_back(grad_gate_low, back_gate) + project_back(grad_up_low, back_up)
    unused, second_pull = jax.vjp(normalize, residual)
    grad_residual = grad_rows.astype(jnp.float32) + second_pull(grad_normed2)[0]
    grad_branch = grad_residual.astype(jnp.bfloat16)
    grad_attended = split_heads(project_back(grad_branch, back_out).astype(jnp.bfloat16))
    masked = masked_scores()
    probs = jnp.exp(masked - log_total)
    probs_again = probs.astype(jnp.bfloat16)
    grad_values_all = jnp.einsum(
        "shqk,sqhd->skhd", probs_again, grad_attended, preferred_element_type=jnp.float32
    )
    grad_probs = jnp.einsum(
        "sqhd,skhd->shqk", grad_attended, value_all, preferred_element_type=jnp.float32
    )
    score_grad = (
        probs * (grad_probs - jnp.sum(probs * grad_probs, axis=-1, keepdims=True))
    ).astype(jnp.bfloat16)
    grad_queries = (
        jnp.einsum("shqk,skhd->sqhd", score_grad, key_all, preferred_element_type=jnp.float32)
        * score_scale
    )
    grad_keys_all = (
        jnp.einsum("shqk,sqhd->skhd", score_grad, queries, preferred_element_type=jnp.float32)
        * score_scale
    )
    grad_keys, grad_values = (
        lax.psum_scatter(
            grad_keys_all.astype(jnp.bfloat16), "ctx", scatter_dimension=1, tiled=True
        ).astype(jnp.float32),
        lax.psum_scatter(
            grad_values_all.astype(jnp.bfloat16), "ctx", scatter_dimension=1, tiled=True
        ).astype(jnp.float32),
    )
    grad_query_low = (
        rotate(grad_queries, cosine, -sine_table).reshape(-1, model_width).astype(jnp.bfloat16)
    )
    grad_key_low = (
        rotate(grad_keys, cosine, -sine_table).reshape(-1, model_width).astype(jnp.bfloat16)
    )
    grad_value_low = grad_values.reshape(-1, model_width).astype(jnp.bfloat16)
    grad_normed = (
        project_back(grad_query_low, back_query)
        + project_back(grad_key_low, back_key)
        + project_back(grad_value_low, back_value)
    )
    unused, first_pull = jax.vjp(normalize, tokens_flat)
    input_grad = (grad_residual + first_pull(grad_normed)[0]).reshape(
        seq_count, span_len, model_width
    )
    weight_grads = (
        shard_gradient(normed, grad_query_low),
        shard_gradient(normed, grad_key_low),
        shard_gradient(normed, grad_value_low),
        shard_gradient(attended_low, grad_branch),
        shard_gradient(normed2, grad_gate_low),
        shard_gradient(normed2, grad_up_low),
        shard_gradient(hidden_low, grad_rows),
    )
    moments = (m_query, m_key, m_value, m_out, m_gate, m_up, m_down)
    new_moments = tuple(
        (momentum_coeff * moment + gradient for moment, gradient in zip(moments, weight_grads))
    )
    head_scale = jnp.sqrt(clip_threshold / jnp.maximum(head_peaks, clip_threshold))
    column_scale = jnp.repeat(head_scale, HEAD_DIM)
    rates = (LEARN_RATE, LEARN_RATE, LEARN_RATE, OUT_RATE, LEARN_RATE, LEARN_RATE, LEARN_RATE)
    updated = [
        matrix.astype(jnp.float32) - rate * moment
        for matrix, moment, rate in zip(shard_list, new_moments, rates)
    ]
    updated[0] = updated[0] * column_scale[None, :]
    updated[1] = updated[1] * column_scale[None, :]
    updated = [matrix.astype(jnp.bfloat16) for matrix in updated]
    return (
        layer_out,
        input_grad,
        weight_grads[0],
        weight_grads[1],
        weight_grads[2],
        weight_grads[3],
        weight_grads[4],
        weight_grads[5],
        weight_grads[6],
        new_moments[0],
        new_moments[1],
        new_moments[2],
        new_moments[3],
        new_moments[4],
        new_moments[5],
        new_moments[6],
        updated[0],
        updated[1],
        updated[2],
        updated[3],
        updated[4],
        updated[5],
        updated[6],
        head_peaks,
        head_scale,
    )


f32=jnp.float32; bf=jnp.bfloat16
NT=(((1,),(1,)),((),())); TN=(((0,),(0,)),((),())); NN=(((1,),(0,)),((),()))
FF2=1408
FFP=1536
FLIPS_A=((0,0),(1,0),(0,1),(1,1))
FLIPS_B=((0,0),(0,1),(1,0),(1,1))
MAIN=pl.BlockSpec(memory_space=pltpu.HBM)
S=jax.ShapeDtypeStruct


def dot(a, b, dims):
    return lax.dot_general(a, b, dims, preferred_element_type=f32)


def aligned(i, m):
    return pl.ds(pl.multiple_of(i * m, m), m)


class Copies:
    def __init__(self, sems):
        self.sems = sems
        self.count = 0

    def start(self, source, target):
        copy = pltpu.make_async_copy(source, target, self.sems.at[self.count])
        self.count += 1
        copy.start()
        return copy


def wait_all(copies):
    for copy in copies:
        copy.wait()


def call(kernel, name, outs, scratch, sems, flops, args, limit, free=0):
    return pl.pallas_call(
        kernel,
        out_shape=tuple(pltpu.HBM(*o) for o in outs),
        in_specs=[pl.BlockSpec(memory_space=pl.ANY)] * free + [MAIN] * (len(args) - free),
        out_specs=(MAIN,) * len(outs),
        scratch_shapes=[pltpu.VMEM(*s) for s in scratch] + [pltpu.SemaphoreType.DMA(n if isinstance(n, tuple) else (n,)) for n in sems],
        compiler_params=pltpu.CompilerParams(vmem_limit_bytes=limit << 20),
        cost_estimate=pl.CostEstimate(flops=flops << 30, bytes_accessed=8 << 20, transcendentals=0),
        name=name,
    )(*args[:free], *(pltpu.with_memory_space_constraint(arg, pltpu.HBM) for arg in args[free:]))


def place_of(p):
    return lax.axis_index("dp") ^ ((p >> 2 & 1) | (p >> 1 & 1) << 1 | (p & 1) << 2)


def turn(values, cosine, signed_sine):
    lane = lax.broadcasted_iota(jnp.int32, cosine.shape, 1)
    first = lane % 64 < 32
    parts = []
    for j in range(values.shape[1] // 128):
        part = values[:, 128 * j : 128 * j + 128]
        partner = jnp.where(first, pltpu.roll(part, 96, 1), pltpu.roll(part, 32, 1))
        parts.append(part * cosine + partner * signed_sine)
    return jnp.concatenate(parts, axis=1)


def layer_norm(x):
    c = x - jnp.mean(x, axis=-1, keepdims=True)
    v = jnp.mean(c * c, axis=-1, keepdims=True)
    return c * lax.rsqrt(v + NORM_EPS)


def wide_pieces(own, by_x, by_y, a_far, b_far):
    return ([own.at[0], by_x.at[0], by_y.at[0], a_far], [own.at[1], by_y.at[1], by_x.at[1], b_far])


def down_pieces(own, by_x, by_y, a_far, b_far):
    low, high = pl.ds(0, 512), pl.ds(512, 512)
    return ([own.at[:, low], by_x.at[:, low], by_y.at[:, low], a_far],
            [own.at[:, high], by_y.at[:, high], by_x.at[:, high], b_far])


def attend_kernel(*refs):
    rows_hbm, weight_hbm, cos_hbm, sin_hbm, id_hbm = refs[:5]
    pieces = sum(wide_pieces(*refs[5:10]), [])
    normed_hbm, mixed_hbm, attended_hbm, total_hbm, peak_hbm, outs_hbm = refs[10:16]
    (act, weight, cos_ref, sin_ref, ids, id_col, normed, mixed_ref, attended, value_t, total_ref,
     peak_ref, outs, sems) = refs[16:]
    n = normed.shape[0]
    go = Copies(sems)
    early = [go.start(rows_hbm.at[pl.ds(344 * i, 256)], act.at[pl.ds(256 * i, 256)]) for i in range(4)]
    middle = [
        go.start(weight_hbm.at[pl.ds(128 * p, 128)], weight.at[aligned(place_of(p), 128)])
        for p in range(8)
    ]
    middle += [go.start(cos_hbm, cos_ref), go.start(sin_hbm, sin_ref), go.start(id_hbm, ids)]
    packs = [go.start(piece.at[:, pl.ds(FF2, 256)], outs.at[i]) for i, piece in enumerate(pieces)]
    wait_all(early)

    def norm(i):
        rows = aligned(i, 256)
        normed[rows, :] = layer_norm(act[rows, :].astype(f32)).astype(bf)

    def mix(i):
        rows = aligned(i, 256)
        mixed = dot(normed[rows, :], weight[...], NN)
        cosine = cos_ref[rows, :]
        sine = sin_ref[rows, :]
        queries = turn(mixed[:, 0:256], cosine, sine).astype(bf)
        mixed_ref[rows, 0:256] = (queries.astype(f32) * 0.125).astype(bf)
        mixed_ref[rows, 256:512] = turn(mixed[:, 256:512], cosine, sine).astype(bf)
        value = mixed[:, 512:768]
        mixed_ref[rows, 512:768] = value.astype(bf)
        value_t[:, rows] = value.T.astype(bf)

    norm(0)
    wait_all(middle)
    wait_all(packs)
    id_col[...] = jnp.broadcast_to(ids[0:1, :], (128, n)).T

    @pl.loop(0, n // 256 - 1)
    def _(i):
        mix(i)
        norm(i + 1)

    mix(n // 256 - 1)
    late = [go.start(normed, normed_hbm), go.start(outs, outs_hbm)]
    late.append(go.start(mixed_ref, mixed_hbm))
    peak_ref[...] = jnp.zeros_like(peak_ref)
    total_ref[...] = jnp.zeros_like(total_ref)

    @pl.loop(0, 2)
    def _(pair):
        lanes = pl.multiple_of(pair * 128, 128)
        lane = lax.broadcasted_iota(jnp.int32, (256, 128), 1)
        best = [None, None]
        for i in range(4):
            width = min(256 * (i + 2), 1024)
            low = 256 * i
            both = mixed_ref[low : low + 256, pl.ds(lanes, 128)]
            keys = mixed_ref[0:width, pl.ds(pl.multiple_of(256 + lanes, 128), 128)]
            values = value_t[pl.ds(lanes, 128), 0:width]
            ok = id_col[low:width, 0:1] <= ids[0:1, low : low + 256]
            outs = []
            for half in range(2):
                q = jnp.where(lane // 64 == half, both, jnp.zeros_like(both))
                s = dot(keys, q, NT)
                tail = jnp.where(ok, s[low:width], MASK_FILL)
                top = jnp.max(tail, axis=0, keepdims=True)
                if i:
                    top = jnp.maximum(top, jnp.max(s[0:low], axis=0, keepdims=True))
                    s = jnp.concatenate([s[0:low], tail], axis=0)
                else:
                    s = tail
                e = jnp.exp(s - top)
                total = jnp.sum(e, axis=0, keepdims=True)
                o = dot(values, e.astype(bf), NN)
                outs.append(o[64 * half : 64 * half + 64] * (1.0 / total))
                total_ref[pl.ds(pair * 2 + half, 1), low : low + 256] = top + jnp.log(total)
                m = jnp.max(top, axis=1, keepdims=True)
                best[half] = m if best[half] is None else jnp.maximum(best[half], m)
            o = jnp.concatenate(outs, axis=0).T.astype(bf)
            attended[low : low + 256, pl.ds(lanes, 128)] = o
        for half in range(2):
            peak_ref[pl.ds(pair * 2 + half, 1), :] = jnp.broadcast_to(best[half], (1, 128))

    late.append(go.start(attended, attended_hbm))
    late.append(go.start(total_ref, total_hbm))
    late.append(go.start(peak_ref, peak_hbm))
    wait_all(late)


def attend(rows_all, weight, cosine, sine, ids, pieces):
    n = cosine.shape[0]
    return call(
        attend_kernel, "attend",
        [((n, 1024), bf), ((n, 768), bf), ((n, 256), bf), ((8, n), f32), ((8, 128), f32),
         ((8, 256, 256), bf)],
        [((n, 1024), bf), ((1024, 768), bf), ((n, 128), f32), ((n, 128), f32), ((8, n), f32),
         ((n, 128), f32), ((n, 1024), bf), ((n, 768), bf), ((n, 256), bf), ((256, n), bf),
         ((8, n), f32), ((8, 128), f32), ((8, 256, 256), bf)],
        [29], 4, (rows_all, weight, cosine, sine, ids, *pieces), 28,
    )


def attend_back_kernel(ga_hbm, mixed_hbm, total_hbm, cos_hbm, sin_hbm, id_hbm, weight_hbm,
                       gm_hbm, gn_hbm,
                       mixed_ref, ga_ref, total_ref, cos_ref, sin_ref, ids, weight,
                       gm_ref, gn_ref, gk_acc, gv_acc, key_t, id_col, sems):
    n = ga_ref.shape[0]
    go = Copies(sems)
    early = [
        go.start(a, b)
        for a, b in ((mixed_hbm, mixed_ref), (ga_hbm, ga_ref), (total_hbm, total_ref),
                     (id_hbm, ids), (cos_hbm, cos_ref), (sin_hbm, sin_ref))
    ]
    late = [
        go.start(weight_hbm.at[pl.ds(128 * p, 128)], weight.at[aligned(place_of(p), 128)])
        for p in range(8)
    ]
    gk_acc[...] = jnp.zeros_like(gk_acc)
    gv_acc[...] = jnp.zeros_like(gv_acc)
    wait_all(early)
    id_col[...] = jnp.broadcast_to(ids[0:1, :], (128, n)).T

    @pl.loop(0, n // 256)
    def _(i):
        rows = aligned(i, 256)
        key_t[:, rows] = mixed_ref[rows, 256:512].astype(f32).T.astype(bf)

    @pl.loop(0, 2)
    def _(pair):
        lanes = pl.multiple_of(pair * 128, 128)
        lane = lax.broadcasted_iota(jnp.int32, (256, 128), 1)
        sub = lax.broadcasted_iota(jnp.int32, (128, 256), 0)
        for i in range(4):
            width = min(256 * (i + 2), 1024)
            low = 256 * i
            k = mixed_ref[0:width, pl.ds(pl.multiple_of(256 + lanes, 128), 128)]
            v = mixed_ref[0:width, pl.ds(pl.multiple_of(512 + lanes, 128), 128)]
            q_all = mixed_ref[low : low + 256, pl.ds(lanes, 128)]
            g_all = ga_ref[low : low + 256, pl.ds(lanes, 128)]
            kt = key_t[pl.ds(lanes, 128), 0:width]
            ok = id_col[low:width, 0:1] <= ids[0:1, low : low + 256]

            def one(half, gq):
                mine = lane // 64 == half
                q = jnp.where(mine, q_all, jnp.zeros_like(q_all))
                g = jnp.where(mine, g_all, jnp.zeros_like(g_all))
                s = dot(k, q, NT) - total_ref[pl.ds(pair * 2 + half, 1), low : low + 256]
                tail = jnp.where(ok, s[low:width], MASK_FILL)
                s = jnp.concatenate([s[0:low], tail], axis=0) if i else tail
                p = jnp.exp(s)
                t = p * dot(v, g, NT)
                delta = jnp.sum(t, axis=0, keepdims=True)
                ds = (t - p * delta).astype(bf)
                gv_acc[0:width, pl.ds(lanes, 128)] += dot(p.astype(bf), g, NN)
                gk_acc[0:width, pl.ds(lanes, 128)] += dot(ds, q, NN)
                return jnp.where(sub // 64 == half, dot(kt, ds, NN), gq)

            gq = one(1, one(0, jnp.zeros((128, 256), f32)))
            gq = gq.T * 0.125
            cosine = cos_ref[low : low + 256, :]
            sine = sin_ref[low : low + 256, :]
            gm_ref[low : low + 256, pl.ds(lanes, 128)] = turn(gq, cosine, -sine).astype(bf)

    wait_all(late)

    @pl.loop(0, n // 256)
    def _(i):
        rows = aligned(i, 256)
        cosine = cos_ref[rows, :]
        sine = sin_ref[rows, :]
        gm_ref[rows, 256:512] = turn(gk_acc[rows, :], cosine, -sine).astype(bf)
        gm_ref[rows, 512:768] = gv_acc[rows, :].astype(bf)
        gn_ref[rows, :] = dot(gm_ref[rows, :], weight[...], NT).astype(bf)
        copy = pltpu.make_async_copy(gn_ref.at[rows], gn_hbm.at[rows], sems.at[14 + i])
        copy.start()

    out = pltpu.make_async_copy(gm_ref, gm_hbm, sems.at[18])
    out.start()
    for i in range(4):
        rows = pl.ds(256 * i, 256)
        pltpu.make_async_copy(gn_ref.at[rows], gn_hbm.at[rows], sems.at[14 + i]).wait()
    out.wait()


def attend_back(mixed, ga, total, cosine, sine, ids, weight):
    n = ga.shape[0]
    return call(
        attend_back_kernel, "attend_back",
        [((n, 768), bf), ((n, 1024), bf)],
        [((n, 768), bf), ((n, 256), bf), ((8, n), f32), ((n, 128), f32), ((n, 128), f32),
         ((8, n), f32), ((1024, 768), bf), ((n, 768), bf), ((n, 1024), bf), ((n, 256), f32),
         ((n, 256), f32), ((256, n), bf), ((n, 128), f32)],
        [19], 0, (ga, mixed, total, cosine, sine, ids, weight), 32, 1,
    )


def weights_kernel(gm_hbm, normed_hbm, okeep_hbm, osend_hbm, keep_hbm, send_hbm,
                   gm_ref, normed_ref, gw, okeep, osend, sems):
    go = Copies(sems)
    first = [go.start(gm_hbm, gm_ref), go.start(normed_hbm, normed_ref)]
    second = [go.start(okeep_hbm, okeep), go.start(osend_hbm, osend)]
    wait_all(first + second)
    cols = pl.ds(768, 1024)
    late = [go.start(okeep, keep_hbm.at[:, cols]), go.start(osend, send_hbm.at[:, cols])]

    @pl.loop(0, 4)
    def _(i):
        cols = aligned(i, 256)
        gw[cols, :] = dot(normed_ref[:, cols], gm_ref[...], TN).astype(bf)

    late += [
        go.start(gw.at[aligned(place_of(p), 128)],
                 (keep_hbm if p < 4 else send_hbm).at[pl.ds(128 * (p % 4), 128), pl.ds(0, 768)])
        for p in range(8)
    ]
    wait_all(late)


def project_weights(gm, normed, okeep, osend):
    n = gm.shape[0]
    return call(
        weights_kernel, "project_weights", [((512, 1792), bf)] * 2,
        [((n, 768), bf), ((n, 1024), bf), ((1024, 768), bf), ((512, 1024), bf), ((512, 1024), bf)],
        [14], 1, (gm, normed, okeep, osend), 24,
    )


def feed_kernel(*refs):
    att_hbm, attp_hbm, act_hbm, actp_hbm, cot_hbm, cotp_hbm = refs[:6]
    a_in, b_in = wide_pieces(*refs[6:11])
    da_in, db_in = down_pieces(*refs[11:16])
    outs = refs[16]
    part_hbm, gnown_hbm, res_hbm, wo_hbm, h_hbm = refs[17:22]
    ga_keep, ga_send, gb_keep, gb_send = refs[22:26]
    (wg, wu, wd, wo, att, act, n2, n2t, cot, res_ref, gn_acc, part, dg, du, hidden,
     sems, osem, tsem) = refs[26:]
    me = lax.axis_index("dp")
    core = me % 2
    yx = me // 2
    go = Copies(sems)
    small = []
    for base, src, own in ((0, att_hbm, act_hbm), (256, attp_hbm, actp_hbm)):
        rows = pl.ds(base, 256)
        small += [go.start(src.at[i], att.at[rows, pl.ds(256 * i, 256)]) for i in range(4)]
        small.append(go.start(own, act.at[rows]))
    places = []
    for p in range(4):
        (ax, ay), (bx, by) = FLIPS_A[p], FLIPS_B[p]
        places.append((yx ^ (ax + 2 * ay), yx ^ (bx + 2 * by)))
    for p, (ja, jb) in enumerate(places):
        for which, src, j, col in ((0, a_in[p], ja, 0), (1, b_in[p], jb, 512)):
            for half in range(2):
                cols = pl.ds(col + 256 * half, 256)
                rows = pl.ds(128 * half, 128)
                small.append(go.start(src.at[rows, pl.ds(FF2, 256)], wo.at[aligned(j * 2 + core, 128), cols]))
                small.append(go.start(outs.at[4 * which + p, rows], wo.at[aligned(j * 2 + 1 - core, 128), cols]))
    big = []
    for p, (ja, jb) in enumerate(places):
        for src, dst, j in ((a_in[p], wg, ja), (b_in[p], wu, jb)):
            for half, c in ((0, core), (1, 1 - core)):
                big.append(go.start(src.at[pl.ds(128 * half, 128), pl.ds(0, FF2)],
                                    dst.at[aligned(j * 2 + c, 128), pl.ds(0, FF2)]))
    big += [go.start(cot_hbm, cot.at[pl.ds(0, 256)]), go.start(cotp_hbm, cot.at[pl.ds(256, 256)])]
    for p, (ja, jb) in enumerate(places):
        big.append(go.start(da_in[p], wd.at[aligned(ja, 352), pl.ds(0, 512)]))
        big.append(go.start(db_in[p], wd.at[aligned(jb, 352), pl.ds(512, 512)]))
    wg[:, FF2:FFP] = jnp.zeros((1024, FFP - FF2), bf)
    wu[:, FF2:FFP] = jnp.zeros((1024, FFP - FF2), bf)
    wd[FF2:FFP, :] = jnp.zeros((FFP - FF2, 1024), bf)
    gn_acc[...] = jnp.zeros_like(gn_acc)
    wait_all(small)
    ogo = Copies(osem)
    done = [ogo.start(wo, wo_hbm)]

    @pl.loop(0, 2)
    def _(i):
        rows = aligned(i, 256)
        res = act[rows, :].astype(f32) + dot(att[rows, :], wo[...], NN)
        res_ref[rows, :] = res
        n = layer_norm(res)
        n2[rows, :] = n.astype(bf)
        n2t[:, rows] = n.T.astype(bf)

    done.append(ogo.start(res_ref.at[pl.ds(0, 256)], res_hbm))
    wait_all(big)

    def tile_copies(t, width):
        copies = []
        cols = pl.ds(pl.multiple_of(t * 256, 256), width)
        for q in range(4):
            fx, fy = FLIPS_A[q]
            rows = aligned(yx ^ (fx + 2 * fy), 256)
            for k, src, dst, slot in ((0, dg, ga_send if fx else ga_keep, fy), (1, du, gb_send if fy else gb_keep, fx)):
                copies.append(pltpu.make_async_copy(
                    src.at[rows, cols], dst.at[pl.ds(256 * slot, 256), cols], tsem.at[t, 2 * q + k]))
        copies.append(pltpu.make_async_copy(hidden.at[:, cols], h_hbm.at[:, cols], tsem.at[t, 8]))
        return copies

    last = FFP // 256 - 1

    @pl.loop(0, last + 1)
    def _(t):
        cols = aligned(t, 256)
        g = dot(n2[...], wg[:, cols], NN)
        u = dot(n2[...], wu[:, cols], NN)
        gh = dot(cot[...], wd[cols, :], NT)
        sig = 1.0 / (1.0 + jnp.exp(-g))
        silu = g * sig
        hidden[:, cols] = (silu * u).astype(bf)
        gu = (gh * silu).astype(bf)
        gg = (gh * u * (sig + silu * (1.0 - sig))).astype(bf)
        dg[:, cols] = dot(n2t[...], gg, NN).astype(bf)
        du[:, cols] = dot(n2t[...], gu, NN).astype(bf)

        @pl.when(t < last)
        def _():
            for copy in tile_copies(t, 256):
                copy.start()

        gn_acc[...] += dot(gg, wg[:, cols], NT) + dot(gu, wu[:, cols], NT)

    ends = tile_copies(last, FF2 - 256 * last)
    for copy in ends:
        copy.start()
    part[...] = gn_acc[256:512, :].astype(bf)
    done.append(ogo.start(part, part_hbm))
    done.append(ogo.start(gn_acc.at[pl.ds(0, 256)], gnown_hbm))
    for t in range(last):
        wait_all(tile_copies(t, 256))
    wait_all(ends)
    wait_all(done)


def feed(att, attp, act, actp, cot, cotp, wide, down, outs):
    big = [((1024, FFP), bf), ((1024, FFP), bf), ((FFP, 1024), bf)]
    return call(
        feed_kernel, "feed",
        [((256, 1024), bf), ((256, 1024), f32), ((256, 1024), f32), ((1024, 1024), bf), ((512, FF2), bf)]
        + [((512, FF2), bf)] * 4,
        big + [((1024, 1024), bf), ((512, 1024), bf), ((512, 1024), bf), ((512, 1024), bf), ((1024, 512), bf),
               ((512, 1024), bf), ((512, 1024), f32), ((512, 1024), f32), ((256, 1024), bf)]
        + big[:2] + [((512, FFP), bf)],
        [68, 4, (6, 9)], 12, (att, attp, act, actp, cot, cotp, *wide, *down, outs), 50, 2,
    )


def finish_kernel(*refs):
    h_hbm, cot_hbm, cotp_hbm, att_hbm, gres_hbm = refs[:5]
    da_in, db_in = down_pieces(*refs[5:10])
    part_hbm, own_hbm, gda_keep, gda_send, gdb_keep, gdb_send, keep_hbm, send_hbm = refs[10:18]
    hidden, cot, att, gres, wd, out, part, dd, gw, sems = refs[18:]
    me = lax.axis_index("dp")
    core = me % 2
    yx = me // 2
    go = Copies(sems)
    first = [go.start(h_hbm, hidden), go.start(cot_hbm, cot.at[pl.ds(0, 256)]),
             go.start(cotp_hbm, cot.at[pl.ds(256, 256)])]
    second = []
    for p in range(4):
        (ax, ay), (bx, by) = FLIPS_A[p], FLIPS_B[p]
        second.append(go.start(da_in[p], wd.at[aligned(yx ^ (ax + 2 * ay), 352), pl.ds(0, 512)]))
        second.append(go.start(db_in[p], wd.at[aligned(yx ^ (bx + 2 * by), 352), pl.ds(512, 512)]))
    third = [go.start(gres_hbm, gres)]
    third += [go.start(att_hbm.at[i], att.at[:, pl.ds(256 * i, 256)]) for i in range(4)]
    wait_all(first)
    done = []

    @pl.loop(0, FF2 // 128)
    def _(t):
        cols = aligned(t, 128)
        dd[cols, :] = dot(hidden[:, cols], cot[...], TN).astype(bf)

    for q in range(4):
        fx, fy = FLIPS_A[q]
        rows = aligned(yx ^ (fx + 2 * fy), 352)
        done.append(go.start(dd.at[rows, pl.ds(0, 512)], (gda_send if fx else gda_keep).at[pl.ds(352 * fy, 352)]))
        done.append(go.start(dd.at[rows, pl.ds(512, 512)], (gdb_send if fy else gdb_keep).at[pl.ds(352 * fx, 352)]))
    wait_all(second)
    part[...] = dot(hidden[256:512, :], wd[...], NN).astype(bf)
    done.append(go.start(part, part_hbm))
    out[...] = dot(hidden[0:256, :], wd[...], NN)
    done.append(go.start(out, own_hbm))
    wait_all(third)
    low = gres[...].astype(bf)

    @pl.loop(0, 4)
    def _(i):
        cols = aligned(i, 256)
        gw[cols, :] = dot(att[:, cols], low, TN).astype(bf)

    for q in range(4):
        fx, fy = FLIPS_A[q]
        j = yx ^ (fx + 2 * fy)
        for dst, c in ((keep_hbm, core), (send_hbm, 1 - core)):
            done.append(go.start(gw.at[aligned(j * 2 + c, 128)], dst.at[pl.ds(128 * (2 * fx + fy), 128)]))
    wait_all(done)


def finish(hidden, cot, cotp, att, gres, down):
    tall = ((256, 1024), f32)
    low = ((256, 1024), bf)
    half = ((512, 1024), bf)
    return call(
        finish_kernel, "finish",
        [low, tall] + [((704, 512), bf)] * 4 + [half] * 2,
        [((512, FF2), bf), half, low, tall, ((FF2, 1024), bf), tall, low, ((FF2, 1024), bf), ((1024, 1024), bf)],
        [34], 60, (hidden, cot, cotp, att, gres, *down), 32,
    )


def branch_kernel(part_hbm, gnown_hbm, res_hbm, cot_hbm, wo_hbm, gres_hbm, gatt_hbm,
                  part, gnown, res_ref, cot, wo, gres_ref, gatt, sems):
    go = Copies(sems)
    first = [
        go.start(a, b)
        for a, b in ((res_hbm, res_ref), (gnown_hbm, gnown), (part_hbm, part), (cot_hbm, cot))
    ]
    late = go.start(wo_hbm, wo)
    wait_all(first)
    res = res_ref[...]
    g = gnown[...] + part[...].astype(f32)
    c = res - jnp.mean(res, axis=-1, keepdims=True)
    r = lax.rsqrt(jnp.mean(c * c, axis=-1, keepdims=True) + NORM_EPS)
    xh = c * r
    d = r * (g - jnp.mean(g, axis=-1, keepdims=True) - xh * jnp.mean(g * xh, axis=-1, keepdims=True))
    gres = cot[...].astype(f32) + d
    gres_ref[...] = gres
    low = gres.astype(bf)
    done = [go.start(gres_ref, gres_hbm)]
    late.wait()
    ga = dot(low, wo[...], NT).astype(bf)
    for z in range(4):
        gatt[z] = ga[:, 256 * z : 256 * z + 256]
    done.append(go.start(gatt, gatt_hbm))
    wait_all(done)


def branch(part, gnown, res, cot, wo):
    tall = ((256, 1024), f32)
    low = ((256, 1024), bf)
    return call(
        branch_kernel, "branch", [tall, ((4, 256, 256), bf)],
        [low, tall, tall, low, ((1024, 1024), bf), tall, ((4, 256, 256), bf)],
        [7], 1, (part, gnown, res, cot, wo), 32, 1,
    )


def update_kernel(coeff_ref, wide_ref, mg, mu, md, wg, wu, wd, *refs):
    outs, (gg, gu, gd, ng, nu, nd, og, ou, od), sems = refs[:9], refs[9:18], refs[18]
    coeff = coeff_ref[0]
    go = Copies(sems)
    done = []
    part = FF2 // 4

    def finish(i, grad, moment, weight, new_moment, new_weight):
        done.append(go.start(grad, outs[i]))
        moved = coeff * moment[...] + grad[...]
        new_moment[...] = moved
        done.append(go.start(new_moment, outs[3 + i]))
        new_weight[...] = (weight[...].astype(f32) - LEARN_RATE * moved).astype(bf)
        done.append(go.start(new_weight, outs[6 + i]))

    for i, (grad, moment, weight, nm, nw) in enumerate(((gg, mg, wg, ng, og), (gu, mu, wu, nu, ou))):
        for side in range(2):
            columns = wide_ref[:, FF2 * (2 * side + i) : FF2 * (2 * side + i + 1)].astype(f32)
            for j in range(4):
                low = part * (2 * j + side)
                grad[:, low : low + part] = columns[:, part * j : part * j + part]
        finish(i, grad, moment, weight, nm, nw)
    for j in range(3):
        rows = min(32, 88 - 32 * j)
        low = 4 * FF2 + 1024 * j
        gd[32 * j : 32 * j + rows, :] = wide_ref[:, low : low + 1024].astype(f32)[0:rows]
    finish(2, gd, md, wd, nd, od)
    wait_all(done)


def update(coeff, wide, moments, weights):
    shapes = [(32, 2 * FF2), (32, 2 * FF2), (88, 1024)]
    outs = [(s, f32) for s in shapes] * 2 + [(s, bf) for s in shapes]
    vmem = pl.BlockSpec(memory_space=pltpu.VMEM)
    return pl.pallas_call(
        update_kernel,
        out_shape=tuple(pltpu.HBM(*o) for o in outs),
        in_specs=[pl.BlockSpec(memory_space=pltpu.SMEM)] + [vmem] * 7,
        out_specs=(MAIN,) * 9,
        scratch_shapes=[pltpu.VMEM(*o) for o in outs] + [pltpu.SemaphoreType.DMA((9,))],
        compiler_params=pltpu.CompilerParams(vmem_limit_bytes=16 << 20),
        cost_estimate=pl.CostEstimate(flops=1 << 20, bytes_accessed=6 << 20, transcendentals=0),
        name="update",
    )(coeff, wide, *moments, *weights)


def swap(array, bit):
    return lax.ppermute(array, "dp", [(i, i ^ bit) for i in range(8)])


def shift(array, bits):
    return lax.ppermute(array, "ctx", [(i, i ^ bits) for i in range(4)])


def add_low(left, right):
    return (left.astype(f32) + right.astype(f32)).astype(bf)


def split_even(matrix):
    n = matrix.shape[1] // 8
    parts = [matrix[:, n * i : n * i + n] for i in range(8)]
    return jnp.concatenate(parts[0::2], axis=1), jnp.concatenate(parts[1::2], axis=1)


def tie(value, *anchors):
    return lax.optimization_barrier((value, *anchors))[0]


def fast_device(
    activations,
    block_ids,
    cotangent,
    w_query,
    w_key,
    w_value,
    w_out,
    w_gate,
    w_up,
    w_down,
    m_query,
    m_key,
    m_value,
    m_out,
    m_gate,
    m_up,
    m_down,
    clip_threshold,
    momentum_coeff,
):
    me = lax.axis_index("dp")
    z = lax.axis_index("ctx")
    core = me % 2
    _, span, width = activations.shape
    length = block_ids.shape[1]
    act = activations.reshape(span, width)
    cot = cotangent.reshape(span, width)
    act_other = swap(act, 1)
    cot_other = swap(cot, 1)
    g0, g1 = split_even(w_gate)
    u0, u1 = split_even(w_up)
    even = jnp.stack([g0, u0])
    odd = jnp.stack([g1, u1])
    flip = core == 1
    mine = jnp.where(flip, odd, even)
    other = swap(jnp.where(flip, even, odd), 1)
    out_rows = jnp.stack([w_out[:, :512], w_out[:, 512:]]).reshape(2, 32, 2, 256)
    wide = jnp.stack([mine, other], axis=1)
    wide = jnp.concatenate([wide, out_rows.transpose(0, 2, 1, 3)], axis=3)
    wide = lax.all_gather(wide, "ctx", axis=2, tiled=True).reshape(2, 256, FF2 + 256)
    padded = jnp.concatenate([act, w_down], axis=0)
    rows_all = lax.all_gather(padded, "ctx", axis=0, tiled=True)
    heads = jnp.stack(
        [
            jnp.concatenate([w[:, 256 * i : 256 * i + 256] for w in (w_query, w_key, w_value)], 1)
            for i in range(4)
        ]
    )
    heads = lax.all_to_all(heads, "ctx", 0, 0, tiled=True).reshape(128, 768)
    hx = swap(heads, 2)
    hy = swap(jnp.concatenate([heads, hx], axis=0), 4)
    four = jnp.concatenate([heads, hy[:128], hx, hy[128:]], axis=0)
    heads_rel = jnp.concatenate([four, swap(four, 1)], axis=0)
    cosine, sine = rotary_tables(jnp.arange(length, dtype=jnp.int32), HEAD_DIM)
    cosine = jnp.concatenate([cosine] * 4, axis=1)
    sine = jnp.concatenate([-sine, sine, -sine, sine], axis=1)
    ids = jnp.broadcast_to(block_ids, (8, length)).astype(f32)
    wide, act_other, cot_other, heads_rel, cosine, sine, ids = lax.optimization_barrier(
        (wide, act_other, cot_other, heads_rel, cosine, sine, ids)
    )

    wide_x, wide_y = swap(wide, 2), swap(wide, 4)
    wide_all = [wide, wide_x, wide_y, swap(wide_x[0], 4), swap(wide_y[1], 2)]
    down = jnp.concatenate([rows_all[344 * i + 256 : 344 * i + 344] for i in range(4)], axis=0)
    down_x, down_y = swap(down, 2), swap(down, 4)
    rows_all, *wide_all = lax.optimization_barrier((rows_all, *wide_all))
    normed, mixed, attended, totals, peaks, outs = attend(
        rows_all, heads_rel, cosine, sine, ids, wide_all
    )
    outs = swap(outs, 1)
    attended, down_x, down_y = lax.optimization_barrier((attended, down_x, down_y))
    down_all = [down, down_x, down_y, swap(down_x[:, :512], 4), swap(down_y[:, 512:], 2)]
    attended = lax.all_to_all(attended.reshape(4, span, 256), "ctx", 0, 0, tiled=True)
    attended_other = swap(tie(attended, *down_all[3:]), 1)
    part, back_own, residual, full_out, hidden, ga_keep, ga_send, gb_keep, gb_send = feed(
        attended, attended_other, act, act_other, cot, cot_other,
        wide_all, down_all, outs,
    )
    part = swap(part, 1)
    ga_send, gb_send, part = lax.optimization_barrier((ga_send, gb_send, part))
    ga_other = swap(ga_send, 2)
    gb_other = swap(gb_send, 4)
    grad_residual, grad_attended = branch(part, back_own, residual, cot, full_out)
    grad_attended = lax.all_to_all(grad_attended, "ctx", 0, 0, tiled=True).reshape(length, 256)
    (out_part, out_own, gda_keep, gda_send, gdb_keep, gdb_send, go_keep, go_send) = finish(
        hidden, cot, cot_other, attended, grad_residual, down_all
    )
    gda_other = swap(gda_send, 2)
    gdb_other = swap(gdb_send, 4)
    grad_attended, out_part = lax.optimization_barrier((grad_attended, out_part))
    layer_out = (residual + (out_own + swap(out_part, 1).astype(f32))).astype(bf)
    grad_mixed, grad_normed = attend_back(
        mixed, grad_attended, totals, cosine, sine, ids, heads_rel
    )
    grad_mixed = tie(grad_mixed, ga_other, gb_other)
    grad_heads = project_weights(grad_mixed, normed, go_keep, go_send)
    ga_keep, gb_keep, gda_keep, gdb_keep, grad_heads = lax.optimization_barrier(
        (ga_keep, gb_keep, gda_keep, gdb_keep, grad_heads)
    )
    grad_a = add_low(ga_keep, ga_other)
    grad_b = add_low(gb_keep, gb_other)
    grad_da = add_low(gda_keep, gda_other)
    grad_db = add_low(gdb_keep, gdb_other)
    grad_a = add_low(grad_a[:256], swap(grad_a[256:], 4))
    grad_b = add_low(grad_b[:256], swap(grad_b[256:], 2))
    grad_da = add_low(grad_da[:352], swap(grad_da[352:], 4))
    grad_db = add_low(grad_db[:352], swap(grad_db[352:], 2))
    def core_rows(which):
        return jnp.concatenate(
            [lax.dynamic_slice_in_dim(g, which * 128, 128, 0) for g in (grad_a, grad_b)], axis=1
        )

    own_half = core_rows(core)
    other_half = swap(core_rows(1 - core), 1)
    grad_d = jnp.concatenate([grad_da, grad_db], axis=1).reshape(4, 88, width)
    grad_d = jnp.pad(grad_d, ((0, 0), (0, 8), (0, 0))).reshape(4, 3, 32, width)
    grad_d = grad_d.transpose(0, 2, 1, 3).reshape(128, 3 * width)
    grad_wide = jnp.concatenate(
        [
            jnp.where(flip, other_half, own_half),
            jnp.where(flip, own_half, other_half),
            grad_d,
        ],
        axis=1,
    )
    grad_wide = lax.psum_scatter(grad_wide, "ctx", scatter_dimension=0, tiled=True)
    peaks = tie(peaks, ga_other)
    peaks = lax.all_to_all(
        jnp.broadcast_to(peaks[None], (32, 8, 128)), ("dp", "ctx"), 0, 0, tiled=True
    )
    head_peaks = jnp.max(peaks.reshape(8, 4, 8, 128), axis=0)[:, :4, 0].reshape(HEADS)
    grad_normed = lax.psum_scatter(grad_normed, "ctx", scatter_dimension=0, tiled=True)
    tokens_wide = act.astype(f32)
    unused, first_pull = jax.vjp(normalize, tokens_wide)
    input_grad = grad_residual + first_pull(grad_normed.astype(f32))[0]
    grad_heads = add_low(grad_heads[0], swap(grad_heads[1], 1))
    grad_heads = add_low(grad_heads[:256], swap(grad_heads[256:], 2))
    grad_heads = add_low(grad_heads[:128], swap(grad_heads[128:], 4))
    grad_heads = lax.all_to_all(grad_heads.reshape(4, 32, 768 + width), "ctx", 0, 0, tiled=True)
    big = update(
        momentum_coeff.reshape(1), grad_wide, (m_gate, m_up, m_down), (w_gate, w_up, w_down)
    )
    grad_heads, *big = lax.optimization_barrier((grad_heads, *big))
    grad_heads = grad_heads.astype(f32)
    parts = grad_heads[:, :, 768:]
    grad_out = parts[0] + parts[1] + (parts[2] + parts[3])
    grad_qkv = [
        jnp.concatenate([grad_heads[i, :, 256 * k : 256 * k + 256] for i in range(4)], axis=1)
        for k in range(3)
    ]
    weight_grads = (*grad_qkv, grad_out)
    moments = (m_query, m_key, m_value, m_out)
    new_moments = tuple(
        (momentum_coeff * moment + gradient for moment, gradient in zip(moments, weight_grads))
    )
    head_scale = jnp.sqrt(clip_threshold / jnp.maximum(head_peaks, clip_threshold))
    column_scale = jnp.repeat(head_scale, HEAD_DIM)
    rates = (LEARN_RATE, LEARN_RATE, LEARN_RATE, OUT_RATE)
    shard_list = (w_query, w_key, w_value, w_out)
    updated = [
        matrix.astype(jnp.float32) - rate * moment
        for matrix, moment, rate in zip(shard_list, new_moments, rates)
    ]
    updated[0] = updated[0] * column_scale[None, :]
    updated[1] = updated[1] * column_scale[None, :]
    updated = [matrix.astype(bf) for matrix in updated]
    return (
        layer_out[None],
        input_grad[None],
        *weight_grads,
        *big[:3],
        *new_moments,
        *big[3:6],
        *updated,
        *big[6:],
        head_peaks,
        head_scale,
    )


def solution(mesh):
    placed = (
        P("dp", "ctx", None),
        P("dp", None),
        P("dp", "ctx", None),
        P(("dp", "ctx"), None),
        P(("dp", "ctx"), None),
        P(("dp", "ctx"), None),
        P(("dp", "ctx"), None),
        P(("dp", "ctx"), None),
        P(("dp", "ctx"), None),
        P(("dp", "ctx"), None),
        P(("dp", "ctx"), None),
        P(("dp", "ctx"), None),
        P(("dp", "ctx"), None),
        P(("dp", "ctx"), None),
        P(("dp", "ctx"), None),
        P(("dp", "ctx"), None),
        P(("dp", "ctx"), None),
        P(),
        P(),
    )
    fits = mesh.shape["dp"] == 8 and mesh.shape["ctx"] == 4
    return jax.shard_map(
        fast_device if fits else per_device,
        mesh=mesh,
        in_specs=placed,
        out_specs=(
            P("dp", "ctx", None),
            P("dp", "ctx", None),
            P(("dp", "ctx"), None),
            P(("dp", "ctx"), None),
            P(("dp", "ctx"), None),
            P(("dp", "ctx"), None),
            P(("dp", "ctx"), None),
            P(("dp", "ctx"), None),
            P(("dp", "ctx"), None),
            P(("dp", "ctx"), None),
            P(("dp", "ctx"), None),
            P(("dp", "ctx"), None),
            P(("dp", "ctx"), None),
            P(("dp", "ctx"), None),
            P(("dp", "ctx"), None),
            P(("dp", "ctx"), None),
            P(("dp", "ctx"), None),
            P(("dp", "ctx"), None),
            P(("dp", "ctx"), None),
            P(("dp", "ctx"), None),
            P(("dp", "ctx"), None),
            P(("dp", "ctx"), None),
            P(("dp", "ctx"), None),
            P(),
            P(),
        ),
        check_vma=False,
    )
```

```python
import math

import jax
import jax.numpy as jnp
from jax import lax
from jax.experimental import pallas as pl
from jax.experimental.pallas import tpu as pltpu
from jax.sharding import PartitionSpec as P

HEADS = 16
HEAD_DIM = 64


NORM_EPS = 1e-05
ROPE_BASE = 10000.0
LEARN_RATE = 0.0001
OUT_RATE = 0.0016
MASK_FILL = -1e30


def normalize(values):
    centred = values - jnp.mean(values, axis=-1, keepdims=True)
    spread = jnp.mean(centred * centred, axis=-1, keepdims=True)
    return centred * lax.rsqrt(spread + NORM_EPS)


def rotary_tables(positions, head_width):
    half_width = head_width // 2
    frequency = ROPE_BASE ** (-(jnp.arange(half_width, dtype=jnp.float32) * 2.0 / head_width))
    angles = positions.astype(jnp.float32)[:, None] * frequency[None, :]
    return (jnp.cos(angles), jnp.sin(angles))


def rotate(vectors, cosine, sine_table):
    half_width = vectors.shape[-1] // 2
    first_half = vectors[..., :half_width]
    second = vectors[..., half_width:]
    cos_wide = cosine[:, None, :]
    sin_wide = sine_table[:, None, :]
    return jnp.concatenate(
        [first_half * cos_wide - second * sin_wide, second * cos_wide + first_half * sin_wide],
        axis=-1,
    )


def swiglu(gate_proj, up_proj):
    return jax.nn.silu(gate_proj) * up_proj


def project(left_rows, matrix):
    return jnp.dot(left_rows, matrix, preferred_element_type=jnp.float32)


def project_back(grad_rows, matrix):
    return lax.dot_general(
        grad_rows, matrix, (((1,), (1,)), ((), ())), preferred_element_type=jnp.float32
    )


def shard_gradient(left_rows, right_rows):
    return lax.psum_scatter(
        lax.dot_general(
            left_rows, right_rows, (((0,), (0,)), ((), ())), preferred_element_type=jnp.float32
        ),
        ("dp", "ctx"),
        scatter_dimension=0,
        tiled=True,
    )


def per_device(
    activations,
    block_ids,
    cotangent,
    w_query,
    w_key,
    w_value,
    w_out,
    w_gate,
    w_up,
    w_down,
    m_query,
    m_key,
    m_value,
    m_out,
    m_gate,
    m_up,
    m_down,
    clip_threshold,
    momentum_coeff,
):
    shard_list = (w_query, w_key, w_value, w_out, w_gate, w_up, w_down)
    gathered = (
        lax.all_gather(shard_list[0], ("dp", "ctx"), axis=0, tiled=True),
        lax.all_gather(shard_list[1], ("dp", "ctx"), axis=0, tiled=True),
        lax.all_gather(shard_list[2], ("dp", "ctx"), axis=0, tiled=True),
        lax.all_gather(shard_list[3], ("dp", "ctx"), axis=0, tiled=True),
        lax.all_gather(shard_list[4], ("dp", "ctx"), axis=0, tiled=True),
        lax.all_gather(shard_list[5], ("dp", "ctx"), axis=0, tiled=True),
        lax.all_gather(shard_list[6], ("dp", "ctx"), axis=0, tiled=True),
    )
    full_query, full_key, full_value, full_out, full_gate, full_up, full_down = gathered
    seq_count, span_len, model_width = activations.shape
    ctx_place = lax.axis_index("ctx")
    positions = ctx_place * span_len + jnp.arange(span_len, dtype=jnp.int32)
    cosine, sine_table = rotary_tables(positions, HEAD_DIM)
    score_scale = 1.0 / math.sqrt(HEAD_DIM)

    def split_heads(matrix):
        return matrix.reshape(seq_count, span_len, HEADS, HEAD_DIM)

    tokens_flat = activations.astype(jnp.float32).reshape(-1, model_width)
    normed = normalize(tokens_flat).astype(jnp.bfloat16)
    queries = rotate(split_heads(project(normed, full_query)), cosine, sine_table).astype(
        jnp.bfloat16
    )
    key_rot = rotate(split_heads(project(normed, full_key)), cosine, sine_table).astype(
        jnp.bfloat16
    )
    value_rot = split_heads(project(normed, full_value)).astype(jnp.bfloat16)
    key_all, value_all = (
        lax.all_gather(key_rot, "ctx", axis=1, tiled=True),
        lax.all_gather(value_rot, "ctx", axis=1, tiled=True),
    )
    query_ids = lax.dynamic_slice_in_dim(block_ids, ctx_place * span_len, span_len, 1)
    allowed = (block_ids[:, None, :] <= query_ids[:, :, None])[:, None]

    def masked_scores():
        scores = (
            jnp.einsum("sqhd,skhd->shqk", queries, key_all, preferred_element_type=jnp.float32)
            * score_scale
        )
        return jnp.where(allowed, scores, MASK_FILL)

    masked = masked_scores()
    local_peaks = jnp.max(masked, axis=(0, 2, 3))
    row_top = jnp.max(masked, axis=-1, keepdims=True)
    log_total = row_top + jnp.log(jnp.sum(jnp.exp(masked - row_top), axis=-1, keepdims=True))
    probs_low = jnp.exp(masked - log_total).astype(jnp.bfloat16)
    attended = jnp.einsum(
        "shqk,skhd->sqhd", probs_low, value_all, preferred_element_type=jnp.float32
    )
    attended_low = attended.reshape(-1, model_width).astype(jnp.bfloat16)
    head_peaks = lax.pmax(local_peaks, ("dp", "ctx"))
    residual = tokens_flat + project(attended_low, full_out)
    normed2 = normalize(residual).astype(jnp.bfloat16)
    gate_proj = project(normed2, full_gate)
    up_proj = project(normed2, full_up)
    hidden_low = swiglu(gate_proj, up_proj).astype(jnp.bfloat16)
    layer_out = (
        (residual + project(hidden_low, full_down))
        .astype(jnp.bfloat16)
        .reshape(seq_count, span_len, model_width)
    )
    back_weights = (
        lax.all_gather(shard_list[0], ("dp", "ctx"), axis=0, tiled=True),
        lax.all_gather(shard_list[1], ("dp", "ctx"), axis=0, tiled=True),
        lax.all_gather(shard_list[2], ("dp", "ctx"), axis=0, tiled=True),
        lax.all_gather(shard_list[3], ("dp", "ctx"), axis=0, tiled=True),
        lax.all_gather(shard_list[4], ("dp", "ctx"), axis=0, tiled=True),
        lax.all_gather(shard_list[5], ("dp", "ctx"), axis=0, tiled=True),
        lax.all_gather(shard_list[6], ("dp", "ctx"), axis=0, tiled=True),
    )
    back_query, back_key, back_value, back_out, back_gate, back_up, back_down = back_weights
    grad_rows = cotangent.reshape(-1, model_width)
    grad_hidden = project_back(grad_rows, back_down)
    unused, gate_pull = jax.vjp(swiglu, gate_proj, up_proj)
    grad_gate_wide, grad_up_wide = gate_pull(grad_hidden)
    grad_gate_low = grad_gate_wide.astype(jnp.bfloat16)
    grad_up_low = grad_up_wide.astype(jnp.bfloat16)
    grad_normed2 = project_back(grad_gate_low, back_gate) + project_back(grad_up_low, back_up)
    unused, second_pull = jax.vjp(normalize, residual)
    grad_residual = grad_rows.astype(jnp.float32) + second_pull(grad_normed2)[0]
    grad_branch = grad_residual.astype(jnp.bfloat16)
    grad_attended = split_heads(project_back(grad_branch, back_out).astype(jnp.bfloat16))
    masked = masked_scores()
    probs = jnp.exp(masked - log_total)
    probs_again = probs.astype(jnp.bfloat16)
    grad_values_all = jnp.einsum(
        "shqk,sqhd->skhd", probs_again, grad_attended, preferred_element_type=jnp.float32
    )
    grad_probs = jnp.einsum(
        "sqhd,skhd->shqk", grad_attended, value_all, preferred_element_type=jnp.float32
    )
    score_grad = (
        probs * (grad_probs - jnp.sum(probs * grad_probs, axis=-1, keepdims=True))
    ).astype(jnp.bfloat16)
    grad_queries = (
        jnp.einsum("shqk,skhd->sqhd", score_grad, key_all, preferred_element_type=jnp.float32)
        * score_scale
    )
    grad_keys_all = (
        jnp.einsum("shqk,sqhd->skhd", score_grad, queries, preferred_element_type=jnp.float32)
        * score_scale
    )
    grad_keys, grad_values = (
        lax.psum_scatter(
            grad_keys_all.astype(jnp.bfloat16), "ctx", scatter_dimension=1, tiled=True
        ).astype(jnp.float32),
        lax.psum_scatter(
            grad_values_all.astype(jnp.bfloat16), "ctx", scatter_dimension=1, tiled=True
        ).astype(jnp.float32),
    )
    grad_query_low = (
        rotate(grad_queries, cosine, -sine_table).reshape(-1, model_width).astype(jnp.bfloat16)
    )
    grad_key_low = (
        rotate(grad_keys, cosine, -sine_table).reshape(-1, model_width).astype(jnp.bfloat16)
    )
    grad_value_low = grad_values.reshape(-1, model_width).astype(jnp.bfloat16)
    grad_normed = (
        project_back(grad_query_low, back_query)
        + project_back(grad_key_low, back_key)
        + project_back(grad_value_low, back_value)
    )
    unused, first_pull = jax.vjp(normalize, tokens_flat)
    input_grad = (grad_residual + first_pull(grad_normed)[0]).reshape(
        seq_count, span_len, model_width
    )
    weight_grads = (
        shard_gradient(normed, grad_query_low),
        shard_gradient(normed, grad_key_low),
        shard_gradient(normed, grad_value_low),
        shard_gradient(attended_low, grad_branch),
        shard_gradient(normed2, grad_gate_low),
        shard_gradient(normed2, grad_up_low),
        shard_gradient(hidden_low, grad_rows),
    )
    moments = (m_query, m_key, m_value, m_out, m_gate, m_up, m_down)
    new_moments = tuple(
        (momentum_coeff * moment + gradient for moment, gradient in zip(moments, weight_grads))
    )
    head_scale = jnp.sqrt(clip_threshold / jnp.maximum(head_peaks, clip_threshold))
    column_scale = jnp.repeat(head_scale, HEAD_DIM)
    rates = (LEARN_RATE, LEARN_RATE, LEARN_RATE, OUT_RATE, LEARN_RATE, LEARN_RATE, LEARN_RATE)
    updated = [
        matrix.astype(jnp.float32) - rate * moment
        for matrix, moment, rate in zip(shard_list, new_moments, rates)
    ]
    updated[0] = updated[0] * column_scale[None, :]
    updated[1] = updated[1] * column_scale[None, :]
    updated = [matrix.astype(jnp.bfloat16) for matrix in updated]
    return (
        layer_out,
        input_grad,
        weight_grads[0],
        weight_grads[1],
        weight_grads[2],
        weight_grads[3],
        weight_grads[4],
        weight_grads[5],
        weight_grads[6],
        new_moments[0],
        new_moments[1],
        new_moments[2],
        new_moments[3],
        new_moments[4],
        new_moments[5],
        new_moments[6],
        updated[0],
        updated[1],
        updated[2],
        updated[3],
        updated[4],
        updated[5],
        updated[6],
        head_peaks,
        head_scale,
    )


f32=jnp.float32; bf=jnp.bfloat16
NT=(((1,),(1,)),((),())); TN=(((0,),(0,)),((),())); NN=(((1,),(0,)),((),()))
FF2=1408
FFP=1536
FLIPS_A=((0,0),(1,0),(0,1),(1,1))
FLIPS_B=((0,0),(0,1),(1,0),(1,1))
MAIN=pl.BlockSpec(memory_space=pltpu.HBM)
S=jax.ShapeDtypeStruct


def dot(a, b, dims):
    return lax.dot_general(a, b, dims, preferred_element_type=f32)


def aligned(i, m):
    return pl.ds(pl.multiple_of(i * m, m), m)


class Copies:
    def __init__(self, sems):
        self.sems = sems
        self.count = 0

    def start(self, source, target):
        copy = pltpu.make_async_copy(source, target, self.sems.at[self.count])
        self.count += 1
        copy.start()
        return copy


def wait_all(copies):
    for copy in copies:
        copy.wait()


def call(kernel, name, outs, scratch, sems, flops, args, limit, free=0):
    return pl.pallas_call(
        kernel,
        out_shape=tuple(pltpu.HBM(*o) for o in outs),
        in_specs=[pl.BlockSpec(memory_space=pl.ANY)] * free + [MAIN] * (len(args) - free),
        out_specs=(MAIN,) * len(outs),
        scratch_shapes=[pltpu.VMEM(*s) for s in scratch] + [pltpu.SemaphoreType.DMA(n if isinstance(n, tuple) else (n,)) for n in sems],
        compiler_params=pltpu.CompilerParams(vmem_limit_bytes=limit << 20),
        cost_estimate=pl.CostEstimate(flops=flops << 30, bytes_accessed=8 << 20, transcendentals=0),
        name=name,
    )(*args[:free], *(pltpu.with_memory_space_constraint(arg, pltpu.HBM) for arg in args[free:]))


def place_of(p):
    return lax.axis_index("dp") ^ ((p >> 2 & 1) | (p >> 1 & 1) << 1 | (p & 1) << 2)


def turn(values, cosine, signed_sine):
    lane = lax.broadcasted_iota(jnp.int32, cosine.shape, 1)
    first = lane % 64 < 32
    parts = []
    for j in range(values.shape[1] // 128):
        part = values[:, 128 * j : 128 * j + 128]
        partner = jnp.where(first, pltpu.roll(part, 96, 1), pltpu.roll(part, 32, 1))
        parts.append(part * cosine + partner * signed_sine)
    return jnp.concatenate(parts, axis=1)


def layer_norm(x):
    c = x - jnp.mean(x, axis=-1, keepdims=True)
    v = jnp.mean(c * c, axis=-1, keepdims=True)
    return c * lax.rsqrt(v + NORM_EPS)


def wide_pieces(own, by_x, by_y, a_far, b_far):
    return ([own.at[0], by_x.at[0], by_y.at[0], a_far], [own.at[1], by_y.at[1], by_x.at[1], b_far])


def down_pieces(own, by_x, by_y, a_far, b_far):
    low, high = pl.ds(0, 512), pl.ds(512, 512)
    return ([own.at[:, low], by_x.at[:, low], by_y.at[:, low], a_far],
            [own.at[:, high], by_y.at[:, high], by_x.at[:, high], b_far])


def attend_kernel(*refs):
    rows_hbm, weight_hbm, cos_hbm, sin_hbm, id_hbm = refs[:5]
    pieces = sum(wide_pieces(*refs[5:10]), [])
    normed_hbm, mixed_hbm, attended_hbm, total_hbm, peak_hbm, outs_hbm = refs[10:16]
    (act, weight, cos_ref, sin_ref, ids, id_col, normed, mixed_ref, attended, value_t, total_ref,
     peak_ref, outs, sems) = refs[16:]
    n = normed.shape[0]
    go = Copies(sems)
    early = [go.start(rows_hbm.at[pl.ds(344 * i, 256)], act.at[pl.ds(256 * i, 256)]) for i in range(4)]
    middle = [
        go.start(weight_hbm.at[pl.ds(128 * p, 128)], weight.at[aligned(place_of(p), 128)])
        for p in range(8)
    ]
    middle += [go.start(cos_hbm, cos_ref), go.start(sin_hbm, sin_ref), go.start(id_hbm, ids)]
    packs = [go.start(piece.at[:, pl.ds(FF2, 256)], outs.at[i]) for i, piece in enumerate(pieces)]
    wait_all(early)

    def norm(i):
        rows = aligned(i, 256)
        normed[rows, :] = layer_norm(act[rows, :].astype(f32)).astype(bf)

    def mix(i):
        rows = aligned(i, 256)
        mixed = dot(normed[rows, :], weight[...], NN)
        cosine = cos_ref[rows, :]
        sine = sin_ref[rows, :]
        queries = turn(mixed[:, 0:256], cosine, sine).astype(bf)
        mixed_ref[rows, 0:256] = (queries.astype(f32) * 0.125).astype(bf)
        mixed_ref[rows, 256:512] = turn(mixed[:, 256:512], cosine, sine).astype(bf)
        value = mixed[:, 512:768]
        mixed_ref[rows, 512:768] = value.astype(bf)
        value_t[:, rows] = value.T.astype(bf)

    norm(0)
    wait_all(middle)
    wait_all(packs)
    id_col[...] = jnp.broadcast_to(ids[0:1, :], (128, n)).T

    @pl.loop(0, n // 256 - 1)
    def _(i):
        mix(i)
        norm(i + 1)

    mix(n // 256 - 1)
    late = [go.start(normed, normed_hbm), go.start(outs, outs_hbm)]
    late.append(go.start(mixed_ref, mixed_hbm))
    peak_ref[...] = jnp.zeros_like(peak_ref)
    total_ref[...] = jnp.zeros_like(total_ref)

    @pl.loop(0, 2)
    def _(pair):
        lanes = pl.multiple_of(pair * 128, 128)
        lane = lax.broadcasted_iota(jnp.int32, (256, 128), 1)
        best = [None, None]
        for i in range(4):
            width = min(256 * (i + 2), 1024)
            low = 256 * i
            both = mixed_ref[low : low + 256, pl.ds(lanes, 128)]
            keys = mixed_ref[0:width, pl.ds(pl.multiple_of(256 + lanes, 128), 128)]
            values = value_t[pl.ds(lanes, 128), 0:width]
            ok = id_col[low:width, 0:1] <= ids[0:1, low : low + 256]
            outs = []
            for half in range(2):
                q = jnp.where(lane // 64 == half, both, jnp.zeros_like(both))
                s = dot(keys, q, NT)
                tail = jnp.where(ok, s[low:width], MASK_FILL)
                top = jnp.max(tail, axis=0, keepdims=True)
                if i:
                    top = jnp.maximum(top, jnp.max(s[0:low], axis=0, keepdims=True))
                    s = jnp.concatenate([s[0:low], tail], axis=0)
                else:
                    s = tail
                e = jnp.exp(s - top)
                total = jnp.sum(e, axis=0, keepdims=True)
                o = dot(values, e.astype(bf), NN)
                outs.append(o[64 * half : 64 * half + 64] * (1.0 / total))
                total_ref[pl.ds(pair * 2 + half, 1), low : low + 256] = top + jnp.log(total)
                m = jnp.max(top, axis=1, keepdims=True)
                best[half] = m if best[half] is None else jnp.maximum(best[half], m)
            o = jnp.concatenate(outs, axis=0).T.astype(bf)
            attended[low : low + 256, pl.ds(lanes, 128)] = o
        for half in range(2):
            peak_ref[pl.ds(pair * 2 + half, 1), :] = jnp.broadcast_to(best[half], (1, 128))

    late.append(go.start(attended, attended_hbm))
    late.append(go.start(total_ref, total_hbm))
    late.append(go.start(peak_ref, peak_hbm))
    wait_all(late)


def attend(rows_all, weight, cosine, sine, ids, pieces):
    n = cosine.shape[0]
    return call(
        attend_kernel, "attend",
        [((n, 1024), bf), ((n, 768), bf), ((n, 256), bf), ((8, n), f32), ((8, 128), f32),
         ((8, 256, 256), bf)],
        [((n, 1024), bf), ((1024, 768), bf), ((n, 128), f32), ((n, 128), f32), ((8, n), f32),
         ((n, 128), f32), ((n, 1024), bf), ((n, 768), bf), ((n, 256), bf), ((256, n), bf),
         ((8, n), f32), ((8, 128), f32), ((8, 256, 256), bf)],
        [29], 4, (rows_all, weight, cosine, sine, ids, *pieces), 28,
    )


def attend_back_kernel(ga_hbm, mixed_hbm, total_hbm, cos_hbm, sin_hbm, id_hbm, weight_hbm,
                       gm_hbm, gn_hbm,
                       mixed_ref, ga_ref, total_ref, cos_ref, sin_ref, ids, weight,
                       gm_ref, gn_ref, gk_acc, gv_acc, key_t, id_col, sems):
    n = ga_ref.shape[0]
    go = Copies(sems)
    early = [
        go.start(a, b)
        for a, b in ((mixed_hbm, mixed_ref), (ga_hbm, ga_ref), (total_hbm, total_ref),
                     (id_hbm, ids), (cos_hbm, cos_ref), (sin_hbm, sin_ref))
    ]
    late = [
        go.start(weight_hbm.at[pl.ds(128 * p, 128)], weight.at[aligned(place_of(p), 128)])
        for p in range(8)
    ]
    gk_acc[...] = jnp.zeros_like(gk_acc)
    gv_acc[...] = jnp.zeros_like(gv_acc)
    wait_all(early)
    id_col[...] = jnp.broadcast_to(ids[0:1, :], (128, n)).T

    @pl.loop(0, n // 256)
    def _(i):
        rows = aligned(i, 256)
        key_t[:, rows] = mixed_ref[rows, 256:512].astype(f32).T.astype(bf)

    @pl.loop(0, 2)
    def _(pair):
        lanes = pl.multiple_of(pair * 128, 128)
        lane = lax.broadcasted_iota(jnp.int32, (256, 128), 1)
        sub = lax.broadcasted_iota(jnp.int32, (128, 256), 0)
        for i in range(4):
            width = min(256 * (i + 2), 1024)
            low = 256 * i
            k = mixed_ref[0:width, pl.ds(pl.multiple_of(256 + lanes, 128), 128)]
            v = mixed_ref[0:width, pl.ds(pl.multiple_of(512 + lanes, 128), 128)]
            q_all = mixed_ref[low : low + 256, pl.ds(lanes, 128)]
            g_all = ga_ref[low : low + 256, pl.ds(lanes, 128)]
            kt = key_t[pl.ds(lanes, 128), 0:width]
            ok = id_col[low:width, 0:1] <= ids[0:1, low : low + 256]

            def one(half, gq):
                mine = lane // 64 == half
                q = jnp.where(mine, q_all, jnp.zeros_like(q_all))
                g = jnp.where(mine, g_all, jnp.zeros_like(g_all))
                s = dot(k, q, NT) - total_ref[pl.ds(pair * 2 + half, 1), low : low + 256]
                tail = jnp.where(ok, s[low:width], MASK_FILL)
                s = jnp.concatenate([s[0:low], tail], axis=0) if i else tail
                p = jnp.exp(s)
                t = p * dot(v, g, NT)
                delta = jnp.sum(t, axis=0, keepdims=True)
                ds = (t - p * delta).astype(bf)
                gv_acc[0:width, pl.ds(lanes, 128)] += dot(p.astype(bf), g, NN)
                gk_acc[0:width, pl.ds(lanes, 128)] += dot(ds, q, NN)
                return jnp.where(sub // 64 == half, dot(kt, ds, NN), gq)

            gq = one(1, one(0, jnp.zeros((128, 256), f32)))
            gq = gq.T * 0.125
            cosine = cos_ref[low : low + 256, :]
            sine = sin_ref[low : low + 256, :]
            gm_ref[low : low + 256, pl.ds(lanes, 128)] = turn(gq, cosine, -sine).astype(bf)

    wait_all(late)

    @pl.loop(0, n // 256)
    def _(i):
        rows = aligned(i, 256)
        cosine = cos_ref[rows, :]
        sine = sin_ref[rows, :]
        gm_ref[rows, 256:512] = turn(gk_acc[rows, :], cosine, -sine).astype(bf)
        gm_ref[rows, 512:768] = gv_acc[rows, :].astype(bf)
        gn_ref[rows, :] = dot(gm_ref[rows, :], weight[...], NT).astype(bf)
        copy = pltpu.make_async_copy(gn_ref.at[rows], gn_hbm.at[rows], sems.at[14 + i])
        copy.start()

    out = pltpu.make_async_copy(gm_ref, gm_hbm, sems.at[18])
    out.start()
    for i in range(4):
        rows = pl.ds(256 * i, 256)
        pltpu.make_async_copy(gn_ref.at[rows], gn_hbm.at[rows], sems.at[14 + i]).wait()
    out.wait()


def attend_back(mixed, ga, total, cosine, sine, ids, weight):
    n = ga.shape[0]
    return call(
        attend_back_kernel, "attend_back",
        [((n, 768), bf), ((n, 1024), bf)],
        [((n, 768), bf), ((n, 256), bf), ((8, n), f32), ((n, 128), f32), ((n, 128), f32),
         ((8, n), f32), ((1024, 768), bf), ((n, 768), bf), ((n, 1024), bf), ((n, 256), f32),
         ((n, 256), f32), ((256, n), bf), ((n, 128), f32)],
        [19], 0, (ga, mixed, total, cosine, sine, ids, weight), 32, 1,
    )


def weights_kernel(gm_hbm, normed_hbm, okeep_hbm, osend_hbm, keep_hbm, send_hbm,
                   gm_ref, normed_ref, gw, okeep, osend, sems):
    go = Copies(sems)
    first = [go.start(gm_hbm, gm_ref), go.start(normed_hbm, normed_ref)]
    second = [go.start(okeep_hbm, okeep), go.start(osend_hbm, osend)]
    wait_all(first + second)
    cols = pl.ds(768, 1024)
    late = [go.start(okeep, keep_hbm.at[:, cols]), go.start(osend, send_hbm.at[:, cols])]

    @pl.loop(0, 4)
    def _(i):
        cols = aligned(i, 256)
        gw[cols, :] = dot(normed_ref[:, cols], gm_ref[...], TN).astype(bf)

    late += [
        go.start(gw.at[aligned(place_of(p), 128)],
                 (keep_hbm if p < 4 else send_hbm).at[pl.ds(128 * (p % 4), 128), pl.ds(0, 768)])
        for p in range(8)
    ]
    wait_all(late)


def project_weights(gm, normed, okeep, osend):
    n = gm.shape[0]
    return call(
        weights_kernel, "project_weights", [((512, 1792), bf)] * 2,
        [((n, 768), bf), ((n, 1024), bf), ((1024, 768), bf), ((512, 1024), bf), ((512, 1024), bf)],
        [14], 1, (gm, normed, okeep, osend), 24,
    )


def feed_kernel(*refs):
    att_hbm, attp_hbm, act_hbm, actp_hbm, cot_hbm, cotp_hbm = refs[:6]
    a_in, b_in = wide_pieces(*refs[6:11])
    da_in, db_in = down_pieces(*refs[11:16])
    outs = refs[16]
    part_hbm, gnown_hbm, res_hbm, wo_hbm, h_hbm = refs[17:22]
    ga_keep, ga_send, gb_keep, gb_send = refs[22:26]
    (wg, wu, wd, wo, att, act, n2, n2t, cot, res_ref, gn_acc, part, dg, du, hidden,
     sems, osem, tsem) = refs[26:]
    me = lax.axis_index("dp")
    core = me % 2
    yx = me // 2
    go = Copies(sems)
    small = []
    for base, src, own in ((0, att_hbm, act_hbm), (256, attp_hbm, actp_hbm)):
        rows = pl.ds(base, 256)
        small += [go.start(src.at[i], att.at[rows, pl.ds(256 * i, 256)]) for i in range(4)]
        small.append(go.start(own, act.at[rows]))
    places = []
    for p in range(4):
        (ax, ay), (bx, by) = FLIPS_A[p], FLIPS_B[p]
        places.append((yx ^ (ax + 2 * ay), yx ^ (bx + 2 * by)))
    for p, (ja, jb) in enumerate(places):
        for which, src, j, col in ((0, a_in[p], ja, 0), (1, b_in[p], jb, 512)):
            for half in range(2):
                cols = pl.ds(col + 256 * half, 256)
                rows = pl.ds(128 * half, 128)
                small.append(go.start(src.at[rows, pl.ds(FF2, 256)], wo.at[aligned(j * 2 + core, 128), cols]))
                small.append(go.start(outs.at[4 * which + p, rows], wo.at[aligned(j * 2 + 1 - core, 128), cols]))
    big = []
    for p, (ja, jb) in enumerate(places):
        for src, dst, j in ((a_in[p], wg, ja), (b_in[p], wu, jb)):
            for half, c in ((0, core), (1, 1 - core)):
                big.append(go.start(src.at[pl.ds(128 * half, 128), pl.ds(0, FF2)],
                                    dst.at[aligned(j * 2 + c, 128), pl.ds(0, FF2)]))
    big += [go.start(cot_hbm, cot.at[pl.ds(0, 256)]), go.start(cotp_hbm, cot.at[pl.ds(256, 256)])]
    for p, (ja, jb) in enumerate(places):
        big.append(go.start(da_in[p], wd.at[aligned(ja, 352), pl.ds(0, 512)]))
        big.append(go.start(db_in[p], wd.at[aligned(jb, 352), pl.ds(512, 512)]))
    wg[:, FF2:FFP] = jnp.zeros((1024, FFP - FF2), bf)
    wu[:, FF2:FFP] = jnp.zeros((1024, FFP - FF2), bf)
    wd[FF2:FFP, :] = jnp.zeros((FFP - FF2, 1024), bf)
    gn_acc[...] = jnp.zeros_like(gn_acc)
    wait_all(small)
    ogo = Copies(osem)
    done = [ogo.start(wo, wo_hbm)]

    @pl.loop(0, 2)
    def _(i):
        rows = aligned(i, 256)
        res = act[rows, :].astype(f32) + dot(att[rows, :], wo[...], NN)
        res_ref[rows, :] = res
        n = layer_norm(res)
        n2[rows, :] = n.astype(bf)
        n2t[:, rows] = n.T.astype(bf)

    done.append(ogo.start(res_ref.at[pl.ds(0, 256)], res_hbm))
    wait_all(big)

    def tile_copies(t, width):
        copies = []
        cols = pl.ds(pl.multiple_of(t * 256, 256), width)
        for q in range(4):
            fx, fy = FLIPS_A[q]
            rows = aligned(yx ^ (fx + 2 * fy), 256)
            for k, src, dst, slot in ((0, dg, ga_send if fx else ga_keep, fy), (1, du, gb_send if fy else gb_keep, fx)):
                copies.append(pltpu.make_async_copy(
                    src.at[rows, cols], dst.at[pl.ds(256 * slot, 256), cols], tsem.at[t, 2 * q + k]))
        copies.append(pltpu.make_async_copy(hidden.at[:, cols], h_hbm.at[:, cols], tsem.at[t, 8]))
        return copies

    last = FFP // 256 - 1

    @pl.loop(0, last + 1)
    def _(t):
        cols = aligned(t, 256)
        g = dot(n2[...], wg[:, cols], NN)
        u = dot(n2[...], wu[:, cols], NN)
        gh = dot(cot[...], wd[cols, :], NT)
        sig = 1.0 / (1.0 + jnp.exp(-g))
        silu = g * sig
        hidden[:, cols] = (silu * u).astype(bf)
        gu = (gh * silu).astype(bf)
        gg = (gh * u * (sig + silu * (1.0 - sig))).astype(bf)
        dg[:, cols] = dot(n2t[...], gg, NN).astype(bf)
        du[:, cols] = dot(n2t[...], gu, NN).astype(bf)

        @pl.when(t < last)
        def _():
            for copy in tile_copies(t, 256):
                copy.start()

        gn_acc[...] += dot(gg, wg[:, cols], NT) + dot(gu, wu[:, cols], NT)

    ends = tile_copies(last, FF2 - 256 * last)
    for copy in ends:
        copy.start()
    part[...] = gn_acc[256:512, :].astype(bf)
    done.append(ogo.start(part, part_hbm))
    done.append(ogo.start(gn_acc.at[pl.ds(0, 256)], gnown_hbm))
    for t in range(last):
        wait_all(tile_copies(t, 256))
    wait_all(ends)
    wait_all(done)


def feed(att, attp, act, actp, cot, cotp, wide, down, outs):
    big = [((1024, FFP), bf), ((1024, FFP), bf), ((FFP, 1024), bf)]
    return call(
        feed_kernel, "feed",
        [((256, 1024), bf), ((256, 1024), f32), ((256, 1024), f32), ((1024, 1024), bf), ((512, FF2), bf)]
        + [((512, FF2), bf)] * 4,
        big + [((1024, 1024), bf), ((512, 1024), bf), ((512, 1024), bf), ((512, 1024), bf), ((1024, 512), bf),
               ((512, 1024), bf), ((512, 1024), f32), ((512, 1024), f32), ((256, 1024), bf)]
        + big[:2] + [((512, FFP), bf)],
        [68, 4, (6, 9)], 12, (att, attp, act, actp, cot, cotp, *wide, *down, outs), 50, 2,
    )


def finish_kernel(*refs):
    h_hbm, cot_hbm, cotp_hbm, att_hbm, gres_hbm = refs[:5]
    da_in, db_in = down_pieces(*refs[5:10])
    part_hbm, own_hbm, gda_keep, gda_send, gdb_keep, gdb_send, keep_hbm, send_hbm = refs[10:18]
    hidden, cot, att, gres, wd, out, part, dd, gw, sems = refs[18:]
    me = lax.axis_index("dp")
    core = me % 2
    yx = me // 2
    go = Copies(sems)
    first = [go.start(h_hbm, hidden), go.start(cot_hbm, cot.at[pl.ds(0, 256)]),
             go.start(cotp_hbm, cot.at[pl.ds(256, 256)])]
    second = []
    for p in range(4):
        (ax, ay), (bx, by) = FLIPS_A[p], FLIPS_B[p]
        second.append(go.start(da_in[p], wd.at[aligned(yx ^ (ax + 2 * ay), 352), pl.ds(0, 512)]))
        second.append(go.start(db_in[p], wd.at[aligned(yx ^ (bx + 2 * by), 352), pl.ds(512, 512)]))
    third = [go.start(gres_hbm, gres)]
    third += [go.start(att_hbm.at[i], att.at[:, pl.ds(256 * i, 256)]) for i in range(4)]
    wait_all(first)
    done = []

    @pl.loop(0, FF2 // 128)
    def _(t):
        cols = aligned(t, 128)
        dd[cols, :] = dot(hidden[:, cols], cot[...], TN).astype(bf)

    for q in range(4):
        fx, fy = FLIPS_A[q]
        rows = aligned(yx ^ (fx + 2 * fy), 352)
        done.append(go.start(dd.at[rows, pl.ds(0, 512)], (gda_send if fx else gda_keep).at[pl.ds(352 * fy, 352)]))
        done.append(go.start(dd.at[rows, pl.ds(512, 512)], (gdb_send if fy else gdb_keep).at[pl.ds(352 * fx, 352)]))
    wait_all(second)
    part[...] = dot(hidden[256:512, :], wd[...], NN).astype(bf)
    done.append(go.start(part, part_hbm))
    out[...] = dot(hidden[0:256, :], wd[...], NN)
    done.append(go.start(out, own_hbm))
    wait_all(third)
    low = gres[...].astype(bf)

    @pl.loop(0, 4)
    def _(i):
        cols = aligned(i, 256)
        gw[cols, :] = dot(att[:, cols], low, TN).astype(bf)

    for q in range(4):
        fx, fy = FLIPS_A[q]
        j = yx ^ (fx + 2 * fy)
        for dst, c in ((keep_hbm, core), (send_hbm, 1 - core)):
            done.append(go.start(gw.at[aligned(j * 2 + c, 128)], dst.at[pl.ds(128 * (2 * fx + fy), 128)]))
    wait_all(done)


def finish(hidden, cot, cotp, att, gres, down):
    tall = ((256, 1024), f32)
    low = ((256, 1024), bf)
    half = ((512, 1024), bf)
    return call(
        finish_kernel, "finish",
        [low, tall] + [((704, 512), bf)] * 4 + [half] * 2,
        [((512, FF2), bf), half, low, tall, ((FF2, 1024), bf), tall, low, ((FF2, 1024), bf), ((1024, 1024), bf)],
        [34], 60, (hidden, cot, cotp, att, gres, *down), 32,
    )


def branch_kernel(part_hbm, gnown_hbm, res_hbm, cot_hbm, wo_hbm, gres_hbm, gatt_hbm,
                  part, gnown, res_ref, cot, wo, gres_ref, gatt, sems):
    go = Copies(sems)
    first = [
        go.start(a, b)
        for a, b in ((res_hbm, res_ref), (gnown_hbm, gnown), (part_hbm, part), (cot_hbm, cot))
    ]
    late = go.start(wo_hbm, wo)
    wait_all(first)
    res = res_ref[...]
    g = gnown[...] + part[...].astype(f32)
    c = res - jnp.mean(res, axis=-1, keepdims=True)
    r = lax.rsqrt(jnp.mean(c * c, axis=-1, keepdims=True) + NORM_EPS)
    xh = c * r
    d = r * (g - jnp.mean(g, axis=-1, keepdims=True) - xh * jnp.mean(g * xh, axis=-1, keepdims=True))
    gres = cot[...].astype(f32) + d
    gres_ref[...] = gres
    low = gres.astype(bf)
    done = [go.start(gres_ref, gres_hbm)]
    late.wait()
    ga = dot(low, wo[...], NT).astype(bf)
    for z in range(4):
        gatt[z] = ga[:, 256 * z : 256 * z + 256]
    done.append(go.start(gatt, gatt_hbm))
    wait_all(done)


def branch(part, gnown, res, cot, wo):
    tall = ((256, 1024), f32)
    low = ((256, 1024), bf)
    return call(
        branch_kernel, "branch", [tall, ((4, 256, 256), bf)],
        [low, tall, tall, low, ((1024, 1024), bf), tall, ((4, 256, 256), bf)],
        [7], 1, (part, gnown, res, cot, wo), 32, 1,
    )


def update_kernel(coeff_ref, wide_ref, mg, mu, md, wg, wu, wd, *refs):
    outs, (gg, gu, gd, ng, nu, nd, og, ou, od), sems = refs[:9], refs[9:18], refs[18]
    coeff = coeff_ref[0]
    go = Copies(sems)
    done = []
    part = FF2 // 4

    def finish(i, grad, moment, weight, new_moment, new_weight):
        done.append(go.start(grad, outs[i]))
        moved = coeff * moment[...] + grad[...]
        new_moment[...] = moved
        done.append(go.start(new_moment, outs[3 + i]))
        new_weight[...] = (weight[...].astype(f32) - LEARN_RATE * moved).astype(bf)
        done.append(go.start(new_weight, outs[6 + i]))

    for i, (grad, moment, weight, nm, nw) in enumerate(((gg, mg, wg, ng, og), (gu, mu, wu, nu, ou))):
        for side in range(2):
            columns = wide_ref[:, FF2 * (2 * side + i) : FF2 * (2 * side + i + 1)].astype(f32)
            for j in range(4):
                low = part * (2 * j + side)
                grad[:, low : low + part] = columns[:, part * j : part * j + part]
        finish(i, grad, moment, weight, nm, nw)
    for j in range(3):
        rows = min(32, 88 - 32 * j)
        low = 4 * FF2 + 1024 * j
        gd[32 * j : 32 * j + rows, :] = wide_ref[:, low : low + 1024].astype(f32)[0:rows]
    finish(2, gd, md, wd, nd, od)
    wait_all(done)


def update(coeff, wide, moments, weights):
    shapes = [(32, 2 * FF2), (32, 2 * FF2), (88, 1024)]
    outs = [(s, f32) for s in shapes] * 2 + [(s, bf) for s in shapes]
    vmem = pl.BlockSpec(memory_space=pltpu.VMEM)
    return pl.pallas_call(
        update_kernel,
        out_shape=tuple(pltpu.HBM(*o) for o in outs),
        in_specs=[pl.BlockSpec(memory_space=pltpu.SMEM)] + [vmem] * 7,
        out_specs=(MAIN,) * 9,
        scratch_shapes=[pltpu.VMEM(*o) for o in outs] + [pltpu.SemaphoreType.DMA((9,))],
        compiler_params=pltpu.CompilerParams(vmem_limit_bytes=16 << 20),
        cost_estimate=pl.CostEstimate(flops=1 << 20, bytes_accessed=6 << 20, transcendentals=0),
        name="update",
    )(coeff, wide, *moments, *weights)


def swap(array, bit):
    return lax.ppermute(array, "dp", [(i, i ^ bit) for i in range(8)])


def shift(array, bits):
    return lax.ppermute(array, "ctx", [(i, i ^ bits) for i in range(4)])


def add_low(left, right):
    return (left.astype(f32) + right.astype(f32)).astype(bf)


def split_even(matrix):
    n = matrix.shape[1] // 8
    parts = [matrix[:, n * i : n * i + n] for i in range(8)]
    return jnp.concatenate(parts[0::2], axis=1), jnp.concatenate(parts[1::2], axis=1)


def tie(value, *anchors):
    return lax.optimization_barrier((value, *anchors))[0]


def fast_device(
    activations,
    block_ids,
    cotangent,
    w_query,
    w_key,
    w_value,
    w_out,
    w_gate,
    w_up,
    w_down,
    m_query,
    m_key,
    m_value,
    m_out,
    m_gate,
    m_up,
    m_down,
    clip_threshold,
    momentum_coeff,
):
    me = lax.axis_index("dp")
    z = lax.axis_index("ctx")
    core = me % 2
    _, span, width = activations.shape
    length = block_ids.shape[1]
    act = activations.reshape(span, width)
    cot = cotangent.reshape(span, width)
    act_other = swap(act, 1)
    cot_other = swap(cot, 1)
    g0, g1 = split_even(w_gate)
    u0, u1 = split_even(w_up)
    even = jnp.stack([g0, u0])
    odd = jnp.stack([g1, u1])
    flip = core == 1
    mine = jnp.where(flip, odd, even)
    other = swap(jnp.where(flip, even, odd), 1)
    out_rows = jnp.stack([w_out[:, :512], w_out[:, 512:]]).reshape(2, 32, 2, 256)
    wide = jnp.stack([mine, other], axis=0)
    wide = jnp.concatenate([wide, out_rows.transpose(2, 0, 1, 3)], axis=3)
    wide = lax.all_gather(wide, "ctx", axis=2, tiled=True).transpose(1, 0, 2, 3).reshape(2, 256, FF2 + 256)
    padded = jnp.concatenate([act, w_down], axis=0)
    rows_all = lax.all_gather(padded, "ctx", axis=0, tiled=True)
    heads = jnp.stack(
        [
            jnp.concatenate([w[:, 256 * i : 256 * i + 256] for w in (w_query, w_key, w_value)], 1)
            for i in range(4)
        ]
    )
    heads = lax.all_to_all(heads, "ctx", 0, 0, tiled=True).reshape(128, 768)
    hx = swap(heads, 2)
    hy = swap(jnp.concatenate([heads, hx], axis=0), 4)
    four = jnp.concatenate([heads, hy[:128], hx, hy[128:]], axis=0)
    heads_rel = jnp.concatenate([four, swap(four, 1)], axis=0)
    cosine, sine = rotary_tables(jnp.arange(length, dtype=jnp.int32), HEAD_DIM)
    cosine = jnp.concatenate([cosine] * 4, axis=1)
    sine = jnp.concatenate([-sine, sine, -sine, sine], axis=1)
    ids = jnp.broadcast_to(block_ids, (8, length)).astype(f32)
    wide, act_other, cot_other, heads_rel, cosine, sine, ids = lax.optimization_barrier(
        (wide, act_other, cot_other, heads_rel, cosine, sine, ids)
    )

    wide_x, wide_y = swap(wide, 2), swap(wide, 4)
    wide_all = [wide, wide_x, wide_y, swap(wide_x[0], 4), swap(wide_y[1], 2)]
    down = jnp.concatenate([rows_all[344 * i + 256 : 344 * i + 344] for i in range(4)], axis=0)
    down_x, down_y = swap(down, 2), swap(down, 4)
    rows_all, *wide_all = lax.optimization_barrier((rows_all, *wide_all))
    normed, mixed, attended, totals, peaks, outs = attend(
        rows_all, heads_rel, cosine, sine, ids, wide_all
    )
    outs = swap(outs, 1)
    attended, down_x, down_y = lax.optimization_barrier((attended, down_x, down_y))
    down_all = [down, down_x, down_y, swap(down_x[:, :512], 4), swap(down_y[:, 512:], 2)]
    attended = lax.all_to_all(attended.reshape(4, span, 256), "ctx", 0, 0, tiled=True)
    attended_other = swap(tie(attended, *down_all[3:]), 1)
    part, back_own, residual, full_out, hidden, ga_keep, ga_send, gb_keep, gb_send = feed(
        attended, attended_other, act, act_other, cot, cot_other,
        wide_all, down_all, outs,
    )
    part = swap(part, 1)
    ga_send, gb_send, part = lax.optimization_barrier((ga_send, gb_send, part))
    ga_other = swap(ga_send, 2)
    gb_other = swap(gb_send, 4)
    grad_residual, grad_attended = branch(part, back_own, residual, cot, full_out)
    grad_attended = lax.all_to_all(grad_attended, "ctx", 0, 0, tiled=True).reshape(length, 256)
    (out_part, out_own, gda_keep, gda_send, gdb_keep, gdb_send, go_keep, go_send) = finish(
        hidden, cot, cot_other, attended, grad_residual, down_all
    )
    gda_other = swap(gda_send, 2)
    gdb_other = swap(gdb_send, 4)
    grad_attended, out_part = lax.optimization_barrier((grad_attended, out_part))
    layer_out = (residual + (out_own + swap(out_part, 1).astype(f32))).astype(bf)
    grad_mixed, grad_normed = attend_back(
        mixed, grad_attended, totals, cosine, sine, ids, heads_rel
    )
    grad_mixed = tie(grad_mixed, ga_other, gb_other)
    grad_heads = project_weights(grad_mixed, normed, go_keep, go_send)
    ga_keep, gb_keep, gda_keep, gdb_keep, grad_heads = lax.optimization_barrier(
        (ga_keep, gb_keep, gda_keep, gdb_keep, grad_heads)
    )
    grad_a = add_low(ga_keep, ga_other)
    grad_b = add_low(gb_keep, gb_other)
    grad_da = add_low(gda_keep, gda_other)
    grad_db = add_low(gdb_keep, gdb_other)
    grad_a = add_low(grad_a[:256], swap(grad_a[256:], 4))
    grad_b = add_low(grad_b[:256], swap(grad_b[256:], 2))
    grad_da = add_low(grad_da[:352], swap(grad_da[352:], 4))
    grad_db = add_low(grad_db[:352], swap(grad_db[352:], 2))
    def core_rows(which):
        return jnp.concatenate(
            [lax.dynamic_slice_in_dim(g, which * 128, 128, 0) for g in (grad_a, grad_b)], axis=1
        )

    own_half = core_rows(core)
    other_half = swap(core_rows(1 - core), 1)
    grad_d = jnp.concatenate([grad_da, grad_db], axis=1).reshape(4, 88, width)
    grad_d = jnp.pad(grad_d, ((0, 0), (0, 8), (0, 0))).reshape(4, 3, 32, width)
    grad_d = grad_d.transpose(0, 2, 1, 3).reshape(128, 3 * width)
    grad_wide = jnp.concatenate(
        [
            jnp.where(flip, other_half, own_half),
            jnp.where(flip, own_half, other_half),
            grad_d,
        ],
        axis=1,
    )
    grad_wide = lax.psum_scatter(grad_wide, "ctx", scatter_dimension=0, tiled=True)
    peaks = tie(peaks, ga_other)
    peaks = lax.all_to_all(
        jnp.broadcast_to(peaks[None], (32, 8, 128)), ("dp", "ctx"), 0, 0, tiled=True
    )
    head_peaks = jnp.max(peaks.reshape(8, 4, 8, 128), axis=0)[:, :4, 0].reshape(HEADS)
    grad_normed = lax.psum_scatter(grad_normed, "ctx", scatter_dimension=0, tiled=True)
    tokens_wide = act.astype(f32)
    unused, first_pull = jax.vjp(normalize, tokens_wide)
    input_grad = grad_residual + first_pull(grad_normed.astype(f32))[0]
    grad_heads = add_low(grad_heads[0], swap(grad_heads[1], 1))
    grad_heads = add_low(grad_heads[:256], swap(grad_heads[256:], 2))
    grad_heads = add_low(grad_heads[:128], swap(grad_heads[128:], 4))
    grad_heads = lax.all_to_all(grad_heads.reshape(4, 32, 768 + width), "ctx", 0, 0, tiled=True)
    big = update(
        momentum_coeff.reshape(1), grad_wide, (m_gate, m_up, m_down), (w_gate, w_up, w_down)
    )
    grad_heads, *big = lax.optimization_barrier((grad_heads, *big))
    grad_heads = grad_heads.astype(f32)
    parts = grad_heads[:, :, 768:]
    grad_out = parts[0] + parts[1] + (parts[2] + parts[3])
    grad_qkv = [
        jnp.concatenate([grad_heads[i, :, 256 * k : 256 * k + 256] for i in range(4)], axis=1)
        for k in range(3)
    ]
    weight_grads = (*grad_qkv, grad_out)
    moments = (m_query, m_key, m_value, m_out)
    new_moments = tuple(
        (momentum_coeff * moment + gradient for moment, gradient in zip(moments, weight_grads))
    )
    head_scale = jnp.sqrt(clip_threshold / jnp.maximum(head_peaks, clip_threshold))
    column_scale = jnp.repeat(head_scale, HEAD_DIM)
    rates = (LEARN_RATE, LEARN_RATE, LEARN_RATE, OUT_RATE)
    shard_list = (w_query, w_key, w_value, w_out)
    updated = [
        matrix.astype(jnp.float32) - rate * moment
        for matrix, moment, rate in zip(shard_list, new_moments, rates)
    ]
    updated[0] = updated[0] * column_scale[None, :]
    updated[1] = updated[1] * column_scale[None, :]
    updated = [matrix.astype(bf) for matrix in updated]
    return (
        layer_out[None],
        input_grad[None],
        *weight_grads,
        *big[:3],
        *new_moments,
        *big[3:6],
        *updated,
        *big[6:],
        head_peaks,
        head_scale,
    )


def solution(mesh):
    placed = (
        P("dp", "ctx", None),
        P("dp", None),
        P("dp", "ctx", None),
        P(("dp", "ctx"), None),
        P(("dp", "ctx"), None),
        P(("dp", "ctx"), None),
        P(("dp", "ctx"), None),
        P(("dp", "ctx"), None),
        P(("dp", "ctx"), None),
        P(("dp", "ctx"), None),
        P(("dp", "ctx"), None),
        P(("dp", "ctx"), None),
        P(("dp", "ctx"), None),
        P(("dp", "ctx"), None),
        P(("dp", "ctx"), None),
        P(("dp", "ctx"), None),
        P(("dp", "ctx"), None),
        P(),
        P(),
    )
    fits = mesh.shape["dp"] == 8 and mesh.shape["ctx"] == 4
    return jax.shard_map(
        fast_device if fits else per_device,
        mesh=mesh,
        in_specs=placed,
        out_specs=(
            P("dp", "ctx", None),
            P("dp", "ctx", None),
            P(("dp", "ctx"), None),
            P(("dp", "ctx"), None),
            P(("dp", "ctx"), None),
            P(("dp", "ctx"), None),
            P(("dp", "ctx"), None),
            P(("dp", "ctx"), None),
            P(("dp", "ctx"), None),
            P(("dp", "ctx"), None),
            P(("dp", "ctx"), None),
            P(("dp", "ctx"), None),
            P(("dp", "ctx"), None),
            P(("dp", "ctx"), None),
            P(("dp", "ctx"), None),
            P(("dp", "ctx"), None),
            P(("dp", "ctx"), None),
            P(("dp", "ctx"), None),
            P(("dp", "ctx"), None),
            P(("dp", "ctx"), None),
            P(("dp", "ctx"), None),
            P(("dp", "ctx"), None),
            P(("dp", "ctx"), None),
            P(),
            P(),
        ),
        check_vma=False,
    )
```
